32 devices in a mesh: ep: 4 (over z), split: 2 (over x), tp: 4 (over y, core).
Axes of the slice: x: 2, y: 2, z: 4, core: 2. Of those that a mesh axis runs over, the one named last changes fastest.
Arguments:
- feats: bfloat16 [2, 16, 1024, 100], P('split', 'ep', 'tp'), may hold values from -6 to 6
- counts: int32 [16, 2], P('ep'), may hold values from 256 to 1024, as said below
- feat_mask: int32 [16, 100], P('ep'), may hold values from 0 to 1, as said below
- cotangent: bfloat16 [2, 16, 1024, 512], P('split', 'ep', 'tp'), may hold values from -6 to 6
- block_weights: float32 [512, 4, 1024], P(('ep', 'split'), 'tp'), may hold values from -4 to 4
- block_moments: float32 [2, 512, 4, 1024], P(None, ('ep', 'split'), 'tp'), may hold values from -1 to 1, as said below
- head_biases: float32 [512, 4], P(('ep', 'split'), 'tp'), may hold values from -1.75 to 1.75
- bias_moments: float32 [2, 512, 4], P(None, ('ep', 'split'), 'tp'), may hold values from -1 to 1, as said below
- encoder: float32 [512, 100], P(('ep', 'split', 'tp')), may hold values from -0.625 to 0.625
- encoder_moments: float32 [2, 512, 100], P(None, ('ep', 'split', 'tp')), may hold values from -1 to 1, as said below
- shared_vectors: float32 [512, 7], P(('ep', 'split', 'tp')), may hold values from -1 to 3
- vector_moments: float32 [2, 512, 7], P(None, ('ep', 'split', 'tp')), may hold values from -1 to 1, as said below
- prompt: float32 [512, 1000], P(('ep', 'split', 'tp')), may hold values from -6 to 6
- prompt_moments: float32 [2, 512, 1000], P(None, ('ep', 'split', 'tp')), may hold values from -1 to 1, as said below
Outputs:
- output: bfloat16 [2, 16, 1024, 512], P('split', 'ep', 'tp')
- input_grad: float32 [2, 16, 1024, 100], P('split', 'ep', 'tp')
- grad_norm: float32 [], replicated
- block_new: float32 [512, 4, 1024], P(('ep', 'split'), 'tp')
- block_first_new: float32 [512, 4, 1024], P(('ep', 'split'), 'tp')
- block_second_new: float32 [512, 4, 1024], P(('ep', 'split'), 'tp')
- block_copy: bfloat16 [512, 4, 1024], P(('ep', 'split'), 'tp')
- biases_new: float32 [512, 4], P(('ep', 'split'), 'tp')
- bias_first_new: float32 [512, 4], P(('ep', 'split'), 'tp')
- bias_second_new: float32 [512, 4], P(('ep', 'split'), 'tp')
- biases_copy: bfloat16 [512, 4], P(('ep', 'split'), 'tp')
- encoder_new: float32 [512, 100], P(('ep', 'split', 'tp'))
- encoder_first_new: float32 [512, 100], P(('ep', 'split', 'tp'))
- encoder_second_new: float32 [512, 100], P(('ep', 'split', 'tp'))
- encoder_copy: bfloat16 [512, 100], P(('ep', 'split', 'tp'))
- vectors_new: float32 [512, 7], P(('ep', 'split', 'tp'))
- vector_first_new: float32 [512, 7], P(('ep', 'split', 'tp'))
- vector_second_new: float32 [512, 7], P(('ep', 'split', 'tp'))
- vectors_copy: bfloat16 [512, 7], P(('ep', 'split', 'tp'))
- prompt_new: float32 [512, 1000], P(('ep', 'split', 'tp'))
- prompt_first_new: float32 [512, 1000], P(('ep', 'split', 'tp'))
- prompt_second_new: float32 [512, 1000], P(('ep', 'split', 'tp'))
- prompt_copy: bfloat16 [512, 1000], P(('ep', 'split', 'tp'))
The draws below stay inside these ranges and needn't reach their ends.
Inputs may be any that keep to these rules, and one draw needn't show every extreme that they name: Column 0 counts an episode's filled context slots and column 1 its filled test slots; filled slots come first. In every draw one episode has every slot filled and another has 256 in both columns. `feat_mask`: an episode uses between 25 and 100 features; one episode uses all of them. `block_moments`: second moments are positive. `bias_moments`: second moments are positive. `encoder_moments`: second moments are positive. `vector_moments`: second moments are positive. `prompt_moments`: second moments are positive.
All inputs are finite; a program needn't handle non-finite values.
Results may differ from the reference program's by a relative error of at most 0.02.
The reference program's roundings to bfloat16 on the way count: a program that leaves them out, or rounds other values in their place, can miss the bound.
Values may be sent and summed in bfloat16 or wider, within the bound.
No kernel may reach another device: no remote copies, remote signals or barrier semaphores. Data moves between devices by JAX's collectives and lax.ppermute only.
A program may use at most 128 MiB of HBM per device.

```python
import jax
import jax.numpy as jnp
from jax import lax

D = 512
HEADS = 4
HEAD = 128
FF = 1024
FEAT = 100
PROMPT = 1000
SLOTS = 1024
ADAM_STEP = 10
EPISODES = 16
SEG = 1024
BIAS_SEG = 512
NKEYS = 2024
NPARAMS = 2665984


def draw_counts(key, part):
    base_key, order_key = jax.random.split(key)
    base_counts = jax.random.randint(base_key, (EPISODES, 2), SLOTS // 4, SLOTS + 1)
    episode_order = jax.random.permutation(order_key, EPISODES)
    full_row = (episode_order == 0)[:, None]
    least_row = (episode_order == 1)[:, None]
    return jnp.where(full_row, SLOTS, jnp.where(least_row, SLOTS // 4, base_counts)).astype(jnp.int32)


def draw_feat_mask(key, part):
    count_key, order_key, rank_key = jax.random.split(key, 3)
    used_counts = jax.random.randint(count_key, (EPISODES,), FEAT // 4, FEAT + 1)
    episode_order = jax.random.permutation(order_key, EPISODES)
    used_counts = jnp.where(episode_order == 0, FEAT, jnp.where(episode_order == 1, FEAT // 4, used_counts))
    rank_keys = jax.random.split(rank_key, EPISODES)
    feature_ranks = jax.vmap(lambda row_key: jax.random.permutation(row_key, FEAT))(rank_keys)
    return (feature_ranks < used_counts[:, None]).astype(jnp.int32)


def draw_block_weights(key, part):
    hidden_units = FF // HEADS
    column = jnp.arange(SEG)
    scale_row = jnp.where(column < 2 * HEAD, 0.8 / D ** 0.5, jnp.where(column < 3 * HEAD, 1.0 / D ** 0.5, jnp.where(column < 4 * HEAD, 6.0 / (HEADS * HEAD) ** 0.5, jnp.where(column < 4 * HEAD + hidden_units, 1.0 / D ** 0.5, 1.0 / FF ** 0.5))))
    values = jax.random.truncated_normal(key, -4.0, 4.0, (D, HEADS, SEG), jnp.float32)
    return values * scale_row


def draw_shared_vectors(key, part):
    random_part = jax.random.truncated_normal(key, -4.0, 4.0, (D, 7), jnp.float32)
    rising = 3.0 ** (jnp.arange(D, dtype=jnp.float32) / (D - 1) - 0.5)
    column = jnp.arange(7)
    gain_values = rising[:, None] * (1.0 + 0.1 * random_part)
    return jnp.where((column == 0) | (column == 2), gain_values, 0.2 * random_part)


def moment_pair(key, shape, grad_scale):
    first_key, second_key = jax.random.split(key)
    first_moment = (1.0 - 0.9) / 0.9 * grad_scale * jax.random.truncated_normal(first_key, -3.0, 3.0, shape, jnp.float32)
    spread_factor = jnp.exp(jax.random.uniform(second_key, shape, jnp.float32, 0.0, jnp.log(4.0)))
    second_moment = (1.0 - 0.999) / 0.999 * grad_scale * grad_scale * spread_factor
    return jnp.stack([first_moment, second_moment])


def draw_block_moments(key, part):
    return moment_pair(key, (D, HEADS, SEG), NPARAMS ** (-0.5))


def draw_bias_moments(key, part):
    return moment_pair(key, (BIAS_SEG, HEADS), 3.0 * NPARAMS ** (-0.5))


def draw_encoder_moments(key, part):
    return moment_pair(key, (D, FEAT), NPARAMS ** (-0.5))


def draw_vector_moments(key, part):
    return moment_pair(key, (D, 7), 3.0 * NPARAMS ** (-0.5))


def draw_prompt_moments(key, part):
    return moment_pair(key, (D, PROMPT), 20.0 / NKEYS * NPARAMS ** (-0.5))


def shard_levels(stream_key, dims, shards, smallest, top_value):
    def one(dim, blocks):
        heights = jax.random.uniform(jax.random.fold_in(jax.random.fold_in(stream_key, 6), dim), (blocks,), jnp.float32, smallest / len(shards), top_value / len(shards))
        return jnp.repeat(jnp.exp(heights), dims[dim] // blocks).reshape((-1,) + (1,) * (len(dims) - dim - 1))

    gain = one(*shards[0])
    for cut in shards[1:]:
        gain = gain * one(*cut)
    return gain


def gaussian(key, shape, width, bound, shards=(), kind=jnp.bfloat16):
    array = jax.random.normal(key, shape, jnp.float32) * width
    if len(shards) > 0:
        array = shard_levels(key, shape, shards, -0.22, 0.18) * array
    return jnp.clip(array, min=-bound, max=bound).astype(kind)


def setup_inputs(seed: int = 0) -> dict:
    key_list = jax.random.split(jax.random.key(seed), 15)
    feats = gaussian(key_list[0], (2, EPISODES, SLOTS, FEAT), 1.0, 6.0, ((0, 2), (1, 4), (2, 4)))
    counts = draw_counts(jax.random.fold_in(key_list[14], 71), 0)
    feat_mask = draw_feat_mask(jax.random.fold_in(key_list[14], 71), 0)
    cotangent = gaussian(key_list[3], (2, EPISODES, SLOTS, D), 1.0, 6.0, ((0, 2), (1, 4), (2, 4)))
    block_weights = draw_block_weights(jax.random.fold_in(key_list[14], 71), 0)
    block_moments = draw_block_moments(jax.random.fold_in(key_list[14], 71), 0)
    head_biases = gaussian(key_list[6], (BIAS_SEG, HEADS), 0.3, 1.75, ((0, 8), (1, 4)), jnp.float32)
    bias_moments = draw_bias_moments(jax.random.fold_in(key_list[14], 71), 0)
    encoder = gaussian(key_list[8], (D, FEAT), FEAT ** -0.5, 0.625, ((0, 32),), jnp.float32)
    encoder_moments = draw_encoder_moments(jax.random.fold_in(key_list[14], 71), 0)
    shared_vectors = draw_shared_vectors(jax.random.fold_in(key_list[14], 71), 0)
    vector_moments = draw_vector_moments(jax.random.fold_in(key_list[14], 71), 0)
    prompt = gaussian(key_list[12], (D, PROMPT), 1.0, 6.0, ((0, 32),), jnp.float32)
    prompt_moments = draw_prompt_moments(jax.random.fold_in(key_list[14], 71), 0)
    return dict(feats=feats, counts=counts, feat_mask=feat_mask, cotangent=cotangent, block_weights=block_weights, block_moments=block_moments, head_biases=head_biases, bias_moments=bias_moments, encoder=encoder, encoder_moments=encoder_moments, shared_vectors=shared_vectors, vector_moments=vector_moments, prompt=prompt, prompt_moments=prompt_moments)


@jax.custom_vjp
def low(v):
    return lax.optimization_barrier(v.astype(jnp.bfloat16)).astype(jnp.float32)

@jax.custom_vjp
def low_back(v):
    return v

def low_keep(v):
    return (low(v), None)

def low_pass(kept, grad):
    return (grad,)

def back_keep(v):
    return (v, None)

def back_low(kept, grad):
    return (low(grad),)
low.defvjp(low_keep, low_pass)
low_back.defvjp(back_keep, back_low)
highest = lax.Precision.HIGHEST
clip_norm = 1.0
beta_one = 0.9
beta_two = 0.999
adam_eps = 1e-08
rate_matrix = 0.15
rate_vector = 0.5
weight_decay = 0.01

def layer_norm(residual, norm_gain, norm_shift):
    centre = lax.optimization_barrier(jnp.mean(residual, axis=-1, keepdims=True))
    centred = residual - centre
    spread = lax.optimization_barrier(jnp.mean(centred * centred, axis=-1, keepdims=True))
    return centred * lax.rsqrt(spread + 1e-05) * norm_gain + norm_shift

def episode(params, episode_item):
    weights, biases, encoder_low, vectors, prompt_low = params
    feat_rows, mask_row, count_pair = episode_item
    hidden_units = FF // HEADS
    feat_ratio = FEAT / jnp.sum(mask_row)
    masked = feat_rows * mask_row
    embedded = feat_ratio * jnp.einsum('gsf,df->gsd', masked, encoder_low, precision=highest) + vectors[:, 6]
    embedded = low_back(embedded)
    rows_low = low(embedded)
    bias_query = biases[0:HEAD].T
    bias_value = biases[HEAD:2 * HEAD].T
    bias_hidden = biases[2 * HEAD:].T
    queries = jnp.einsum('gsd,dhc->gshc', rows_low, weights[:, :, 0:HEAD], precision=highest) + bias_query
    queries = low(low_back(queries))
    context_kv = jnp.einsum('sd,dhc->shc', rows_low[0], weights[:, :, HEAD:3 * HEAD], precision=highest)
    context_keys = low(low_back(context_kv[..., 0:HEAD]))
    context_values = low(low_back(context_kv[..., HEAD:] + bias_value))
    prompt_kv = jnp.einsum('dp,dhc->phc', prompt_low, weights[:, :, HEAD:3 * HEAD], precision=highest)
    key_rows = jnp.concatenate([low(prompt_kv[..., 0:HEAD]), context_keys], axis=0)
    value_rows = jnp.concatenate([low(prompt_kv[..., HEAD:] + bias_value), context_values], axis=0)
    slot_ids = jnp.arange(SLOTS, dtype=jnp.int32)
    key_live = jnp.concatenate([jnp.ones((PROMPT,), dtype=bool), slot_ids < count_pair[0]])
    scores = jnp.einsum('gshc,khc->ghsk', queries, key_rows, precision=highest) * HEAD ** (-0.5)
    scores = low_back(scores)
    scores = jnp.where(key_live, scores, -1e+30)
    attn_probs = low(jax.nn.softmax(scores, axis=-1))
    attended = jnp.einsum('ghsk,khc->gshc', attn_probs, value_rows, precision=highest)
    attended = low(low_back(attended))
    attn_out = jnp.einsum('gshc,dhc->gsd', attended, weights[:, :, 3 * HEAD:4 * HEAD], precision=highest) + vectors[:, 4]
    attn_out = low_back(attn_out)
    normed_first = layer_norm(embedded + attn_out, vectors[:, 0], vectors[:, 1])
    first_low = low(normed_first)
    hidden_pre = jnp.einsum('gsd,dhf->gshf', first_low, weights[:, :, 4 * HEAD:4 * HEAD + hidden_units], precision=highest) + bias_hidden
    hidden_pre = low_back(hidden_pre)
    hidden_act = low(jax.nn.gelu(hidden_pre, approximate=False))
    mlp_out = jnp.einsum('gshf,dhf->gsd', hidden_act, weights[:, :, 4 * HEAD + hidden_units:], precision=highest) + vectors[:, 5]
    mlp_out = low_back(mlp_out)
    normed_final = layer_norm(normed_first + mlp_out, vectors[:, 2], vectors[:, 3])
    row_live = (slot_ids[None, :] < count_pair[:, None]).astype(normed_final.dtype)
    return normed_final * row_live[:, :, None]

def adam_update(weight, moments, gradient, factor, step_rate, decay_rate):
    clipped = gradient * factor
    first_moment = beta_one * moments[0] + (1.0 - beta_one) * clipped
    second_moment = beta_two * moments[1] + (1.0 - beta_two) * clipped * clipped
    first_hat = first_moment / (1.0 - beta_one ** ADAM_STEP)
    second_hat = second_moment / (1.0 - beta_two ** ADAM_STEP)
    updated = weight - step_rate * (first_hat / (jnp.sqrt(second_hat) + adam_eps) + decay_rate * weight)
    return (updated, first_moment, second_moment, updated.astype(jnp.bfloat16))

def reference(feats, counts, feat_mask, cotangent, block_weights, block_moments, head_biases, bias_moments, encoder, encoder_moments, shared_vectors, vector_moments, prompt, prompt_moments):
    mask_rows = feat_mask.astype(jnp.float32)
    checked = jax.checkpoint(episode)

    def forward(weights, biases, encoder_in, vectors, prompt_in, feat_in):
        params = (low(weights), low(biases), low(encoder_in), low(vectors), low(prompt_in))
        episode_items = (jnp.transpose(feat_in, (1, 0, 2, 3)), mask_rows, counts)
        stacked = lax.map(lambda episode_item: checked(params, episode_item), episode_items)
        return jnp.transpose(stacked, (1, 0, 2, 3))
    result, pullback = jax.vjp(forward, block_weights, head_biases, encoder, shared_vectors, prompt, feats.astype(jnp.float32))
    gradients = pullback(cotangent.astype(jnp.float32))
    grad_block, grad_bias, grad_encoder, grad_vectors, grad_prompt, input_grad = gradients
    squares = jnp.sum(grad_block * grad_block) + jnp.sum(grad_bias * grad_bias) + jnp.sum(grad_encoder * grad_encoder) + jnp.sum(grad_vectors * grad_vectors) + jnp.sum(grad_prompt * grad_prompt)
    grad_norm = jnp.sqrt(squares)
    factor = jnp.minimum(1.0, clip_norm / (grad_norm + 1e-06))
    block_new, block_first_new, block_second_new, block_copy = adam_update(block_weights, block_moments, grad_block, factor, rate_matrix, weight_decay)
    biases_new, bias_first_new, bias_second_new, biases_copy = adam_update(head_biases, bias_moments, grad_bias, factor, rate_vector, 0.0)
    encoder_new, encoder_first_new, encoder_second_new, encoder_copy = adam_update(encoder, encoder_moments, grad_encoder, factor, rate_matrix, weight_decay)
    vectors_new, vector_first_new, vector_second_new, vectors_copy = adam_update(shared_vectors, vector_moments, grad_vectors, factor, rate_vector, 0.0)
    prompt_new, prompt_first_new, prompt_second_new, prompt_copy = adam_update(prompt, prompt_moments, grad_prompt, factor, rate_vector, weight_decay)
    return (result.astype(jnp.bfloat16), input_grad, grad_norm, block_new, block_first_new, block_second_new, block_copy, biases_new, bias_first_new, bias_second_new, biases_copy, encoder_new, encoder_first_new, encoder_second_new, encoder_copy, vectors_new, vector_first_new, vector_second_new, vectors_copy, prompt_new, prompt_first_new, prompt_second_new, prompt_copy)
```

```python
import jax
import jax.numpy as jnp
from jax import lax
from jax.sharding import PartitionSpec as P

HEADS = 4
HEAD = 128
FF = 1024
HID = FF // HEADS
FEAT = 100
PROMPT = 1000
SLOTS = 1024
ADAM_STEP = 10
PAD = 1024
WIDE = 128

ln_eps = 1e-05
neg_big = -1e30
clip_norm = 1.0
beta_one = 0.9
beta_two = 0.999
adam_eps = 1e-08
rate_matrix = 0.15
rate_vector = 0.5
weight_decay = 0.01
AXES = ("ep", "split", "tp")
bf16 = jnp.bfloat16
f32 = jnp.float32


def swap(value, ep=0, split=0, row=0, core=0):
    sizes = [lax.axis_size(a) for a in AXES]
    pairs = []
    for a in range(sizes[0]):
        for b in range(sizes[1]):
            for t in range(sizes[2]):
                other = ((a ^ ep) * sizes[1] + (b ^ split)) * sizes[2] + (t ^ (2 * row + core))
                pairs.append(((a * sizes[1] + b) * sizes[2] + t, other))
    return lax.ppermute(value, AXES, pairs)


def pick(low, high, bit):
    return jnp.where(bit == 0, low, high), jnp.where(bit == 0, high, low)


def plane_swap(piece):
    got = {}
    for b in (0, 1):
        for r in (0, 1):
            sent = piece(b, r)
            got[b, r] = sent if (b, r) == (0, 0) else swap(sent, split=b, row=r)
    return got


def gather_ep(shard):
    count = lax.axis_size("ep")
    if count > 4:
        return lax.all_gather(shard, "ep", axis=0)
    place = lax.axis_index("ep")
    parts = [shard] + [swap(shard, ep=k) for k in range(1, count)]
    bit = 1
    while bit < count:
        moved = list(parts)
        for k in range(count):
            if not k & bit:
                moved[k], moved[k | bit] = pick(parts[k], parts[k | bit], (place // bit) % 2)
        parts = moved
        bit *= 2
    return jnp.stack(parts)


def reduce_ep(parts):
    count = lax.axis_size("ep")
    if count > 4:
        return lax.psum_scatter(parts.astype(f32), "ep", scatter_dimension=0, tiled=True)[0]
    place = lax.axis_index("ep")
    total = lax.dynamic_index_in_dim(parts, place, 0, keepdims=False).astype(f32)
    for k in range(1, count):
        piece = lax.dynamic_index_in_dim(parts, place ^ k, 0, keepdims=False)
        total = total + swap(piece, ep=k).astype(f32)
    return total


def norm_rows(residual, norm_gain, norm_shift):
    centre = jnp.mean(residual, axis=-1, keepdims=True)
    centred = residual - centre
    spread = jnp.mean(centred * centred, axis=-1, keepdims=True)
    inverse = lax.rsqrt(spread + ln_eps)
    normed = centred * inverse
    return (normed * norm_gain + norm_shift, normed, inverse)


def norm_back(grad_out, normed, inverse, norm_gain):
    scaled = grad_out * norm_gain
    mean_plain = jnp.mean(scaled, axis=-1, keepdims=True)
    mean_mixed = jnp.mean(scaled * normed, axis=-1, keepdims=True)
    grad_in = inverse * (scaled - mean_plain - normed * mean_mixed)
    return (grad_in, jnp.sum(grad_out * normed, axis=0), jnp.sum(grad_out, axis=0))


def adam_update(weight, moments, gradient, factor, step_rate, decay_rate):
    clipped = gradient * factor
    first_moment = beta_one * moments[0] + (1.0 - beta_one) * clipped
    second_moment = beta_two * moments[1] + (1.0 - beta_two) * clipped * clipped
    first_hat = first_moment / (1.0 - beta_one**ADAM_STEP)
    second_hat = second_moment / (1.0 - beta_two**ADAM_STEP)
    updated = weight - step_rate * (
        first_hat / (jnp.sqrt(second_hat) + adam_eps) + decay_rate * weight
    )
    return (updated, first_moment, second_moment, updated.astype(bf16))


def dot(a, b, dims):
    return lax.dot_general(a, b, (dims, ((), ())), preferred_element_type=f32)


def split_dot(a, b, dims):
    high = a.astype(bf16)
    low = (a - high.astype(f32)).astype(bf16)
    return dot(high, b, dims) + dot(low, b, dims)


def attend(queries, keys, values, bias):
    scale = HEAD**-0.5

    def one(item):
        query, key, value = item
        scores = dot(query, key, ((1,), (1,))) * scale + bias
        top = jnp.max(scores, axis=-1, keepdims=True)
        raised = jnp.exp(scores - top)
        total = jnp.sum(raised, axis=-1, keepdims=True)
        probs = (raised / total).astype(bf16)
        return dot(probs, value, ((1,), (0,))).astype(bf16), top + jnp.log(total)

    return lax.map(one, (queries, keys, values))


def attend_back(queries, keys, values, bias, log_total, grad_out):
    scale = HEAD**-0.5

    def one(item):
        query, key, value, lse, grad = item
        scores = dot(query, key, ((1,), (1,))) * scale + bias
        probs = jnp.exp(scores - lse)
        grad_probs = dot(grad, value, ((1,), (1,)))
        delta = jnp.sum(probs * grad_probs, axis=-1, keepdims=True)
        grad_scores = (probs * (grad_probs - delta)).astype(bf16)
        grad_query = (dot(grad_scores, key, ((1,), (0,))) * scale).astype(bf16)
        grad_key = dot(grad_scores, query, ((0,), (0,))) * scale
        grad_value = dot(probs.astype(bf16), grad, ((0,), (0,)))
        return grad_query, grad_key, grad_value

    return lax.map(one, (queries, keys, values, log_total, grad_out))


def shards(
    feats,
    counts,
    feat_mask,
    cotangent,
    block_weights,
    block_moments,
    head_biases,
    bias_moments,
    encoder,
    encoder_moments,
    shared_vectors,
    vector_moments,
    prompt,
    prompt_moments,
):
    n_ep = lax.axis_size("ep")
    side = lax.axis_index("split")
    row = lax.axis_index("tp") // 2
    core = lax.axis_index("tp") % 2
    chip = side * 2 + row
    rows = feats.shape[2]
    half = 2 * rows
    width = cotangent.shape[3]
    slab = block_weights.shape[0]
    strip = encoder.shape[0]

    def canonical(got):
        first = [jnp.concatenate(pick(got[b, 0], got[b, 1], row), axis=0) for b in (0, 1)]
        return jnp.concatenate(pick(first[0], first[1], side), axis=0)

    def to_chip(array):
        return plane_swap(
            lambda b, r: lax.dynamic_index_in_dim(array[0], chip ^ (2 * b + r), 0, keepdims=False)
        )

    def from_chip(own_rows):
        blocks = own_rows.reshape((4, rows) + own_rows.shape[1:])
        got = plane_swap(
            lambda b, r: lax.dynamic_index_in_dim(blocks, chip ^ (2 * b + r), 0, keepdims=False)
        )
        first = [jnp.stack(pick(got[b, 0], got[b, 1], row)) for b in (0, 1)]
        return jnp.concatenate(pick(first[0], first[1], side), axis=0)[None]

    feats_own = canonical(to_chip(feats))
    mask_row = lax.dynamic_index_in_dim(feat_mask, chip, 0, keepdims=False)
    count_pair = lax.dynamic_index_in_dim(counts, chip, 0, keepdims=False)
    masked_own = feats_own * mask_row.astype(bf16)
    masked_other = swap(masked_own, core=1)
    mask_float = mask_row.astype(f32)
    feat_ratio = FEAT / jnp.sum(mask_float)

    block_low = block_weights[:, 0, :].astype(bf16)
    project_part = block_low[:, 0 : 3 * HEAD]
    rest_part = block_low[:, 3 * HEAD :]
    small_part = jnp.concatenate(
        [
            encoder.astype(bf16),
            shared_vectors.astype(bf16),
            head_biases.astype(bf16).reshape(strip, slab // strip),
        ],
        axis=1,
    )
    small_part = jnp.pad(small_part, ((0, 0), (0, WIDE - small_part.shape[1])))
    prompt_part = prompt.astype(bf16)

    def gather_heads(shard):
        along = gather_ep(shard)
        got = plane_swap(lambda b, r: along)
        return [
            jnp.stack(pick(got[0, r], got[1, r], side), axis=1).reshape(width, shard.shape[1])
            for r in (0, 1)
        ]

    def gather_strips(shard):
        along = gather_ep(shard)
        got = plane_swap(lambda b, r: along)
        by_row = [jnp.stack(pick(got[b, 0], got[b, 1], row), axis=1) for b in (0, 1)]
        both = jnp.stack(pick(by_row[0], by_row[1], side), axis=1)
        other = swap(both, core=1)
        return jnp.stack(pick(both, other, core), axis=3)

    small_all = gather_strips(small_part)
    prompt_low = gather_strips(prompt_part).reshape(width, PROMPT)
    encoder_low = small_all[..., 0:FEAT].reshape(width, FEAT)
    vectors = small_all[..., FEAT : FEAT + 7].reshape(width, 7).astype(f32)
    bias_all = small_all[..., FEAT + 7 : FEAT + 7 + slab // strip].astype(f32)
    bias_all = jnp.transpose(bias_all, (2, 3, 0, 1, 4, 5)).reshape(2, 2, width)

    def by_slot(table):
        rows_first = jnp.stack(pick(table[0], table[1], row))
        cores_first = jnp.stack(pick(rows_first[:, 0], rows_first[:, 1], core))
        return cores_first.reshape(4, table.shape[-1])

    bias_slots = by_slot(bias_all)
    bias_query = bias_slots[0:2, 0:HEAD]
    bias_value = bias_slots[0:2, HEAD : 2 * HEAD]
    bias_hidden = bias_slots[:, 2 * HEAD :].reshape(4 * HID)
    w_project = gather_heads(project_part)
    rest_own = gather_heads(rest_part)
    rest_own = jnp.stack(rest_own)
    rest_other = swap(rest_own, core=1)
    rest_all = jnp.concatenate([rest_own, rest_other], axis=0)
    w_output = jnp.concatenate([rest_all[k, :, 0:HEAD] for k in range(4)], axis=1)
    w_hidden = jnp.concatenate([rest_all[k, :, HEAD : HEAD + HID] for k in range(4)], axis=1)
    w_return = jnp.concatenate([rest_all[k, :, HEAD + HID :] for k in range(4)], axis=1)
    w_query = jnp.concatenate([w[:, 0:HEAD] for w in w_project], axis=1)
    w_key = jnp.concatenate([w[:, HEAD : 2 * HEAD] for w in w_project], axis=1)
    w_value = jnp.concatenate([w[:, 2 * HEAD :] for w in w_project], axis=1)

    masked_all = jnp.concatenate(
        [masked_own[0:half], masked_other[0:half], masked_own[half:], masked_other[half:]], axis=0
    )
    embed_all = feat_ratio * dot(masked_all, encoder_low, ((1,), (1,))) + vectors[:, 6]
    rows_low = embed_all.astype(bf16)
    embedded = jnp.concatenate([embed_all[0:half], embed_all[2 * half : 3 * half]], axis=0)
    context_low = rows_low[0:SLOTS]

    lane = jnp.arange(rows, dtype=jnp.int32)

    def slots_of(which_core):
        return jnp.concatenate([which_core * rows + lane, (2 + which_core) * rows + lane])

    own_slots = slots_of(core)
    key_slots = jnp.concatenate([own_slots, slots_of(1 - core)])
    key_live = jnp.concatenate([jnp.arange(PAD) < PROMPT, key_slots < count_pair[0]])
    key_bias = jnp.where(key_live, 0.0, neg_big)[None, :].astype(f32)
    row_live = jnp.concatenate([own_slots < count_pair[0], own_slots < count_pair[1]])
    row_live = row_live.astype(f32)[:, None]

    query = (dot(rows_low, w_query, ((1,), (0,))) + bias_query.reshape(-1)).astype(bf16)
    key_ctx = dot(context_low, w_key, ((1,), (0,))).astype(bf16)
    value_ctx = (dot(context_low, w_value, ((1,), (0,))) + bias_value.reshape(-1)).astype(bf16)
    key_prompt = dot(prompt_low, w_key, ((0,), (0,))).astype(bf16)
    value_prompt = (dot(prompt_low, w_value, ((0,), (0,))) + bias_value.reshape(-1)).astype(bf16)
    gap = ((0, PAD - PROMPT), (0, 0))
    keys = jnp.concatenate([jnp.pad(key_prompt, gap), key_ctx], axis=0)
    values = jnp.concatenate([jnp.pad(value_prompt, gap), value_ctx], axis=0)

    def heads_first(flat):
        return jnp.stack([flat[:, 0:HEAD], flat[:, HEAD:]])

    def chunked(flat):
        return heads_first(flat).reshape(4, SLOTS, HEAD)

    def doubled(flat):
        stacked = heads_first(flat)
        return jnp.stack([stacked[0], stacked[0], stacked[1], stacked[1]])

    queries = chunked(query)
    keys_four = doubled(keys)
    values_four = doubled(values)
    attended, log_total = attend(queries, keys_four, values_four, key_bias)
    attended = attended.reshape(2, 4, half, HEAD)

    def own_of(array):
        return jnp.concatenate([array[:, 0], array[:, 2]], axis=1)

    def other_of(array):
        return jnp.concatenate([array[:, 1], array[:, 3]], axis=1)

    attended_own = own_of(attended)
    attended_got = swap(other_of(attended), core=1)
    attended_rows = jnp.concatenate(
        [attended_own[0], attended_own[1], attended_got[0], attended_got[1]], axis=1
    )
    attn_out = dot(attended_rows, w_output, ((1,), (1,))) + vectors[:, 4]
    normed_first, normed_one, inverse_one = norm_rows(
        embedded + attn_out, vectors[:, 0], vectors[:, 1]
    )
    first_low = normed_first.astype(bf16)
    hidden_pre = dot(first_low, w_hidden, ((1,), (0,))) + bias_hidden
    hidden_value, gelu_pull = jax.vjp(
        lambda pre_value: jax.nn.gelu(pre_value, approximate=False), hidden_pre
    )
    hidden_act = hidden_value.astype(bf16)
    mlp_out = dot(hidden_act, w_return, ((1,), (1,))) + vectors[:, 5]
    normed_final, normed_two, inverse_two = norm_rows(
        normed_first + mlp_out, vectors[:, 2], vectors[:, 3]
    )
    output_final = from_chip((normed_final * row_live).astype(bf16))

    grad_final = canonical(to_chip(cotangent)).astype(f32) * row_live
    grad_two, gain_two, shift_two = norm_back(grad_final, normed_two, inverse_two, vectors[:, 2])
    grad_mlp = grad_two.astype(bf16)
    bias_two = jnp.sum(grad_mlp.astype(f32), axis=0)
    grad_return = dot(grad_mlp, hidden_act, ((0,), (0,)))
    grad_act = dot(grad_mlp, w_return, ((1,), (0,)))
    grad_pre = gelu_pull(grad_act)[0].astype(bf16)
    grad_bias_hidden = jnp.sum(grad_pre.astype(f32), axis=0)
    grad_hidden = dot(first_low, grad_pre, ((0,), (0,)))
    grad_first = grad_two + dot(grad_pre, w_hidden, ((1,), (1,)))
    grad_one, gain_one, shift_one = norm_back(grad_first, normed_one, inverse_one, vectors[:, 0])
    grad_attn = grad_one.astype(bf16)
    bias_out = jnp.sum(grad_attn.astype(f32), axis=0)
    grad_output = dot(grad_attn, attended_rows, ((0,), (0,)))
    grad_attended = dot(grad_attn, w_output, ((1,), (0,))).astype(bf16)

    def slot_grads(k):
        return jnp.concatenate(
            [
                grad_output[:, k * HEAD : (k + 1) * HEAD],
                grad_hidden[:, k * HID : (k + 1) * HID],
                grad_return[:, k * HID : (k + 1) * HID],
            ],
            axis=1,
        )

    rest_mine = jnp.stack([slot_grads(0), slot_grads(1)])
    rest_sent = jnp.stack([slot_grads(2), slot_grads(3)]).astype(bf16)
    rest_pair = (rest_mine + swap(rest_sent, core=1).astype(f32)).astype(bf16)

    def reduce_heads(pair):
        blocks = pair.reshape(2, n_ep, 2, slab, pair.shape[-1])
        got = plane_swap(
            lambda b, r: lax.dynamic_index_in_dim(blocks[r], side ^ b, 1, keepdims=False)
        )
        total = sum(part.astype(f32) for part in got.values())
        return reduce_ep(total.astype(pair.dtype))

    def reduce_strips(whole):
        blocks = whole.reshape(n_ep, 2, 2, 2, strip, whole.shape[-1])
        mine = lax.dynamic_index_in_dim(blocks, core, 3, keepdims=False)
        sent = lax.dynamic_index_in_dim(blocks, 1 - core, 3, keepdims=False)
        pair = (mine.astype(f32) + swap(sent, core=1).astype(f32)).astype(whole.dtype)

        def piece(b, r):
            half_piece = lax.dynamic_index_in_dim(pair, side ^ b, 1, keepdims=False)
            return lax.dynamic_index_in_dim(half_piece, row ^ r, 1, keepdims=False)

        got = plane_swap(piece)
        total = sum(part.astype(f32) for part in got.values())
        return reduce_ep(total.astype(whole.dtype))

    summed_rest = reduce_heads(rest_pair)

    grad_four = grad_attended.reshape(2, half, 4, HEAD)
    grad_mine = jnp.transpose(grad_four[:, :, 0:2], (2, 0, 1, 3))
    grad_sent = jnp.transpose(grad_four[:, :, 2:4], (2, 0, 1, 3))
    grad_got = swap(grad_sent, core=1)
    grad_heads = jnp.stack([grad_mine, grad_got], axis=2).reshape(4, SLOTS, HEAD)
    grad_query, grad_key, grad_value = attend_back(
        queries, keys_four, values_four, key_bias, log_total, grad_heads
    )
    grad_query = jnp.concatenate(
        [grad_query[0:2].reshape(2 * SLOTS, HEAD), grad_query[2:4].reshape(2 * SLOTS, HEAD)], axis=1
    )
    grad_key = jnp.concatenate([grad_key[0] + grad_key[1], grad_key[2] + grad_key[3]], axis=1)
    grad_value = jnp.concatenate(
        [grad_value[0] + grad_value[1], grad_value[2] + grad_value[3]], axis=1
    )
    grad_prompt_key = grad_key[0:PROMPT]
    grad_prompt_value = grad_value[0:PROMPT]
    context_key = grad_key[PAD:].astype(bf16)
    context_value = grad_value[PAD:].astype(bf16)
    grad_wq = dot(rows_low, grad_query, ((0,), (0,)))
    grad_wk = dot(context_low, context_key, ((0,), (0,)))
    grad_wv = dot(context_low, context_value, ((0,), (0,)))
    grad_wk = grad_wk + split_dot(grad_prompt_key, prompt_low, ((0,), (1,))).T
    grad_wv = grad_wv + split_dot(grad_prompt_value, prompt_low, ((0,), (1,))).T
    grad_prompt = (
        split_dot(grad_prompt_key, w_key, ((1,), (1,)))
        + split_dot(grad_prompt_value, w_value, ((1,), (1,)))
    ).T
    grad_bias_query = jnp.sum(grad_query.astype(f32), axis=0).reshape(2, HEAD)
    grad_bias_value = jnp.sum(context_value.astype(f32), axis=0) + jnp.sum(
        grad_prompt_value, axis=0
    )
    grad_bias_value = grad_bias_value.reshape(2, HEAD)

    back_rows = dot(grad_query, w_query, ((1,), (1,)))
    back_context = dot(context_key, w_key, ((1,), (1,))) + dot(context_value, w_value, ((1,), (1,)))
    back_rows = back_rows.reshape(2, 2, half, width)
    back_context = back_context.reshape(2, half, width)
    back_own = jnp.concatenate([back_rows[0, 0] + back_context[0], back_rows[1, 0]], axis=0)
    back_other = jnp.concatenate([back_rows[0, 1] + back_context[1], back_rows[1, 1]], axis=0)
    back_got = swap(back_other.astype(bf16), core=1).astype(f32)
    grad_input_low = (grad_one + back_own + back_got).astype(bf16)
    grad_encoder = feat_ratio * dot(grad_input_low, masked_own, ((0,), (0,)))
    grad_embed_bias = jnp.sum(grad_input_low.astype(f32), axis=0)
    input_grad = feat_ratio * dot(grad_input_low, encoder_low, ((1,), (0,))) * mask_float
    input_final = from_chip(input_grad)

    project_pair = jnp.stack(
        [
            jnp.concatenate(
                [g[:, k * HEAD : (k + 1) * HEAD] for g in (grad_wq, grad_wk, grad_wv)], axis=1
            )
            for k in (0, 1)
        ]
    ).astype(bf16)
    summed_project = reduce_heads(project_pair)
    summed_block = jnp.concatenate([summed_project, summed_rest], axis=1)[:, None, :]

    grad_vectors = jnp.stack(
        [gain_one, shift_one, gain_two, shift_two, bias_out, bias_two, grad_embed_bias], axis=1
    )
    bias_slots_grad = jnp.concatenate(
        [
            jnp.pad(grad_bias_query, ((0, 2), (0, 0))),
            jnp.pad(grad_bias_value, ((0, 2), (0, 0))),
            grad_bias_hidden.reshape(4, HID),
        ],
        axis=1,
    )
    by_core = bias_slots_grad.reshape(2, 2, width)
    core_ordered = jnp.stack(pick(by_core[0], by_core[1], core), axis=1)
    bias_abs = jnp.stack(pick(core_ordered[0], core_ordered[1], row))
    bias_abs = bias_abs.reshape(2, 2, n_ep, 2, strip, slab // strip)
    bias_abs = jnp.transpose(bias_abs, (2, 3, 0, 1, 4, 5)).reshape(width, slab // strip)
    grad_small = jnp.concatenate([grad_encoder, grad_vectors, bias_abs], axis=1)
    grad_small = jnp.pad(grad_small, ((0, 0), (0, WIDE - grad_small.shape[1])))
    summed_small = reduce_strips(grad_small)
    summed_prompt = reduce_strips(grad_prompt.astype(bf16))
    summed_encoder = summed_small[:, 0:FEAT]
    summed_vectors = summed_small[:, FEAT : FEAT + 7]
    summed_bias = summed_small[:, FEAT + 7 : FEAT + 7 + slab // strip].reshape(slab, 1)

    local_squares = (
        jnp.sum(summed_block * summed_block)
        + jnp.sum(summed_small * summed_small)
        + jnp.sum(summed_prompt * summed_prompt)
    )
    square_tile = jnp.full((8, 128), local_squares)
    square_tile = square_tile + swap(square_tile, core=1)
    got = plane_swap(lambda b, r: square_tile)
    square_tile = (got[0, 0] + got[1, 0]) + (got[0, 1] + got[1, 1])
    if n_ep > 4:
        square_tile = lax.psum(square_tile, "ep")
    else:
        square_tile = jnp.sum(gather_ep(square_tile), axis=0)
    grad_norm = jnp.sqrt(square_tile[0, 0])
    factor = jnp.minimum(1.0, clip_norm / (grad_norm + 1e-06))
    block_out = adam_update(
        block_weights, block_moments, summed_block, factor, rate_matrix, weight_decay
    )
    bias_out_new = adam_update(head_biases, bias_moments, summed_bias, factor, rate_vector, 0.0)
    encoder_out = adam_update(
        encoder, encoder_moments, summed_encoder, factor, rate_matrix, weight_decay
    )
    vector_out = adam_update(
        shared_vectors, vector_moments, summed_vectors, factor, rate_vector, 0.0
    )
    prompt_out = adam_update(
        prompt, prompt_moments, summed_prompt, factor, rate_vector, weight_decay
    )
    return (
        (output_final, input_final, grad_norm)
        + block_out
        + bias_out_new
        + encoder_out
        + vector_out
        + prompt_out
    )


def solution(mesh):
    data = P("split", "ep", "tp", None)
    block = P(("ep", "split"), "tp", None)
    bias = P(("ep", "split"), "tp")
    strip = P(AXES, None)
    placed = (
        data,
        P("ep", None),
        P("ep", None),
        data,
        block,
        P(None, ("ep", "split"), "tp", None),
        bias,
        P(None, ("ep", "split"), "tp"),
        strip,
        P(None, AXES, None),
        strip,
        P(None, AXES, None),
        strip,
        P(None, AXES, None),
    )
    return jax.shard_map(
        shards,
        mesh=mesh,
        in_specs=placed,
        out_specs=(data, data, P()) + (block,) * 4 + (bias,) * 4 + (strip,) * 12,
        check_vma=False,
    )
```

```python
import functools

import jax
import jax.numpy as jnp
from jax import lax
from jax.experimental import pallas as pl
from jax.experimental.pallas import tpu as pltpu
from jax.sharding import PartitionSpec as P

HEADS = 4
HEAD = 128
FF = 1024
HID = FF // HEADS
FEAT = 100
PROMPT = 1000
SLOTS = 1024
ADAM_STEP = 10
PAD = 1024
WIDE = 128

ln_eps = 1e-05
neg_big = -1e30
clip_norm = 1.0
beta_one = 0.9
beta_two = 0.999
adam_eps = 1e-08
rate_matrix = 0.15
rate_vector = 0.5
weight_decay = 0.01
AXES = ("ep", "split", "tp")
bf16 = jnp.bfloat16
f32 = jnp.float32
score_scale = HEAD**-0.5


def swap(value, ep=0, split=0, row=0, core=0):
    sizes = [lax.axis_size(a) for a in AXES]
    pairs = []
    for a in range(sizes[0]):
        for b in range(sizes[1]):
            for t in range(sizes[2]):
                other = ((a ^ ep) * sizes[1] + (b ^ split)) * sizes[2] + (t ^ (2 * row + core))
                pairs.append(((a * sizes[1] + b) * sizes[2] + t, other))
    return lax.ppermute(value, AXES, pairs)


def pick(low, high, bit):
    return jnp.where(bit == 0, low, high), jnp.where(bit == 0, high, low)


def plane_swap(piece):
    got = {}
    for b in (0, 1):
        for r in (0, 1):
            sent = piece(b, r)
            got[b, r] = sent if (b, r) == (0, 0) else swap(sent, split=b, row=r)
    return got


def tie(value, other):
    return lax.optimization_barrier((value, other))[0]


def gather_ep(shard, name):
    count = lax.axis_size("ep")
    if count > 4:
        return lax.all_gather(shard, "ep", axis=0)
    parts = [shard] + [swap(shard, ep=k) for k in range(1, count)]
    return place(parts, lax.axis_index("ep"), name)


def reduce_plane(parts, places, name):
    count = parts[0].shape[0]
    if count > 4:
        total = sum(part.astype(f32) for part in parts)
        return [lax.psum_scatter(total, "ep", scatter_dimension=0, tiled=True)[0]]
    pieces = sum_plane(parts, places, name)
    return [pieces[0]] + [swap(pieces[k], ep=k) for k in range(1, count)]


def adam_update(weight, moments, gradient, factor, step_rate, decay_rate):
    clipped = gradient * factor
    first_moment = beta_one * moments[0] + (1.0 - beta_one) * clipped
    second_moment = beta_two * moments[1] + (1.0 - beta_two) * clipped * clipped
    first_hat = first_moment / (1.0 - beta_one**ADAM_STEP)
    second_hat = second_moment / (1.0 - beta_two**ADAM_STEP)
    updated = weight - step_rate * (
        first_hat / (jnp.sqrt(second_hat) + adam_eps) + decay_rate * weight
    )
    return (updated, first_moment, second_moment, updated.astype(bf16))


def dot(a, b, dims):
    return lax.dot_general(a, b, (dims, ((), ())), preferred_element_type=f32)


NN = ((1,), (0,))
NT = ((1,), (1,))
TN = ((0,), (0,))


def cost(micros):
    return pl.CostEstimate(flops=int(micros * 1e9), transcendentals=0, bytes_accessed=int(micros * 3e6))


def whole():
    return pl.BlockSpec(memory_space=pltpu.VMEM)


def shape_of(shape, dtype):
    return jax.ShapeDtypeStruct(shape, dtype)


def project_body(ratio, own, other, enc, vec, wp, bias, prompt, x_ref, q_ref, k_ref, kt_ref, v_ref, vt_ref):
    step = pl.program_id(0)
    rows = jnp.where(step < 2, own[...], other[...])
    low = (ratio[0] * dot(rows, enc[...], NT) + vec[6:7, :]).astype(bf16)
    x_ref[...] = low
    for h in range(2):
        q_ref[h] = (dot(low, wp[h, :, 0:HEAD], NN) + bias[h : h + 1, 0:HEAD]).astype(bf16)

    def keys_from(source):
        for h in range(2):
            key = dot(source, wp[h, :, HEAD : 2 * HEAD], NN).astype(bf16)
            shift = bias[h : h + 1, HEAD : 2 * HEAD]
            value = (dot(source, wp[h, :, 2 * HEAD : 3 * HEAD], NN) + shift).astype(bf16)
            k_ref[h] = key
            v_ref[h] = value
            kt_ref[h] = key.T
            vt_ref[h] = value.T

    @pl.when(step % 2 == 0)
    def _():
        keys_from(low)

    @pl.when(step % 2 == 1)
    def _():
        keys_from(prompt[...].T)


def project(ratio, own, other, enc, vec, wp, bias, prompt):
    half = own.shape[0] // 2
    width = enc.shape[0]
    keys = PAD + SLOTS
    spot = lambda i: jnp.where(i % 2 == 0, 2 + i // 2, i // 2)
    tall = pl.BlockSpec((2, half, HEAD), lambda i: (0, spot(i), 0))
    flat = pl.BlockSpec((2, HEAD, half), lambda i: (0, 0, spot(i)))
    return pl.pallas_call(
        project_body,
        grid=(4,),
        in_specs=[
            pl.BlockSpec(memory_space=pltpu.SMEM),
            pl.BlockSpec((half, WIDE), lambda i: (jnp.minimum(i, 1), 0)),
            pl.BlockSpec((half, WIDE), lambda i: (jnp.maximum(i - 2, 0), 0)),
            whole(),
            whole(),
            whole(),
            whole(),
            pl.BlockSpec((width, half), lambda i: (0, i // 2)),
        ],
        out_specs=[
            pl.BlockSpec((half, width), lambda i: (i, 0)),
            pl.BlockSpec((2, half, HEAD), lambda i: (0, i, 0)),
            tall,
            flat,
            tall,
            flat,
        ],
        out_shape=[
            shape_of((4 * half, width), bf16),
            shape_of((2, 4 * half, HEAD), bf16),
            shape_of((2, keys, HEAD), bf16),
            shape_of((2, HEAD, keys), bf16),
            shape_of((2, keys, HEAD), bf16),
            shape_of((2, HEAD, keys), bf16),
        ],
        cost_estimate=cost(9),
        name="project",
    )(ratio, own, other, enc, vec, wp, bias, prompt)


def attend_body(q_ref, k_ref, vt_ref, bias_ref, o_ref, lse_ref):
    scores = dot(k_ref[0], q_ref[0], NT) * score_scale + bias_ref[...]
    top = jnp.max(scores, axis=0, keepdims=True)
    raised = jnp.exp(scores - top)
    total = jnp.sum(raised, axis=0, keepdims=True)
    out = dot(vt_ref[0], raised.astype(bf16), NN) / total
    o_ref[...] = out.T.astype(bf16)
    lse_ref[0] = top + jnp.log(total)


def attend(q, k, vt, bias, which):
    size = 512
    blocks = SLOTS // size
    keys = k.shape[1]
    return pl.pallas_call(
        attend_body,
        grid=(2, blocks),
        in_specs=[
            pl.BlockSpec((1, size, HEAD), lambda h, i: (h, which * blocks + i, 0)),
            pl.BlockSpec((1, keys, HEAD), lambda h, i: (h, 0, 0)),
            pl.BlockSpec((1, HEAD, keys), lambda h, i: (h, 0, 0)),
            pl.BlockSpec((keys, 1), lambda h, i: (0, 0)),
        ],
        out_specs=[
            pl.BlockSpec((size, HEAD), lambda h, i: (i, h)),
            pl.BlockSpec((1, 1, size), lambda h, i: (h, 0, i)),
        ],
        out_shape=[shape_of((SLOTS, 2 * HEAD), bf16), shape_of((2, 1, SLOTS), f32)],
        cost_estimate=cost(10),
        name="attend",
    )(q, k, vt, bias)


def attend_back_body(q_ref, k_ref, kt_ref, v_ref, bias_ref, la_ref, lb_ref, da_ref, db_ref, dq_ref, dk_ref, dv_ref):
    step = pl.program_id(1)
    mine = step < 2
    query = q_ref[0]
    grad = jnp.where(mine, da_ref[...], db_ref[...])
    lse = jnp.where(mine, la_ref[0], lb_ref[0])
    probs = jnp.exp(dot(k_ref[0], query, NT) * score_scale + (bias_ref[...] - lse))
    grad_probs = dot(v_ref[0], grad, NT)
    delta = jnp.sum(probs * grad_probs, axis=0, keepdims=True)
    grad_scores = (probs * (grad_probs - delta)).astype(bf16)
    back = dot(kt_ref[0], grad_scores, NN) * score_scale
    dq_ref[...] = back.T.astype(bf16)
    grad_key = dot(grad_scores, query, NN) * score_scale
    grad_value = dot(probs.astype(bf16), grad, NN)

    @pl.when(step == 0)
    def _():
        dk_ref[0] = grad_key
        dv_ref[0] = grad_value

    @pl.when(step > 0)
    def _():
        dk_ref[0] += grad_key
        dv_ref[0] += grad_value


def attend_back(q, k, kt, v, bias, lse_own, lse_other, grad_own, grad_other):
    size = 512
    keys = k.shape[1]
    tall = pl.BlockSpec((1, keys, HEAD), lambda h, i: (h, 0, 0))
    first = lambda i: jnp.minimum(i, 1)
    second = lambda i: jnp.maximum(i - 2, 0)
    return pl.pallas_call(
        attend_back_body,
        grid=(2, 2 * SLOTS // size),
        in_specs=[
            pl.BlockSpec((1, size, HEAD), lambda h, i: (h, i, 0)),
            tall,
            pl.BlockSpec((1, HEAD, keys), lambda h, i: (h, 0, 0)),
            tall,
            pl.BlockSpec((keys, 1), lambda h, i: (0, 0)),
            pl.BlockSpec((1, 1, size), lambda h, i: (h, 0, first(i))),
            pl.BlockSpec((1, 1, size), lambda h, i: (h, 0, second(i))),
            pl.BlockSpec((size, HEAD), lambda h, i: (first(i), h)),
            pl.BlockSpec((size, HEAD), lambda h, i: (second(i), h)),
        ],
        out_specs=[pl.BlockSpec((size, HEAD), lambda h, i: (i, h)), tall, tall],
        out_shape=[
            shape_of((2 * SLOTS, 2 * HEAD), bf16),
            shape_of((2, keys, HEAD), f32),
            shape_of((2, keys, HEAD), f32),
        ],
        cost_estimate=cost(32),
        name="attend_back",
    )(q, k, kt, v, bias, lse_own, lse_other, grad_own, grad_other)


erfc_terms = (
    -1.26551223,
    1.00002368,
    0.37409196,
    0.09678418,
    -0.18628806,
    0.27886807,
    -1.13520398,
    1.48851587,
    -0.82215223,
    0.17087277,
)


def gelu_pair(t):
    z = jnp.abs(t) * (0.5**0.5)
    k = 1.0 / (1.0 + 0.5 * z)
    series = jnp.full_like(t, erfc_terms[-1])
    for term in erfc_terms[-2::-1]:
        series = series * k + term
    tail = 0.5 * k * jnp.exp(series - z * z)
    cumulative = jnp.where(t >= 0.0, 1.0 - tail, tail)
    density = jnp.exp(-0.5 * t * t) * 0.3989422804014327
    return t * cumulative, cumulative + t * density


def middle_body(
    sc,
    ratio,
    rows_ref,
    oa_ref,
    ob_ref,
    c0,
    c1,
    c2,
    c3,
    enc,
    vec,
    b1,
    ra,
    rb,
    y0,
    y1,
    y2,
    y3,
    da_ref,
    db_ref,
    dr_ref,
    ga,
    gb,
    gvec,
    gb1,
    cot,
    acc,
):
    step = pl.program_id(0)
    count = rows_ref.shape[0]
    for k, ref in enumerate((c0, c1, c2, c3)):

        @pl.when(step == k)
        def _(ref=ref):
            cot[...] = ref[...]

    @pl.when(step == 0)
    def _():
        acc[...] = jnp.zeros_like(acc)
        gvec[...] = jnp.zeros_like(gvec)
        gb1[...] = jnp.zeros_like(gb1)

    group = sc[0] ^ (step // 2)
    quarter = 2 * (sc[1] ^ (step % 2)) + sc[2]
    limit = jnp.where(group == 0, sc[4], sc[5])
    slot = quarter * count + lax.broadcasted_iota(jnp.int32, (count, 1), 0)
    live = (slot < limit).astype(f32)

    def weight(k, low, high):
        return (ra if k < 2 else rb)[k % 2, :, low:high]

    def row(k):
        return vec[k : k + 1, :]

    gain_one, shift_one, gain_two, shift_two, b_out, b_two, b_enc = (row(k) for k in range(7))
    embedded = ratio[0] * dot(rows_ref[...], enc[...], NT) + b_enc
    out_pair = [
        jnp.concatenate([weight(2 * k, 0, HEAD), weight(2 * k + 1, 0, HEAD)], axis=1)
        for k in (0, 1)
    ]
    attn = dot(oa_ref[...], out_pair[0], NT) + dot(ob_ref[...], out_pair[1], NT) + b_out

    def norm(residual):
        centred = residual - jnp.mean(residual, axis=-1, keepdims=True)
        inverse = lax.rsqrt(jnp.mean(centred * centred, axis=-1, keepdims=True) + ln_eps)
        return centred * inverse, inverse

    def back(grad, normed, inverse, gain):
        scaled = grad * gain
        plain = jnp.mean(scaled, axis=-1, keepdims=True)
        mixed = jnp.mean(scaled * normed, axis=-1, keepdims=True)
        return inverse * (scaled - plain - normed * mixed)

    def add_row(k, value):
        gvec[k : k + 1, :] += jnp.sum(value, axis=0, keepdims=True)

    normed_one, inverse_one = norm(embedded + attn)
    first = normed_one * gain_one + shift_one
    first_low = first.astype(bf16)
    mlp = b_two
    acts, slopes = [], []
    for k in range(4):
        pre = dot(first_low, weight(k, HEAD, HEAD + HID), NN) + b1[k : k + 1, 2 * HEAD :]
        act, slope = gelu_pair(pre)
        acts.append(act.astype(bf16))
        slopes.append(slope)
        mlp = mlp + dot(acts[k], weight(k, HEAD + HID, HEAD + 2 * HID), NT)
    normed_two, inverse_two = norm(first + mlp)
    out = ((normed_two * gain_two + shift_two) * live).astype(bf16)
    for k, ref in enumerate((y0, y1, y2, y3)):

        @pl.when(step == k)
        def _(ref=ref):
            ref[...] = out

    grad_y = cot[...].astype(f32) * live
    add_row(2, grad_y * normed_two)
    add_row(3, grad_y)
    grad_two = back(grad_y, normed_two, inverse_two, gain_two)
    grad_low = grad_two.astype(bf16)
    add_row(5, grad_low.astype(f32))
    grad_flip = grad_low.T
    first_flip = first_low.T
    grad_first = grad_two
    for k in range(4):
        acc[k, :, HEAD + HID :] += dot(grad_flip, acts[k], NN)
        grad_act = dot(grad_low, weight(k, HEAD + HID, HEAD + 2 * HID), NN)
        grad_pre = (grad_act * slopes[k]).astype(bf16)
        gb1[k : k + 1, :] += jnp.sum(grad_pre.astype(f32), axis=0, keepdims=True)
        acc[k, :, HEAD : HEAD + HID] += dot(first_flip, grad_pre, NN)
        grad_first = grad_first + dot(grad_pre, weight(k, HEAD, HEAD + HID), NT)
    add_row(0, grad_first * normed_one)
    add_row(1, grad_first)
    grad_one = back(grad_first, normed_one, inverse_one, gain_one)
    dr_ref[...] = grad_one
    attn_low = grad_one.astype(bf16)
    add_row(4, attn_low.astype(f32))
    attn_flip = attn_low.T
    for k, (source, target) in enumerate(((oa_ref, da_ref), (ob_ref, db_ref))):
        both = dot(attn_flip, source[...], NN)
        acc[2 * k, :, 0:HEAD] += both[:, 0:HEAD]
        acc[2 * k + 1, :, 0:HEAD] += both[:, HEAD:]
        target[...] = dot(attn_low, out_pair[k], NN).astype(bf16)

    @pl.when(step == 3)
    def _():
        ga[...] = acc[0:2].astype(bf16)
        gb[...] = acc[2:4].astype(bf16)


def middle(sc, ratio, rows, o_own, o_other, cots, enc, vec, b1, rest_own, rest_other):
    size = rows.shape[0] // 4
    width = enc.shape[0]
    spot = lambda i, sc: (2 * (sc[0] ^ (i // 2)) + (sc[1] ^ (i % 2)), 0)
    pair = pl.BlockSpec((size, 2 * HEAD), spot)
    smem = pl.BlockSpec(memory_space=pltpu.SMEM)
    fixed = pl.BlockSpec((size, width), lambda i, sc: (0, 0))
    weight = rest_own.shape
    return pl.pallas_call(
        middle_body,
        grid_spec=pltpu.PrefetchScalarGridSpec(
            num_scalar_prefetch=1,
            grid=(4,),
            in_specs=[smem, pl.BlockSpec((size, WIDE), spot), pair, pair]
            + [fixed] * 4
            + [whole()] * 5,
            out_specs=[fixed] * 4
            + [pair, pair, pl.BlockSpec((size, width), spot)]
            + [
                pl.BlockSpec(weight, lambda i, sc: (0, 0, 0)),
                pl.BlockSpec(weight, lambda i, sc: (0, 0, 0)),
                pl.BlockSpec((8, width), lambda i, sc: (0, 0)),
                pl.BlockSpec((4, HID), lambda i, sc: (0, 0)),
            ],
            scratch_shapes=[
                pltpu.VMEM((size, width), bf16),
                pltpu.VMEM((4,) + weight[1:], f32),
            ],
        ),
        out_shape=[shape_of((size, width), bf16)] * 4
        + [
            shape_of((4 * size, 2 * HEAD), bf16),
            shape_of((4 * size, 2 * HEAD), bf16),
            shape_of((4 * size, width), f32),
            shape_of(weight, bf16),
            shape_of(weight, bf16),
            shape_of((8, width), f32),
            shape_of((4, HID), f32),
        ],
        cost_estimate=cost(25),
        name="middle",
    )(sc, ratio, rows, o_own, o_other, *cots, enc, vec, b1, rest_own, rest_other)


def simple(body, out_shape, *args, scalars=None, scratch=(), name=None):
    specs = [whole()] * len(args)
    if scalars is not None:
        specs = [pl.BlockSpec(memory_space=pltpu.SMEM)] + specs
        args = (scalars,) + args
    many = isinstance(out_shape, (list, tuple))
    return pl.pallas_call(
        body,
        in_specs=specs,
        out_specs=[whole()] * len(out_shape) if many else whole(),
        out_shape=out_shape,
        scratch_shapes=scratch,
        cost_estimate=cost(2),
        name=name,
    )(*args)


def place(parts, index, name):
    def body(sc, *refs):
        for k, ref in enumerate(refs[:-1]):
            refs[-1][sc[0] ^ k] = ref[...]

    first = parts[0]
    return simple(
        body,
        shape_of((len(parts),) + first.shape, first.dtype),
        *parts,
        scalars=index.reshape(1).astype(jnp.int32),
        name=name,
    )


TAIL = 3 * HEAD
VEC = 104


def with_bias(prompt, bias):
    wide = jnp.pad(prompt, [(0, 0)] * (prompt.ndim - 1) + [(0, 3 * TAIL - prompt.shape[-1])])
    row = jnp.pad(
        bias[..., None, :].astype(prompt.dtype),
        [(0, 0)] * (bias.ndim - 1)
        + [(0, prompt.shape[-2] - 1), (PAD, 3 * TAIL - PAD - bias.shape[-1])],
    )
    return wide + row


def in_chunks(wide):
    lead, strip = wide.shape[:-2], wide.shape[-2]
    parts = jnp.swapaxes(wide.reshape(lead + (strip, 3, TAIL)), -3, -2)
    return parts.reshape(lead + (3 * strip, TAIL))


def small_tile(encoder, vectors):
    return jnp.concatenate(
        [
            jnp.pad(encoder, ((0, 0), (0, VEC - FEAT))),
            jnp.pad(vectors, ((0, 0), (0, WIDE - VEC - 7))),
        ],
        axis=1,
    )


def pack_parts(block, prompt, encoder, vectors, biases):
    slab, strip = block.shape[0], prompt.shape[0]
    flat = block.reshape(slab * 8, HEAD)
    out = [shape_of((slab + 4 * strip, TAIL), bf16), shape_of((slab, 8 * HEAD - TAIL), bf16)]
    if 2 * slab != WIDE:
        low = block.reshape(slab, 8 * HEAD).astype(bf16)
        chunks = in_chunks(with_bias(prompt.astype(bf16), biases[:, 0]))
        small = jnp.pad(small_tile(encoder, vectors), ((0, 0), (0, TAIL - WIDE))).astype(bf16)
        return jnp.concatenate([low[:, 0:TAIL], chunks, small], axis=0), low[:, TAIL:]

    def body(block_ref, prompt_ref, enc_ref, vec_ref, bias_ref, main_ref, rest_ref, tall, tile):
        for j in range(8):
            lanes = block_ref[pl.ds(j, slab, stride=8), :].astype(bf16)
            if j < 3:
                main_ref[0:slab, j * HEAD : (j + 1) * HEAD] = lanes
            else:
                rest_ref[:, (j - 3) * HEAD : (j - 2) * HEAD] = lanes
        low = prompt_ref[...].astype(bf16)
        for k in range(2):
            rows = slice(slab + k * strip, slab + (k + 1) * strip)
            main_ref[rows, :] = low[:, k * TAIL : (k + 1) * TAIL]
        rows = slice(slab + 2 * strip, slab + 3 * strip)
        main_ref[rows, WIDE : 2 * WIDE] = jnp.zeros((strip, WIDE), bf16)
        main_ref[rows, 0 : PROMPT - 2 * TAIL] = low[:, 2 * TAIL :]
        tile[...] = jnp.zeros_like(tile)
        tile[0:1, 0:slab] = bias_ref[...]
        main_ref[rows, 2 * WIDE :] = tile[...].astype(bf16)
        tall[...] = jnp.zeros_like(tall)
        tall[VEC : VEC + 7, :] = vec_ref[...]
        tile[...] = tall[...].T
        tile[:, 0:FEAT] = enc_ref[...]
        rows = slice(slab + 3 * strip, slab + 4 * strip)
        main_ref[rows, 0:WIDE] = tile[...].astype(bf16)
        main_ref[rows, WIDE:] = jnp.zeros((strip, TAIL - WIDE), bf16)

    return simple(
        body,
        out,
        flat,
        prompt,
        encoder,
        vectors.T,
        biases.T,
        scratch=[pltpu.VMEM((WIDE, strip), f32), pltpu.VMEM((strip, WIDE), f32)],
        name="pack_parts",
    )


def unpack_main(tops, lows, places, slab, strip):
    n_ep = tops[0].shape[0]
    if 2 * slab != WIDE:
        side, row, core = places[0], places[1], places[2]

        def ordered(parts, axis):
            cores = []
            for group in parts:
                sides = []
                for b in (0, 1):
                    sides.append(jnp.stack(pick(group[2 * b], group[2 * b + 1], row), axis=axis))
                cores.append(jnp.stack(pick(sides[0], sides[1], side), axis=axis))
            return jnp.stack(pick(cores[0], cores[1], core), axis=axis + 2)

        heads = [
            jnp.stack(pick(tops[r][:, 0:slab], tops[2 + r][:, 0:slab], side), axis=1) for r in (0, 1)
        ]
        whole_low = ordered([[t[:, slab:] for t in tops], [t[:, slab:] for t in lows]], 1)
        chunks = whole_low[..., 0 : 3 * strip, :].reshape((n_ep, 2, 2, 2, 3, strip, TAIL))
        wide = jnp.swapaxes(chunks, -3, -2).reshape((n_ep, 2, 2, 2, strip, 3 * TAIL))
        small = whole_low[..., 3 * strip :, 0:WIDE]
        vec = small.reshape(n_ep * 8 * strip, WIDE).astype(f32).T[VEC : VEC + 8]
        biases = []
        for group in (tops, lows):
            for r in (0, 1):
                spot = slab + 2 * strip
                pair = [
                    group[2 * b + r][:, spot, PAD - 2 * TAIL : PAD - 2 * TAIL + slab] for b in (0, 1)
                ]
                biases.append(jnp.stack(pick(pair[0], pair[1], side), axis=1).reshape(-1))
        return jnp.stack(heads), wide, small, vec, jnp.stack(biases).astype(f32)

    def body(sc, t0, t1, t2, t3, l0, l1, l2, l3, wp_ref, prompt_ref, small_ref, vec_ref, bias_ref):
        side, row, core = sc[0], sc[1], sc[2]
        refs = (t0, t1, t2, t3)
        low_refs = (l0, l1, l2, l3)
        bias_tiles = {}
        for b in range(2):
            for r in range(2):
                k = 2 * b + r
                wp_ref[r, :, side ^ b] = refs[k][:, 0:slab, :]
                for other in range(2):
                    spot = core ^ other
                    part = (low_refs if other else refs)[k][:, slab:, :]
                    for j in range(3):
                        lanes = slice(j * TAIL, (j + 1) * TAIL)
                        rows = slice(j * strip, (j + 1) * strip)
                        prompt_ref[:, side ^ b, row ^ r, spot, :, lanes] = part[:, rows, :]
                    small_ref[:, side ^ b, row ^ r, spot] = part[:, 3 * strip :, 0:WIDE]
                    bias_tiles[b, r, other] = part[:, 2 * strip : 2 * strip + 8, TAIL - WIDE :].astype(f32)
        flip = small_ref[...].reshape(n_ep * 8 * strip, WIDE).astype(f32).T
        vec_ref[...] = flip[VEC : VEC + 8]
        low_half = lax.broadcasted_iota(jnp.int32, (1, WIDE), 1) < slab
        for r in range(2):
            for other in range(2):
                for e in range(n_ep):
                    mine = bias_tiles[0, r, other][e, 0:1]
                    theirs = bias_tiles[1, r, other][e, 0:1]
                    first = jnp.where(side == 0, mine, theirs)
                    second = jnp.where(side == 0, theirs, mine)
                    row_tile = jnp.where(low_half, first, pltpu.roll(second, slab, 1))
                    k = r + 2 * other
                    bias_ref[k : k + 1, e * WIDE : (e + 1) * WIDE] = row_tile

    return simple(
        body,
        [
            shape_of((2, n_ep, 2, slab, TAIL), bf16),
            shape_of((n_ep, 2, 2, 2, strip, 3 * TAIL), bf16),
            shape_of((n_ep, 2, 2, 2, strip, WIDE), bf16),
            shape_of((8, n_ep * 2 * slab), f32),
            shape_of((4, n_ep * 2 * slab), f32),
        ],
        *tops,
        *lows,
        scalars=places,
        name="unpack_main",
    )


def unpack_rest(tops, places):
    n_ep, slab, width = tops[0].shape

    def body(sc, t0, t1, t2, t3, out_ref):
        for k, ref in enumerate((t0, t1, t2, t3)):
            out_ref[k % 2, :, sc[0] ^ (k // 2)] = ref[...]

    return simple(
        body, shape_of((2, n_ep, 2, slab, width), bf16), *tops, scalars=places, name="unpack_rest"
    )


def back_body(order, dq_ref, dk_ref, dv_ref, wp, other_ref, own_ref):
    step = pl.program_id(0)

    def columns(k):
        return jnp.concatenate([wp[h, :, k * HEAD : (k + 1) * HEAD] for h in range(2)], axis=1)

    def both(ref):
        return jnp.concatenate([ref[h].astype(bf16) for h in range(2)], axis=1)

    base = dot(dq_ref[...], columns(0), NT)

    def store(value):
        @pl.when(step < 2)
        def _():
            other_ref[...] = value.astype(bf16)

        @pl.when(step >= 2)
        def _():
            own_ref[...] = value

    @pl.when(step % 2 == 0)
    def _():
        store(base + dot(both(dk_ref), columns(1), NT) + dot(both(dv_ref), columns(2), NT))

    @pl.when(step % 2 == 1)
    def _():
        store(base)


def back_rows(dq, dk, dv, wp):
    half = dq.shape[0] // 4
    width = wp.shape[1]
    turn = lambda i: (i + 2) % 4
    key = pl.BlockSpec((2, half, HEAD), lambda i: (0, 3 - i // 2, 0))
    return pl.pallas_call(
        functools.partial(back_body, None),
        grid=(4,),
        in_specs=[pl.BlockSpec((half, 2 * HEAD), lambda i: (turn(i), 0)), key, key, whole()],
        out_specs=[
            pl.BlockSpec((half, width), lambda i: (jnp.minimum(i, 1), 0)),
            pl.BlockSpec((half, width), lambda i: (jnp.maximum(i - 2, 0), 0)),
        ],
        out_shape=[shape_of((2 * half, width), bf16), shape_of((2 * half, width), f32)],
        cost_estimate=cost(6),
        name="back_rows",
    )(dq, dk, dv, wp)


def weight_body(x_ref, dq_ref, dk_ref, dv_ref, prompt, wp, gb1, gw_ref, gp_ref, gb_ref, acc, gq_ref, gv_ref):
    step = pl.program_id(0)

    @pl.when(step == 0)
    def _():
        acc[...] = jnp.zeros_like(acc)
        gq_ref[...] = jnp.zeros_like(gq_ref)
        gv_ref[...] = jnp.zeros_like(gv_ref)

    flip = x_ref[...].T
    acc[0] += dot(flip, dq_ref[...], NN)
    gq_ref[...] += jnp.sum(dq_ref[...].astype(f32), axis=0, keepdims=True)
    grad_key = jnp.concatenate([dk_ref[h] for h in range(2)], axis=1)
    grad_value = jnp.concatenate([dv_ref[h] for h in range(2)], axis=1)
    key_high = grad_key.astype(bf16)
    value_high = grad_value.astype(bf16)

    @pl.when(step % 2 == 0)
    def _():
        acc[1] += dot(flip, key_high, NN)
        acc[2] += dot(flip, value_high, NN)
        gv_ref[...] += jnp.sum(value_high.astype(f32), axis=0, keepdims=True)

    @pl.when(step % 2 == 1)
    def _():
        key_low = (grad_key - key_high.astype(f32)).astype(bf16)
        value_low = (grad_value - value_high.astype(f32)).astype(bf16)
        source = prompt[...]
        acc[1] += dot(source, key_high, NN) + dot(source, key_low, NN)
        acc[2] += dot(source, value_high, NN) + dot(source, value_low, NN)
        gv_ref[...] += jnp.sum(grad_value, axis=0, keepdims=True)
        w_key, w_value = (
            jnp.concatenate([wp[h, :, k * HEAD : (k + 1) * HEAD] for h in range(2)], axis=1)
            for k in (1, 2)
        )
        total = dot(w_key, key_high, NT) + dot(w_key, key_low, NT)
        total = total + dot(w_value, value_high, NT) + dot(w_value, value_low, NT)
        gp_ref[...] = total.astype(bf16)

    @pl.when(step == 3)
    def _():
        for h in range(2):
            for k in range(3):
                lanes = slice(h * HEAD, (h + 1) * HEAD)
                gw_ref[h, :, k * HEAD : (k + 1) * HEAD] = acc[k, :, lanes].astype(bf16)
            gb_ref[h : h + 1, 0:HEAD] = gq_ref[:, h * HEAD : (h + 1) * HEAD]
            gb_ref[h : h + 1, HEAD : 2 * HEAD] = gv_ref[:, h * HEAD : (h + 1) * HEAD]
        gb_ref[2:4, 0 : 2 * HEAD] = jnp.zeros((2, 2 * HEAD), f32)
        gb_ref[:, 2 * HEAD :] = gb1[...]


def weight_grads(x, dq, dk, dv, prompt, wp, gb1):
    half = dq.shape[0] // 4
    width = wp.shape[1]
    spot = lambda i: jnp.where(i % 2 == 0, 2 + i // 2, i // 2)
    key = pl.BlockSpec((2, half, HEAD), lambda i: (0, spot(i), 0))
    return pl.pallas_call(
        weight_body,
        grid=(4,),
        in_specs=[
            pl.BlockSpec((half, width), lambda i: (i, 0)),
            pl.BlockSpec((half, 2 * HEAD), lambda i: (i, 0)),
            key,
            key,
            pl.BlockSpec((width, half), lambda i: (0, i // 2)),
            whole(),
            whole(),
        ],
        out_specs=[
            pl.BlockSpec((2, width, TAIL), lambda i: (0, 0, 0)),
            pl.BlockSpec((width, half), lambda i: (0, i // 2)),
            pl.BlockSpec((4, width), lambda i: (0, 0)),
        ],
        out_shape=[
            shape_of((2, width, TAIL), bf16),
            shape_of((width, PAD), bf16),
            shape_of((4, width), f32),
        ],
        scratch_shapes=[pltpu.VMEM((3, width, 2 * HEAD), f32)]
        + [pltpu.VMEM((1, 2 * HEAD), f32)] * 2,
        cost_estimate=cost(9),
        name="weight_grads",
    )(x, dq, dk, dv, prompt, wp, gb1)


def input_body(sc, ratio, dr_ref, own_ref, got_ref, rows_ref, enc, mask, rows_grad, i0, i1, i2, i3, small_ref, acc, bias):
    step = pl.program_id(0)
    low = (dr_ref[...] + own_ref[...] + got_ref[...].astype(f32)).astype(bf16)
    part = dot(low.T, rows_ref[...], NN) * ratio[0]
    part_bias = jnp.sum(low.astype(f32), axis=0, keepdims=True)

    @pl.when(step == 0)
    def _():
        acc[...] = part
        bias[...] = part_bias

    @pl.when(step > 0)
    def _():
        acc[...] += part
        bias[...] += part_bias

    grad = dot(enc[...].T, low, NT) * ratio[0] * mask[...]
    for k, ref in enumerate((i0, i1, i2, i3)):

        @pl.when(step == k)
        def _(ref=ref):
            ref[...] = grad[0:VEC]

    @pl.when(step == 3)
    def _():
        width = acc.shape[0]
        rows = jnp.concatenate(
            [
                jnp.zeros((VEC, width), f32),
                rows_grad[0:6],
                bias[...],
                jnp.zeros((WIDE - VEC - 7, width), f32),
            ],
            axis=0,
        )
        small_ref[...] = (acc[...] + rows.T).astype(bf16)


def input_grads(sc, ratio, dr, own, got, rows, enc, mask, rows_grad):
    size = rows.shape[0] // 4
    width = enc.shape[0]
    spot = lambda i, sc: (2 * (sc[0] ^ (i // 2)) + (sc[1] ^ (i % 2)), 0)
    block = pl.BlockSpec((size, width), spot)
    fixed = pl.BlockSpec((VEC, size), lambda i, sc: (0, 0))
    return pl.pallas_call(
        input_body,
        grid_spec=pltpu.PrefetchScalarGridSpec(
            num_scalar_prefetch=1,
            grid=(4,),
            in_specs=[
                pl.BlockSpec(memory_space=pltpu.SMEM),
                block,
                block,
                block,
                pl.BlockSpec((size, WIDE), spot),
                whole(),
                whole(),
                whole(),
            ],
            out_specs=[fixed] * 4 + [pl.BlockSpec((width, WIDE), lambda i, sc: (0, 0))],
            scratch_shapes=[pltpu.VMEM((width, WIDE), f32), pltpu.VMEM((1, width), f32)],
        ),
        out_shape=[shape_of((VEC, size), f32)] * 4 + [shape_of((width, WIDE), bf16)],
        cost_estimate=cost(6),
        name="input_grads",
    )(sc, ratio, dr, own, got, rows, enc, mask, rows_grad)


def split_prompt(grad, bias_rows, places, n_ep, strip):
    blocks = grad.reshape(n_ep, 2, 2, 2, strip, PAD)
    if 8 * strip != WIDE:
        row, core = places[1], places[2]
        table = bias_rows.reshape(2, 2, n_ep, 2, 4 * strip)
        both = []
        for other in (0, 1):
            by_row = jnp.stack(pick(table[other, 0], table[other, 1], row), axis=2)
            part = lax.dynamic_index_in_dim(blocks, core ^ other, 3, keepdims=False)
            both.append(in_chunks(with_bias(part, by_row)))
        return both

    def body(sc, grad_ref, bias_ref, mine_ref, sent_ref):
        row, core = sc[1], sc[2]
        first = lax.broadcasted_iota(jnp.int32, (strip, WIDE), 0) == 0
        low_half = lax.broadcasted_iota(jnp.int32, (1, WIDE), 1) < 4 * strip
        for s in range(2):
            for r in range(2):
                for other, ref in enumerate((mine_ref, sent_ref)):
                    for j in range(3):
                        rows = slice(j * strip, (j + 1) * strip)
                        high = min(PAD, (j + 1) * TAIL)
                        part = grad_ref[:, s, row ^ r, core ^ other, :, j * TAIL : high]
                        ref[:, s, row ^ r, rows, 0 : high - j * TAIL] = part
                    for e in range(n_ep):
                        k = r + 2 * other
                        tile = bias_ref[k : k + 1, e * WIDE : (e + 1) * WIDE]
                        if s == 1:
                            tile = pltpu.roll(tile, WIDE - 4 * strip, 1)
                        tile = jnp.where(low_half, tile, 0.0)
                        tile = jnp.where(first, tile, 0.0).astype(bf16)
                        ref[e, s, row ^ r, 2 * strip : 3 * strip, PAD - 2 * TAIL :] = tile

    shape = shape_of((n_ep, 2, 2, 3 * strip, TAIL), bf16)
    return simple(body, [shape, shape], blocks, bias_rows, scalars=places, name="split_prompt")


def split_small(grad, places, n_ep, strip):
    blocks = grad.reshape(n_ep * 4, 2, strip, WIDE)

    def body(sc, grad_ref, mine_ref, sent_ref):
        mine_ref[...] = grad_ref[:, sc[2]]
        sent_ref[...] = grad_ref[:, 1 - sc[2]]

    shape = shape_of((n_ep * 4, strip, WIDE), bf16)
    return simple(body, [shape, shape], blocks, scalars=places, name="split_small")


def pack_main(gw, mine, got, small_mine, small_got, places, slab, strip):
    n_ep = mine.shape[0]
    heads = gw.reshape(2, n_ep, 2, slab, TAIL)
    small_mine = small_mine.reshape(n_ep, 2, 2, strip, WIDE)
    small_got = small_got.reshape(n_ep, 2, 2, strip, WIDE)
    if 2 * slab != WIDE:
        pair = (mine.astype(f32) + got.astype(f32)).astype(bf16)
        small = (small_mine.astype(f32) + small_got.astype(f32)).astype(bf16)
        small = jnp.pad(small, [(0, 0)] * 4 + [(0, TAIL - WIDE)])
        low = jnp.concatenate([pair, small], axis=3)
        outs = []
        for b in (0, 1):
            for r in (0, 1):
                side, row = places[0] ^ b, places[1] ^ r
                part = lax.dynamic_index_in_dim(low, side, 1, keepdims=False)
                part = lax.dynamic_index_in_dim(part, row, 1, keepdims=False)
                head = lax.dynamic_index_in_dim(heads[r], side, 1, keepdims=False)
                outs.append(jnp.concatenate([head, part], axis=1))
        return outs

    def body(sc, gw_ref, a_ref, b_ref, c_ref, d_ref, *outs):
        for b in range(2):
            for r in range(2):
                out = outs[2 * b + r]
                side, row = sc[0] ^ b, sc[1] ^ r
                out[:, 0:slab, :] = gw_ref[r, :, side]
                pair = a_ref[:, side, row].astype(f32) + b_ref[:, side, row].astype(f32)
                out[:, slab : slab + 3 * strip, :] = pair.astype(bf16)
                pair = c_ref[:, side, row].astype(f32) + d_ref[:, side, row].astype(f32)
                out[:, slab + 3 * strip :, 0:WIDE] = pair.astype(bf16)
                out[:, slab + 3 * strip :, WIDE:] = jnp.zeros((n_ep, strip, TAIL - WIDE), bf16)

    shape = shape_of((n_ep, slab + 4 * strip, TAIL), bf16)
    return simple(
        body, [shape] * 4, heads, mine, got, small_mine, small_got, scalars=places, name="pack_main"
    )


def pack_rest(mine, got, places, n_ep, slab):
    width = mine.shape[-1]
    mine = mine.reshape(2, n_ep, 2, slab, width)
    got = got.reshape(2, n_ep, 2, slab, width)

    def body(sc, a_ref, b_ref, *outs):
        for b in range(2):
            for r in range(2):
                pair = a_ref[r, :, sc[0] ^ b].astype(f32) + b_ref[r, :, sc[0] ^ b].astype(f32)
                outs[2 * b + r][...] = pair.astype(bf16)

    shape = shape_of((n_ep, slab, width), bf16)
    return simple(body, [shape] * 4, mine, got, scalars=places, name="pack_rest")


def sum_plane(parts, places, name):
    n_ep = parts[0].shape[0]

    def body(sc, *refs):
        ins, outs = refs[: len(parts)], refs[len(parts) :]
        for k, out in enumerate(outs):
            spot = sc[6] ^ k
            total = ins[0][spot].astype(f32)
            for ref in ins[1:]:
                total = total + ref[spot].astype(f32)
            out[...] = total.astype(bf16)

    shape = shape_of(parts[0].shape[1:], bf16)
    return simple(body, [shape] * n_ep, *parts, scalars=places, name=name)


def final_sums(mains, rests, slab, strip):
    def body(*refs):
        main_refs, rest_refs = refs[: len(mains)], refs[len(mains) : len(mains) + len(rests)]
        block_ref, prompt_ref, small_ref, bias_ref, square_ref = refs[len(mains) + len(rests) :]

        def added(group):
            total = group[0][...].astype(f32)
            for ref in group[1:]:
                total = total + ref[...].astype(f32)
            return total

        main, rest = added(main_refs), added(rest_refs)
        square = jnp.sum(jnp.sum(main * main, axis=0, keepdims=True), axis=1, keepdims=True)
        square = square + jnp.sum(
            jnp.sum(rest * rest, axis=0, keepdims=True), axis=1, keepdims=True
        )
        for j in range(8):
            if j < 3:
                tile = main[0:slab, j * HEAD : (j + 1) * HEAD]
            else:
                tile = rest[:, (j - 3) * HEAD : (j - 2) * HEAD]
            block_ref[pl.ds(j, slab, stride=8), :] = tile
        for j in range(3):
            part = main[slab + j * strip : slab + (j + 1) * strip]
            high = min(PROMPT, (j + 1) * TAIL)
            prompt_ref[:, j * TAIL : high] = part[:, 0 : high - j * TAIL]
        small_ref[...] = main[slab + 3 * strip :, 0:WIDE]
        bias_ref[...] = main[slab + 2 * strip : slab + 2 * strip + 1, TAIL - WIDE :]
        square_ref[...] = jnp.broadcast_to(square, (8, 128))

    return simple(
        body,
        [
            shape_of((slab * 8, HEAD), f32),
            shape_of((strip, PROMPT), f32),
            shape_of((strip, WIDE), f32),
            shape_of((1, WIDE), f32),
            shape_of((8, 128), f32),
        ],
        *mains,
        *rests,
        name="final_sums",
    )


def adam_all(squares, params, moments, grads):
    slab = params[0].shape[0] // 8
    rates = (rate_matrix, rate_vector, rate_matrix, rate_vector, rate_vector)
    decays = (weight_decay, weight_decay, weight_decay, 0.0, 0.0)
    count = squares.shape[0]

    def body(sq_ref, *refs):
        weights, moment_refs, grad_refs, outs = refs[0:5], refs[5:10], refs[10:14], refs[14:]
        total = sq_ref[0, 0:1, 0:1]
        for k in range(1, count):
            total = total + sq_ref[k, 0:1, 0:1]
        norm = jnp.sqrt(total)
        outs[0][...] = norm
        factor = jnp.minimum(1.0, clip_norm / (norm + 1e-06))
        small = grad_refs[2][...]
        picked = (
            grad_refs[0][...],
            grad_refs[1][...],
            small[:, 0:FEAT],
            small.T[VEC : VEC + 7],
            grad_refs[3][:, 0:slab],
        )
        for k in range(5):
            both = moment_refs[k]
            pair = (both[:, 0], both[:, 1]) if k == 3 else (both[0], both[1])
            news = adam_update(weights[k][...], pair, picked[k], factor, rates[k], decays[k])
            for m in range(3):
                outs[1 + 4 * k + m][...] = news[m]
            if k > 0:
                outs[4 + 4 * k][...] = news[3]
        for j in range(8):
            tile = outs[1][pl.ds(j, slab, stride=8), :]
            outs[4][:, j * HEAD : (j + 1) * HEAD] = tile.astype(bf16)

    shapes = [shape_of((1, 1), f32)]
    for k, param in enumerate(params):
        low = (slab, 8 * HEAD) if k == 0 else param.shape
        shapes += [shape_of(param.shape, f32)] * 3 + [shape_of(low, bf16)]
    return simple(body, shapes, squares, *params, *moments, *grads, name="adam_all")


def shards(
    feats,
    counts,
    feat_mask,
    cotangent,
    block_weights,
    block_moments,
    head_biases,
    bias_moments,
    encoder,
    encoder_moments,
    shared_vectors,
    vector_moments,
    prompt,
    prompt_moments,
):
    n_ep = lax.axis_size("ep")
    side = lax.axis_index("split")
    row = lax.axis_index("tp") // 2
    core = lax.axis_index("tp") % 2
    chip = side * 2 + row
    rows = feats.shape[2]
    width = cotangent.shape[3]
    slab = block_weights.shape[0]
    strip = encoder.shape[0]
    quad = [(b, r) for b in (0, 1) for r in (0, 1)]

    mask_row = lax.dynamic_index_in_dim(feat_mask, chip, 0, keepdims=False)
    count_pair = lax.dynamic_index_in_dim(counts, chip, 0, keepdims=False)
    mask_float = mask_row.astype(f32)
    ratio = (FEAT / jnp.sum(mask_float)).reshape(1)
    spot = jnp.arange(8, dtype=jnp.int32)
    places = jnp.pad(count_pair, (4, 2)).astype(jnp.int32)
    for k, value in ((0, side), (1, row), (2, core), (3, chip), (6, lax.axis_index("ep"))):
        places = places + jnp.where(spot == k, value, 0)

    def canonical(got):
        first = [jnp.concatenate(pick(got[b, 0], got[b, 1], row), axis=0) for b in (0, 1)]
        return jnp.concatenate(pick(first[0], first[1], side), axis=0)

    def to_chip(array):
        return plane_swap(
            lambda b, r: lax.dynamic_index_in_dim(array[0], chip ^ (2 * b + r), 0, keepdims=False)
        )

    main_part, rest_part = pack_parts(
        block_weights, prompt, encoder, shared_vectors, head_biases
    )
    got = to_chip(feats)
    main_along = gather_ep(main_part, "stack_main")
    feats_own = canonical(got)
    masked_own = jnp.pad(feats_own * mask_row.astype(bf16), ((0, 0), (0, WIDE - FEAT)))
    masked_other = swap(masked_own, core=1)
    tops = plane_swap(lambda b, r: main_along)
    tops = [tops[key] for key in quad]
    lows = [swap(top, core=1) for top in tops]
    w_project, prompt_low, small_low, vector_rows, bias_rows = unpack_main(
        tops, lows, places, slab, strip
    )
    w_project = w_project.reshape(2, width, TAIL)
    prompt_low = prompt_low.reshape(width, 3 * TAIL)
    encoder_low = small_low.reshape(width, WIDE)

    rest_part = tie(rest_part, main_along)
    rest_along = gather_ep(rest_part, "stack_rest")
    rest_along = tie(rest_along, tops[3])
    rest_tops = plane_swap(lambda b, r: rest_along)
    rest_own = unpack_rest([rest_tops[key] for key in quad], places)
    rest_own = rest_own.reshape(2, width, -1)
    rest_other = swap(rest_own, core=1)

    lane = jnp.arange(rows, dtype=jnp.int32)

    def slots_of(which_core):
        return jnp.concatenate([which_core * rows + lane, (2 + which_core) * rows + lane])

    key_slots = jnp.concatenate([slots_of(core), slots_of(1 - core)])
    key_live = jnp.concatenate([jnp.arange(PAD) < PROMPT, key_slots < count_pair[0]])
    key_bias = jnp.where(key_live, 0.0, neg_big)[:, None].astype(f32)
    rows_low, query, keys, keys_flip, values, values_flip = project(
        ratio,
        masked_own,
        masked_other,
        encoder_low,
        vector_rows,
        w_project,
        bias_rows,
        prompt_low,
    )
    attended_other, lse_other = attend(query, keys, values_flip, key_bias, 1)
    attended_got = swap(attended_other, core=1)
    attended_own, lse_own = attend(query, keys, values_flip, key_bias, 0)
    cots = to_chip(tie(cotangent, tops[3]))
    (y0, y1, y2, y3, grad_own, grad_sent, grad_one, rest_mine, rest_sent, grad_rows, grad_hidden_row) = middle(
        places,
        ratio,
        masked_own,
        attended_own,
        attended_got,
        [cots[key] for key in quad],
        encoder_low,
        vector_rows,
        bias_rows,
        rest_own,
        rest_other,
    )
    grad_got = swap(grad_sent, core=1)
    rest_got = swap(rest_sent, core=1)
    outs = (y0, y1, y2, y3)
    outs = plane_swap(lambda b, r: outs[2 * b + r])
    output_final = place([outs[key] for key in quad], chip, "place_output")[None]
    rest_parts = pack_rest(rest_mine, rest_got, places, n_ep, slab)
    rest_tops = plane_swap(lambda b, r: rest_parts[2 * b + r])
    rest_pieces = reduce_plane([rest_tops[key] for key in quad], places, "sum_rest")

    query_again, *unused = lax.optimization_barrier((query, *rest_parts))
    grad_query, grad_key, grad_value = attend_back(
        query_again, keys, keys_flip, values, key_bias, lse_own, lse_other, grad_own, grad_got
    )
    back_other, back_own = back_rows(grad_query, grad_key, grad_value, w_project)
    back_got = swap(back_other, core=1)
    grad_project, grad_prompt, grad_bias = weight_grads(
        rows_low, grad_query, grad_key, grad_value, prompt_low, w_project, grad_hidden_row
    )
    prompt_mine, prompt_sent = split_prompt(grad_prompt, grad_bias, places, n_ep, strip)
    prompt_got = swap(prompt_sent, core=1)
    i0, i1, i2, i3, grad_small = input_grads(
        places,
        ratio,
        grad_one,
        back_own,
        back_got,
        masked_own,
        encoder_low,
        jnp.pad(mask_float, (0, WIDE - FEAT)).reshape(WIDE, 1),
        grad_rows,
    )
    small_mine, small_sent = split_small(grad_small, places, n_ep, strip)
    small_got = swap(small_sent, core=1)
    main_parts = pack_main(
        grad_project, prompt_mine, prompt_got, small_mine, small_got, places, slab, strip
    )
    main_tops = plane_swap(lambda b, r: main_parts[2 * b + r])
    ins = (i0, i1, i2, i3)
    ins = plane_swap(lambda b, r: ins[2 * b + r])
    main_pieces = reduce_plane([main_tops[key] for key in quad], places, "sum_main")
    input_final = place([ins[key] for key in quad], chip, "place_input")
    input_final = jnp.transpose(input_final[:, 0:FEAT], (0, 2, 1))[None]

    grad_block, grad_prompt_own, grad_small_own, grad_bias_own, square_tile = final_sums(
        main_pieces, rest_pieces, slab, strip
    )
    square_tile = square_tile + swap(square_tile, core=1)
    got = plane_swap(lambda b, r: square_tile)
    square_tile = (got[0, 0] + got[1, 0]) + (got[0, 1] + got[1, 1])
    if n_ep > 4:
        squares = lax.psum(square_tile, "ep")[None]
    else:
        squares = gather_ep(square_tile, "stack_square")
    grad_norm, *news = adam_all(
        squares,
        (
            block_weights.reshape(slab * 8, HEAD),
            prompt,
            encoder,
            shared_vectors.T,
            head_biases.T,
        ),
        (
            block_moments.reshape(2, slab * 8, HEAD),
            prompt_moments,
            encoder_moments,
            jnp.transpose(vector_moments, (2, 0, 1)),
            jnp.transpose(bias_moments, (0, 2, 1)),
        ),
        (grad_block, grad_prompt_own, grad_small_own, grad_bias_own),
    )
    block_out = tuple(part.reshape(block_weights.shape) for part in news[0:4])
    prompt_out = tuple(news[4:8])
    encoder_out = tuple(news[8:12])
    vector_out = tuple(part.T for part in news[12:16])
    bias_out = tuple(part.T for part in news[16:20])
    return (
        (output_final, input_final, grad_norm.reshape(()))
        + block_out
        + bias_out
        + encoder_out
        + vector_out
        + prompt_out
    )


def solution(mesh):
    data = P("split", "ep", "tp", None)
    block = P(("ep", "split"), "tp", None)
    bias = P(("ep", "split"), "tp")
    strip = P(AXES, None)
    placed = (
        data,
        P("ep", None),
        P("ep", None),
        data,
        block,
        P(None, ("ep", "split"), "tp", None),
        bias,
        P(None, ("ep", "split"), "tp"),
        strip,
        P(None, AXES, None),
        strip,
        P(None, AXES, None),
        strip,
        P(None, AXES, None),
    )
    return jax.shard_map(
        shards,
        mesh=mesh,
        in_specs=placed,
        out_specs=(data, data, P()) + (block,) * 4 + (bias,) * 4 + (strip,) * 12,
        check_vma=False,
    )
```

```python
import functools

import jax
import jax.numpy as jnp
from jax import lax
from jax.experimental import pallas as pl
from jax.experimental.pallas import tpu as pltpu
from jax.sharding import PartitionSpec as P

HEADS = 4
HEAD = 128
FF = 1024
HID = FF // HEADS
FEAT = 100
PROMPT = 1000
SLOTS = 1024
ADAM_STEP = 10
PAD = 1024
WIDE = 128

ln_eps = 1e-05
neg_big = -1e30
clip_norm = 1.0
beta_one = 0.9
beta_two = 0.999
adam_eps = 1e-08
rate_matrix = 0.15
rate_vector = 0.5
weight_decay = 0.01
AXES = ("ep", "split", "tp")
bf16 = jnp.bfloat16
f32 = jnp.float32
score_scale = HEAD**-0.5


def swap(value, ep=0, split=0, row=0, core=0):
    sizes = [lax.axis_size(a) for a in AXES]
    pairs = []
    for a in range(sizes[0]):
        for b in range(sizes[1]):
            for t in range(sizes[2]):
                other = ((a ^ ep) * sizes[1] + (b ^ split)) * sizes[2] + (t ^ (2 * row + core))
                pairs.append(((a * sizes[1] + b) * sizes[2] + t, other))
    return lax.ppermute(value, AXES, pairs)


def pick(low, high, bit):
    return jnp.where(bit == 0, low, high), jnp.where(bit == 0, high, low)


def plane_swap(piece):
    got = {}
    for b in (0, 1):
        for r in (0, 1):
            sent = piece(b, r)
            got[b, r] = sent if (b, r) == (0, 0) else swap(sent, split=b, row=r)
    return got


def tie(value, other):
    return lax.optimization_barrier((value, other))[0]


def gather_ep(shard):
    count = lax.axis_size("ep")
    if count > 4:
        return [lax.all_gather(shard, "ep", axis=0)]
    return [shard] + [swap(shard, ep=k) for k in range(1, count)]


def stack_ep(parts, name):
    return parts[0] if len(parts) == 1 else place(parts, lax.axis_index("ep"), name)


def reduce_ep(total, pieces):
    count = lax.axis_size("ep")
    if count > 4:
        return [lax.psum_scatter(total, "ep", scatter_dimension=0, tiled=True)[0]]
    return [pieces[0]] + [swap(pieces[k], ep=k) for k in range(1, count)]


def adam_update(weight, moments, gradient, factor, step_rate, decay_rate):
    clipped = gradient * factor
    first_moment = beta_one * moments[0] + (1.0 - beta_one) * clipped
    second_moment = beta_two * moments[1] + (1.0 - beta_two) * clipped * clipped
    first_hat = first_moment / (1.0 - beta_one**ADAM_STEP)
    second_hat = second_moment / (1.0 - beta_two**ADAM_STEP)
    updated = weight - step_rate * (
        first_hat / (jnp.sqrt(second_hat) + adam_eps) + decay_rate * weight
    )
    return (updated, first_moment, second_moment, updated.astype(bf16))


def dot(a, b, dims):
    return lax.dot_general(a, b, (dims, ((), ())), preferred_element_type=f32)


NN = ((1,), (0,))
NT = ((1,), (1,))
TN = ((0,), (0,))


def cost(micros):
    return pl.CostEstimate(flops=int(micros * 3e8), transcendentals=0, bytes_accessed=int(micros * 1e6))


def whole():
    return pl.BlockSpec(memory_space=pltpu.VMEM)


def shape_of(shape, dtype):
    return jax.ShapeDtypeStruct(shape, dtype)


def project_body(ratio, sc, own, other, enc, vec, wp, bias, prompt, x_ref, q_ref, k_ref, kt_ref, v_ref, vt_ref, extra_ref):
    step = pl.program_id(0)

    @pl.when(step == 0)
    def _():
        half = own.shape[0]
        size = half // 2
        key = lax.broadcasted_iota(jnp.int32, extra_ref.shape[1:], 0)
        lane = lax.broadcasted_iota(jnp.int32, extra_ref.shape[1:], 1)
        inner = key - PAD
        place = inner % half
        slot = (2 * (place // size) + (sc[2] ^ (inner // half))) * size + place % size
        limit = jnp.where(key < PAD, PROMPT, sc[4])
        bias = jnp.where(jnp.where(key < PAD, key, slot) >= limit, neg_big, 0.0)
        bias = jnp.where(lane == 3, bias, 0.0)
        for h in range(2):
            ones = jnp.where((lane >= 4 * h) & (lane < 4 * h + 3), 1.0, 0.0)
            extra_ref[h] = (bias + ones).astype(bf16)

    rows = jnp.where(step < 2, own[...], other[...])
    low = (ratio[0] * dot(rows, enc[...], NT) + vec[6:7, :]).astype(bf16)
    x_ref[...] = low
    for h in range(2):
        q_ref[h] = (dot(low, wp[h, :, 0:HEAD], NN) + bias[h : h + 1, 0:HEAD]).astype(bf16)

    def keys_from(source):
        for h in range(2):
            key = dot(source, wp[h, :, HEAD : 2 * HEAD], NN).astype(bf16)
            shift = bias[h : h + 1, HEAD : 2 * HEAD]
            value = (dot(source, wp[h, :, 2 * HEAD : 3 * HEAD], NN) + shift).astype(bf16)
            k_ref[h] = key
            v_ref[h] = value
            kt_ref[h] = key.T
            vt_ref[h] = value.T

    @pl.when(step % 2 == 0)
    def _():
        keys_from(low)

    @pl.when(step % 2 == 1)
    def _():
        keys_from(prompt[...].T)


def project(ratio, places, own, other, enc, vec, wp, bias, prompt):
    half = own.shape[0] // 2
    width = enc.shape[0]
    keys = PAD + SLOTS
    spot = lambda i: jnp.where(i % 2 == 0, 2 + i // 2, i // 2)
    tall = pl.BlockSpec((2, half, HEAD), lambda i: (0, spot(i), 0))
    flat = pl.BlockSpec((2, HEAD, half), lambda i: (0, 0, spot(i)))
    return pl.pallas_call(
        project_body,
        grid=(4,),
        in_specs=[
            pl.BlockSpec(memory_space=pltpu.SMEM),
            pl.BlockSpec(memory_space=pltpu.SMEM),
            pl.BlockSpec((half, WIDE), lambda i: (jnp.minimum(i, 1), 0)),
            pl.BlockSpec((half, WIDE), lambda i: (jnp.maximum(i - 2, 0), 0)),
            whole(),
            whole(),
            whole(),
            whole(),
            pl.BlockSpec((width, half), lambda i: (0, i // 2)),
        ],
        out_specs=[
            pl.BlockSpec((half, width), lambda i: (i, 0)),
            pl.BlockSpec((2, half, HEAD), lambda i: (0, i, 0)),
            tall,
            flat,
            tall,
            flat,
            pl.BlockSpec((2, keys, WIDE), lambda i: (0, 0, 0)),
        ],
        out_shape=[
            pltpu.HBM((4 * half, width), bf16),
            pltpu.HBM((2, 4 * half, HEAD), bf16),
            pltpu.HBM((2, keys, HEAD), bf16),
            pltpu.HBM((2, HEAD, keys), bf16),
            pltpu.HBM((2, keys, HEAD), bf16),
            pltpu.HBM((2, HEAD, keys), bf16),
            pltpu.HBM((2, keys, WIDE), bf16),
        ],
        compiler_params=pltpu.CompilerParams(vmem_limit_bytes=32 << 20),
        cost_estimate=cost(9),
        name="project",
    )(ratio, places, *held((own, other, enc, vec, wp, bias, prompt)))


CHUNK = 1024
base_two = 1.4426950408889634


def three_terms(value):
    high = value.astype(bf16).astype(f32)
    middle = (value - high).astype(bf16).astype(f32)
    return high, middle, value - high - middle


def attend_body(q_ref, k_ref, x_ref, vt_ref, o_ref, extra_ref, *scratch):
    head = pl.program_id(0)
    keys, size = scratch[0].shape
    count = q_ref.shape[1] // size
    steepness = score_scale * base_two
    lane = lax.broadcasted_iota(jnp.int32, (size, WIDE), 1)
    place = lax.broadcasted_iota(jnp.int32, (WIDE, size), 0)
    one = jnp.where(lane == 3, 1.0, 0.0).astype(bf16)
    top = None
    for b in range(count + 1):
        fresh_ref, old_ref = scratch[b % 2], scratch[(b + 1) % 2]
        if b < count:
            query = jnp.concatenate([q_ref[0, b * size : (b + 1) * size], one], axis=1)
            partial = jnp.full((8, size), -jnp.inf, f32)
        if b > 0:
            shift = top * steepness
            total = jnp.zeros((8, size), f32)
            out = jnp.zeros((HEAD, size), f32)
        for c in range(keys // CHUNK):
            span = slice(c * CHUNK, (c + 1) * CHUNK)
            if b < count:
                wide = jnp.concatenate([k_ref[0, span], x_ref[0, span]], axis=1)
                fresh = dot(wide, query, NT)
                fresh_ref[span] = fresh
                partial = jnp.maximum(partial, jnp.max(fresh.reshape(CHUNK // 8, 8, size), axis=0))
            if b > 0:
                raised = jnp.exp2(old_ref[span] * steepness - shift)
                total = total + jnp.sum(raised.reshape(CHUNK // 8, 8, size), axis=0)
                out = out + dot(vt_ref[0, :, span], raised.astype(bf16), NN)
        if b > 0:
            rows = slice((b - 1) * size, b * size)
            total = jnp.sum(total, axis=0, keepdims=True)
            o_ref[rows] = (out / total).T.astype(bf16)
            terms = three_terms(-(top + jnp.log(total) / score_scale))
            tile = jnp.where(place == 3, 1.0, 0.0)
            for k in range(3):
                tile = tile + jnp.where(place == 4 * head + k, terms[k], 0.0)
            extra_ref[0, rows] = tile.T.astype(bf16)
        if b < count:
            top = jnp.max(partial, axis=0, keepdims=True)


BLOCK = 512


def attend(q, k, extra, vt, which):
    keys = k.shape[1]
    tall = pl.BlockSpec((1, keys, HEAD), lambda h: (h, 0, 0))
    return pl.pallas_call(
        attend_body,
        grid=(2,),
        in_specs=[
            pl.BlockSpec((1, SLOTS, HEAD), lambda h: (h, which, 0)),
            tall,
            pl.BlockSpec((1, keys, WIDE), lambda h: (0, 0, 0)),
            pl.BlockSpec((1, HEAD, keys), lambda h: (h, 0, 0)),
        ],
        out_specs=[
            pl.BlockSpec((SLOTS, HEAD), lambda h: (0, h)),
            pl.BlockSpec((1, SLOTS, WIDE), lambda h: (h, 0, 0)),
        ],
        out_shape=[shape_of((SLOTS, 2 * HEAD), bf16), shape_of((2, SLOTS, WIDE), bf16)],
        scratch_shapes=[pltpu.VMEM((keys, BLOCK), f32)] * 2,
        cost_estimate=cost(6),
        name="attend",
    )(q, k, extra, vt)


BACK_BLOCK = 256
BACK_CHUNK = 1024


def attend_back_body(q_ref, k_ref, x_ref, kt_ref, v_ref, qa_ref, qb_ref, da_ref, db_ref, ea_ref, eb_ref, dq_ref, dk_ref, dv_ref, *scratch):
    size = scratch[0].shape[1]
    keys = k_ref.shape[1]
    rows = q_ref.shape[1]
    count = rows // size
    steepness = score_scale * base_two
    mine = pl.program_id(1) == 0

    @pl.when(mine)
    def _():
        dk_ref[...] = jnp.zeros_like(dk_ref)
        dv_ref[...] = jnp.zeros_like(dv_ref)

    for b in range(count + 1):
        probs_ref, slopes_ref = scratch[2 * (b % 2) : 2 * (b % 2) + 2]
        old_probs, old_slopes = scratch[2 - 2 * (b % 2) : 4 - 2 * (b % 2)]
        if b < count:
            span = slice(b * size, (b + 1) * size)
            query = q_ref[0, span]
            grad = jnp.where(mine, da_ref[span], db_ref[span])
            aside = jnp.where(mine, qa_ref[0, span], qb_ref[0, span])
            sums = jnp.where(mine, ea_ref[span], eb_ref[span])
            query_wide = jnp.concatenate([query, aside], axis=1)
            grad_wide = jnp.concatenate([grad, sums], axis=1)
        if b > 0:
            back = jnp.zeros((HEAD, size), f32)
        for c in range(keys // BACK_CHUNK):
            span = slice(c * BACK_CHUNK, (c + 1) * BACK_CHUNK)
            if b < count:
                extra = x_ref[0, span]
                scores = dot(jnp.concatenate([k_ref[0, span], extra], axis=1), query_wide, NT)
                slopes = dot(jnp.concatenate([v_ref[0, span], extra], axis=1), grad_wide, NT)
                probs = jnp.exp2(scores * steepness)
                probs_ref[span] = probs.astype(bf16)
                slopes_ref[span] = (probs * slopes).astype(bf16)
            if b > 0:
                back = back + dot(kt_ref[0, :, span], old_slopes[span], NN)
                grad_key = dot(query_flip, old_slopes[span], NT) * score_scale
                grad_value = dot(grad_flip, old_probs[span], NT)
                dk_ref[0, :, span] += grad_key
                dv_ref[0, :, span] += grad_value
        if b > 0:
            dq_ref[(b - 1) * size : b * size] = (back * score_scale).T.astype(bf16)
        if b < count:
            query_flip, grad_flip = query.T, grad.T


def attend_back(q, k, extra, kt, v, extra_own, extra_other, grad_own, grad_other):
    keys = k.shape[1]
    tall = pl.BlockSpec((1, keys, HEAD), lambda h, i: (h, 0, 0))
    flat = pl.BlockSpec((1, HEAD, keys), lambda h, i: (h, 0, 0))
    aside = pl.BlockSpec((1, SLOTS, WIDE), lambda h, i: (h, 0, 0))
    grad = pl.BlockSpec((SLOTS, HEAD), lambda h, i: (0, h))
    sums = pl.BlockSpec((SLOTS, HEAD), lambda h, i: (0, 2))
    return pl.pallas_call(
        attend_back_body,
        grid=(2, 2),
        in_specs=[
            pl.BlockSpec((1, SLOTS, HEAD), lambda h, i: (h, i, 0)),
            tall,
            tall,
            flat,
            tall,
            aside,
            aside,
            grad,
            grad,
            sums,
            sums,
        ],
        out_specs=[pl.BlockSpec((SLOTS, HEAD), lambda h, i: (i, h)), flat, flat],
        out_shape=[
            shape_of((2 * SLOTS, 2 * HEAD), bf16),
            shape_of((2, HEAD, keys), f32),
            shape_of((2, HEAD, keys), f32),
        ],
        scratch_shapes=[pltpu.VMEM((keys, BACK_BLOCK), bf16)] * 4,
        cost_estimate=cost(20),
        name="attend_back",
    )(
        q,
        k,
        extra,
        kt,
        v,
        extra_own,
        extra_other,
        grad_own,
        grad_other,
        grad_own,
        grad_other,
    )


erfc_terms = (
    -1.26551223,
    1.00002368,
    0.37409196,
    0.09678418,
    -0.18628806,
    0.27886807,
    -1.13520398,
    1.48851587,
    -0.82215223,
    0.17087277,
)


def gelu_pair(t):
    z = jnp.abs(t) * (0.5**0.5)
    k = 1.0 / (1.0 + 0.5 * z)
    series = jnp.full_like(t, erfc_terms[-1])
    for term in erfc_terms[-2::-1]:
        series = series * k + term
    tail = 0.5 * k * jnp.exp(series - z * z)
    cumulative = jnp.where(t >= 0.0, 1.0 - tail, tail)
    density = jnp.exp(-0.5 * t * t) * 0.3989422804014327
    return t * cumulative, cumulative + t * density


def middle_body(
    sc,
    ratio,
    rows_ref,
    oa_ref,
    ob_ref,
    c0,
    c1,
    c2,
    c3,
    enc,
    vec,
    b1,
    ra,
    rb,
    y0,
    y1,
    y2,
    y3,
    da_ref,
    db_ref,
    dr_ref,
    ga,
    gb,
    gvec,
    gb1,
    cot,
    acc,
):
    step = pl.program_id(0)
    count = rows_ref.shape[0]
    for k, ref in enumerate((c0, c1, c2, c3)):

        @pl.when(step == k)
        def _(ref=ref):
            cot[...] = ref[...]

    @pl.when(step == 0)
    def _():
        acc[...] = jnp.zeros_like(acc)
        gvec[...] = jnp.zeros_like(gvec)
        gb1[...] = jnp.zeros_like(gb1)

    group = sc[0] ^ (step // 2)
    quarter = 2 * (sc[1] ^ (step % 2)) + sc[2]
    limit = jnp.where(group == 0, sc[4], sc[5])
    slot = quarter * count + lax.broadcasted_iota(jnp.int32, (count, 1), 0)
    live = (slot < limit).astype(f32)

    def weight(k, low, high):
        return (ra if k < 2 else rb)[k % 2, :, low:high]

    def row(k):
        return vec[k : k + 1, :]

    gain_one, shift_one, gain_two, shift_two, b_out, b_two, b_enc = (row(k) for k in range(7))
    embedded = ratio[0] * dot(rows_ref[...], enc[...], NT) + b_enc
    out_pair = [
        jnp.concatenate([weight(2 * k, 0, HEAD), weight(2 * k + 1, 0, HEAD)], axis=1)
        for k in (0, 1)
    ]
    attn = dot(oa_ref[...], out_pair[0], NT) + dot(ob_ref[...], out_pair[1], NT) + b_out

    def norm(residual):
        centred = residual - jnp.mean(residual, axis=-1, keepdims=True)
        inverse = lax.rsqrt(jnp.mean(centred * centred, axis=-1, keepdims=True) + ln_eps)
        return centred * inverse, inverse

    def back(grad, normed, inverse, gain):
        scaled = grad * gain
        plain = jnp.mean(scaled, axis=-1, keepdims=True)
        mixed = jnp.mean(scaled * normed, axis=-1, keepdims=True)
        return inverse * (scaled - plain - normed * mixed)

    def add_row(k, value):
        gvec[k : k + 1, :] += jnp.sum(value, axis=0, keepdims=True)

    normed_one, inverse_one = norm(embedded + attn)
    first = normed_one * gain_one + shift_one
    first_low = first.astype(bf16)
    mlp = b_two
    acts, slopes = [], []
    for k in range(4):
        pre = dot(first_low, weight(k, HEAD, HEAD + HID), NN) + b1[k : k + 1, 2 * HEAD :]
        act, slope = gelu_pair(pre)
        acts.append(act.astype(bf16))
        slopes.append(slope)
        mlp = mlp + dot(acts[k], weight(k, HEAD + HID, HEAD + 2 * HID), NT)
    normed_two, inverse_two = norm(first + mlp)
    out = ((normed_two * gain_two + shift_two) * live).astype(bf16)
    for k, ref in enumerate((y0, y1, y2, y3)):

        @pl.when(step == k)
        def _(ref=ref):
            ref[...] = out

    grad_y = cot[...].astype(f32) * live
    add_row(2, grad_y * normed_two)
    add_row(3, grad_y)
    grad_two = back(grad_y, normed_two, inverse_two, gain_two)
    grad_low = grad_two.astype(bf16)
    add_row(5, grad_low.astype(f32))
    grad_flip = grad_low.T
    first_flip = first_low.T
    grad_first = grad_two
    for k in range(4):
        acc[k, :, HEAD + HID :] += dot(grad_flip, acts[k], NN)
        grad_act = dot(grad_low, weight(k, HEAD + HID, HEAD + 2 * HID), NN)
        grad_pre = (grad_act * slopes[k]).astype(bf16)
        gb1[k : k + 1, :] += jnp.sum(grad_pre.astype(f32), axis=0, keepdims=True)
        acc[k, :, HEAD : HEAD + HID] += dot(first_flip, grad_pre, NN)
        grad_first = grad_first + dot(grad_pre, weight(k, HEAD, HEAD + HID), NT)
    add_row(0, grad_first * normed_one)
    add_row(1, grad_first)
    grad_one = back(grad_first, normed_one, inverse_one, gain_one)
    dr_ref[...] = grad_one
    attn_low = grad_one.astype(bf16)
    add_row(4, attn_low.astype(f32))
    attn_flip = attn_low.T
    for k, (source, target) in enumerate(((oa_ref, da_ref), (ob_ref, db_ref))):
        both = dot(attn_flip, source[...], NN)
        acc[2 * k, :, 0:HEAD] += both[:, 0:HEAD]
        acc[2 * k + 1, :, 0:HEAD] += both[:, HEAD:]
        both = dot(attn_low, out_pair[k], NN).astype(bf16)
        target[:, 0 : 2 * HEAD] = both
        product = both.astype(f32) * source[...].astype(f32)
        lane = lax.broadcasted_iota(jnp.int32, (count, WIDE), 1)
        tile = jnp.zeros((count, WIDE), f32)
        for h in range(2):
            sums = jnp.sum(product[:, h * HEAD : (h + 1) * HEAD], axis=1, keepdims=True)
            for m, term in enumerate(three_terms(-sums)):
                tile = tile + jnp.where(lane == 4 * h + m, term, 0.0)
        target[:, 2 * HEAD :] = tile.astype(bf16)

    @pl.when(step == 3)
    def _():
        ga[...] = acc[0:2].astype(bf16)
        gb[...] = acc[2:4].astype(bf16)


def middle(sc, ratio, rows, o_own, o_other, cots, enc, vec, b1, rest_own, rest_other):
    size = rows.shape[0] // 4
    width = enc.shape[0]
    spot = lambda i, sc: (2 * (sc[0] ^ (i // 2)) + (sc[1] ^ (i % 2)), 0)
    pair = pl.BlockSpec((size, 2 * HEAD), spot)
    smem = pl.BlockSpec(memory_space=pltpu.SMEM)
    fixed = pl.BlockSpec((size, width), lambda i, sc: (0, 0))
    weight = rest_own.shape
    return pl.pallas_call(
        middle_body,
        grid_spec=pltpu.PrefetchScalarGridSpec(
            num_scalar_prefetch=1,
            grid=(4,),
            in_specs=[smem, pl.BlockSpec((size, WIDE), spot), pair, pair]
            + [fixed] * 4
            + [whole()] * 5,
            out_specs=[fixed] * 4
            + [pl.BlockSpec((size, 3 * HEAD), spot)] * 2
            + [pl.BlockSpec((size, width), spot)]
            + [
                pl.BlockSpec(weight, lambda i, sc: (0, 0, 0)),
                pl.BlockSpec(weight, lambda i, sc: (0, 0, 0)),
                pl.BlockSpec((8, width), lambda i, sc: (0, 0)),
                pl.BlockSpec((4, HID), lambda i, sc: (0, 0)),
            ],
            scratch_shapes=[
                pltpu.VMEM((size, width), bf16),
                pltpu.VMEM((4,) + weight[1:], f32),
            ],
        ),
        out_shape=[pltpu.VMEM((size, width), bf16)] * 4
        + [
            pltpu.HBM((4 * size, 3 * HEAD), bf16),
            pltpu.HBM((4 * size, 3 * HEAD), bf16),
            pltpu.HBM((4 * size, width), f32),
            pltpu.VMEM(weight, bf16),
            pltpu.VMEM(weight, bf16),
            pltpu.HBM((8, width), f32),
            pltpu.HBM((4, HID), f32),
        ],
        compiler_params=pltpu.CompilerParams(vmem_limit_bytes=44 << 20),
        cost_estimate=cost(25),
        name="middle",
    )(sc, ratio, rows, o_own, o_other, *cots, enc, vec, b1, *held((rest_own, rest_other)))


def held(args, near=True):
    space = pltpu.VMEM if near else pltpu.HBM
    return tuple(pltpu.with_memory_space_constraint(arg, space) for arg in args)


def simple(body, out_shape, *args, scalars=None, scratch=(), near=(True, True), name=None):
    specs = [whole()] * len(args)
    args = held(args, near[0])
    if scalars is not None:
        specs = [pl.BlockSpec(memory_space=pltpu.SMEM)] + specs
        args = (scalars,) + args
    many = isinstance(out_shape, (list, tuple))
    if near[1]:
        kept = lambda shape: pltpu.VMEM(shape.shape, shape.dtype)
        out_shape = [kept(shape) for shape in out_shape] if many else kept(out_shape)
    return pl.pallas_call(
        body,
        in_specs=specs,
        out_specs=[whole()] * len(out_shape) if many else whole(),
        out_shape=out_shape,
        scratch_shapes=scratch,
        compiler_params=pltpu.CompilerParams(vmem_limit_bytes=16 << 20),
        cost_estimate=cost(2),
        name=name,
    )(*args)


def place(parts, index, name, near=(True, True)):
    def body(sc, *refs):
        for k, ref in enumerate(refs[:-1]):
            refs[-1][sc[0] ^ k] = ref[...]

    first = parts[0]
    return simple(
        body,
        shape_of((len(parts),) + first.shape, first.dtype),
        *parts,
        scalars=index.reshape(1).astype(jnp.int32),
        near=near,
        name=name,
    )


TAIL = 3 * HEAD
FEAT_ROWS = 112
LAST = 112
VEC = 104


def spread(row):
    parts = row.reshape(row.shape[:-1] + (4, row.shape[-1] // 4))
    room = WIDE - LAST - parts.shape[-1]
    return jnp.pad(parts, [(0, 0)] * (parts.ndim - 1) + [(LAST, room)])


def widened(prompt):
    return jnp.pad(prompt, [(0, 0)] * (prompt.ndim - 1) + [(0, 3 * TAIL - prompt.shape[-1])])


def with_bias(prompt, bias):
    row = jnp.pad(
        bias[..., None, :].astype(prompt.dtype),
        [(0, 0)] * (bias.ndim - 1)
        + [(0, prompt.shape[-2] - 1), (PAD, 3 * TAIL - PAD - bias.shape[-1])],
    )
    return widened(prompt) + row


def in_chunks(wide):
    lead, strip = wide.shape[:-2], wide.shape[-2]
    parts = jnp.swapaxes(wide.reshape(lead + (strip, 3, TAIL)), -3, -2)
    return parts.reshape(lead + (3 * strip, TAIL))


def pack_parts(block, prompt, encoder, vectors, biases):
    slab, strip = block.shape[0], prompt.shape[0]
    flat = block.reshape(slab * 8, HEAD)
    out = [shape_of((slab + 3 * strip, TAIL), bf16), shape_of((slab, 8 * HEAD - TAIL), bf16)]
    if 2 * slab != WIDE:
        low = block.reshape(slab, 8 * HEAD).astype(bf16)
        small = jnp.concatenate(
            [
                jnp.pad(encoder, ((0, 0), (0, VEC - FEAT))),
                jnp.pad(vectors, ((0, 0), (0, LAST - VEC - 7))),
                jnp.pad(biases.reshape(strip, 4), ((0, 0), (0, WIDE - LAST - 4))),
            ],
            axis=1,
        )
        chunks = in_chunks(
            jnp.concatenate([jnp.pad(prompt, ((0, 0), (0, PAD - PROMPT))), small], axis=1)
        )
        return jnp.concatenate([low[:, 0:TAIL], chunks.astype(bf16)], axis=0), low[:, TAIL:]

    def body(block_ref, prompt_ref, enc_ref, vec_ref, bias_ref, main_ref, rest_ref, tall, tile, line):
        for j in range(8):
            lanes = block_ref[pl.ds(j, slab, stride=8), :].astype(bf16)
            if j < 3:
                main_ref[0:slab, j * HEAD : (j + 1) * HEAD] = lanes
            else:
                rest_ref[:, (j - 3) * HEAD : (j - 2) * HEAD] = lanes
        low = prompt_ref[...].astype(bf16)
        for k in range(2):
            rows = slice(slab + k * strip, slab + (k + 1) * strip)
            main_ref[rows, :] = low[:, k * TAIL : (k + 1) * TAIL]
        rows = slice(slab + 2 * strip, slab + 3 * strip)
        main_ref[rows, WIDE : 2 * WIDE] = jnp.zeros((strip, WIDE), bf16)
        main_ref[rows, 0 : PROMPT - 2 * TAIL] = low[:, 2 * TAIL :]
        tall[...] = jnp.zeros_like(tall)
        tall[VEC : VEC + 7, :] = vec_ref[...]
        tile[...] = tall[...].T
        tile[:, 0:FEAT] = enc_ref[...]
        line[...] = jnp.zeros_like(line)
        line[:, 0:slab] = bias_ref[...]
        main_ref[rows, 2 * WIDE :] = (tile[...] + spread_row(line[...], strip)).astype(bf16)

    return simple(
        body,
        out,
        flat,
        prompt,
        encoder,
        vectors.T,
        biases.T,
        near=(False, True),
        scratch=[
            pltpu.VMEM((WIDE, strip), f32),
            pltpu.VMEM((strip, WIDE), f32),
            pltpu.VMEM((1, WIDE), f32),
        ],
        name="pack_parts",
    )


def spread_row(row, strip):
    place = lax.broadcasted_iota(jnp.int32, (strip, WIDE), 0)
    lane = lax.broadcasted_iota(jnp.int32, (strip, WIDE), 1)
    total = jnp.zeros((strip, WIDE), f32)
    for k in range(4):
        turned = jnp.broadcast_to(pltpu.roll(row, LAST - k * strip, 1), (strip, WIDE))
        total = total + jnp.where((place == k) & (lane >= LAST), turned, 0.0)
    return total


def gathered_row(tile, strip):
    lane = lax.broadcasted_iota(jnp.int32, (1, WIDE), 1)
    total = jnp.zeros((1, WIDE), f32)
    for k in range(4):
        turned = pltpu.roll(tile[k : k + 1], (k * strip - LAST) % WIDE, 1)
        total = total + jnp.where(lane // strip == k, turned, 0.0)
    return total


def join_features(parts, places):
    feats, rows = parts[0].shape

    def body(sc, *refs):
        for k, ref in enumerate(refs[:-1]):
            spot = 2 * (sc[0] ^ (k // 2)) + (sc[1] ^ (k % 2))
            refs[-1][spot, 0:feats] = ref[...]

    return simple(
        body, shape_of((4, FEAT_ROWS, rows), bf16), *parts, scalars=places, name="join_features"
    )


def unpack_main(tops, lows, feats, feats_low, mask, places, slab, strip):
    n_ep = tops[0].shape[0]
    rows = feats.shape[2]
    plain = 2 * slab != WIDE
    shapes = [
        shape_of((2, n_ep, 2, slab, TAIL), bf16),
        shape_of((n_ep, 2, 2, 2, strip, 3 * TAIL), bf16),
        shape_of((n_ep, 2, 2, 2, strip, WIDE), bf16),
        shape_of((8, n_ep * 2 * slab), f32),
        shape_of((4, n_ep * 2 * slab), f32),
        shape_of((4 * rows, WIDE), bf16),
        shape_of((4 * rows, WIDE), bf16),
    ]

    def features(mask_ref, source, target):
        for p in range(4):
            flip = jnp.concatenate([source[p], jnp.zeros((WIDE - FEAT_ROWS, rows), bf16)], axis=0)
            piece = jnp.where(mask_ref[...] > 0.0, flip.T.astype(f32), 0.0).astype(bf16)
            target[p * rows : (p + 1) * rows, :] = piece

    if plain:
        side, row, core = places[0], places[1], places[2]

        def ordered(parts, axis):
            cores = []
            for group in parts:
                sides = []
                for b in (0, 1):
                    sides.append(jnp.stack(pick(group[2 * b], group[2 * b + 1], row), axis=axis))
                cores.append(jnp.stack(pick(sides[0], sides[1], side), axis=axis))
            return jnp.stack(pick(cores[0], cores[1], core), axis=axis + 2)

        heads = [
            jnp.stack(pick(tops[r][:, 0:slab], tops[2 + r][:, 0:slab], side), axis=1) for r in (0, 1)
        ]
        chunks = ordered([[t[:, slab:] for t in tops], [t[:, slab:] for t in lows]], 1)
        chunks = chunks.reshape((n_ep, 2, 2, 2, 3, strip, TAIL))
        wide = jnp.swapaxes(chunks, -3, -2).reshape((n_ep, 2, 2, 2, strip, 3 * TAIL))
        small = wide[..., PAD:]
        vec = small.reshape(n_ep * 8 * strip, WIDE).astype(f32).T[VEC : VEC + 8]
        biases = []
        for group in (tops, lows):
            for r in (0, 1):
                pair = [
                    group[2 * b + r][:, slab + 2 * strip :, PAD - 2 * TAIL + LAST :][..., 0:4]
                    for b in (0, 1)
                ]
                biases.append(jnp.stack(pick(pair[0], pair[1], side), axis=1).reshape(-1))
        def both(mask_ref, a, b, c, d):
            features(mask_ref, a, c)
            features(mask_ref, b, d)

        masked = simple(
            both,
            shapes[5:],
            mask,
            feats,
            feats_low,
            near=(False, False),
            name="features",
        )
        return [jnp.stack(heads), wide, small, vec, jnp.stack(biases).astype(f32), *masked]

    def body(sc, t0, t1, t2, t3, l0, l1, l2, l3, fa, fb, mask_ref, *outs):
        wp_ref, prompt_ref, small_ref, vec_ref, bias_ref, own_ref, other_ref = outs
        side, row, core = sc[0], sc[1], sc[2]
        groups = ((t0, t1, t2, t3), (l0, l1, l2, l3))
        bias_tiles = {}
        for b in range(2):
            for r in range(2):
                k = 2 * b + r
                wp_ref[r, :, side ^ b] = groups[0][k][:, 0:slab, :]
                for other in range(2):
                    spot = core ^ other
                    part = groups[other][k][:, slab:, :]
                    for j in range(3):
                        lanes = slice(j * TAIL, (j + 1) * TAIL)
                        span = slice(j * strip, (j + 1) * strip)
                        prompt_ref[:, side ^ b, row ^ r, spot, :, lanes] = part[:, span, :]
                    tile = part[:, 2 * strip :, TAIL - WIDE :]
                    small_ref[:, side ^ b, row ^ r, spot] = tile
                    bias_tiles[b, r, other] = tile.astype(f32)
        flip = small_ref[...].reshape(n_ep * 8 * strip, WIDE).astype(f32).T
        vec_ref[...] = flip[VEC : VEC + 8]
        low_half = lax.broadcasted_iota(jnp.int32, (1, WIDE), 1) < slab
        for r in range(2):
            for other in range(2):
                for e in range(n_ep):
                    mine = gathered_row(bias_tiles[0, r, other][e], strip)
                    theirs = gathered_row(bias_tiles[1, r, other][e], strip)
                    first = jnp.where(side == 0, mine, theirs)
                    second = jnp.where(side == 0, theirs, mine)
                    row_tile = jnp.where(low_half, first, pltpu.roll(second, slab, 1))
                    k = r + 2 * other
                    bias_ref[k : k + 1, e * WIDE : (e + 1) * WIDE] = row_tile
        features(mask_ref, fa, own_ref)
        features(mask_ref, fb, other_ref)

    return simple(
        body, shapes, *tops, *lows, feats, feats_low, mask, scalars=places, name="unpack_main"
    )


def unpack_rest(tops, places):
    n_ep, slab, width = tops[0].shape

    def body(sc, t0, t1, t2, t3, out_ref):
        for k, ref in enumerate((t0, t1, t2, t3)):
            out_ref[k % 2, :, sc[0] ^ (k // 2)] = ref[...]

    return simple(
        body, shape_of((2, n_ep, 2, slab, width), bf16), *tops, scalars=places, name="unpack_rest"
    )


def back_body(dq_ref, dk_ref, dv_ref, wp, out_ref):
    def columns(k):
        return jnp.concatenate([wp[h, :, k * HEAD : (k + 1) * HEAD] for h in range(2)], axis=1)

    def both(ref):
        return jnp.concatenate([ref[h].astype(bf16) for h in range(2)], axis=0).T

    total = dot(dq_ref[...], columns(0), NT)

    @pl.when(pl.program_id(0) == 0)
    def _():
        more = dot(both(dk_ref), columns(1), NT) + dot(both(dv_ref), columns(2), NT)
        out_ref[...] = (total + more).astype(out_ref.dtype)

    @pl.when(pl.program_id(0) == 1)
    def _():
        out_ref[...] = total.astype(out_ref.dtype)


def back_rows(dq, dk, dv, wp, which, dtype):
    half = dq.shape[0] // 4
    width = wp.shape[1]
    key = pl.BlockSpec((2, HEAD, half), lambda i: (0, 0, 2 + which))
    return pl.pallas_call(
        back_body,
        grid=(2,),
        in_specs=[pl.BlockSpec((half, 2 * HEAD), lambda i: (2 * which + i, 0)), key, key, whole()],
        out_specs=pl.BlockSpec((half, width), lambda i: (i, 0)),
        out_shape=pltpu.HBM((2 * half, width), dtype),
        compiler_params=pltpu.CompilerParams(vmem_limit_bytes=32 << 20),
        cost_estimate=cost(3),
        name="back_rows",
    )(*held((dq, dk, dv, wp), False))


def weight_body(x_ref, dq_ref, dk_ref, dv_ref, prompt, wp, gb1, gw_ref, gp_ref, gb_ref, acc, gq_ref, gv_ref):
    step = pl.program_id(0)

    @pl.when(step == 0)
    def _():
        acc[...] = jnp.zeros_like(acc)
        gq_ref[...] = jnp.zeros_like(gq_ref)
        gv_ref[...] = jnp.zeros_like(gv_ref)

    flip = x_ref[...].T
    acc[0] += dot(flip, dq_ref[...], NN)
    gq_ref[...] += jnp.sum(dq_ref[...].astype(f32), axis=0, keepdims=True)
    grad_key = jnp.concatenate([dk_ref[h] for h in range(2)], axis=0)
    grad_value = jnp.concatenate([dv_ref[h] for h in range(2)], axis=0)
    key_high = grad_key.astype(bf16)
    value_high = grad_value.astype(bf16)
    ones = jnp.ones((8, grad_key.shape[1]), bf16)
    gv_ref[...] += dot(ones, value_high, NT)[0:1]

    @pl.when(step % 2 == 0)
    def _():
        acc[1] += dot(flip, key_high, NT)
        acc[2] += dot(flip, value_high, NT)

    @pl.when(step % 2 == 1)
    def _():
        key_low = (grad_key - key_high.astype(f32)).astype(bf16)
        value_low = (grad_value - value_high.astype(f32)).astype(bf16)
        source = prompt[...]
        acc[1] += dot(source, key_high, NT) + dot(source, key_low, NT)
        acc[2] += dot(source, value_high, NT) + dot(source, value_low, NT)
        gv_ref[...] += dot(ones, value_low, NT)[0:1]
        w_key, w_value = (
            jnp.concatenate([wp[h, :, k * HEAD : (k + 1) * HEAD] for h in range(2)], axis=1)
            for k in (1, 2)
        )
        total = dot(w_key, key_high, NN) + dot(w_key, key_low, NN)
        total = total + dot(w_value, value_high, NN) + dot(w_value, value_low, NN)
        gp_ref[...] = total.astype(bf16)

    @pl.when(step == 3)
    def _():
        for h in range(2):
            for k in range(3):
                lanes = slice(h * HEAD, (h + 1) * HEAD)
                gw_ref[h, :, k * HEAD : (k + 1) * HEAD] = acc[k, :, lanes].astype(bf16)
            gb_ref[h : h + 1, 0:HEAD] = gq_ref[:, h * HEAD : (h + 1) * HEAD]
            gb_ref[h : h + 1, HEAD : 2 * HEAD] = gv_ref[:, h * HEAD : (h + 1) * HEAD]
        gb_ref[2:4, 0 : 2 * HEAD] = jnp.zeros((2, 2 * HEAD), f32)
        gb_ref[:, 2 * HEAD :] = gb1[...]


def weight_grads(x, dq, dk, dv, prompt, wp, gb1):
    half = dq.shape[0] // 4
    width = wp.shape[1]
    spot = lambda i: jnp.where(i % 2 == 0, 2 + i // 2, i // 2)
    key = pl.BlockSpec((2, HEAD, half), lambda i: (0, 0, spot(i)))
    return pl.pallas_call(
        weight_body,
        grid=(4,),
        in_specs=[
            pl.BlockSpec((half, width), lambda i: (i, 0)),
            pl.BlockSpec((half, 2 * HEAD), lambda i: (i, 0)),
            key,
            key,
            pl.BlockSpec((width, half), lambda i: (0, i // 2)),
            whole(),
            whole(),
        ],
        out_specs=[
            pl.BlockSpec((2, width, TAIL), lambda i: (0, 0, 0)),
            pl.BlockSpec((width, half), lambda i: (0, i // 2)),
            pl.BlockSpec((4, width), lambda i: (0, 0)),
        ],
        out_shape=[
            pltpu.VMEM((2, width, TAIL), bf16),
            pltpu.VMEM((width, PAD), bf16),
            pltpu.VMEM((4, width), f32),
        ],
        compiler_params=pltpu.CompilerParams(vmem_limit_bytes=40 << 20),
        scratch_shapes=[pltpu.VMEM((3, width, 2 * HEAD), f32)]
        + [pltpu.VMEM((1, 2 * HEAD), f32)] * 2,
        cost_estimate=cost(9),
        name="weight_grads",
    )(*held((x, dq, dk, dv, prompt, wp), False), gb1)


def input_body(sc, ratio, dr_ref, own_ref, got_ref, rows_ref, enc, mask, rows_grad, i0, i1, i2, i3, small_ref, acc, bias):
    step = pl.program_id(0)
    low = (dr_ref[...] + own_ref[...] + got_ref[...].astype(f32)).astype(bf16)
    part = dot(low.T, rows_ref[...], NN) * ratio[0]
    part_bias = jnp.sum(low.astype(f32), axis=0, keepdims=True)

    @pl.when(step == 0)
    def _():
        acc[...] = part
        bias[...] = part_bias

    @pl.when(step > 0)
    def _():
        acc[...] += part
        bias[...] += part_bias

    grad = dot(enc[...].T, low, NT) * ratio[0] * mask[...]
    for k, ref in enumerate((i0, i1, i2, i3)):

        @pl.when(step == k)
        def _(ref=ref):
            ref[...] = grad[0:FEAT_ROWS].astype(bf16)

    @pl.when(step == 3)
    def _():
        width = acc.shape[0]
        rows = jnp.concatenate(
            [
                jnp.zeros((VEC, width), f32),
                rows_grad[0:6],
                bias[...],
                jnp.zeros((WIDE - VEC - 7, width), f32),
            ],
            axis=0,
        )
        small_ref[...] = (acc[...] + rows.T).astype(bf16)


def input_grads(sc, ratio, dr, own, got, rows, enc, mask, rows_grad):
    size = rows.shape[0] // 4
    width = enc.shape[0]
    spot = lambda i, sc: (2 * (sc[0] ^ (i // 2)) + (sc[1] ^ (i % 2)), 0)
    block = pl.BlockSpec((size, width), spot)
    fixed = pl.BlockSpec((FEAT_ROWS, size), lambda i, sc: (0, 0))
    return pl.pallas_call(
        input_body,
        grid_spec=pltpu.PrefetchScalarGridSpec(
            num_scalar_prefetch=1,
            grid=(4,),
            in_specs=[
                pl.BlockSpec(memory_space=pltpu.SMEM),
                block,
                block,
                block,
                pl.BlockSpec((size, WIDE), spot),
                whole(),
                whole(),
                whole(),
            ],
            out_specs=[fixed] * 4 + [pl.BlockSpec((width, WIDE), lambda i, sc: (0, 0))],
            scratch_shapes=[pltpu.VMEM((width, WIDE), f32), pltpu.VMEM((1, width), f32)],
        ),
        out_shape=[pltpu.VMEM((FEAT_ROWS, size), bf16)] * 4 + [pltpu.VMEM((width, WIDE), bf16)],
        compiler_params=pltpu.CompilerParams(vmem_limit_bytes=32 << 20),
        cost_estimate=cost(6),
        name="input_grads",
    )(sc, ratio, *held((dr, own, got, rows), False), enc, mask, rows_grad)


def split_prompt(grad, bias_rows, places, n_ep, strip):
    blocks = grad.reshape(n_ep, 2, 2, 2, strip, PAD)
    if 8 * strip != WIDE:
        row, core = places[1], places[2]
        table = bias_rows.reshape(2, 2, n_ep, 2, 4 * strip)
        both = []
        for other in (0, 1):
            by_row = jnp.stack(pick(table[other, 0], table[other, 1], row), axis=2)
            part = lax.dynamic_index_in_dim(blocks, core ^ other, 3, keepdims=False)
            both.append(in_chunks(with_bias(part, by_row)))
        return both

    def body(sc, grad_ref, bias_ref, mine_ref, sent_ref):
        row, core = sc[1], sc[2]
        first = lax.broadcasted_iota(jnp.int32, (strip, WIDE), 0) == 0
        low_half = lax.broadcasted_iota(jnp.int32, (1, WIDE), 1) < 4 * strip
        for s in range(2):
            for r in range(2):
                for other, ref in enumerate((mine_ref, sent_ref)):
                    for j in range(3):
                        rows = slice(j * strip, (j + 1) * strip)
                        high = min(PAD, (j + 1) * TAIL)
                        part = grad_ref[:, s, row ^ r, core ^ other, :, j * TAIL : high]
                        ref[:, s, row ^ r, rows, 0 : high - j * TAIL] = part
                    for e in range(n_ep):
                        k = r + 2 * other
                        tile = bias_ref[k : k + 1, e * WIDE : (e + 1) * WIDE]
                        if s == 1:
                            tile = pltpu.roll(tile, WIDE - 4 * strip, 1)
                        tile = jnp.where(low_half, tile, 0.0)
                        tile = jnp.where(first, tile, 0.0).astype(bf16)
                        ref[e, s, row ^ r, 2 * strip : 3 * strip, PAD - 2 * TAIL :] = tile

    shape = shape_of((n_ep, 2, 2, 3 * strip, TAIL), bf16)
    return simple(body, [shape, shape], blocks, bias_rows, scalars=places, name="split_prompt")


def split_small(grad, places, n_ep, strip):
    blocks = grad.reshape(n_ep * 4, 2, strip, WIDE)

    def body(sc, grad_ref, mine_ref, sent_ref):
        mine_ref[...] = grad_ref[:, sc[2]]
        sent_ref[...] = grad_ref[:, 1 - sc[2]]

    shape = shape_of((n_ep * 4, strip, WIDE), bf16)
    return simple(body, [shape, shape], blocks, scalars=places, name="split_small")


def pack_main(gw, mine, got, places, slab, strip):
    n_ep = mine.shape[0]
    heads = gw.reshape(2, n_ep, 2, slab, TAIL)
    if 2 * slab != WIDE:
        pair = (mine.astype(f32) + got.astype(f32)).astype(bf16)
        outs = []
        for b in (0, 1):
            for r in (0, 1):
                side, row = places[0] ^ b, places[1] ^ r
                part = lax.dynamic_index_in_dim(pair, side, 1, keepdims=False)
                part = lax.dynamic_index_in_dim(part, row, 1, keepdims=False)
                head = lax.dynamic_index_in_dim(heads[r], side, 1, keepdims=False)
                outs.append(jnp.concatenate([head, part], axis=1))
        return outs

    def body(sc, gw_ref, a_ref, b_ref, *outs):
        for b in range(2):
            for r in range(2):
                out = outs[2 * b + r]
                side, row = sc[0] ^ b, sc[1] ^ r
                out[:, 0:slab, :] = gw_ref[r, :, side]
                pair = a_ref[:, side, row].astype(f32) + b_ref[:, side, row].astype(f32)
                out[:, slab : slab + 3 * strip, :] = pair.astype(bf16)

    shape = shape_of((n_ep, slab + 3 * strip, TAIL), bf16)
    return simple(body, [shape] * 4, heads, mine, got, scalars=places, name="pack_main")


def pack_small(ins, mine, got, places, n_ep, strip):
    rows = ins[0].shape[1]
    mine = mine.reshape(n_ep, 2, 2, strip, WIDE)
    got = got.reshape(n_ep, 2, 2, strip, WIDE)
    total = FEAT_ROWS + n_ep * strip
    if 8 * strip != WIDE:
        pair = (mine.astype(f32) + got.astype(f32)).astype(bf16)
        outs = []
        for k in range(4):
            part = lax.dynamic_index_in_dim(pair, places[0] ^ (k // 2), 1, keepdims=False)
            part = lax.dynamic_index_in_dim(part, places[1] ^ (k % 2), 1, keepdims=False)
            part = jnp.pad(part.reshape(n_ep * strip, WIDE), ((0, 0), (0, rows - WIDE)))
            outs.append(jnp.concatenate([ins[k], part], axis=0))
        return outs

    def body(sc, *refs):
        in_refs, a_ref, b_ref, outs = refs[0:4], refs[4], refs[5], refs[6:]
        for k in range(4):
            side, row = sc[0] ^ (k // 2), sc[1] ^ (k % 2)
            outs[k][0:FEAT_ROWS] = in_refs[k][...]
            pair = a_ref[:, side, row].astype(f32) + b_ref[:, side, row].astype(f32)
            outs[k][FEAT_ROWS:, 0:WIDE] = pair.reshape(n_ep * strip, WIDE).astype(bf16)

    return simple(
        body, [shape_of((total, rows), bf16)] * 4, *ins, mine, got, scalars=places, name="pack_small"
    )


def pack_rest(mine, got, outs, places, n_ep, slab):
    width = mine.shape[-1]
    rows, lanes = outs[0].shape
    count = n_ep * slab
    mine = mine.reshape(2, n_ep, 2, slab, width)
    got = got.reshape(2, n_ep, 2, slab, width)

    def body(sc, a_ref, b_ref, *refs):
        for k in range(4):
            side = sc[0] ^ (k // 2)
            pair = a_ref[k % 2, :, side].astype(f32) + b_ref[k % 2, :, side].astype(f32)
            refs[4 + k][0:count] = pair.reshape(count, width).astype(bf16)
            refs[4 + k][count:, 0:lanes] = refs[k][...]

    shape = shape_of((count + rows, width), bf16)
    return simple(body, [shape] * 4, mine, got, *outs, scalars=places, name="pack_rest")


def sum_rest(parts, places, n_ep, slab):
    width = parts[0].shape[1]
    if n_ep > 4:
        total = sum(part[0 : n_ep * slab].astype(f32) for part in parts)
        return reduce_ep(total.reshape(n_ep, slab, width), None)

    def body(sc, *refs):
        ins, outs = refs[: len(parts)], refs[len(parts) :]
        for k, out in enumerate(outs):
            spot = pl.multiple_of((sc[6] ^ k) * slab, slab)
            total = ins[0][pl.ds(spot, slab), :].astype(f32)
            for ref in ins[1:]:
                total = total + ref[pl.ds(spot, slab), :].astype(f32)
            out[...] = total.astype(bf16)

    pieces = simple(
        body, [shape_of((slab, width), bf16)] * n_ep, *parts, scalars=places, name="sum_rest"
    )
    return reduce_ep(None, pieces)


def sum_main(mains, smalls, places, slab, strip):
    n_ep = mains[0].shape[0]
    if n_ep > 4:
        total = sum(part.astype(f32) for part in mains)
        small = sum(part[FEAT_ROWS:, 0:WIDE].astype(f32) for part in smalls)
        small = jnp.pad(small.reshape(n_ep, strip, WIDE), ((0, 0), (0, 0), (0, TAIL - WIDE)))
        return reduce_ep(jnp.concatenate([total, small], axis=1), None)

    def body(sc, *refs):
        main_refs, small_refs, outs = refs[0:4], refs[4:8], refs[8:]
        for k, out in enumerate(outs):
            spot = sc[6] ^ k
            total = main_refs[0][spot].astype(f32)
            for ref in main_refs[1:]:
                total = total + ref[spot].astype(f32)
            out[0 : slab + 3 * strip] = total.astype(bf16)
            where = pl.multiple_of(FEAT_ROWS + spot * strip, strip)
            total = small_refs[0][pl.ds(where, strip), 0:WIDE].astype(f32)
            for ref in small_refs[1:]:
                total = total + ref[pl.ds(where, strip), 0:WIDE].astype(f32)
            out[slab + 3 * strip :, 0:WIDE] = total.astype(bf16)
            out[slab + 3 * strip :, WIDE:] = jnp.zeros((strip, TAIL - WIDE), bf16)

    shape = shape_of((slab + 4 * strip, TAIL), bf16)
    pieces = simple(body, [shape] * n_ep, *mains, *smalls, scalars=places, name="sum_main")
    return reduce_ep(None, pieces)


def place_rows(parts, index, begin, shape, dtype, name):
    def body(sc, *refs):
        for k, ref in enumerate(refs[:-1]):
            refs[-1][sc[0] ^ k] = ref[begin : begin + shape[0], 0 : shape[1]].astype(dtype)

    return simple(
        body,
        shape_of((len(parts),) + shape, dtype),
        *parts,
        scalars=index.reshape(1).astype(jnp.int32),
        near=(True, False),
        name=name,
    )


def final_sums(mains, rests, slab, strip):
    def body(*refs):
        main_refs, rest_refs = refs[: len(mains)], refs[len(mains) : len(mains) + len(rests)]
        block_ref, prompt_ref, small_ref, bias_ref, square_ref = refs[len(mains) + len(rests) :]

        def added(group):
            total = group[0][...].astype(f32)
            for ref in group[1:]:
                total = total + ref[...].astype(f32)
            return total

        main, rest = added(main_refs), added(rest_refs)
        square = jnp.sum(jnp.sum(main * main, axis=0, keepdims=True), axis=1, keepdims=True)
        square = square + jnp.sum(
            jnp.sum(rest * rest, axis=0, keepdims=True), axis=1, keepdims=True
        )
        for j in range(8):
            if j < 3:
                tile = main[0:slab, j * HEAD : (j + 1) * HEAD]
            else:
                tile = rest[:, (j - 3) * HEAD : (j - 2) * HEAD]
            block_ref[pl.ds(j, slab, stride=8), :] = tile
        for j in range(3):
            part = main[slab + j * strip : slab + (j + 1) * strip]
            high = min(PROMPT, (j + 1) * TAIL)
            prompt_ref[:, j * TAIL : high] = part[:, 0 : high - j * TAIL]
        small_ref[...] = main[slab + 3 * strip :, 0:WIDE]
        bias_ref[...] = main[slab + 2 * strip : slab + 2 * strip + 1, TAIL - WIDE :]
        square_ref[...] = jnp.broadcast_to(square, (8, 128))

    return simple(
        body,
        [
            shape_of((slab * 8, HEAD), f32),
            shape_of((strip, PROMPT), f32),
            shape_of((strip, WIDE), f32),
            shape_of((1, WIDE), f32),
            shape_of((8, 128), f32),
        ],
        *mains,
        *rests,
        name="final_sums",
    )


def adam_all(squares, params, moments, grads):
    slab = params[0].shape[0] // 8
    rates = (rate_matrix, rate_vector, rate_matrix, rate_vector, rate_vector)
    decays = (weight_decay, weight_decay, weight_decay, 0.0, 0.0)
    count = squares.shape[0]

    def body(sq_ref, *refs):
        weights, moment_refs, grad_refs, outs = refs[0:5], refs[5:10], refs[10:14], refs[14:]
        total = sq_ref[0, 0:1, 0:1]
        for k in range(1, count):
            total = total + sq_ref[k, 0:1, 0:1]
        norm = jnp.sqrt(total)
        outs[0][...] = norm
        factor = jnp.minimum(1.0, clip_norm / (norm + 1e-06))
        small = grad_refs[2][...]
        picked = (
            grad_refs[0][...],
            grad_refs[1][...],
            small[:, 0:FEAT],
            small.T[VEC : VEC + 7],
            grad_refs[3][:, 0:slab],
        )
        for k in range(5):
            both = moment_refs[k]
            pair = (both[:, 0], both[:, 1]) if k == 3 else (both[0], both[1])
            news = adam_update(weights[k][...], pair, picked[k], factor, rates[k], decays[k])
            for m in range(3):
                outs[1 + 4 * k + m][...] = news[m]
            if k > 0:
                outs[4 + 4 * k][...] = news[3]
        for j in range(8):
            tile = outs[1][pl.ds(j, slab, stride=8), :]
            outs[4][:, j * HEAD : (j + 1) * HEAD] = tile.astype(bf16)

    shapes = [shape_of((1, 1), f32)]
    for k, param in enumerate(params):
        low = (slab, 8 * HEAD) if k == 0 else param.shape
        shapes += [shape_of(param.shape, f32)] * 3 + [shape_of(low, bf16)]
    return simple(body, shapes, squares, *params, *moments, *grads, near=(True, False), name="adam_all")


def shards(
    feats,
    counts,
    feat_mask,
    cotangent,
    block_weights,
    block_moments,
    head_biases,
    bias_moments,
    encoder,
    encoder_moments,
    shared_vectors,
    vector_moments,
    prompt,
    prompt_moments,
):
    n_ep = lax.axis_size("ep")
    side = lax.axis_index("split")
    row = lax.axis_index("tp") // 2
    core = lax.axis_index("tp") % 2
    chip = side * 2 + row
    rows = feats.shape[2]
    width = cotangent.shape[3]
    slab = block_weights.shape[0]
    strip = encoder.shape[0]

    mask_row = lax.dynamic_index_in_dim(feat_mask, chip, 0, keepdims=False)
    count_pair = lax.dynamic_index_in_dim(counts, chip, 0, keepdims=False)
    mask_float = mask_row.astype(f32)
    ratio = (FEAT / jnp.sum(mask_float)).reshape(1)
    spot = jnp.arange(8, dtype=jnp.int32)
    places = jnp.pad(count_pair, (4, 2)).astype(jnp.int32)
    for k, value in ((0, side), (1, row), (2, core), (3, chip), (6, lax.axis_index("ep"))):
        places = places + jnp.where(spot == k, value, 0)

    def to_chip(array):
        return plane_list(
            [lax.dynamic_index_in_dim(array[0], chip ^ k, 0, keepdims=False) for k in range(4)]
        )

    def plane_list(parts):
        got = plane_swap(lambda b, r: parts[2 * b + r])
        return [got[b, r] for b in (0, 1) for r in (0, 1)]

    main_part, rest_part = pack_parts(
        block_weights, prompt, encoder, shared_vectors, head_biases
    )
    mask_wide = jnp.pad(mask_float, (0, WIDE - FEAT)).reshape(1, WIDE)
    flipped = jnp.transpose(feats[0], (0, 2, 1))
    main_pieces = gather_ep(main_part)
    feats_parts = plane_list(
        [lax.dynamic_index_in_dim(flipped, chip ^ k, 0, keepdims=False) for k in range(4)]
    )
    main_pieces, feats_parts = lax.optimization_barrier((main_pieces, feats_parts))
    feats_own = join_features(feats_parts, places)
    feats_other = swap(feats_own, core=1)
    main_along = stack_ep(main_pieces, "stack_main")
    tops = plane_list([main_along] * 4)
    lows = [swap(top, core=1) for top in tops]
    w_project, prompt_low, small_low, vector_rows, bias_rows, masked_own, masked_other = unpack_main(
        tops, lows, feats_own, feats_other, mask_wide, places, slab, strip
    )
    w_project = w_project.reshape(2, width, TAIL)
    prompt_low = prompt_low.reshape(width, 3 * TAIL)
    encoder_low = small_low.reshape(width, WIDE)

    rest_along = stack_ep(gather_ep(tie(rest_part, feats_other)), "stack_rest")
    cots = to_chip(tie(cotangent, w_project))

    rows_low, query, keys, keys_flip, values, values_flip, key_extra = project(
        ratio,
        places,
        masked_own,
        masked_other,
        encoder_low,
        vector_rows,
        w_project,
        bias_rows,
        prompt_low,
    )
    query, rest_along, cots = lax.optimization_barrier((query, rest_along, cots))
    rest_tops = plane_list([rest_along] * 4)
    attended_other, extra_other = attend(query, keys, key_extra, values_flip, 1)
    attended_got = swap(attended_other, core=1)
    query_own = tie(query, (attended_other, rest_tops[1]))
    attended_own, extra_own = attend(query_own, keys, key_extra, values_flip, 0)
    rest_own = unpack_rest(tie(rest_tops, attended_own), places)
    rest_own = rest_own.reshape(2, width, -1)
    rest_other = swap(rest_own, core=1)
    (y0, y1, y2, y3, grad_own, grad_sent, grad_one, rest_mine, rest_sent, grad_rows, grad_hidden_row) = middle(
        places,
        ratio,
        masked_own,
        attended_own,
        attended_got,
        cots,
        encoder_low,
        vector_rows,
        bias_rows,
        rest_own,
        rest_other,
    )
    grad_got = swap(grad_sent, core=1)
    rest_got = swap(rest_sent, core=1)
    rest_parts = pack_rest(rest_mine, rest_got, (y0, y1, y2, y3), places, n_ep, slab)
    rest_tops = plane_list(rest_parts)
    query_again, *unused = lax.optimization_barrier((query, *rest_parts))
    grad_query, grad_key, grad_value = attend_back(
        query_again,
        keys,
        key_extra,
        keys_flip,
        values,
        extra_own,
        extra_other,
        grad_own,
        grad_got,
    )
    rest_tops, grad_query = lax.optimization_barrier((rest_tops, grad_query))
    rest_pieces = sum_rest(rest_tops, places, n_ep, slab)
    grad_project, grad_prompt, grad_bias = weight_grads(
        rows_low, grad_query, grad_key, grad_value, prompt_low, w_project, grad_hidden_row
    )
    prompt_mine, prompt_sent = split_prompt(grad_prompt, grad_bias, places, n_ep, strip)
    prompt_got = swap(prompt_sent, core=1)
    back_other = back_rows(grad_query, grad_key, grad_value, w_project, 1, bf16)
    back_got = swap(back_other, core=1)
    prompt_got = tie(prompt_got, back_other)
    main_parts = pack_main(grad_project, prompt_mine, prompt_got, places, slab, strip)
    main_tops = plane_list(main_parts)
    grad_query, *unused = lax.optimization_barrier((grad_query, *main_parts))
    back_own = back_rows(grad_query, grad_key, grad_value, w_project, 0, f32)
    i0, i1, i2, i3, grad_small = input_grads(
        places,
        ratio,
        grad_one,
        back_own,
        back_got,
        masked_own,
        encoder_low,
        mask_wide.reshape(WIDE, 1),
        grad_rows,
    )
    grad_small, rest_pieces = lax.optimization_barrier((grad_small, rest_pieces))
    small_mine, small_sent = split_small(grad_small, places, n_ep, strip)
    small_got = swap(small_sent, core=1)
    small_tops = plane_list(
        pack_small((i0, i1, i2, i3), small_mine, small_got, places, n_ep, strip)
    )
    output_final = place_rows(
        rest_tops, chip, n_ep * slab, (rows, width), bf16, "place_output"
    )
    main_tops, output_final = lax.optimization_barrier((main_tops, output_final))
    main_pieces = sum_main(main_tops, small_tops, places, slab, strip)
    input_final = place_rows(small_tops, chip, 0, (FEAT_ROWS, rows), f32, "place_input")
    input_final = jnp.transpose(input_final[:, 0:FEAT], (0, 2, 1))[None]

    grad_block, grad_prompt_own, grad_small_own, grad_bias_own, square_tile = final_sums(
        main_pieces, rest_pieces, slab, strip
    )
    square_tile = square_tile + swap(square_tile, core=1)
    got = plane_swap(lambda b, r: square_tile)
    square_tile = (got[0, 0] + got[1, 0]) + (got[0, 1] + got[1, 1])
    if n_ep > 4:
        squares = lax.psum(square_tile, "ep")[None]
    else:
        squares = stack_ep(gather_ep(square_tile), "stack_square")
    grad_norm, *news = adam_all(
        squares,
        (
            block_weights.reshape(slab * 8, HEAD),
            prompt,
            encoder,
            shared_vectors.T,
            head_biases.T,
        ),
        (
            block_moments.reshape(2, slab * 8, HEAD),
            prompt_moments,
            encoder_moments,
            jnp.transpose(vector_moments, (2, 0, 1)),
            jnp.transpose(bias_moments, (0, 2, 1)),
        ),
        (grad_block, grad_prompt_own, grad_small_own, grad_bias_own),
    )
    block_out = tuple(part.reshape(block_weights.shape) for part in news[0:4])
    prompt_out = tuple(news[4:8])
    encoder_out = tuple(news[8:12])
    vector_out = tuple(part.T for part in news[12:16])
    bias_out = tuple(part.T for part in news[16:20])
    return (
        (output_final[None], input_final, grad_norm.reshape(()))
        + block_out
        + bias_out
        + encoder_out
        + vector_out
        + prompt_out
    )


def solution(mesh):
    data = P("split", "ep", "tp", None)
    block = P(("ep", "split"), "tp", None)
    bias = P(("ep", "split"), "tp")
    strip = P(AXES, None)
    placed = (
        data,
        P("ep", None),
        P("ep", None),
        data,
        block,
        P(None, ("ep", "split"), "tp", None),
        bias,
        P(None, ("ep", "split"), "tp"),
        strip,
        P(None, AXES, None),
        strip,
        P(None, AXES, None),
        strip,
        P(None, AXES, None),
    )
    return jax.shard_map(
        shards,
        mesh=mesh,
        in_specs=placed,
        out_specs=(data, data, P()) + (block,) * 4 + (bias,) * 4 + (strip,) * 12,
        check_vma=False,
    )
```

```python
import functools

import jax
import jax.numpy as jnp
from jax import lax
from jax.experimental import pallas as pl
from jax.experimental.pallas import tpu as pltpu
from jax.sharding import PartitionSpec as P

HEADS = 4
HEAD = 128
FF = 1024
HID = FF // HEADS
FEAT = 100
PROMPT = 1000
SLOTS = 1024
ADAM_STEP = 10
PAD = 1024
WIDE = 128

ln_eps = 1e-05
neg_big = -1e30
clip_norm = 1.0
beta_one = 0.9
beta_two = 0.999
adam_eps = 1e-08
rate_matrix = 0.15
rate_vector = 0.5
weight_decay = 0.01
AXES = ("ep", "split", "tp")
bf16 = jnp.bfloat16
f32 = jnp.float32
score_scale = HEAD**-0.5


def swap(value, ep=0, split=0, row=0, core=0):
    sizes = [lax.axis_size(a) for a in AXES]
    pairs = []
    for a in range(sizes[0]):
        for b in range(sizes[1]):
            for t in range(sizes[2]):
                other = ((a ^ ep) * sizes[1] + (b ^ split)) * sizes[2] + (t ^ (2 * row + core))
                pairs.append(((a * sizes[1] + b) * sizes[2] + t, other))
    return lax.ppermute(value, AXES, pairs)


def pick(low, high, bit):
    return jnp.where(bit == 0, low, high), jnp.where(bit == 0, high, low)


def plane_swap(piece):
    got = {}
    for b in (0, 1):
        for r in (0, 1):
            sent = piece(b, r)
            got[b, r] = sent if (b, r) == (0, 0) else swap(sent, split=b, row=r)
    return got


def tie(value, other):
    return lax.optimization_barrier((value, other))[0]


def gather_ep(shard):
    count = lax.axis_size("ep")
    if count > 4:
        return [lax.all_gather(shard, "ep", axis=0)]
    return [shard] + [swap(shard, ep=k) for k in range(1, count)]


def stack_ep(parts, name):
    return parts[0] if len(parts) == 1 else place(parts, lax.axis_index("ep"), name)


def reduce_ep(total, pieces):
    count = lax.axis_size("ep")
    if count > 4:
        return [lax.psum_scatter(total, "ep", scatter_dimension=0, tiled=True)[0]]
    return [pieces[0]] + [swap(pieces[k], ep=k) for k in range(1, count)]


def adam_update(weight, moments, gradient, factor, step_rate, decay_rate):
    clipped = gradient * factor
    first_moment = beta_one * moments[0] + (1.0 - beta_one) * clipped
    second_moment = beta_two * moments[1] + (1.0 - beta_two) * clipped * clipped
    first_hat = first_moment / (1.0 - beta_one**ADAM_STEP)
    second_hat = second_moment / (1.0 - beta_two**ADAM_STEP)
    updated = weight - step_rate * (
        first_hat / (jnp.sqrt(second_hat) + adam_eps) + decay_rate * weight
    )
    return (updated, first_moment, second_moment, updated.astype(bf16))


def dot(a, b, dims):
    return lax.dot_general(a, b, (dims, ((), ())), preferred_element_type=f32)


NN = ((1,), (0,))
NT = ((1,), (1,))
TN = ((0,), (0,))


def cost(micros):
    return pl.CostEstimate(flops=int(micros * 3e8), transcendentals=0, bytes_accessed=int(micros * 1e6))


def whole():
    return pl.BlockSpec(memory_space=pltpu.VMEM)


def shape_of(shape, dtype):
    return jax.ShapeDtypeStruct(shape, dtype)


def project_body(ratio, sc, own, other, enc, vec, wp, bias, prompt, x_ref, q_ref, k_ref, kt_ref, v_ref, vt_ref, extra_ref):
    step = pl.program_id(0)

    @pl.when(step == 0)
    def _():
        half = own.shape[0]
        size = half // 2
        key = lax.broadcasted_iota(jnp.int32, extra_ref.shape[1:], 0)
        lane = lax.broadcasted_iota(jnp.int32, extra_ref.shape[1:], 1)
        inner = key - PAD
        place = inner % half
        slot = (2 * (place // size) + (sc[2] ^ (inner // half))) * size + place % size
        limit = jnp.where(key < PAD, PROMPT, sc[4])
        bias = jnp.where(jnp.where(key < PAD, key, slot) >= limit, neg_big, 0.0)
        bias = jnp.where(lane == 3, bias, 0.0)
        for h in range(2):
            ones = jnp.where((lane >= 4 * h) & (lane < 4 * h + 3), 1.0, 0.0)
            extra_ref[h] = (bias + ones).astype(bf16)

    rows = jnp.where(step < 2, own[...], other[...])
    low = (ratio[0] * dot(rows, enc[...], NT) + vec[6:7, :]).astype(bf16)
    x_ref[...] = low
    for h in range(2):
        q_ref[h] = (dot(low, wp[h, :, 0:HEAD], NN) + bias[h : h + 1, 0:HEAD]).astype(bf16)

    def keys_from(source):
        for h in range(2):
            key = dot(source, wp[h, :, HEAD : 2 * HEAD], NN).astype(bf16)
            shift = bias[h : h + 1, HEAD : 2 * HEAD]
            value = (dot(source, wp[h, :, 2 * HEAD : 3 * HEAD], NN) + shift).astype(bf16)
            k_ref[h] = key
            v_ref[h] = value
            kt_ref[h] = key.T
            vt_ref[h] = value.T

    @pl.when(step % 2 == 0)
    def _():
        keys_from(low)

    @pl.when(step % 2 == 1)
    def _():
        keys_from(prompt[...].T)


def project(ratio, places, own, other, enc, vec, wp, bias, prompt):
    half = own.shape[0] // 2
    width = enc.shape[0]
    keys = PAD + SLOTS
    spot = lambda i: jnp.where(i % 2 == 0, 2 + i // 2, i // 2)
    tall = pl.BlockSpec((2, half, HEAD), lambda i: (0, spot(i), 0))
    flat = pl.BlockSpec((2, HEAD, half), lambda i: (0, 0, spot(i)))
    return pl.pallas_call(
        project_body,
        grid=(4,),
        in_specs=[
            pl.BlockSpec(memory_space=pltpu.SMEM),
            pl.BlockSpec(memory_space=pltpu.SMEM),
            pl.BlockSpec((half, WIDE), lambda i: (jnp.minimum(i, 1), 0)),
            pl.BlockSpec((half, WIDE), lambda i: (jnp.maximum(i - 2, 0), 0)),
            whole(),
            whole(),
            whole(),
            whole(),
            pl.BlockSpec((width, half), lambda i: (0, i // 2)),
        ],
        out_specs=[
            pl.BlockSpec((half, width), lambda i: (i, 0)),
            pl.BlockSpec((2, half, HEAD), lambda i: (0, i, 0)),
            tall,
            flat,
            tall,
            flat,
            pl.BlockSpec((2, keys, WIDE), lambda i: (0, 0, 0)),
        ],
        out_shape=[
            pltpu.HBM((4 * half, width), bf16),
            pltpu.HBM((2, 4 * half, HEAD), bf16),
            pltpu.HBM((2, keys, HEAD), bf16),
            pltpu.HBM((2, HEAD, keys), bf16),
            pltpu.HBM((2, keys, HEAD), bf16),
            pltpu.HBM((2, HEAD, keys), bf16),
            pltpu.HBM((2, keys, WIDE), bf16),
        ],
        compiler_params=pltpu.CompilerParams(vmem_limit_bytes=32 << 20),
        cost_estimate=cost(9),
        name="project",
    )(ratio, places, *held((own, other, enc, vec, wp, bias, prompt)))


CHUNK = 1024
base_two = 1.4426950408889634


def three_terms(value):
    high = value.astype(bf16).astype(f32)
    middle = (value - high).astype(bf16).astype(f32)
    return high, middle, value - high - middle


def attend_body(q_ref, k_ref, x_ref, vt_ref, o_ref, extra_ref, *scratch):
    head = pl.program_id(0)
    keys, size = scratch[0].shape
    count = q_ref.shape[1] // size
    steepness = score_scale * base_two
    lane = lax.broadcasted_iota(jnp.int32, (size, WIDE), 1)
    place = lax.broadcasted_iota(jnp.int32, (WIDE, size), 0)
    one = jnp.where(lane == 3, 1.0, 0.0).astype(bf16)
    top = None
    for b in range(count + 1):
        fresh_ref, old_ref = scratch[b % 2], scratch[(b + 1) % 2]
        if b < count:
            query = jnp.concatenate([q_ref[0, b * size : (b + 1) * size], one], axis=1)
            partial = jnp.full((8, size), -jnp.inf, f32)
        if b > 0:
            shift = top * steepness
            total = jnp.zeros((8, size), f32)
            out = jnp.zeros((HEAD, size), f32)
        for c in range(keys // CHUNK):
            span = slice(c * CHUNK, (c + 1) * CHUNK)
            if b < count:
                wide = jnp.concatenate([k_ref[0, span], x_ref[0, span]], axis=1)
                fresh = dot(wide, query, NT)
                fresh_ref[span] = fresh
                partial = jnp.maximum(partial, jnp.max(fresh.reshape(CHUNK // 8, 8, size), axis=0))
            if b > 0:
                raised = jnp.exp2(old_ref[span] * steepness - shift)
                total = total + jnp.sum(raised.reshape(CHUNK // 8, 8, size), axis=0)
                out = out + dot(vt_ref[0, :, span], raised.astype(bf16), NN)
        if b > 0:
            rows = slice((b - 1) * size, b * size)
            total = jnp.sum(total, axis=0, keepdims=True)
            o_ref[rows] = (out / total).T.astype(bf16)
            terms = three_terms(-(top + jnp.log(total) / score_scale))
            tile = jnp.where(place == 3, 1.0, 0.0)
            for k in range(3):
                tile = tile + jnp.where(place == 4 * head + k, terms[k], 0.0)
            extra_ref[0, rows] = tile.T.astype(bf16)
        if b < count:
            top = jnp.max(partial, axis=0, keepdims=True)


BLOCK = 512


def attend(q, k, extra, vt, which):
    keys = k.shape[1]
    tall = pl.BlockSpec((1, keys, HEAD), lambda h: (h, 0, 0))
    return pl.pallas_call(
        attend_body,
        grid=(2,),
        in_specs=[
            pl.BlockSpec((1, SLOTS, HEAD), lambda h: (h, which, 0)),
            tall,
            pl.BlockSpec((1, keys, WIDE), lambda h: (0, 0, 0)),
            pl.BlockSpec((1, HEAD, keys), lambda h: (h, 0, 0)),
        ],
        out_specs=[
            pl.BlockSpec((SLOTS, HEAD), lambda h: (0, h)),
            pl.BlockSpec((1, SLOTS, WIDE), lambda h: (h, 0, 0)),
        ],
        out_shape=[pltpu.HBM((SLOTS, 2 * HEAD), bf16), pltpu.HBM((2, SLOTS, WIDE), bf16)],
        scratch_shapes=[pltpu.VMEM((keys, BLOCK), f32)] * 2,
        compiler_params=pltpu.CompilerParams(vmem_limit_bytes=32 << 20),
        cost_estimate=cost(6),
        name="attend",
    )(*held((q, k, extra, vt), False))


BACK_BLOCK = 256
BACK_CHUNK = 1024


def attend_back_body(q_ref, k_ref, x_ref, kt_ref, v_ref, qa_ref, qb_ref, da_ref, db_ref, ea_ref, eb_ref, dq_ref, dk_ref, dv_ref, *scratch):
    size = scratch[0].shape[1]
    keys = k_ref.shape[1]
    rows = q_ref.shape[1]
    count = rows // size
    steepness = score_scale * base_two
    mine = pl.program_id(1) == 0

    @pl.when(mine)
    def _():
        dk_ref[...] = jnp.zeros_like(dk_ref)
        dv_ref[...] = jnp.zeros_like(dv_ref)

    for b in range(count + 1):
        probs_ref, slopes_ref = scratch[2 * (b % 2) : 2 * (b % 2) + 2]
        old_probs, old_slopes = scratch[2 - 2 * (b % 2) : 4 - 2 * (b % 2)]
        if b < count:
            span = slice(b * size, (b + 1) * size)
            query = q_ref[0, span]
            grad = jnp.where(mine, da_ref[span], db_ref[span])
            aside = jnp.where(mine, qa_ref[0, span], qb_ref[0, span])
            sums = jnp.where(mine, ea_ref[span], eb_ref[span])
            query_wide = jnp.concatenate([query, aside], axis=1)
            grad_wide = jnp.concatenate([grad, sums], axis=1)
        if b > 0:
            back = jnp.zeros((HEAD, size), f32)
        for c in range(keys // BACK_CHUNK):
            span = slice(c * BACK_CHUNK, (c + 1) * BACK_CHUNK)
            if b < count:
                extra = x_ref[0, span]
                scores = dot(jnp.concatenate([k_ref[0, span], extra], axis=1), query_wide, NT)
                slopes = dot(jnp.concatenate([v_ref[0, span], extra], axis=1), grad_wide, NT)
                probs = jnp.exp2(scores * steepness)
                probs_ref[span] = probs.astype(bf16)
                slopes_ref[span] = (probs * slopes).astype(bf16)
            if b > 0:
                back = back + dot(kt_ref[0, :, span], old_slopes[span], NN)
                grad_key = dot(query_flip, old_slopes[span], NT) * score_scale
                grad_value = dot(grad_flip, old_probs[span], NT)
                dk_ref[0, :, span] += grad_key
                dv_ref[0, :, span] += grad_value
        if b > 0:
            dq_ref[(b - 1) * size : b * size] = (back * score_scale).T.astype(bf16)
        if b < count:
            query_flip, grad_flip = query.T, grad.T


def attend_back(q, k, extra, kt, v, extra_own, extra_other, grad_own, grad_other):
    keys = k.shape[1]
    tall = pl.BlockSpec((1, keys, HEAD), lambda h, i: (h, 0, 0))
    flat = pl.BlockSpec((1, HEAD, keys), lambda h, i: (h, 0, 0))
    aside = pl.BlockSpec((1, SLOTS, WIDE), lambda h, i: (h, 0, 0))
    grad = pl.BlockSpec((SLOTS, HEAD), lambda h, i: (0, h))
    sums = pl.BlockSpec((SLOTS, HEAD), lambda h, i: (0, 2))
    return pl.pallas_call(
        attend_back_body,
        grid=(2, 2),
        in_specs=[
            pl.BlockSpec((1, SLOTS, HEAD), lambda h, i: (h, i, 0)),
            tall,
            tall,
            flat,
            tall,
            aside,
            aside,
            grad,
            grad,
            sums,
            sums,
        ],
        out_specs=[pl.BlockSpec((SLOTS, HEAD), lambda h, i: (i, h)), flat, flat],
        out_shape=[
            pltpu.HBM((2 * SLOTS, 2 * HEAD), bf16),
            pltpu.HBM((2, HEAD, keys), f32),
            pltpu.HBM((2, HEAD, keys), f32),
        ],
        scratch_shapes=[pltpu.VMEM((keys, BACK_BLOCK), bf16)] * 4,
        compiler_params=pltpu.CompilerParams(vmem_limit_bytes=40 << 20),
        cost_estimate=cost(20),
        name="attend_back",
    )(
        *held((q, k, extra, kt, v, extra_own, extra_other), False),
        *held((grad_own, grad_other, grad_own, grad_other), (False, True, False, True)),
    )


erfc_terms = (
    -1.26551223,
    1.00002368,
    0.37409196,
    0.09678418,
    -0.18628806,
    0.27886807,
    -1.13520398,
    1.48851587,
    -0.82215223,
    0.17087277,
)


def gelu_pair(t):
    z = jnp.abs(t) * (0.5**0.5)
    k = 1.0 / (1.0 + 0.5 * z)
    series = jnp.full_like(t, erfc_terms[-1])
    for term in erfc_terms[-2::-1]:
        series = series * k + term
    tail = 0.5 * k * jnp.exp(series - z * z)
    cumulative = jnp.where(t >= 0.0, 1.0 - tail, tail)
    density = jnp.exp(-0.5 * t * t) * 0.3989422804014327
    return t * cumulative, cumulative + t * density


def middle_body(
    sc,
    ratio,
    rows_ref,
    oa_ref,
    ob_ref,
    c0,
    c1,
    c2,
    c3,
    enc,
    vec,
    b1,
    ra,
    rb,
    y0,
    y1,
    y2,
    y3,
    da_ref,
    db_ref,
    dr_ref,
    ga,
    gb,
    gvec,
    gb1,
    cot,
    acc,
):
    step = pl.program_id(0)
    count = rows_ref.shape[0]
    for k, ref in enumerate((c0, c1, c2, c3)):

        @pl.when(step == k)
        def _(ref=ref):
            cot[...] = ref[...]

    @pl.when(step == 0)
    def _():
        acc[...] = jnp.zeros_like(acc)
        gvec[...] = jnp.zeros_like(gvec)
        gb1[...] = jnp.zeros_like(gb1)

    group = sc[0] ^ (step // 2)
    quarter = 2 * (sc[1] ^ (step % 2)) + sc[2]
    limit = jnp.where(group == 0, sc[4], sc[5])
    slot = quarter * count + lax.broadcasted_iota(jnp.int32, (count, 1), 0)
    live = (slot < limit).astype(f32)

    def weight(k, low, high):
        return (ra if k < 2 else rb)[k % 2, :, low:high]

    def row(k):
        return vec[k : k + 1, :]

    gain_one, shift_one, gain_two, shift_two, b_out, b_two, b_enc = (row(k) for k in range(7))
    embedded = ratio[0] * dot(rows_ref[...], enc[...], NT) + b_enc
    out_pair = [
        jnp.concatenate([weight(2 * k, 0, HEAD), weight(2 * k + 1, 0, HEAD)], axis=1)
        for k in (0, 1)
    ]
    attn = dot(oa_ref[...], out_pair[0], NT) + dot(ob_ref[...], out_pair[1], NT) + b_out

    def norm(residual):
        centred = residual - jnp.mean(residual, axis=-1, keepdims=True)
        inverse = lax.rsqrt(jnp.mean(centred * centred, axis=-1, keepdims=True) + ln_eps)
        return centred * inverse, inverse

    def back(grad, normed, inverse, gain):
        scaled = grad * gain
        plain = jnp.mean(scaled, axis=-1, keepdims=True)
        mixed = jnp.mean(scaled * normed, axis=-1, keepdims=True)
        return inverse * (scaled - plain - normed * mixed)

    def add_row(k, value):
        gvec[k : k + 1, :] += jnp.sum(value, axis=0, keepdims=True)

    normed_one, inverse_one = norm(embedded + attn)
    first = normed_one * gain_one + shift_one
    first_low = first.astype(bf16)
    mlp = b_two
    acts, slopes = [], []
    for k in range(4):
        pre = dot(first_low, weight(k, HEAD, HEAD + HID), NN) + b1[k : k + 1, 2 * HEAD :]
        act, slope = gelu_pair(pre)
        acts.append(act.astype(bf16))
        slopes.append(slope)
        mlp = mlp + dot(acts[k], weight(k, HEAD + HID, HEAD + 2 * HID), NT)
    normed_two, inverse_two = norm(first + mlp)
    out = ((normed_two * gain_two + shift_two) * live).astype(bf16)
    for k, ref in enumerate((y0, y1, y2, y3)):

        @pl.when(step == k)
        def _(ref=ref):
            ref[...] = out

    grad_y = cot[...].astype(f32) * live
    add_row(2, grad_y * normed_two)
    add_row(3, grad_y)
    grad_two = back(grad_y, normed_two, inverse_two, gain_two)
    grad_low = grad_two.astype(bf16)
    add_row(5, grad_low.astype(f32))
    grad_flip = grad_low.T
    first_flip = first_low.T
    grad_first = grad_two
    for k in range(4):
        acc[k, :, HEAD + HID :] += dot(grad_flip, acts[k], NN)
        grad_act = dot(grad_low, weight(k, HEAD + HID, HEAD + 2 * HID), NN)
        grad_pre = (grad_act * slopes[k]).astype(bf16)
        gb1[k : k + 1, :] += jnp.sum(grad_pre.astype(f32), axis=0, keepdims=True)
        acc[k, :, HEAD : HEAD + HID] += dot(first_flip, grad_pre, NN)
        grad_first = grad_first + dot(grad_pre, weight(k, HEAD, HEAD + HID), NT)
    add_row(0, grad_first * normed_one)
    add_row(1, grad_first)
    grad_one = back(grad_first, normed_one, inverse_one, gain_one)
    dr_ref[...] = grad_one
    attn_low = grad_one.astype(bf16)
    add_row(4, attn_low.astype(f32))
    attn_flip = attn_low.T
    for k, (source, target) in enumerate(((oa_ref, da_ref), (ob_ref, db_ref))):
        both = dot(attn_flip, source[...], NN)
        acc[2 * k, :, 0:HEAD] += both[:, 0:HEAD]
        acc[2 * k + 1, :, 0:HEAD] += both[:, HEAD:]
        both = dot(attn_low, out_pair[k], NN).astype(bf16)
        target[:, 0 : 2 * HEAD] = both
        product = both.astype(f32) * source[...].astype(f32)
        lane = lax.broadcasted_iota(jnp.int32, (count, WIDE), 1)
        tile = jnp.zeros((count, WIDE), f32)
        for h in range(2):
            sums = jnp.sum(product[:, h * HEAD : (h + 1) * HEAD], axis=1, keepdims=True)
            for m, term in enumerate(three_terms(-sums)):
                tile = tile + jnp.where(lane == 4 * h + m, term, 0.0)
        target[:, 2 * HEAD :] = tile.astype(bf16)

    @pl.when(step == 3)
    def _():
        ga[...] = acc[0:2].astype(bf16)
        gb[...] = acc[2:4].astype(bf16)


def middle(sc, ratio, rows, o_own, o_other, cots, enc, vec, b1, rest_own, rest_other):
    size = rows.shape[0] // 4
    width = enc.shape[0]
    spot = lambda i, sc: (2 * (sc[0] ^ (i // 2)) + (sc[1] ^ (i % 2)), 0)
    pair = pl.BlockSpec((size, 2 * HEAD), spot)
    smem = pl.BlockSpec(memory_space=pltpu.SMEM)
    fixed = pl.BlockSpec((size, width), lambda i, sc: (0, 0))
    weight = rest_own.shape
    return pl.pallas_call(
        middle_body,
        grid_spec=pltpu.PrefetchScalarGridSpec(
            num_scalar_prefetch=1,
            grid=(4,),
            in_specs=[smem, pl.BlockSpec((size, WIDE), spot), pair, pair]
            + [fixed] * 4
            + [whole()] * 5,
            out_specs=[fixed] * 4
            + [pl.BlockSpec((size, 3 * HEAD), spot)] * 2
            + [pl.BlockSpec((size, width), spot)]
            + [
                pl.BlockSpec(weight, lambda i, sc: (0, 0, 0)),
                pl.BlockSpec(weight, lambda i, sc: (0, 0, 0)),
                pl.BlockSpec((8, width), lambda i, sc: (0, 0)),
                pl.BlockSpec((4, HID), lambda i, sc: (0, 0)),
            ],
            scratch_shapes=[
                pltpu.VMEM((size, width), bf16),
                pltpu.VMEM((4,) + weight[1:], f32),
            ],
        ),
        out_shape=[pltpu.VMEM((size, width), bf16)] * 4
        + [
            pltpu.HBM((4 * size, 3 * HEAD), bf16),
            pltpu.HBM((4 * size, 3 * HEAD), bf16),
            pltpu.HBM((4 * size, width), f32),
            pltpu.VMEM(weight, bf16),
            pltpu.VMEM(weight, bf16),
            pltpu.HBM((8, width), f32),
            pltpu.HBM((4, HID), f32),
        ],
        compiler_params=pltpu.CompilerParams(vmem_limit_bytes=44 << 20),
        cost_estimate=cost(25),
        name="middle",
    )(
        sc,
        ratio,
        rows,
        o_own,
        o_other,
        *held(cots),
        enc,
        vec,
        b1,
        *held((rest_own, rest_other)),
    )


def held(args, near=True):
    if isinstance(near, bool):
        near = [near] * len(args)
    spaces = [pltpu.VMEM if flag else pltpu.HBM for flag in near]
    return tuple(map(pltpu.with_memory_space_constraint, args, spaces))


def simple(body, out_shape, *args, scalars=None, scratch=(), near=(True, True), name=None):
    specs = [whole()] * len(args)
    args = held(args, near[0])
    if scalars is not None:
        specs = [pl.BlockSpec(memory_space=pltpu.SMEM)] + specs
        args = (scalars,) + args
    many = isinstance(out_shape, (list, tuple))
    if near[1]:
        kept = lambda shape: pltpu.VMEM(shape.shape, shape.dtype)
        out_shape = [kept(shape) for shape in out_shape] if many else kept(out_shape)
    return pl.pallas_call(
        body,
        in_specs=specs,
        out_specs=[whole()] * len(out_shape) if many else whole(),
        out_shape=out_shape,
        scratch_shapes=scratch,
        compiler_params=pltpu.CompilerParams(vmem_limit_bytes=16 << 20),
        cost_estimate=cost(2),
        name=name,
    )(*args)


def place(parts, index, name, near=(True, True)):
    def body(sc, *refs):
        for k, ref in enumerate(refs[:-1]):
            refs[-1][sc[0] ^ k] = ref[...]

    first = parts[0]
    return simple(
        body,
        shape_of((len(parts),) + first.shape, first.dtype),
        *parts,
        scalars=index.reshape(1).astype(jnp.int32),
        near=near,
        name=name,
    )


TAIL = 3 * HEAD
FEAT_ROWS = 112
LAST = 112
VEC = 104


def spread(row):
    parts = row.reshape(row.shape[:-1] + (4, row.shape[-1] // 4))
    room = WIDE - LAST - parts.shape[-1]
    return jnp.pad(parts, [(0, 0)] * (parts.ndim - 1) + [(LAST, room)])


def widened(prompt):
    return jnp.pad(prompt, [(0, 0)] * (prompt.ndim - 1) + [(0, 3 * TAIL - prompt.shape[-1])])


def with_bias(prompt, bias):
    row = jnp.pad(
        bias[..., None, :].astype(prompt.dtype),
        [(0, 0)] * (bias.ndim - 1)
        + [(0, prompt.shape[-2] - 1), (PAD, 3 * TAIL - PAD - bias.shape[-1])],
    )
    return widened(prompt) + row


def in_chunks(wide):
    lead, strip = wide.shape[:-2], wide.shape[-2]
    parts = jnp.swapaxes(wide.reshape(lead + (strip, 3, TAIL)), -3, -2)
    return parts.reshape(lead + (3 * strip, TAIL))


def pack_parts(block, prompt, encoder, vectors, biases):
    slab, strip = block.shape[0], prompt.shape[0]
    flat = block.reshape(slab * 8, HEAD)
    out = [shape_of((slab + 3 * strip, TAIL), bf16), shape_of((slab, 8 * HEAD - TAIL), bf16)]
    if 2 * slab != WIDE:
        low = block.reshape(slab, 8 * HEAD).astype(bf16)
        small = jnp.concatenate(
            [
                jnp.pad(encoder, ((0, 0), (0, VEC - FEAT))),
                jnp.pad(vectors, ((0, 0), (0, LAST - VEC - 7))),
                jnp.pad(biases.reshape(strip, 4), ((0, 0), (0, WIDE - LAST - 4))),
            ],
            axis=1,
        )
        chunks = in_chunks(
            jnp.concatenate([jnp.pad(prompt, ((0, 0), (0, PAD - PROMPT))), small], axis=1)
        )
        return jnp.concatenate([low[:, 0:TAIL], chunks.astype(bf16)], axis=0), low[:, TAIL:]

    def body(block_ref, prompt_ref, enc_ref, vec_ref, bias_ref, main_ref, rest_ref, tall, tile, line):
        for j in range(8):
            lanes = block_ref[pl.ds(j, slab, stride=8), :].astype(bf16)
            if j < 3:
                main_ref[0:slab, j * HEAD : (j + 1) * HEAD] = lanes
            else:
                rest_ref[:, (j - 3) * HEAD : (j - 2) * HEAD] = lanes
        low = prompt_ref[...].astype(bf16)
        for k in range(2):
            rows = slice(slab + k * strip, slab + (k + 1) * strip)
            main_ref[rows, :] = low[:, k * TAIL : (k + 1) * TAIL]
        rows = slice(slab + 2 * strip, slab + 3 * strip)
        main_ref[rows, WIDE : 2 * WIDE] = jnp.zeros((strip, WIDE), bf16)
        main_ref[rows, 0 : PROMPT - 2 * TAIL] = low[:, 2 * TAIL :]
        tall[...] = jnp.zeros_like(tall)
        tall[VEC : VEC + 7, :] = vec_ref[...]
        tile[...] = tall[...].T
        tile[:, 0:FEAT] = enc_ref[...]
        line[...] = jnp.zeros_like(line)
        line[:, 0:slab] = bias_ref[...]
        main_ref[rows, 2 * WIDE :] = (tile[...] + spread_row(line[...], strip)).astype(bf16)

    return simple(
        body,
        out,
        flat,
        prompt,
        encoder,
        vectors.T,
        biases.T,
        near=(False, True),
        scratch=[
            pltpu.VMEM((WIDE, strip), f32),
            pltpu.VMEM((strip, WIDE), f32),
            pltpu.VMEM((1, WIDE), f32),
        ],
        name="pack_parts",
    )


def spread_row(row, strip):
    place = lax.broadcasted_iota(jnp.int32, (strip, WIDE), 0)
    lane = lax.broadcasted_iota(jnp.int32, (strip, WIDE), 1)
    total = jnp.zeros((strip, WIDE), f32)
    for k in range(4):
        turned = jnp.broadcast_to(pltpu.roll(row, LAST - k * strip, 1), (strip, WIDE))
        total = total + jnp.where((place == k) & (lane >= LAST), turned, 0.0)
    return total


def gathered_row(tile, strip):
    lane = lax.broadcasted_iota(jnp.int32, (1, WIDE), 1)
    total = jnp.zeros((1, WIDE), f32)
    for k in range(4):
        turned = pltpu.roll(tile[k : k + 1], (k * strip - LAST) % WIDE, 1)
        total = total + jnp.where(lane // strip == k, turned, 0.0)
    return total


FEAT_SPAN = 80
FEAT_CUTS = ((0, 0, 0, 0, 80), (1, 0, 0, 80, 112), (1, 32, 1, 0, 48), (2, 0, 1, 48, 112))


def build_main(parts, flipped, places):
    count = len(parts)
    size, lanes = parts[0].shape
    feats, rows = flipped.shape[1:]

    def body(sc, *refs):
        ins, flip_ref, outs = refs[:count], refs[count], refs[count + 1 :]
        for k, out in enumerate(outs):
            for e, ref in enumerate(ins):
                at = pl.multiple_of((sc[6] ^ e) * size, 16)
                out[pl.ds(at, size), :] = ref[...]
            wide = jnp.concatenate(
                [flip_ref[sc[3] ^ k], jnp.zeros((FEAT_ROWS - feats, rows), bf16)], axis=0
            )
            for column, row, tile, begin, end in FEAT_CUTS:
                at = slice(count * size + row, count * size + row + end - begin)
                part = wide[begin:end, tile * WIDE : (tile + 1) * WIDE]
                out[at, column * WIDE : (column + 1) * WIDE] = part

    shape = shape_of((count * size + FEAT_SPAN, lanes), bf16)
    return simple(body, [shape] * 4, *parts, flipped, scalars=places, name="build_main")


def join_features(parts, places):
    feats, rows = parts[0].shape

    def body(sc, *refs):
        for k, ref in enumerate(refs[:-1]):
            spot = 2 * (sc[0] ^ (k // 2)) + (sc[1] ^ (k % 2))
            refs[-1][spot, 0:feats] = ref[...]

    return simple(
        body, shape_of((4, FEAT_ROWS, rows), bf16), *parts, scalars=places, name="join_features"
    )


def unpack_main(tops, lows, feats, feats_low, mask, places, n_ep, slab, strip, rows):
    plain = 2 * slab != WIDE
    size = slab + 3 * strip
    shapes = [
        shape_of((2, n_ep, 2, slab, TAIL), bf16),
        shape_of((n_ep, 2, 2, 2, strip, 3 * TAIL), bf16),
        shape_of((n_ep, 2, 2, 2, strip, WIDE), bf16),
        shape_of((8, n_ep * 2 * slab), f32),
        shape_of((4, n_ep * 2 * slab), f32),
        shape_of((4 * rows, WIDE), bf16),
        shape_of((4 * rows, WIDE), bf16),
    ]

    def features(mask_ref, source, target):
        for p in range(4):
            flip = jnp.concatenate([source[p], jnp.zeros((WIDE - FEAT_ROWS, rows), bf16)], axis=0)
            piece = jnp.where(mask_ref[...] > 0.0, flip.T.astype(f32), 0.0).astype(bf16)
            target[p * rows : (p + 1) * rows, :] = piece

    if plain:
        side, row, core = places[0], places[1], places[2]

        def ordered(parts, axis):
            cores = []
            for group in parts:
                sides = []
                for b in (0, 1):
                    sides.append(jnp.stack(pick(group[2 * b], group[2 * b + 1], row), axis=axis))
                cores.append(jnp.stack(pick(sides[0], sides[1], side), axis=axis))
            return jnp.stack(pick(cores[0], cores[1], core), axis=axis + 2)

        heads = [
            jnp.stack(pick(tops[r][:, 0:slab], tops[2 + r][:, 0:slab], side), axis=1) for r in (0, 1)
        ]
        chunks = ordered([[t[:, slab:] for t in tops], [t[:, slab:] for t in lows]], 1)
        chunks = chunks.reshape((n_ep, 2, 2, 2, 3, strip, TAIL))
        wide = jnp.swapaxes(chunks, -3, -2).reshape((n_ep, 2, 2, 2, strip, 3 * TAIL))
        small = wide[..., PAD:]
        vec = small.reshape(n_ep * 8 * strip, WIDE).astype(f32).T[VEC : VEC + 8]
        biases = []
        for group in (tops, lows):
            for r in (0, 1):
                pair = [
                    group[2 * b + r][:, slab + 2 * strip :, PAD - 2 * TAIL + LAST :][..., 0:4]
                    for b in (0, 1)
                ]
                biases.append(jnp.stack(pick(pair[0], pair[1], side), axis=1).reshape(-1))
        def both(mask_ref, a, b, c, d):
            features(mask_ref, a, c)
            features(mask_ref, b, d)

        masked = simple(
            both,
            shapes[5:],
            mask,
            feats,
            feats_low,
            near=(False, False),
            name="features",
        )
        return [jnp.stack(heads), wide, small, vec, jnp.stack(biases).astype(f32), *masked]

    def body(sc, t0, t1, t2, t3, l0, l1, l2, l3, mask_ref, *outs):
        wp_ref, prompt_ref, small_ref, vec_ref, bias_ref, own_ref, other_ref = outs
        side, row, core = sc[0], sc[1], sc[2]
        groups = ((t0, t1, t2, t3), (l0, l1, l2, l3))
        bias_tiles = {}
        for b in range(2):
            for r in range(2):
                k = 2 * b + r
                for other in range(2):
                    spot = core ^ other
                    source = groups[other][k]
                    full = source[0 : n_ep * size].reshape(n_ep, size, TAIL)
                    if other == 0:
                        wp_ref[r, :, side ^ b] = full[:, 0:slab, :]
                    part = full[:, slab:, :]
                    tiles = ([], [])
                    for column, line, tile, begin, end in FEAT_CUTS:
                        at = slice(n_ep * size + line, n_ep * size + line + end - begin)
                        tiles[tile].append(source[at, column * WIDE : (column + 1) * WIDE])
                    blank = jnp.zeros((WIDE - FEAT_ROWS, rows), bf16)
                    flip = jnp.concatenate([jnp.concatenate(t, axis=0) for t in tiles], axis=1)
                    flip = jnp.concatenate([flip, blank], axis=0)
                    piece = jnp.where(mask_ref[...] > 0.0, flip.T.astype(f32), 0.0).astype(bf16)
                    at = pl.multiple_of((2 * (side ^ b) + (row ^ r)) * rows, rows)
                    (other_ref if other else own_ref)[pl.ds(at, rows), :] = piece
                    for j in range(3):
                        lanes = slice(j * TAIL, (j + 1) * TAIL)
                        span = slice(j * strip, (j + 1) * strip)
                        prompt_ref[:, side ^ b, row ^ r, spot, :, lanes] = part[:, span, :]
                    tile = part[:, 2 * strip :, TAIL - WIDE :]
                    small_ref[:, side ^ b, row ^ r, spot] = tile
                    bias_tiles[b, r, other] = tile.astype(f32)
        flip = small_ref[...].reshape(n_ep * 8 * strip, WIDE).astype(f32).T
        vec_ref[...] = flip[VEC : VEC + 8]
        low_half = lax.broadcasted_iota(jnp.int32, (1, WIDE), 1) < slab
        for r in range(2):
            for other in range(2):
                for e in range(n_ep):
                    mine = gathered_row(bias_tiles[0, r, other][e], strip)
                    theirs = gathered_row(bias_tiles[1, r, other][e], strip)
                    first = jnp.where(side == 0, mine, theirs)
                    second = jnp.where(side == 0, theirs, mine)
                    row_tile = jnp.where(low_half, first, pltpu.roll(second, slab, 1))
                    k = r + 2 * other
                    bias_ref[k : k + 1, e * WIDE : (e + 1) * WIDE] = row_tile

    return simple(body, shapes, *tops, *lows, mask, scalars=places, name="unpack_main")


def unpack_rest(tops, places):
    n_ep, slab, width = tops[0].shape

    def body(sc, t0, t1, t2, t3, out_ref):
        for k, ref in enumerate((t0, t1, t2, t3)):
            out_ref[k % 2, :, sc[0] ^ (k // 2)] = ref[...]

    return simple(
        body, shape_of((2, n_ep, 2, slab, width), bf16), *tops, scalars=places, name="unpack_rest"
    )


def weight_body(n_ep, strip, sc, x_ref, dq_ref, dk_ref, dv_ref, prompt, wp, gb1, gw_ref, mine_ref, sent_ref, own_ref, other_ref, acc, gq_ref, gv_ref, gp_ref, gb_ref):
    step = pl.program_id(0)

    @pl.when(step == 0)
    def _():
        acc[...] = jnp.zeros_like(acc)
        gq_ref[...] = jnp.zeros_like(gq_ref)
        gv_ref[...] = jnp.zeros_like(gv_ref)

    def columns(k):
        return jnp.concatenate([wp[h, :, k * HEAD : (k + 1) * HEAD] for h in range(2)], axis=1)

    flip = x_ref[...].T
    grad_query = dq_ref[...]
    acc[0] += dot(flip, grad_query, NN)
    gq_ref[...] += jnp.sum(grad_query.astype(f32), axis=0, keepdims=True)
    grad_key = jnp.concatenate([dk_ref[h] for h in range(2)], axis=0)
    grad_value = jnp.concatenate([dv_ref[h] for h in range(2)], axis=0)
    key_high = grad_key.astype(bf16)
    value_high = grad_value.astype(bf16)
    ones = jnp.ones((8, grad_key.shape[1]), bf16)
    gv_ref[...] += dot(ones, value_high, NT)[0:1]
    back = dot(grad_query, columns(0), NT)

    def store(value):
        @pl.when(step < 2)
        def _():
            own_ref[...] = value

        @pl.when(step >= 2)
        def _():
            other_ref[...] = value.astype(bf16)

    @pl.when(step % 2 == 0)
    def _():
        acc[1] += dot(flip, key_high, NT)
        acc[2] += dot(flip, value_high, NT)
        store(back + dot(key_high.T, columns(1), NT) + dot(value_high.T, columns(2), NT))

    @pl.when(step % 2 == 1)
    def _():
        store(back)
        key_low = (grad_key - key_high.astype(f32)).astype(bf16)
        value_low = (grad_value - value_high.astype(f32)).astype(bf16)
        source = prompt[...]
        acc[1] += dot(source, key_high, NT) + dot(source, key_low, NT)
        acc[2] += dot(source, value_high, NT) + dot(source, value_low, NT)
        gv_ref[...] += dot(ones, value_low, NT)[0:1]
        total = dot(columns(1), key_high, NN) + dot(columns(1), key_low, NN)
        total = total + dot(columns(2), value_high, NN) + dot(columns(2), value_low, NN)
        gp_ref[step // 2] = total.astype(bf16)

    @pl.when(step == 3)
    def _():
        for h in range(2):
            for k in range(3):
                lanes = slice(h * HEAD, (h + 1) * HEAD)
                gw_ref[h, :, k * HEAD : (k + 1) * HEAD] = acc[k, :, lanes].astype(bf16)
            gb_ref[h : h + 1, 0:HEAD] = gq_ref[:, h * HEAD : (h + 1) * HEAD]
            gb_ref[h : h + 1, HEAD : 2 * HEAD] = gv_ref[:, h * HEAD : (h + 1) * HEAD]
        gb_ref[2:4, 0 : 2 * HEAD] = jnp.zeros((2, 2 * HEAD), f32)
        gb_ref[:, 2 * HEAD :] = gb1[...]
        if strip % 16:
            mine_ref[...] = gp_ref[...]
            sent_ref[...] = gb_ref[...]
            return
        half = gp_ref.shape[2]
        row, core = sc[1], sc[2]
        first = lax.broadcasted_iota(jnp.int32, (strip, WIDE), 0) == 0
        low_half = lax.broadcasted_iota(jnp.int32, (1, WIDE), 1) < 4 * strip
        for other, ref in enumerate((mine_ref, sent_ref)):
            for e in range(n_ep):
                for s in range(2):
                    for r in range(2):
                        y = row ^ r
                        at = ((e * 2 + s) * 2 + y) * 2 + (core ^ other)
                        at = pl.ds(pl.multiple_of(at * strip, strip), strip)
                        for tile in range(PAD // WIDE):
                            lanes = slice(tile * WIDE % half, tile * WIDE % half + WIDE)
                            j, place = tile // 3, tile % 3
                            rows = slice(j * strip, (j + 1) * strip)
                            to = slice(place * WIDE, (place + 1) * WIDE)
                            ref[e, s, y, rows, to] = gp_ref[tile * WIDE // half, at, lanes]
                        k = r + 2 * other
                        tile = gb_ref[k : k + 1, e * WIDE : (e + 1) * WIDE]
                        if s == 1:
                            tile = pltpu.roll(tile, WIDE - 4 * strip, 1)
                        tile = jnp.where(low_half, tile, 0.0)
                        tile = jnp.where(first, tile, 0.0).astype(bf16)
                        ref[e, s, y, 2 * strip : 3 * strip, 2 * WIDE :] = tile


def weight_grads(places, x, dq, dk, dv, prompt, wp, gb1, n_ep, strip):
    half = x.shape[0] // 4
    width = wp.shape[1]
    spot = lambda i: jnp.where(i % 2 == 0, 2 + i // 2, i // 2)
    key = pl.BlockSpec((2, HEAD, half), lambda i: (0, 0, spot(i)))
    if strip % 16:
        shapes = [pltpu.VMEM((2, width, half), bf16), pltpu.VMEM((4, width), f32)]
    else:
        strips = (n_ep, 2, 2, 3 * strip, TAIL)
        shapes = [pltpu.HBM(strips, bf16), pltpu.VMEM(strips, bf16)]
    fixed = [
        pl.BlockSpec(shape.shape, functools.partial(lambda n, i: (0,) * n, len(shape.shape)))
        for shape in shapes
    ]
    out = pl.pallas_call(
        functools.partial(weight_body, n_ep, strip),
        grid=(4,),
        in_specs=[
            pl.BlockSpec(memory_space=pltpu.SMEM),
            pl.BlockSpec((half, width), lambda i: (i, 0)),
            pl.BlockSpec((half, 2 * HEAD), lambda i: (i, 0)),
            key,
            key,
            pl.BlockSpec((width, half), lambda i: (0, i // 2)),
            whole(),
            whole(),
        ],
        out_specs=[pl.BlockSpec((2, width, TAIL), lambda i: (0, 0, 0))]
        + fixed
        + [
            pl.BlockSpec((half, width), lambda i: (jnp.minimum(i, 1), 0)),
            pl.BlockSpec((half, width), lambda i: (jnp.maximum(i - 2, 0), 0)),
        ],
        out_shape=[pltpu.HBM((2, width, TAIL), bf16)]
        + shapes
        + [pltpu.HBM((2 * half, width), f32), pltpu.HBM((2 * half, width), bf16)],
        scratch_shapes=[pltpu.VMEM((3, width, 2 * HEAD), f32)]
        + [pltpu.VMEM((1, 2 * HEAD), f32)] * 2
        + [pltpu.VMEM((2, width, half), bf16), pltpu.VMEM((4, width), f32)],
        compiler_params=pltpu.CompilerParams(vmem_limit_bytes=40 << 20),
        cost_estimate=cost(9),
        name="weight_grads",
    )(places, *held((x, dq, dk, dv, prompt, wp), False), gb1)
    grad_project, mine, sent, back_own, back_other = out
    if strip % 16:
        row, core = places[1], places[2]
        grad = jnp.concatenate([mine[0], mine[1]], axis=1)
        blocks = grad.reshape(n_ep, 2, 2, 2, strip, PAD)
        table = sent.reshape(2, 2, n_ep, 2, 4 * strip)
        both = []
        for other in (0, 1):
            by_row = jnp.stack(pick(table[other, 0], table[other, 1], row), axis=2)
            part = lax.dynamic_index_in_dim(blocks, core ^ other, 3, keepdims=False)
            both.append(in_chunks(with_bias(part, by_row)))
        mine, sent = both
    return grad_project, mine, sent, back_own, back_other


def input_body(sc, ratio, dr_ref, own_ref, got_ref, rows_ref, enc, mask, rows_grad, i0, i1, i2, i3, small_ref, acc, bias):
    step = pl.program_id(0)
    low = (dr_ref[...] + own_ref[...] + got_ref[...].astype(f32)).astype(bf16)
    part = dot(low.T, rows_ref[...], NN) * ratio[0]
    part_bias = jnp.sum(low.astype(f32), axis=0, keepdims=True)

    @pl.when(step == 0)
    def _():
        acc[...] = part
        bias[...] = part_bias

    @pl.when(step > 0)
    def _():
        acc[...] += part
        bias[...] += part_bias

    grad = dot(enc[...].T, low, NT) * ratio[0] * mask[...]
    for k, ref in enumerate((i0, i1, i2, i3)):

        @pl.when(step == k)
        def _(ref=ref):
            ref[...] = grad[0:FEAT_ROWS].astype(bf16)

    @pl.when(step == 3)
    def _():
        width = acc.shape[0]
        rows = jnp.concatenate(
            [
                jnp.zeros((VEC, width), f32),
                rows_grad[0:6],
                bias[...],
                jnp.zeros((WIDE - VEC - 7, width), f32),
            ],
            axis=0,
        )
        small_ref[...] = (acc[...] + rows.T).astype(bf16)


def input_grads(sc, ratio, dr, own, got, rows, enc, mask, rows_grad):
    size = rows.shape[0] // 4
    width = enc.shape[0]
    spot = lambda i, sc: (2 * (sc[0] ^ (i // 2)) + (sc[1] ^ (i % 2)), 0)
    block = pl.BlockSpec((size, width), spot)
    fixed = pl.BlockSpec((FEAT_ROWS, size), lambda i, sc: (0, 0))
    return pl.pallas_call(
        input_body,
        grid_spec=pltpu.PrefetchScalarGridSpec(
            num_scalar_prefetch=1,
            grid=(4,),
            in_specs=[
                pl.BlockSpec(memory_space=pltpu.SMEM),
                block,
                block,
                block,
                pl.BlockSpec((size, WIDE), spot),
                whole(),
                whole(),
                whole(),
            ],
            out_specs=[fixed] * 4 + [pl.BlockSpec((width, WIDE), lambda i, sc: (0, 0))],
            scratch_shapes=[pltpu.VMEM((width, WIDE), f32), pltpu.VMEM((1, width), f32)],
        ),
        out_shape=[pltpu.VMEM((FEAT_ROWS, size), bf16)] * 4 + [pltpu.VMEM((width, WIDE), bf16)],
        compiler_params=pltpu.CompilerParams(vmem_limit_bytes=32 << 20),
        cost_estimate=cost(6),
        name="input_grads",
    )(sc, ratio, *held((dr, own, got, rows), False), enc, mask, rows_grad)


def split_small(grad, places, n_ep, strip):
    blocks = grad.reshape(n_ep * 4, 2, strip, WIDE)

    def body(sc, grad_ref, mine_ref, sent_ref):
        mine_ref[...] = grad_ref[:, sc[2]]
        sent_ref[...] = grad_ref[:, 1 - sc[2]]

    shape = shape_of((n_ep * 4, strip, WIDE), bf16)
    return simple(body, [shape, shape], blocks, scalars=places, name="split_small")


def pack_main(gw, mine, got, places, slab, strip):
    n_ep = mine.shape[0]
    heads = gw.reshape(2, n_ep, 2, slab, TAIL)
    if 2 * slab != WIDE:
        pair = (mine.astype(f32) + got.astype(f32)).astype(bf16)
        outs = []
        for b in (0, 1):
            for r in (0, 1):
                side, row = places[0] ^ b, places[1] ^ r
                part = lax.dynamic_index_in_dim(pair, side, 1, keepdims=False)
                part = lax.dynamic_index_in_dim(part, row, 1, keepdims=False)
                head = lax.dynamic_index_in_dim(heads[r], side, 1, keepdims=False)
                outs.append(jnp.concatenate([head, part], axis=1))
        return outs

    def body(sc, gw_ref, a_ref, b_ref, *outs):
        for b in range(2):
            for r in range(2):
                out = outs[2 * b + r]
                side, row = sc[0] ^ b, sc[1] ^ r
                out[:, 0:slab, :] = gw_ref[r, :, side]
                pair = a_ref[:, side, row].astype(f32) + b_ref[:, side, row].astype(f32)
                out[:, slab : slab + 3 * strip, :] = pair.astype(bf16)

    shape = shape_of((n_ep, slab + 3 * strip, TAIL), bf16)
    return simple(
        body,
        [shape] * 4,
        heads,
        mine,
        got,
        scalars=places,
        near=((False, False, True), True),
        name="pack_main",
    )


def pack_small(ins, mine, got, places, n_ep, strip):
    rows = ins[0].shape[1]
    mine = mine.reshape(n_ep, 2, 2, strip, WIDE)
    got = got.reshape(n_ep, 2, 2, strip, WIDE)
    total = FEAT_ROWS + n_ep * strip
    if 8 * strip != WIDE:
        pair = (mine.astype(f32) + got.astype(f32)).astype(bf16)
        outs = []
        for k in range(4):
            part = lax.dynamic_index_in_dim(pair, places[0] ^ (k // 2), 1, keepdims=False)
            part = lax.dynamic_index_in_dim(part, places[1] ^ (k % 2), 1, keepdims=False)
            part = jnp.pad(part.reshape(n_ep * strip, WIDE), ((0, 0), (0, rows - WIDE)))
            outs.append(jnp.concatenate([ins[k], part], axis=0))
        return outs

    def body(sc, *refs):
        in_refs, a_ref, b_ref, outs = refs[0:4], refs[4], refs[5], refs[6:]
        for k in range(4):
            side, row = sc[0] ^ (k // 2), sc[1] ^ (k % 2)
            outs[k][0:FEAT_ROWS] = in_refs[k][...]
            pair = a_ref[:, side, row].astype(f32) + b_ref[:, side, row].astype(f32)
            outs[k][FEAT_ROWS:, 0:WIDE] = pair.reshape(n_ep * strip, WIDE).astype(bf16)

    return simple(
        body, [shape_of((total, rows), bf16)] * 4, *ins, mine, got, scalars=places, name="pack_small"
    )


def subtiles(rows, lanes, width):
    out = []
    across = width // WIDE
    for n in range(rows // 16 * (lanes // WIDE)):
        g, t = divmod(n, lanes // WIDE)
        row, col = divmod(n, across)
        here = (slice(16 * g, 16 * (g + 1)), slice(WIDE * t, WIDE * (t + 1)))
        out.append((here, (16 * row, slice(WIDE * col, WIDE * (col + 1)))))
    return out


def place_tiles(parts, index, begin, rows, lanes, name):
    width = parts[0].shape[1]

    def body(sc, *refs):
        for k, ref in enumerate(refs[:-1]):
            for here, there in subtiles(rows, lanes, width):
                tile = ref[begin + there[0] : begin + there[0] + 16, there[1]]
                refs[-1][sc[0] ^ k, here[0], here[1]] = tile

    return simple(
        body,
        shape_of((len(parts), rows, lanes), bf16),
        *parts,
        scalars=index.reshape(1).astype(jnp.int32),
        near=(True, False),
        name=name,
    )


def pack_rest(mine, got, outs, places, n_ep, slab):
    width = mine.shape[-1]
    rows, lanes = outs[0].shape
    count = n_ep * slab
    mine = mine.reshape(2, n_ep, 2, slab, width)
    got = got.reshape(2, n_ep, 2, slab, width)

    def body(sc, a_ref, b_ref, *refs):
        for k in range(4):
            side = sc[0] ^ (k // 2)
            pair = a_ref[k % 2, :, side].astype(f32) + b_ref[k % 2, :, side].astype(f32)
            refs[4 + k][0:count] = pair.reshape(count, width).astype(bf16)
            for here, there in subtiles(rows, lanes, width):
                refs[4 + k][count + there[0] : count + there[0] + 16, there[1]] = refs[k][here]

    extra = subtiles(rows, lanes, width)[-1][1][0] + 16
    shape = shape_of((count + extra, width), bf16)
    return simple(body, [shape] * 4, mine, got, *outs, scalars=places, name="pack_rest")


def sum_rest(parts, later, places, n_ep, slab):
    width = parts[0].shape[1]
    if n_ep != 4:
        total = sum(part[0 : n_ep * slab].astype(f32) for part in parts)
        total = total.reshape(n_ep, slab, width)
        return [lax.psum_scatter(total, "ep", scatter_dimension=0, tiled=True)[0]]

    def body(sc, *refs):
        ins, outs = refs[: len(parts)], refs[len(parts) :]
        for k in range(4):
            spot = pl.multiple_of((sc[6] ^ k) * slab, slab)
            total = ins[0][pl.ds(spot, slab), :].astype(f32)
            for ref in ins[1:]:
                total = total + ref[pl.ds(spot, slab), :].astype(f32)
            outs[k // 2][k % 2] = total.astype(bf16)

    near, far = simple(
        body, [shape_of((2, slab, width), bf16)] * 2, *parts, scalars=places, name="sum_rest"
    )
    got = swap(far, ep=2)

    def added(a_ref, b_ref, own_ref, sent_ref):
        own_ref[...] = (a_ref[0].astype(f32) + b_ref[0].astype(f32)).astype(bf16)
        sent_ref[...] = (a_ref[1].astype(f32) + b_ref[1].astype(f32)).astype(bf16)

    got = tie(got, later)
    own, sent = simple(added, [shape_of((slab, width), bf16)] * 2, near, got, name="add_rest")
    return [own, swap(sent, ep=1)]


def sum_main(mains, smalls, places, slab, strip):
    n_ep = mains[0].shape[0]
    if n_ep > 4:
        total = sum(part.astype(f32) for part in mains)
        small = sum(part[FEAT_ROWS:, 0:WIDE].astype(f32) for part in smalls)
        small = jnp.pad(small.reshape(n_ep, strip, WIDE), ((0, 0), (0, 0), (0, TAIL - WIDE)))
        return reduce_ep(jnp.concatenate([total, small], axis=1), None)

    def body(sc, *refs):
        main_refs, small_refs, outs = refs[0:4], refs[4:8], refs[8:]
        for k, out in enumerate(outs):
            spot = sc[6] ^ k
            total = main_refs[0][spot].astype(f32)
            for ref in main_refs[1:]:
                total = total + ref[spot].astype(f32)
            out[0 : slab + 3 * strip] = total.astype(bf16)
            where = pl.multiple_of(FEAT_ROWS + spot * strip, strip)
            total = small_refs[0][pl.ds(where, strip), 0:WIDE].astype(f32)
            for ref in small_refs[1:]:
                total = total + ref[pl.ds(where, strip), 0:WIDE].astype(f32)
            out[slab + 3 * strip :, 0:WIDE] = total.astype(bf16)
            out[slab + 3 * strip :, WIDE:] = jnp.zeros((strip, TAIL - WIDE), bf16)

    shape = shape_of((slab + 4 * strip, TAIL), bf16)
    pieces = simple(body, [shape] * n_ep, *mains, *smalls, scalars=places, name="sum_main")
    return reduce_ep(None, pieces)


def place_rows(parts, index, begin, shape, dtype, name):
    def body(sc, *refs):
        for k, ref in enumerate(refs[:-1]):
            refs[-1][sc[0] ^ k] = ref[begin : begin + shape[0], 0 : shape[1]].astype(dtype)

    return simple(
        body,
        shape_of((len(parts),) + shape, dtype),
        *parts,
        scalars=index.reshape(1).astype(jnp.int32),
        near=(True, False),
        name=name,
    )


def final_sums(mains, rests, slab, strip):
    def body(*refs):
        main_refs, rest_refs = refs[: len(mains)], refs[len(mains) : len(mains) + len(rests)]
        block_ref, prompt_ref, small_ref, bias_ref, square_ref = refs[len(mains) + len(rests) :]

        def added(group):
            total = group[0][...].astype(f32)
            for ref in group[1:]:
                total = total + ref[...].astype(f32)
            return total

        main, rest = added(main_refs), added(rest_refs)
        square = jnp.sum(jnp.sum(main * main, axis=0, keepdims=True), axis=1, keepdims=True)
        square = square + jnp.sum(
            jnp.sum(rest * rest, axis=0, keepdims=True), axis=1, keepdims=True
        )
        for j in range(8):
            if j < 3:
                tile = main[0:slab, j * HEAD : (j + 1) * HEAD]
            else:
                tile = rest[:, (j - 3) * HEAD : (j - 2) * HEAD]
            block_ref[pl.ds(j, slab, stride=8), :] = tile
        for j in range(3):
            part = main[slab + j * strip : slab + (j + 1) * strip]
            high = min(PROMPT, (j + 1) * TAIL)
            prompt_ref[:, j * TAIL : high] = part[:, 0 : high - j * TAIL]
        small_ref[...] = main[slab + 3 * strip :, 0:WIDE]
        bias_ref[...] = main[slab + 2 * strip : slab + 2 * strip + 1, TAIL - WIDE :]
        square_ref[...] = jnp.broadcast_to(square, (8, 128))

    return simple(
        body,
        [
            shape_of((slab * 8, HEAD), f32),
            shape_of((strip, PROMPT), f32),
            shape_of((strip, WIDE), f32),
            shape_of((1, WIDE), f32),
            shape_of((8, 128), f32),
        ],
        *mains,
        *rests,
        name="final_sums",
    )


def adam_all(squares, params, moments, grads):
    slab = params[0].shape[0] // 8
    rates = (rate_matrix, rate_vector, rate_matrix, rate_vector, rate_vector)
    decays = (weight_decay, weight_decay, weight_decay, 0.0, 0.0)
    count = squares.shape[0]

    def body(sq_ref, *refs):
        weights, moment_refs, grad_refs, outs = refs[0:5], refs[5:10], refs[10:14], refs[14:]
        total = sq_ref[0, 0:1, 0:1]
        for k in range(1, count):
            total = total + sq_ref[k, 0:1, 0:1]
        norm = jnp.sqrt(total)
        outs[0][...] = norm
        factor = jnp.minimum(1.0, clip_norm / (norm + 1e-06))
        small = grad_refs[2][...]
        picked = (
            grad_refs[0][...],
            grad_refs[1][...],
            small[:, 0:FEAT],
            small.T[VEC : VEC + 7],
            grad_refs[3][:, 0:slab],
        )
        for k in range(5):
            both = moment_refs[k]
            pair = (both[:, 0], both[:, 1]) if k == 3 else (both[0], both[1])
            news = adam_update(weights[k][...], pair, picked[k], factor, rates[k], decays[k])
            for m in range(3):
                outs[1 + 4 * k + m][...] = news[m]
            if k > 0:
                outs[4 + 4 * k][...] = news[3]
        for j in range(8):
            tile = outs[1][pl.ds(j, slab, stride=8), :]
            outs[4][:, j * HEAD : (j + 1) * HEAD] = tile.astype(bf16)

    shapes = [shape_of((1, 1), f32)]
    for k, param in enumerate(params):
        low = (slab, 8 * HEAD) if k == 0 else param.shape
        shapes += [shape_of(param.shape, f32)] * 3 + [shape_of(low, bf16)]
    return simple(body, shapes, squares, *params, *moments, *grads, near=(True, False), name="adam_all")


def shards(
    feats,
    counts,
    feat_mask,
    cotangent,
    block_weights,
    block_moments,
    head_biases,
    bias_moments,
    encoder,
    encoder_moments,
    shared_vectors,
    vector_moments,
    prompt,
    prompt_moments,
):
    n_ep = lax.axis_size("ep")
    side = lax.axis_index("split")
    row = lax.axis_index("tp") // 2
    core = lax.axis_index("tp") % 2
    chip = side * 2 + row
    rows = feats.shape[2]
    width = cotangent.shape[3]
    slab = block_weights.shape[0]
    strip = encoder.shape[0]

    mask_row = lax.dynamic_index_in_dim(feat_mask, chip, 0, keepdims=False)
    count_pair = lax.dynamic_index_in_dim(counts, chip, 0, keepdims=False)
    mask_float = mask_row.astype(f32)
    ratio = (FEAT / jnp.sum(mask_float)).reshape(1)
    spot = jnp.arange(8, dtype=jnp.int32)
    places = jnp.pad(count_pair, (4, 2)).astype(jnp.int32)
    for k, value in ((0, side), (1, row), (2, core), (3, chip), (6, lax.axis_index("ep"))):
        places = places + jnp.where(spot == k, value, 0)

    def to_chip(array):
        return plane_list(
            [lax.dynamic_index_in_dim(array[0], chip ^ k, 0, keepdims=False) for k in range(4)]
        )

    def plane_list(parts):
        got = plane_swap(lambda b, r: parts[2 * b + r])
        return [got[b, r] for b in (0, 1) for r in (0, 1)]

    main_part, rest_part = pack_parts(
        block_weights, prompt, encoder, shared_vectors, head_biases
    )
    mask_wide = jnp.pad(mask_float, (0, WIDE - FEAT)).reshape(1, WIDE)
    flipped = jnp.transpose(tie(feats, main_part)[0], (0, 2, 1))
    main_pieces = gather_ep(main_part)
    feats_own, feats_other = None, None
    if 2 * slab == WIDE:
        tops = plane_list(build_main(main_pieces, flipped, places))
    else:
        feats_own = join_features(
            plane_list(
                [lax.dynamic_index_in_dim(flipped, chip ^ k, 0, keepdims=False) for k in range(4)]
            ),
            places,
        )
        feats_other = swap(feats_own, core=1)
        tops = plane_list([stack_ep(main_pieces, "stack_main")] * 4)
    lows = [swap(top, core=1) for top in tops]
    w_project, prompt_low, small_low, vector_rows, bias_rows, masked_own, masked_other = unpack_main(
        tops, lows, feats_own, feats_other, mask_wide, places, n_ep, slab, strip, rows
    )
    w_project = w_project.reshape(2, width, TAIL)
    prompt_low = prompt_low.reshape(width, 3 * TAIL)
    encoder_low = small_low.reshape(width, WIDE)

    rest_along = stack_ep(gather_ep(tie(rest_part, lows[0])), "stack_rest")
    lows, rest_along = lax.optimization_barrier((lows, rest_along))

    cots = to_chip(tie(cotangent, w_project))
    rows_low, query, keys, keys_flip, values, values_flip, key_extra = project(
        ratio,
        places,
        masked_own,
        masked_other,
        encoder_low,
        vector_rows,
        w_project,
        bias_rows,
        prompt_low,
    )
    query, rest_along, cots = lax.optimization_barrier((query, rest_along, cots))
    rest_tops = plane_list([rest_along] * 4)
    attended_other, extra_other = attend(query, keys, key_extra, values_flip, 1)
    attended_got = swap(attended_other, core=1)
    query_own = tie(query, (attended_other, rest_tops[1]))
    attended_own, extra_own = attend(query_own, keys, key_extra, values_flip, 0)
    rest_own = unpack_rest(tie(rest_tops, attended_own), places)
    rest_own = rest_own.reshape(2, width, -1)
    rest_other = swap(rest_own, core=1)
    (y0, y1, y2, y3, grad_own, grad_sent, grad_one, rest_mine, rest_sent, grad_rows, grad_hidden_row) = middle(
        places,
        ratio,
        masked_own,
        attended_own,
        attended_got,
        cots,
        encoder_low,
        vector_rows,
        bias_rows,
        rest_own,
        rest_other,
    )
    grad_got = swap(grad_sent, core=1)
    rest_got = swap(rest_sent, core=1)
    rest_parts = pack_rest(rest_mine, rest_got, (y0, y1, y2, y3), places, n_ep, slab)
    rest_tops = plane_list(rest_parts)
    query_again, *unused = lax.optimization_barrier((query, *rest_parts))
    grad_query, grad_key, grad_value = attend_back(
        query_again,
        keys,
        key_extra,
        keys_flip,
        values,
        extra_own,
        extra_other,
        grad_own,
        grad_got,
    )
    rest_tops, grad_query = lax.optimization_barrier((rest_tops, grad_query))
    grad_project, prompt_mine, prompt_sent, back_own, back_other = weight_grads(
        places,
        rows_low,
        grad_query,
        grad_key,
        grad_value,
        prompt_low,
        w_project,
        grad_hidden_row,
        n_ep,
        strip,
    )
    prompt_got = swap(prompt_sent, core=1)
    back_got = swap(back_other, core=1)
    main_parts = pack_main(grad_project, prompt_mine, prompt_got, places, slab, strip)
    main_tops = plane_list(main_parts)
    back_own = tie(back_own, main_parts)
    i0, i1, i2, i3, grad_small = input_grads(
        places,
        ratio,
        grad_one,
        back_own,
        back_got,
        masked_own,
        encoder_low,
        mask_wide.reshape(WIDE, 1),
        grad_rows,
    )
    small_mine, small_sent = split_small(grad_small, places, n_ep, strip)
    small_got = swap(small_sent, core=1)
    small_parts = pack_small((i0, i1, i2, i3), small_mine, small_got, places, n_ep, strip)
    small_tops = plane_list(small_parts)
    rest_pieces = sum_rest(tie(rest_tops, main_parts), grad_small, places, n_ep, slab)
    output_final = place_tiles(rest_tops, chip, n_ep * slab, rows, width, "place_output")
    main_tops, output_final, rest_pieces = lax.optimization_barrier(
        (main_tops, output_final, rest_pieces)
    )
    main_pieces = sum_main(main_tops, small_tops, places, slab, strip)
    input_final = place_rows(small_tops, chip, 0, (FEAT_ROWS, rows), f32, "place_input")
    input_final = jnp.transpose(input_final[:, 0:FEAT], (0, 2, 1))[None]

    grad_block, grad_prompt_own, grad_small_own, grad_bias_own, square_tile = final_sums(
        main_pieces, rest_pieces, slab, strip
    )
    square_tile = square_tile + swap(square_tile, core=1)
    got = plane_swap(lambda b, r: square_tile)
    square_tile = (got[0, 0] + got[1, 0]) + (got[0, 1] + got[1, 1])
    if n_ep > 4:
        squares = lax.psum(square_tile, "ep")[None]
    else:
        squares = stack_ep(gather_ep(square_tile), "stack_square")
    grad_norm, *news = adam_all(
        squares,
        (
            block_weights.reshape(slab * 8, HEAD),
            prompt,
            encoder,
            shared_vectors.T,
            head_biases.T,
        ),
        (
            block_moments.reshape(2, slab * 8, HEAD),
            prompt_moments,
            encoder_moments,
            jnp.transpose(vector_moments, (2, 0, 1)),
            jnp.transpose(bias_moments, (0, 2, 1)),
        ),
        (grad_block, grad_prompt_own, grad_small_own, grad_bias_own),
    )
    block_out = tuple(part.reshape(block_weights.shape) for part in news[0:4])
    prompt_out = tuple(news[4:8])
    encoder_out = tuple(news[8:12])
    vector_out = tuple(part.T for part in news[12:16])
    bias_out = tuple(part.T for part in news[16:20])
    return (
        (output_final[None], input_final, grad_norm.reshape(()))
        + block_out
        + bias_out
        + encoder_out
        + vector_out
        + prompt_out
    )


def solution(mesh):
    data = P("split", "ep", "tp", None)
    block = P(("ep", "split"), "tp", None)
    bias = P(("ep", "split"), "tp")
    strip = P(AXES, None)
    placed = (
        data,
        P("ep", None),
        P("ep", None),
        data,
        block,
        P(None, ("ep", "split"), "tp", None),
        bias,
        P(None, ("ep", "split"), "tp"),
        strip,
        P(None, AXES, None),
        strip,
        P(None, AXES, None),
        strip,
        P(None, AXES, None),
    )
    return jax.shard_map(
        shards,
        mesh=mesh,
        in_specs=placed,
        out_specs=(data, data, P()) + (block,) * 4 + (bias,) * 4 + (strip,) * 12,
        check_vma=False,
    )
```

```python
import functools

import jax
import jax.numpy as jnp
from jax import lax
from jax.experimental import pallas as pl
from jax.experimental.pallas import tpu as pltpu
from jax.sharding import PartitionSpec as P

HEADS = 4
HEAD = 128
FF = 1024
HID = FF // HEADS
FEAT = 100
PROMPT = 1000
SLOTS = 1024
ADAM_STEP = 10
PAD = 1024
WIDE = 128

ln_eps = 1e-05
neg_big = -1e30
clip_norm = 1.0
beta_one = 0.9
beta_two = 0.999
adam_eps = 1e-08
rate_matrix = 0.15
rate_vector = 0.5
weight_decay = 0.01
AXES = ("ep", "split", "tp")
bf16 = jnp.bfloat16
f32 = jnp.float32
score_scale = HEAD**-0.5


def swap(value, ep=0, split=0, row=0, core=0):
    sizes = [lax.axis_size(a) for a in AXES]
    pairs = []
    for a in range(sizes[0]):
        for b in range(sizes[1]):
            for t in range(sizes[2]):
                other = ((a ^ ep) * sizes[1] + (b ^ split)) * sizes[2] + (t ^ (2 * row + core))
                pairs.append(((a * sizes[1] + b) * sizes[2] + t, other))
    return lax.ppermute(value, AXES, pairs)


def pick(low, high, bit):
    return jnp.where(bit == 0, low, high), jnp.where(bit == 0, high, low)


def plane_swap(piece):
    got = {}
    for b in (0, 1):
        for r in (0, 1):
            sent = piece(b, r)
            got[b, r] = sent if (b, r) == (0, 0) else swap(sent, split=b, row=r)
    return got


def tie(value, other):
    return lax.optimization_barrier((value, other))[0]


def gather_ep(shard):
    count = lax.axis_size("ep")
    if count > 4:
        return [lax.all_gather(shard, "ep", axis=0)]
    return [shard] + [swap(shard, ep=k) for k in range(1, count)]


def stack_ep(parts, name):
    return parts[0] if len(parts) == 1 else place(parts, lax.axis_index("ep"), name)


def reduce_ep(total, pieces):
    count = lax.axis_size("ep")
    if count > 4:
        return [lax.psum_scatter(total, "ep", scatter_dimension=0, tiled=True)[0]]
    return [pieces[0]] + [swap(pieces[k], ep=k) for k in range(1, count)]


def adam_update(weight, moments, gradient, factor, step_rate, decay_rate):
    clipped = gradient * factor
    first_moment = beta_one * moments[0] + (1.0 - beta_one) * clipped
    second_moment = beta_two * moments[1] + (1.0 - beta_two) * clipped * clipped
    first_hat = first_moment / (1.0 - beta_one**ADAM_STEP)
    second_hat = second_moment / (1.0 - beta_two**ADAM_STEP)
    updated = weight - step_rate * (
        first_hat / (jnp.sqrt(second_hat) + adam_eps) + decay_rate * weight
    )
    return (updated, first_moment, second_moment, updated.astype(bf16))


def dot(a, b, dims):
    return lax.dot_general(a, b, (dims, ((), ())), preferred_element_type=f32)


NN = ((1,), (0,))
NT = ((1,), (1,))
TN = ((0,), (0,))


def cost(micros):
    return pl.CostEstimate(flops=int(micros * 3e8), transcendentals=0, bytes_accessed=int(micros * 1e6))


def whole():
    return pl.BlockSpec(memory_space=pltpu.VMEM)


def shape_of(shape, dtype):
    return jax.ShapeDtypeStruct(shape, dtype)


def project_body(ratio, sc, own, other, enc, vec, wp, bias, prompt, x_ref, q_ref, k_ref, kt_ref, v_ref, vt_ref, extra_ref):
    step = pl.program_id(0)

    @pl.when(step == 0)
    def _():
        size = own.shape[0] // 2
        lane = lax.broadcasted_iota(jnp.int32, (size, WIDE), 1)
        line = lax.broadcasted_iota(jnp.int32, (size, WIDE), 0)
        ones = [jnp.where((lane >= 4 * h) & (lane < 4 * h + 3), 1.0, 0.0) for h in range(2)]
        for begin in range(0, extra_ref.shape[1], size):
            if begin < PAD:
                left = PROMPT - begin
            else:
                other, quarter = divmod((begin - PAD) // size, 2)
                left = sc[4] - (2 * quarter + (sc[2] ^ other)) * size
            bias = jnp.where((lane == 3) & (line >= left), neg_big, 0.0)
            for h in range(2):
                extra_ref[h, begin : begin + size] = (bias + ones[h]).astype(bf16)

    rows = jnp.where(step < 2, own[...], other[...])
    low = (ratio[0] * dot(rows, enc[...], NT) + vec[6:7, :]).astype(bf16)
    x_ref[...] = low
    for h in range(2):
        q_ref[h] = (dot(low, wp[h, :, 0:HEAD], NN) + bias[h : h + 1, 0:HEAD]).astype(bf16)

    def keys_from(source):
        for h in range(2):
            key = dot(source, wp[h, :, HEAD : 2 * HEAD], NN).astype(bf16)
            shift = bias[h : h + 1, HEAD : 2 * HEAD]
            value = (dot(source, wp[h, :, 2 * HEAD : 3 * HEAD], NN) + shift).astype(bf16)
            k_ref[h] = key
            v_ref[h] = value
            kt_ref[h] = key.T
            vt_ref[h] = value.T

    @pl.when(step % 2 == 0)
    def _():
        keys_from(low)

    @pl.when(step % 2 == 1)
    def _():
        keys_from(prompt[...].T)


def project(ratio, places, own, other, enc, vec, wp, bias, prompt):
    half = own.shape[0] // 2
    width = enc.shape[0]
    keys = PAD + SLOTS
    spot = lambda i: jnp.where(i % 2 == 0, 2 + i // 2, i // 2)
    tall = pl.BlockSpec((2, half, HEAD), lambda i: (0, spot(i), 0))
    flat = pl.BlockSpec((2, HEAD, half), lambda i: (0, 0, spot(i)))
    return pl.pallas_call(
        project_body,
        grid=(4,),
        in_specs=[
            pl.BlockSpec(memory_space=pltpu.SMEM),
            pl.BlockSpec(memory_space=pltpu.SMEM),
            pl.BlockSpec((half, WIDE), lambda i: (jnp.minimum(i, 1), 0)),
            pl.BlockSpec((half, WIDE), lambda i: (jnp.maximum(i - 2, 0), 0)),
            whole(),
            whole(),
            whole(),
            whole(),
            pl.BlockSpec((width, half), lambda i: (0, i // 2)),
        ],
        out_specs=[
            pl.BlockSpec((half, width), lambda i: (i, 0)),
            pl.BlockSpec((2, half, HEAD), lambda i: (0, i, 0)),
            tall,
            flat,
            tall,
            flat,
            pl.BlockSpec((2, keys, WIDE), lambda i: (0, 0, 0)),
        ],
        out_shape=[
            pltpu.HBM((4 * half, width), bf16),
            pltpu.HBM((2, 4 * half, HEAD), bf16),
            pltpu.HBM((2, keys, HEAD), bf16),
            pltpu.HBM((2, HEAD, keys), bf16),
            pltpu.HBM((2, keys, HEAD), bf16),
            pltpu.HBM((2, HEAD, keys), bf16),
            pltpu.HBM((2, keys, WIDE), bf16),
        ],
        compiler_params=pltpu.CompilerParams(vmem_limit_bytes=32 << 20),
        cost_estimate=cost(9),
        name="project",
    )(ratio, places, *held((own, other, enc, vec, wp, bias, prompt)))


CHUNK = 1024
base_two = 1.4426950408889634


def three_terms(value):
    high = value.astype(bf16).astype(f32)
    middle = (value - high).astype(bf16).astype(f32)
    return high, middle, value - high - middle


def attend_body(q_ref, k_ref, x_ref, vt_ref, o_ref, extra_ref, *scratch):
    head = pl.program_id(0)
    keys, size = scratch[0].shape
    count = q_ref.shape[1] // size
    steepness = score_scale * base_two
    lane = lax.broadcasted_iota(jnp.int32, (size, WIDE), 1)
    place = lax.broadcasted_iota(jnp.int32, (WIDE, size), 0)
    one = jnp.where(lane == 3, 1.0, 0.0).astype(bf16)
    top = None
    for b in range(count + 1):
        fresh_ref, old_ref = scratch[b % 2], scratch[(b + 1) % 2]
        if b < count:
            query = jnp.concatenate([q_ref[0, b * size : (b + 1) * size], one], axis=1)
            partial = jnp.full((8, size), -jnp.inf, f32)
        if b > 0:
            shift = top * steepness
            total = jnp.zeros((8, size), f32)
            out = jnp.zeros((HEAD, size), f32)
        for c in range(keys // CHUNK):
            span = slice(c * CHUNK, (c + 1) * CHUNK)
            if b < count:
                wide = jnp.concatenate([k_ref[0, span], x_ref[0, span]], axis=1)
                fresh = dot(wide, query, NT)
                fresh_ref[span] = fresh
                partial = jnp.maximum(partial, jnp.max(fresh.reshape(CHUNK // 8, 8, size), axis=0))
            if b > 0:
                raised = jnp.exp2(old_ref[span] * steepness - shift)
                total = total + jnp.sum(raised.reshape(CHUNK // 8, 8, size), axis=0)
                out = out + dot(vt_ref[0, :, span], raised.astype(bf16), NN)
        if b > 0:
            rows = slice((b - 1) * size, b * size)
            total = jnp.sum(total, axis=0, keepdims=True)
            o_ref[rows] = (out / total).T.astype(bf16)
            terms = three_terms(-(top + jnp.log(total) / score_scale))
            tile = jnp.where(place == 3, 1.0, 0.0)
            for k in range(3):
                tile = tile + jnp.where(place == 4 * head + k, terms[k], 0.0)
            extra_ref[0, rows] = tile.T.astype(bf16)
        if b < count:
            top = jnp.max(partial, axis=0, keepdims=True)


BLOCK = 512


def attend(q, k, extra, vt, which):
    keys = k.shape[1]
    tall = pl.BlockSpec((1, keys, HEAD), lambda h: (h, 0, 0))
    return pl.pallas_call(
        attend_body,
        grid=(2,),
        in_specs=[
            pl.BlockSpec((1, SLOTS, HEAD), lambda h: (h, which, 0)),
            tall,
            pl.BlockSpec((1, keys, WIDE), lambda h: (0, 0, 0)),
            pl.BlockSpec((1, HEAD, keys), lambda h: (h, 0, 0)),
        ],
        out_specs=[
            pl.BlockSpec((SLOTS, HEAD), lambda h: (0, h)),
            pl.BlockSpec((1, SLOTS, WIDE), lambda h: (h, 0, 0)),
        ],
        out_shape=[pltpu.HBM((SLOTS, 2 * HEAD), bf16), pltpu.HBM((2, SLOTS, WIDE), bf16)],
        scratch_shapes=[pltpu.VMEM((keys, BLOCK), f32)] * 2,
        compiler_params=pltpu.CompilerParams(vmem_limit_bytes=32 << 20),
        cost_estimate=cost(6),
        name="attend",
    )(*held((q, k, extra, vt), False))


BACK_BLOCK = 256
BACK_CHUNK = 1024


def attend_back_body(q_ref, k_ref, x_ref, kt_ref, v_ref, qa_ref, qb_ref, da_ref, db_ref, ea_ref, eb_ref, dq_ref, dk_ref, dv_ref, *scratch):
    size = scratch[0].shape[1]
    keys = k_ref.shape[1]
    rows = q_ref.shape[1]
    count = rows // size
    steepness = score_scale * base_two
    mine = pl.program_id(1) == 0

    @pl.when(mine)
    def _():
        dk_ref[...] = jnp.zeros_like(dk_ref)
        dv_ref[...] = jnp.zeros_like(dv_ref)

    for b in range(count + 1):
        probs_ref, slopes_ref = scratch[2 * (b % 2) : 2 * (b % 2) + 2]
        old_probs, old_slopes = scratch[2 - 2 * (b % 2) : 4 - 2 * (b % 2)]
        if b < count:
            span = slice(b * size, (b + 1) * size)
            query = q_ref[0, span]
            grad = jnp.where(mine, da_ref[span], db_ref[span])
            aside = jnp.where(mine, qa_ref[0, span], qb_ref[0, span])
            sums = jnp.where(mine, ea_ref[span], eb_ref[span])
            query_wide = jnp.concatenate([query, aside], axis=1)
            grad_wide = jnp.concatenate([grad, sums], axis=1)
        if b > 0:
            back = jnp.zeros((HEAD, size), f32)
        for c in range(keys // BACK_CHUNK):
            span = slice(c * BACK_CHUNK, (c + 1) * BACK_CHUNK)
            if b < count:
                extra = x_ref[0, span]
                scores = dot(jnp.concatenate([k_ref[0, span], extra], axis=1), query_wide, NT)
                slopes = dot(jnp.concatenate([v_ref[0, span], extra], axis=1), grad_wide, NT)
                probs = jnp.exp2(scores * steepness)
                probs_ref[span] = probs.astype(bf16)
                slopes_ref[span] = (probs * slopes).astype(bf16)
            if b > 0:
                back = back + dot(kt_ref[0, :, span], old_slopes[span], NN)
                grad_key = dot(query_flip, old_slopes[span], NT) * score_scale
                grad_value = dot(grad_flip, old_probs[span], NT)
                dk_ref[0, :, span] += grad_key
                dv_ref[0, :, span] += grad_value
        if b > 0:
            dq_ref[(b - 1) * size : b * size] = (back * score_scale).T.astype(bf16)
        if b < count:
            query_flip, grad_flip = query.T, grad.T


def attend_back(q, k, extra, kt, v, extra_own, extra_other, grad_own, grad_other):
    keys = k.shape[1]
    tall = pl.BlockSpec((1, keys, HEAD), lambda h, i: (h, 0, 0))
    flat = pl.BlockSpec((1, HEAD, keys), lambda h, i: (h, 0, 0))
    aside = pl.BlockSpec((1, SLOTS, WIDE), lambda h, i: (h, 0, 0))
    grad = pl.BlockSpec((SLOTS, HEAD), lambda h, i: (0, h))
    sums = pl.BlockSpec((SLOTS, HEAD), lambda h, i: (0, 2))
    return pl.pallas_call(
        attend_back_body,
        grid=(2, 2),
        in_specs=[
            pl.BlockSpec((1, SLOTS, HEAD), lambda h, i: (h, i, 0)),
            tall,
            tall,
            flat,
            tall,
            aside,
            aside,
            grad,
            grad,
            sums,
            sums,
        ],
        out_specs=[pl.BlockSpec((SLOTS, HEAD), lambda h, i: (i, h)), flat, flat],
        out_shape=[
            pltpu.HBM((2 * SLOTS, 2 * HEAD), bf16),
            pltpu.HBM((2, HEAD, keys), f32),
            pltpu.HBM((2, HEAD, keys), f32),
        ],
        scratch_shapes=[pltpu.VMEM((keys, BACK_BLOCK), bf16)] * 4,
        compiler_params=pltpu.CompilerParams(vmem_limit_bytes=40 << 20),
        cost_estimate=cost(20),
        name="attend_back",
    )(
        *held((q, k, extra, kt, v, extra_own, extra_other), False),
        *held((grad_own, grad_other, grad_own, grad_other), (False, True, False, True)),
    )


erfc_terms = (
    -1.26551223,
    1.00002368,
    0.37409196,
    0.09678418,
    -0.18628806,
    0.27886807,
    -1.13520398,
    1.48851587,
    -0.82215223,
    0.17087277,
)


def gelu_pair(t):
    z = jnp.abs(t) * (0.5**0.5)
    k = 1.0 / (1.0 + 0.5 * z)
    series = jnp.full_like(t, erfc_terms[-1])
    for term in erfc_terms[-2::-1]:
        series = series * k + term
    tail = 0.5 * k * jnp.exp(series - z * z)
    cumulative = jnp.where(t >= 0.0, 1.0 - tail, tail)
    density = jnp.exp(-0.5 * t * t) * 0.3989422804014327
    return t * cumulative, cumulative + t * density


def middle_body(
    sc,
    ratio,
    rows_ref,
    oa_ref,
    ob_ref,
    c0,
    c1,
    c2,
    c3,
    enc,
    vec,
    b1,
    ra,
    rb,
    y0,
    y1,
    y2,
    y3,
    da_ref,
    db_ref,
    dr_ref,
    ga,
    gb,
    gvec,
    gb1,
    cot,
    late,
    acc,
):
    step = pl.program_id(0)
    count = rows_ref.shape[0]
    part = count // 2

    def quarter_rows(k):
        return pl.ds(pl.multiple_of((sc[1] ^ (k % 2)) * part, part), part)

    for k, ref in enumerate((c0, c1, c2, c3)):

        @pl.when(step == k // 2)
        def _(k=k, ref=ref):
            cot[quarter_rows(k), :] = ref[...]

    @pl.when(step == 0)
    def _():
        gvec[...] = jnp.zeros_like(gvec)
        gb1[...] = jnp.zeros_like(gb1)

    def gather(k, low, high, value):
        acc[k, :, low:high] = jnp.where(step > 0, acc[k, :, low:high], 0.0) + value

    group = sc[0] ^ step
    limit = jnp.where(group == 0, sc[4], sc[5])
    line = lax.broadcasted_iota(jnp.int32, (count, 1), 0)
    slot = line + sc[2] * part + jnp.where(line >= part, part, 0)
    live = (slot < limit).astype(f32)

    def weight(k, low, high):
        return (ra if k < 2 else rb)[k % 2, :, low:high]

    def row(k):
        return vec[k : k + 1, :]

    gain_one, shift_one, gain_two, shift_two, b_out, b_two, b_enc = (row(k) for k in range(7))
    embedded = ratio[0] * dot(rows_ref[...], enc[...], NT) + b_enc
    out_pair = [
        jnp.concatenate([weight(2 * k, 0, HEAD), weight(2 * k + 1, 0, HEAD)], axis=1)
        for k in (0, 1)
    ]
    attn = dot(oa_ref[...], out_pair[0], NT) + dot(ob_ref[...], out_pair[1], NT) + b_out

    def norm(residual):
        centred = residual - jnp.mean(residual, axis=-1, keepdims=True)
        inverse = lax.rsqrt(jnp.mean(centred * centred, axis=-1, keepdims=True) + ln_eps)
        return centred * inverse, inverse

    def back(grad, normed, inverse, gain):
        scaled = grad * gain
        plain = jnp.mean(scaled, axis=-1, keepdims=True)
        mixed = jnp.mean(scaled * normed, axis=-1, keepdims=True)
        return inverse * (scaled - plain - normed * mixed)

    def add_row(k, value):
        gvec[k : k + 1, :] += jnp.sum(value, axis=0, keepdims=True)

    normed_one, inverse_one = norm(embedded + attn)
    first = normed_one * gain_one + shift_one
    first_low = first.astype(bf16)
    mlp = b_two
    acts, slopes = [], []
    for k in range(4):
        pre = dot(first_low, weight(k, HEAD, HEAD + HID), NN) + b1[k : k + 1, 2 * HEAD :]
        act, slope = gelu_pair(pre)
        acts.append(act.astype(bf16))
        slopes.append(slope)
        mlp = mlp + dot(acts[k], weight(k, HEAD + HID, HEAD + 2 * HID), NT)
    normed_two, inverse_two = norm(first + mlp)
    late[...] = ((normed_two * gain_two + shift_two) * live).astype(bf16)
    for k, ref in enumerate((y0, y1, y2, y3)):

        @pl.when(step == k // 2)
        def _(k=k, ref=ref):
            ref[...] = late[quarter_rows(k), :]

    grad_y = cot[...].astype(f32) * live
    add_row(2, grad_y * normed_two)
    add_row(3, grad_y)
    grad_two = back(grad_y, normed_two, inverse_two, gain_two)
    grad_low = grad_two.astype(bf16)
    add_row(5, grad_low.astype(f32))
    grad_flip = grad_low.T
    first_flip = first_low.T
    grad_first = grad_two
    for k in range(4):
        gather(k, HEAD + HID, HEAD + 2 * HID, dot(grad_flip, acts[k], NN))
        grad_act = dot(grad_low, weight(k, HEAD + HID, HEAD + 2 * HID), NN)
        grad_pre = (grad_act * slopes[k]).astype(bf16)
        gb1[k : k + 1, :] += jnp.sum(grad_pre.astype(f32), axis=0, keepdims=True)
        gather(k, HEAD, HEAD + HID, dot(first_flip, grad_pre, NN))
        grad_first = grad_first + dot(grad_pre, weight(k, HEAD, HEAD + HID), NT)
    add_row(0, grad_first * normed_one)
    add_row(1, grad_first)
    grad_one = back(grad_first, normed_one, inverse_one, gain_one)
    dr_ref[...] = grad_one
    attn_low = grad_one.astype(bf16)
    add_row(4, attn_low.astype(f32))
    attn_flip = attn_low.T
    for k, (source, target) in enumerate(((oa_ref, da_ref), (ob_ref, db_ref))):
        both = dot(attn_flip, source[...], NN)
        gather(2 * k, 0, HEAD, both[:, 0:HEAD])
        gather(2 * k + 1, 0, HEAD, both[:, HEAD:])
        both = dot(attn_low, out_pair[k], NN).astype(bf16)
        target[:, 0 : 2 * HEAD] = both
        product = both.astype(f32) * source[...].astype(f32)
        lane = lax.broadcasted_iota(jnp.int32, (count, WIDE), 1)
        tile = jnp.zeros((count, WIDE), f32)
        for h in range(2):
            sums = jnp.sum(product[:, h * HEAD : (h + 1) * HEAD], axis=1, keepdims=True)
            for m, term in enumerate(three_terms(-sums)):
                tile = tile + jnp.where(lane == 4 * h + m, term, 0.0)
        target[:, 2 * HEAD :] = tile.astype(bf16)

    @pl.when(step == 1)
    def _():
        ga[...] = acc[0:2].astype(bf16)
        gb[...] = acc[2:4].astype(bf16)


def middle(sc, ratio, rows, o_own, o_other, cots, enc, vec, b1, rest_own, rest_other):
    size = rows.shape[0] // 4
    block = 2 * size
    width = enc.shape[0]
    spot = lambda i, sc: (sc[0] ^ i, 0)
    pair = pl.BlockSpec((block, 2 * HEAD), spot)
    smem = pl.BlockSpec(memory_space=pltpu.SMEM)
    fixed = pl.BlockSpec((size, width), lambda i, sc: (0, 0))
    weight = rest_own.shape
    return pl.pallas_call(
        middle_body,
        grid_spec=pltpu.PrefetchScalarGridSpec(
            num_scalar_prefetch=1,
            grid=(2,),
            in_specs=[smem, pl.BlockSpec((block, WIDE), spot), pair, pair]
            + [fixed] * 4
            + [whole()] * 5,
            out_specs=[fixed] * 4
            + [pl.BlockSpec((block, 3 * HEAD), spot)] * 2
            + [pl.BlockSpec((block, width), spot)]
            + [
                pl.BlockSpec(weight, lambda i, sc: (0, 0, 0)),
                pl.BlockSpec(weight, lambda i, sc: (0, 0, 0)),
                pl.BlockSpec((8, width), lambda i, sc: (0, 0)),
                pl.BlockSpec((4, HID), lambda i, sc: (0, 0)),
            ],
            scratch_shapes=[
                pltpu.VMEM((block, width), bf16),
                pltpu.VMEM((block, width), bf16),
                pltpu.VMEM((4,) + weight[1:], f32),
            ],
        ),
        out_shape=[pltpu.VMEM((size, width), bf16)] * 4
        + [
            pltpu.HBM((4 * size, 3 * HEAD), bf16),
            pltpu.HBM((4 * size, 3 * HEAD), bf16),
            pltpu.HBM((4 * size, width), f32),
            pltpu.VMEM(weight, bf16),
            pltpu.VMEM(weight, bf16),
            pltpu.HBM((8, width), f32),
            pltpu.HBM((4, HID), f32),
        ],
        compiler_params=pltpu.CompilerParams(vmem_limit_bytes=44 << 20),
        cost_estimate=cost(25),
        name="middle",
    )(
        sc,
        ratio,
        rows,
        o_own,
        o_other,
        *held(cots),
        enc,
        vec,
        b1,
        *held((rest_own, rest_other)),
    )


def held(args, near=True):
    if isinstance(near, bool):
        near = [near] * len(args)
    spaces = [pltpu.VMEM if flag else pltpu.HBM for flag in near]
    return tuple(map(pltpu.with_memory_space_constraint, args, spaces))


def simple(body, out_shape, *args, scalars=None, scratch=(), near=(True, True), name=None):
    specs = [whole()] * len(args)
    args = held(args, near[0])
    if scalars is not None:
        specs = [pl.BlockSpec(memory_space=pltpu.SMEM)] + specs
        args = (scalars,) + args
    many = isinstance(out_shape, (list, tuple))
    if near[1]:
        kept = lambda shape: pltpu.VMEM(shape.shape, shape.dtype)
        out_shape = [kept(shape) for shape in out_shape] if many else kept(out_shape)
    return pl.pallas_call(
        body,
        in_specs=specs,
        out_specs=[whole()] * len(out_shape) if many else whole(),
        out_shape=out_shape,
        scratch_shapes=scratch,
        compiler_params=pltpu.CompilerParams(vmem_limit_bytes=16 << 20),
        cost_estimate=cost(2),
        name=name,
    )(*args)


def place(parts, index, name, near=(True, True)):
    def body(sc, *refs):
        for k, ref in enumerate(refs[:-1]):
            refs[-1][sc[0] ^ k] = ref[...]

    first = parts[0]
    return simple(
        body,
        shape_of((len(parts),) + first.shape, first.dtype),
        *parts,
        scalars=index.reshape(1).astype(jnp.int32),
        near=near,
        name=name,
    )


TAIL = 3 * HEAD
FEAT_ROWS = 112
LAST = 112
VEC = 104


def spread(row):
    parts = row.reshape(row.shape[:-1] + (4, row.shape[-1] // 4))
    room = WIDE - LAST - parts.shape[-1]
    return jnp.pad(parts, [(0, 0)] * (parts.ndim - 1) + [(LAST, room)])


def widened(prompt):
    return jnp.pad(prompt, [(0, 0)] * (prompt.ndim - 1) + [(0, 3 * TAIL - prompt.shape[-1])])


def with_bias(prompt, bias):
    row = jnp.pad(
        bias[..., None, :].astype(prompt.dtype),
        [(0, 0)] * (bias.ndim - 1)
        + [(0, prompt.shape[-2] - 1), (PAD, 3 * TAIL - PAD - bias.shape[-1])],
    )
    return widened(prompt) + row


def in_chunks(wide):
    lead, strip = wide.shape[:-2], wide.shape[-2]
    parts = jnp.swapaxes(wide.reshape(lead + (strip, 3, TAIL)), -3, -2)
    return parts.reshape(lead + (3 * strip, TAIL))


def pack_parts(block, prompt, encoder, vectors, biases):
    slab, strip = block.shape[0], prompt.shape[0]
    flat = block.reshape(slab * 8, HEAD)
    out = [shape_of((slab + 3 * strip, TAIL), bf16), shape_of((slab, 8 * HEAD - TAIL), bf16)]
    if 2 * slab != WIDE:
        low = block.reshape(slab, 8 * HEAD).astype(bf16)
        small = jnp.concatenate(
            [
                jnp.pad(encoder, ((0, 0), (0, VEC - FEAT))),
                jnp.pad(vectors, ((0, 0), (0, LAST - VEC - 7))),
                jnp.pad(biases.reshape(strip, 4), ((0, 0), (0, WIDE - LAST - 4))),
            ],
            axis=1,
        )
        chunks = in_chunks(
            jnp.concatenate([jnp.pad(prompt, ((0, 0), (0, PAD - PROMPT))), small], axis=1)
        )
        return jnp.concatenate([low[:, 0:TAIL], chunks.astype(bf16)], axis=0), low[:, TAIL:]

    def body(block_ref, prompt_ref, enc_ref, vec_ref, bias_ref, main_ref, rest_ref, tall, tile, line):
        for j in range(8):
            lanes = block_ref[pl.ds(j, slab, stride=8), :].astype(bf16)
            if j < 3:
                main_ref[0:slab, j * HEAD : (j + 1) * HEAD] = lanes
            else:
                rest_ref[:, (j - 3) * HEAD : (j - 2) * HEAD] = lanes
        low = prompt_ref[...].astype(bf16)
        for k in range(2):
            rows = slice(slab + k * strip, slab + (k + 1) * strip)
            main_ref[rows, :] = low[:, k * TAIL : (k + 1) * TAIL]
        rows = slice(slab + 2 * strip, slab + 3 * strip)
        main_ref[rows, WIDE : 2 * WIDE] = jnp.zeros((strip, WIDE), bf16)
        main_ref[rows, 0 : PROMPT - 2 * TAIL] = low[:, 2 * TAIL :]
        tall[...] = jnp.zeros_like(tall)
        tall[VEC : VEC + 7, :] = vec_ref[...]
        tile[...] = tall[...].T
        tile[:, 0:FEAT] = enc_ref[...]
        line[...] = jnp.zeros_like(line)
        line[:, 0:slab] = bias_ref[...]
        main_ref[rows, 2 * WIDE :] = (tile[...] + spread_row(line[...], strip)).astype(bf16)

    return simple(
        body,
        out,
        flat,
        prompt,
        encoder,
        vectors.T,
        biases.T,
        near=(False, True),
        scratch=[
            pltpu.VMEM((WIDE, strip), f32),
            pltpu.VMEM((strip, WIDE), f32),
            pltpu.VMEM((1, WIDE), f32),
        ],
        name="pack_parts",
    )


def spread_row(row, strip):
    place = lax.broadcasted_iota(jnp.int32, (strip, WIDE), 0)
    lane = lax.broadcasted_iota(jnp.int32, (strip, WIDE), 1)
    total = jnp.zeros((strip, WIDE), f32)
    for k in range(4):
        turned = jnp.broadcast_to(pltpu.roll(row, LAST - k * strip, 1), (strip, WIDE))
        total = total + jnp.where((place == k) & (lane >= LAST), turned, 0.0)
    return total


def gathered_row(tile, strip):
    lane = lax.broadcasted_iota(jnp.int32, (1, WIDE), 1)
    total = jnp.zeros((1, WIDE), f32)
    for k in range(4):
        turned = pltpu.roll(tile[k : k + 1], (k * strip - LAST) % WIDE, 1)
        total = total + jnp.where(lane // strip == k, turned, 0.0)
    return total


FEAT_SPAN = 80
FEAT_CUTS = ((0, 0, 0, 0, 80), (1, 0, 0, 80, 112), (1, 32, 1, 0, 48), (2, 0, 1, 48, 112))


def build_main(parts, flipped, places):
    count = len(parts)
    size, lanes = parts[0].shape
    feats, rows = flipped.shape[1:]

    def body(sc, *refs):
        ins, flip_ref, outs = refs[:count], refs[count], refs[count + 1 :]
        for k, out in enumerate(outs):
            for e, ref in enumerate(ins):
                at = pl.multiple_of((sc[6] ^ e) * size, 16)
                out[pl.ds(at, size), :] = ref[...]
            wide = jnp.concatenate(
                [flip_ref[sc[3] ^ k], jnp.zeros((FEAT_ROWS - feats, rows), bf16)], axis=0
            )
            for column, row, tile, begin, end in FEAT_CUTS:
                at = slice(count * size + row, count * size + row + end - begin)
                part = wide[begin:end, tile * WIDE : (tile + 1) * WIDE]
                out[at, column * WIDE : (column + 1) * WIDE] = part

    shape = shape_of((count * size + FEAT_SPAN, lanes), bf16)
    return simple(body, [shape] * 4, *parts, flipped, scalars=places, name="build_main")


def join_features(parts, places):
    feats, rows = parts[0].shape

    def body(sc, *refs):
        for k, ref in enumerate(refs[:-1]):
            spot = 2 * (sc[0] ^ (k // 2)) + (sc[1] ^ (k % 2))
            refs[-1][spot, 0:feats] = ref[...]

    return simple(
        body, shape_of((4, FEAT_ROWS, rows), bf16), *parts, scalars=places, name="join_features"
    )


def unpack_main(tops, lows, feats, feats_low, mask, places, n_ep, slab, strip, rows):
    plain = 2 * slab != WIDE
    size = slab + 3 * strip
    shapes = [
        shape_of((2, n_ep, 2, slab, TAIL), bf16),
        shape_of((n_ep, 2, 2, 2, strip, 3 * TAIL), bf16),
        shape_of((n_ep, 2, 2, 2, strip, WIDE), bf16),
        shape_of((8, n_ep * 2 * slab), f32),
        shape_of((4, n_ep * 2 * slab), f32),
        shape_of((4 * rows, WIDE), bf16),
        shape_of((4 * rows, WIDE), bf16),
    ]

    def features(mask_ref, source, target):
        for p in range(4):
            flip = jnp.concatenate([source[p], jnp.zeros((WIDE - FEAT_ROWS, rows), bf16)], axis=0)
            piece = jnp.where(mask_ref[...] > 0.0, flip.T.astype(f32), 0.0).astype(bf16)
            target[p * rows : (p + 1) * rows, :] = piece

    if plain:
        side, row, core = places[0], places[1], places[2]

        def ordered(parts, axis):
            cores = []
            for group in parts:
                sides = []
                for b in (0, 1):
                    sides.append(jnp.stack(pick(group[2 * b], group[2 * b + 1], row), axis=axis))
                cores.append(jnp.stack(pick(sides[0], sides[1], side), axis=axis))
            return jnp.stack(pick(cores[0], cores[1], core), axis=axis + 2)

        heads = [
            jnp.stack(pick(tops[r][:, 0:slab], tops[2 + r][:, 0:slab], side), axis=1) for r in (0, 1)
        ]
        chunks = ordered([[t[:, slab:] for t in tops], [t[:, slab:] for t in lows]], 1)
        chunks = chunks.reshape((n_ep, 2, 2, 2, 3, strip, TAIL))
        wide = jnp.swapaxes(chunks, -3, -2).reshape((n_ep, 2, 2, 2, strip, 3 * TAIL))
        small = wide[..., PAD:]
        vec = small.reshape(n_ep * 8 * strip, WIDE).astype(f32).T[VEC : VEC + 8]
        biases = []
        for group in (tops, lows):
            for r in (0, 1):
                pair = [
                    group[2 * b + r][:, slab + 2 * strip :, PAD - 2 * TAIL + LAST :][..., 0:4]
                    for b in (0, 1)
                ]
                biases.append(jnp.stack(pick(pair[0], pair[1], side), axis=1).reshape(-1))
        def both(mask_ref, a, b, c, d):
            features(mask_ref, a, c)
            features(mask_ref, b, d)

        masked = simple(
            both,
            shapes[5:],
            mask,
            feats,
            feats_low,
            near=(False, False),
            name="features",
        )
        return [jnp.stack(heads), wide, small, vec, jnp.stack(biases).astype(f32), *masked]

    def body(sc, t0, t1, t2, t3, l0, l1, l2, l3, mask_ref, *outs):
        wp_ref, prompt_ref, small_ref, vec_ref, bias_ref, own_ref, other_ref = outs
        side, row, core = sc[0], sc[1], sc[2]
        groups = ((t0, t1, t2, t3), (l0, l1, l2, l3))
        bias_tiles = {}
        for b in range(2):
            for r in range(2):
                k = 2 * b + r
                for other in range(2):
                    spot = core ^ other
                    source = groups[other][k]
                    full = source[0 : n_ep * size].reshape(n_ep, size, TAIL)
                    if other == 0:
                        wp_ref[r, :, side ^ b] = full[:, 0:slab, :]
                    part = full[:, slab:, :]
                    tiles = ([], [])
                    for column, line, tile, begin, end in FEAT_CUTS:
                        at = slice(n_ep * size + line, n_ep * size + line + end - begin)
                        tiles[tile].append(source[at, column * WIDE : (column + 1) * WIDE])
                    blank = jnp.zeros((WIDE - FEAT_ROWS, rows), bf16)
                    flip = jnp.concatenate([jnp.concatenate(t, axis=0) for t in tiles], axis=1)
                    flip = jnp.concatenate([flip, blank], axis=0)
                    piece = jnp.where(mask_ref[...] > 0.0, flip.T.astype(f32), 0.0).astype(bf16)
                    at = pl.multiple_of((2 * (side ^ b) + (row ^ r)) * rows, rows)
                    (other_ref if other else own_ref)[pl.ds(at, rows), :] = piece
                    for j in range(3):
                        lanes = slice(j * TAIL, (j + 1) * TAIL)
                        span = slice(j * strip, (j + 1) * strip)
                        prompt_ref[:, side ^ b, row ^ r, spot, :, lanes] = part[:, span, :]
                    tile = part[:, 2 * strip :, TAIL - WIDE :]
                    small_ref[:, side ^ b, row ^ r, spot] = tile
                    bias_tiles[b, r, other] = tile.astype(f32)
        flip = small_ref[...].reshape(n_ep * 8 * strip, WIDE).astype(f32).T
        vec_ref[...] = flip[VEC : VEC + 8]
        low_half = lax.broadcasted_iota(jnp.int32, (1, WIDE), 1) < slab
        for r in range(2):
            for other in range(2):
                for e in range(n_ep):
                    mine = gathered_row(bias_tiles[0, r, other][e], strip)
                    theirs = gathered_row(bias_tiles[1, r, other][e], strip)
                    first = jnp.where(side == 0, mine, theirs)
                    second = jnp.where(side == 0, theirs, mine)
                    row_tile = jnp.where(low_half, first, pltpu.roll(second, slab, 1))
                    k = r + 2 * other
                    bias_ref[k : k + 1, e * WIDE : (e + 1) * WIDE] = row_tile

    return simple(body, shapes, *tops, *lows, mask, scalars=places, name="unpack_main")


def unpack_rest(tops, lows, places):
    n_ep, slab, width = tops[0].shape

    def body(sc, *refs):
        for k in range(8):
            refs[8 + k // 4][k % 2, :, sc[0] ^ (k % 4 // 2)] = refs[k][...]

    return simple(
        body,
        [shape_of((2, n_ep, 2, slab, width), bf16)] * 2,
        *tops,
        *lows,
        scalars=places,
        name="unpack_rest",
    )


def weight_body(n_ep, strip, sc, x_ref, dq_ref, dk_ref, dv_ref, prompt, wp, gb1, gw_ref, mine_ref, sent_ref, own_ref, other_ref, acc, gq_ref, gv_ref, gp_ref, gb_ref):
    step = pl.program_id(0)

    @pl.when(step == 0)
    def _():
        acc[...] = jnp.zeros_like(acc)
        gq_ref[...] = jnp.zeros_like(gq_ref)
        gv_ref[...] = jnp.zeros_like(gv_ref)

    def columns(k):
        return jnp.concatenate([wp[h, :, k * HEAD : (k + 1) * HEAD] for h in range(2)], axis=1)

    flip = x_ref[...].T
    grad_query = dq_ref[...]
    acc[0] += dot(flip, grad_query, NN)
    gq_ref[...] += jnp.sum(grad_query.astype(f32), axis=0, keepdims=True)
    grad_key = jnp.concatenate([dk_ref[h] for h in range(2)], axis=0)
    grad_value = jnp.concatenate([dv_ref[h] for h in range(2)], axis=0)
    key_high = grad_key.astype(bf16)
    value_high = grad_value.astype(bf16)
    ones = jnp.ones((8, grad_key.shape[1]), bf16)
    gv_ref[...] += dot(ones, value_high, NT)[0:1]
    back = dot(grad_query, columns(0), NT)

    def store(value):
        @pl.when(step < 2)
        def _():
            own_ref[...] = value

        @pl.when(step >= 2)
        def _():
            other_ref[...] = value.astype(bf16)

    @pl.when(step % 2 == 0)
    def _():
        acc[1] += dot(flip, key_high, NT)
        acc[2] += dot(flip, value_high, NT)
        store(back + dot(key_high.T, columns(1), NT) + dot(value_high.T, columns(2), NT))

    @pl.when(step % 2 == 1)
    def _():
        store(back)
        key_low = (grad_key - key_high.astype(f32)).astype(bf16)
        value_low = (grad_value - value_high.astype(f32)).astype(bf16)
        source = prompt[...]
        acc[1] += dot(source, key_high, NT) + dot(source, key_low, NT)
        acc[2] += dot(source, value_high, NT) + dot(source, value_low, NT)
        gv_ref[...] += dot(ones, value_low, NT)[0:1]
        total = dot(columns(1), key_high, NN) + dot(columns(1), key_low, NN)
        total = total + dot(columns(2), value_high, NN) + dot(columns(2), value_low, NN)
        gp_ref[step // 2] = total.astype(bf16)

    @pl.when(step == 3)
    def _():
        for h in range(2):
            for k in range(3):
                lanes = slice(h * HEAD, (h + 1) * HEAD)
                gw_ref[h, :, k * HEAD : (k + 1) * HEAD] = acc[k, :, lanes].astype(bf16)
            gb_ref[h : h + 1, 0:HEAD] = gq_ref[:, h * HEAD : (h + 1) * HEAD]
            gb_ref[h : h + 1, HEAD : 2 * HEAD] = gv_ref[:, h * HEAD : (h + 1) * HEAD]
        gb_ref[2:4, 0 : 2 * HEAD] = jnp.zeros((2, 2 * HEAD), f32)
        gb_ref[:, 2 * HEAD :] = gb1[...]
        if strip % 16:
            mine_ref[...] = gp_ref[...]
            sent_ref[...] = gb_ref[...]
            return
        half = gp_ref.shape[2]
        row, core = sc[1], sc[2]
        first = lax.broadcasted_iota(jnp.int32, (strip, WIDE), 0) == 0
        low_half = lax.broadcasted_iota(jnp.int32, (1, WIDE), 1) < 4 * strip
        for other, ref in enumerate((mine_ref, sent_ref)):
            for e in range(n_ep):
                for s in range(2):
                    for r in range(2):
                        y = row ^ r
                        at = ((e * 2 + s) * 2 + y) * 2 + (core ^ other)
                        at = pl.ds(pl.multiple_of(at * strip, strip), strip)
                        for tile in range(PAD // WIDE):
                            lanes = slice(tile * WIDE % half, tile * WIDE % half + WIDE)
                            j, place = tile // 3, tile % 3
                            rows = slice(j * strip, (j + 1) * strip)
                            to = slice(place * WIDE, (place + 1) * WIDE)
                            ref[e, s, y, rows, to] = gp_ref[tile * WIDE // half, at, lanes]
                        k = r + 2 * other
                        tile = gb_ref[k : k + 1, e * WIDE : (e + 1) * WIDE]
                        if s == 1:
                            tile = pltpu.roll(tile, WIDE - 4 * strip, 1)
                        tile = jnp.where(low_half, tile, 0.0)
                        tile = jnp.where(first, tile, 0.0).astype(bf16)
                        ref[e, s, y, 2 * strip : 3 * strip, 2 * WIDE :] = tile


def weight_grads(places, x, dq, dk, dv, prompt, wp, gb1, n_ep, strip):
    half = x.shape[0] // 4
    width = wp.shape[1]
    spot = lambda i: jnp.where(i % 2 == 0, 2 + i // 2, i // 2)
    key = pl.BlockSpec((2, HEAD, half), lambda i: (0, 0, spot(i)))
    if strip % 16:
        shapes = [pltpu.VMEM((2, width, half), bf16), pltpu.VMEM((4, width), f32)]
    else:
        strips = (n_ep, 2, 2, 3 * strip, TAIL)
        shapes = [pltpu.HBM(strips, bf16), pltpu.VMEM(strips, bf16)]
    fixed = [
        pl.BlockSpec(shape.shape, functools.partial(lambda n, i: (0,) * n, len(shape.shape)))
        for shape in shapes
    ]
    out = pl.pallas_call(
        functools.partial(weight_body, n_ep, strip),
        grid=(4,),
        in_specs=[
            pl.BlockSpec(memory_space=pltpu.SMEM),
            pl.BlockSpec((half, width), lambda i: (i, 0)),
            pl.BlockSpec((half, 2 * HEAD), lambda i: (i, 0)),
            key,
            key,
            pl.BlockSpec((width, half), lambda i: (0, i // 2)),
            whole(),
            whole(),
        ],
        out_specs=[pl.BlockSpec((2, width, TAIL), lambda i: (0, 0, 0))]
        + fixed
        + [
            pl.BlockSpec((half, width), lambda i: (jnp.minimum(i, 1), 0)),
            pl.BlockSpec((half, width), lambda i: (jnp.maximum(i - 2, 0), 0)),
        ],
        out_shape=[pltpu.HBM((2, width, TAIL), bf16)]
        + shapes
        + [pltpu.HBM((2 * half, width), f32), pltpu.HBM((2 * half, width), bf16)],
        scratch_shapes=[pltpu.VMEM((3, width, 2 * HEAD), f32)]
        + [pltpu.VMEM((1, 2 * HEAD), f32)] * 2
        + [pltpu.VMEM((2, width, half), bf16), pltpu.VMEM((4, width), f32)],
        compiler_params=pltpu.CompilerParams(vmem_limit_bytes=40 << 20),
        cost_estimate=cost(9),
        name="weight_grads",
    )(places, *held((x, dq, dk, dv, prompt, wp), False), gb1)
    grad_project, mine, sent, back_own, back_other = out
    if strip % 16:
        row, core = places[1], places[2]
        grad = jnp.concatenate([mine[0], mine[1]], axis=1)
        blocks = grad.reshape(n_ep, 2, 2, 2, strip, PAD)
        table = sent.reshape(2, 2, n_ep, 2, 4 * strip)
        both = []
        for other in (0, 1):
            by_row = jnp.stack(pick(table[other, 0], table[other, 1], row), axis=2)
            part = lax.dynamic_index_in_dim(blocks, core ^ other, 3, keepdims=False)
            both.append(in_chunks(with_bias(part, by_row)))
        mine, sent = both
    return grad_project, mine, sent, back_own, back_other


def input_body(sc, ratio, dr_ref, own_ref, got_ref, rows_ref, enc, mask, rows_grad, i0, i1, i2, i3, small_ref, acc, bias):
    step = pl.program_id(0)
    low = (dr_ref[...] + own_ref[...] + got_ref[...].astype(f32)).astype(bf16)
    part = dot(low.T, rows_ref[...], NN) * ratio[0]
    part_bias = jnp.sum(low.astype(f32), axis=0, keepdims=True)

    @pl.when(step == 0)
    def _():
        acc[...] = part
        bias[...] = part_bias

    @pl.when(step > 0)
    def _():
        acc[...] += part
        bias[...] += part_bias

    grad = dot(enc[...].T, low, NT)[0:FEAT_ROWS] * ratio[0] * mask[0:FEAT_ROWS]
    for k, ref in enumerate((i0, i1, i2, i3)):

        @pl.when(step == k // 2)
        def _(k=k, ref=ref):
            first = sc[1] ^ (k % 2) == 0
            part = ref.shape[1]
            ref[...] = jnp.where(first, grad[:, 0:part], grad[:, part:]).astype(bf16)

    @pl.when(step == 1)
    def _():
        width = acc.shape[0]
        rows = jnp.concatenate(
            [
                jnp.zeros((VEC, width), f32),
                rows_grad[0:6],
                bias[...],
                jnp.zeros((WIDE - VEC - 7, width), f32),
            ],
            axis=0,
        )
        small_ref[...] = (acc[...] + rows.T).astype(bf16)


def input_grads(sc, ratio, dr, own, got, rows, enc, mask, rows_grad):
    size = rows.shape[0] // 4
    width = enc.shape[0]
    spot = lambda i, sc: (sc[0] ^ i, 0)
    block = pl.BlockSpec((2 * size, width), spot)
    fixed = pl.BlockSpec((FEAT_ROWS, size), lambda i, sc: (0, 0))
    return pl.pallas_call(
        input_body,
        grid_spec=pltpu.PrefetchScalarGridSpec(
            num_scalar_prefetch=1,
            grid=(2,),
            in_specs=[
                pl.BlockSpec(memory_space=pltpu.SMEM),
                block,
                block,
                block,
                pl.BlockSpec((2 * size, WIDE), spot),
                whole(),
                whole(),
                whole(),
            ],
            out_specs=[fixed] * 4 + [pl.BlockSpec((width, WIDE), lambda i, sc: (0, 0))],
            scratch_shapes=[pltpu.VMEM((width, WIDE), f32), pltpu.VMEM((1, width), f32)],
        ),
        out_shape=[pltpu.VMEM((FEAT_ROWS, size), bf16)] * 4 + [pltpu.VMEM((width, WIDE), bf16)],
        compiler_params=pltpu.CompilerParams(vmem_limit_bytes=32 << 20),
        cost_estimate=cost(6),
        name="input_grads",
    )(sc, ratio, *held((dr, own, got, rows), False), enc, mask, rows_grad)


def split_small(grad, places, n_ep, strip):
    blocks = grad.reshape(n_ep * 4, 2, strip, WIDE)

    def body(sc, grad_ref, mine_ref, sent_ref):
        mine_ref[...] = grad_ref[:, sc[2]]
        sent_ref[...] = grad_ref[:, 1 - sc[2]]

    shape = shape_of((n_ep * 4, strip, WIDE), bf16)
    return simple(body, [shape, shape], blocks, scalars=places, name="split_small")


def pack_main(gw, mine, got, places, slab, strip):
    n_ep = mine.shape[0]
    heads = gw.reshape(2, n_ep, 2, slab, TAIL)
    if 2 * slab != WIDE:
        pair = (mine.astype(f32) + got.astype(f32)).astype(bf16)
        outs = []
        for b in (0, 1):
            for r in (0, 1):
                side, row = places[0] ^ b, places[1] ^ r
                part = lax.dynamic_index_in_dim(pair, side, 1, keepdims=False)
                part = lax.dynamic_index_in_dim(part, row, 1, keepdims=False)
                head = lax.dynamic_index_in_dim(heads[r], side, 1, keepdims=False)
                outs.append(jnp.concatenate([head, part], axis=1))
        return outs

    def body(sc, gw_ref, a_ref, b_ref, *outs):
        for b in range(2):
            for r in range(2):
                out = outs[2 * b + r]
                side, row = sc[0] ^ b, sc[1] ^ r
                out[:, 0:slab, :] = gw_ref[r, :, side]
                pair = a_ref[:, side, row].astype(f32) + b_ref[:, side, row].astype(f32)
                out[:, slab : slab + 3 * strip, :] = pair.astype(bf16)

    shape = shape_of((n_ep, slab + 3 * strip, TAIL), bf16)
    return simple(
        body,
        [shape] * 4,
        heads,
        mine,
        got,
        scalars=places,
        near=((False, False, True), True),
        name="pack_main",
    )


def pack_small(ins, mine, got, places, n_ep, strip):
    rows = ins[0].shape[1]
    mine = mine.reshape(n_ep, 2, 2, strip, WIDE)
    got = got.reshape(n_ep, 2, 2, strip, WIDE)
    total = FEAT_ROWS + n_ep * strip
    if 8 * strip != WIDE:
        pair = (mine.astype(f32) + got.astype(f32)).astype(bf16)
        outs = []
        for k in range(4):
            part = lax.dynamic_index_in_dim(pair, places[0] ^ (k // 2), 1, keepdims=False)
            part = lax.dynamic_index_in_dim(part, places[1] ^ (k % 2), 1, keepdims=False)
            part = jnp.pad(part.reshape(n_ep * strip, WIDE), ((0, 0), (0, rows - WIDE)))
            outs.append(jnp.concatenate([ins[k], part], axis=0))
        return outs

    def body(sc, *refs):
        in_refs, a_ref, b_ref, outs = refs[0:4], refs[4], refs[5], refs[6:]
        for k in range(4):
            side, row = sc[0] ^ (k // 2), sc[1] ^ (k % 2)
            outs[k][0:FEAT_ROWS] = in_refs[k][...]
            pair = a_ref[:, side, row].astype(f32) + b_ref[:, side, row].astype(f32)
            outs[k][FEAT_ROWS:, 0:WIDE] = pair.reshape(n_ep * strip, WIDE).astype(bf16)

    return simple(
        body, [shape_of((total, rows), bf16)] * 4, *ins, mine, got, scalars=places, name="pack_small"
    )


def subtiles(rows, lanes, width):
    out = []
    across = width // WIDE
    for n in range(rows // 16 * (lanes // WIDE)):
        g, t = divmod(n, lanes // WIDE)
        row, col = divmod(n, across)
        here = (slice(16 * g, 16 * (g + 1)), slice(WIDE * t, WIDE * (t + 1)))
        out.append((here, (16 * row, slice(WIDE * col, WIDE * (col + 1)))))
    return out


def place_tiles(parts, index, begin, rows, lanes, name):
    width = parts[0].shape[1]

    def body(sc, *refs):
        for k, ref in enumerate(refs[:-1]):
            for here, there in subtiles(rows, lanes, width):
                tile = ref[begin + there[0] : begin + there[0] + 16, there[1]]
                refs[-1][sc[0] ^ k, here[0], here[1]] = tile

    return simple(
        body,
        shape_of((len(parts), rows, lanes), bf16),
        *parts,
        scalars=index.reshape(1).astype(jnp.int32),
        near=(True, False),
        name=name,
    )


def pack_rest(mine, got, outs, places, n_ep, slab):
    width = mine.shape[-1]
    rows, lanes = outs[0].shape
    count = n_ep * slab
    mine = mine.reshape(2, n_ep, 2, slab, width)
    got = got.reshape(2, n_ep, 2, slab, width)

    def body(sc, a_ref, b_ref, *refs):
        for k in range(4):
            side = sc[0] ^ (k // 2)
            pair = a_ref[k % 2, :, side].astype(f32) + b_ref[k % 2, :, side].astype(f32)
            refs[4 + k][0:count] = pair.reshape(count, width).astype(bf16)
            for here, there in subtiles(rows, lanes, width):
                refs[4 + k][count + there[0] : count + there[0] + 16, there[1]] = refs[k][here]

    extra = subtiles(rows, lanes, width)[-1][1][0] + 16
    shape = shape_of((count + extra, width), bf16)
    return simple(body, [shape] * 4, mine, got, *outs, scalars=places, name="pack_rest")


def sum_rest(parts, later, places, n_ep, slab):
    width = parts[0].shape[1]
    if n_ep != 4:
        total = sum(part[0 : n_ep * slab].astype(f32) for part in parts)
        total = total.reshape(n_ep, slab, width)
        return [lax.psum_scatter(total, "ep", scatter_dimension=0, tiled=True)[0]]

    def body(sc, *refs):
        ins, outs = refs[: len(parts)], refs[len(parts) :]
        for k in range(4):
            spot = pl.multiple_of((sc[6] ^ k) * slab, slab)
            total = ins[0][pl.ds(spot, slab), :].astype(f32)
            for ref in ins[1:]:
                total = total + ref[pl.ds(spot, slab), :].astype(f32)
            outs[k // 2][k % 2] = total.astype(bf16)

    near, far = simple(
        body, [shape_of((2, slab, width), bf16)] * 2, *parts, scalars=places, name="sum_rest"
    )
    got = swap(far, ep=2)

    def added(a_ref, b_ref, own_ref, sent_ref):
        own_ref[...] = (a_ref[0].astype(f32) + b_ref[0].astype(f32)).astype(bf16)
        sent_ref[...] = (a_ref[1].astype(f32) + b_ref[1].astype(f32)).astype(bf16)

    got = tie(got, later)
    own, sent = simple(added, [shape_of((slab, width), bf16)] * 2, near, got, name="add_rest")
    return [own, swap(sent, ep=1)]


def sum_main(mains, smalls, places, slab, strip):
    n_ep = mains[0].shape[0]
    if n_ep > 4:
        total = sum(part.astype(f32) for part in mains)
        small = sum(part[FEAT_ROWS:, 0:WIDE].astype(f32) for part in smalls)
        small = jnp.pad(small.reshape(n_ep, strip, WIDE), ((0, 0), (0, 0), (0, TAIL - WIDE)))
        return reduce_ep(jnp.concatenate([total, small], axis=1), None)

    def body(sc, *refs):
        main_refs, small_refs, outs = refs[0:4], refs[4:8], refs[8:]
        for k, out in enumerate(outs):
            spot = sc[6] ^ k
            total = main_refs[0][spot].astype(f32)
            for ref in main_refs[1:]:
                total = total + ref[spot].astype(f32)
            out[0 : slab + 3 * strip] = total.astype(bf16)
            where = pl.multiple_of(FEAT_ROWS + spot * strip, strip)
            total = small_refs[0][pl.ds(where, strip), 0:WIDE].astype(f32)
            for ref in small_refs[1:]:
                total = total + ref[pl.ds(where, strip), 0:WIDE].astype(f32)
            out[slab + 3 * strip :, 0:WIDE] = total.astype(bf16)
            out[slab + 3 * strip :, WIDE:] = jnp.zeros((strip, TAIL - WIDE), bf16)

    shape = shape_of((slab + 4 * strip, TAIL), bf16)
    pieces = simple(body, [shape] * n_ep, *mains, *smalls, scalars=places, name="sum_main")
    return reduce_ep(None, pieces)


def place_rows(parts, index, begin, shape, dtype, name):
    def body(sc, *refs):
        for k, ref in enumerate(refs[:-1]):
            refs[-1][sc[0] ^ k] = ref[begin : begin + shape[0], 0 : shape[1]].astype(dtype)

    return simple(
        body,
        shape_of((len(parts),) + shape, dtype),
        *parts,
        scalars=index.reshape(1).astype(jnp.int32),
        near=(True, False),
        name=name,
    )


def final_sums(mains, rests, slab, strip):
    def body(*refs):
        main_refs, rest_refs = refs[: len(mains)], refs[len(mains) : len(mains) + len(rests)]
        block_ref, prompt_ref, small_ref, bias_ref, square_ref = refs[len(mains) + len(rests) :]

        def added(group):
            total = group[0][...].astype(f32)
            for ref in group[1:]:
                total = total + ref[...].astype(f32)
            return total

        main, rest = added(main_refs), added(rest_refs)
        square = jnp.sum(jnp.sum(main * main, axis=0, keepdims=True), axis=1, keepdims=True)
        square = square + jnp.sum(
            jnp.sum(rest * rest, axis=0, keepdims=True), axis=1, keepdims=True
        )
        for j in range(8):
            if j < 3:
                tile = main[0:slab, j * HEAD : (j + 1) * HEAD]
            else:
                tile = rest[:, (j - 3) * HEAD : (j - 2) * HEAD]
            block_ref[pl.ds(j, slab, stride=8), :] = tile
        for j in range(3):
            part = main[slab + j * strip : slab + (j + 1) * strip]
            high = min(PROMPT, (j + 1) * TAIL)
            prompt_ref[:, j * TAIL : high] = part[:, 0 : high - j * TAIL]
        small_ref[...] = main[slab + 3 * strip :, 0:WIDE]
        bias_ref[...] = main[slab + 2 * strip : slab + 2 * strip + 1, TAIL - WIDE :]
        square_ref[...] = jnp.broadcast_to(square, (8, 128))

    return simple(
        body,
        [
            shape_of((slab * 8, HEAD), f32),
            shape_of((strip, PROMPT), f32),
            shape_of((strip, WIDE), f32),
            shape_of((1, WIDE), f32),
            shape_of((8, 128), f32),
        ],
        *mains,
        *rests,
        name="final_sums",
    )


def adam_all(squares, params, moments, grads):
    slab = params[0].shape[0] // 8
    rates = (rate_matrix, rate_vector, rate_matrix, rate_vector, rate_vector)
    decays = (weight_decay, weight_decay, weight_decay, 0.0, 0.0)
    count = squares.shape[0]

    def body(sq_ref, *refs):
        weights, moment_refs, grad_refs, outs = refs[0:5], refs[5:10], refs[10:14], refs[14:]
        total = sq_ref[0, 0:1, 0:1]
        for k in range(1, count):
            total = total + sq_ref[k, 0:1, 0:1]
        norm = jnp.sqrt(total)
        outs[0][...] = norm
        factor = jnp.minimum(1.0, clip_norm / (norm + 1e-06))
        small = grad_refs[2][...]
        picked = (
            grad_refs[0][...],
            grad_refs[1][...],
            small[:, 0:FEAT],
            small.T[VEC : VEC + 7],
            grad_refs[3][:, 0:slab],
        )
        for k in range(5):
            both = moment_refs[k]
            pair = (both[:, 0], both[:, 1]) if k == 3 else (both[0], both[1])
            news = adam_update(weights[k][...], pair, picked[k], factor, rates[k], decays[k])
            for m in range(3):
                outs[1 + 4 * k + m][...] = news[m]
            if k > 0:
                outs[4 + 4 * k][...] = news[3]
        for j in range(8):
            tile = outs[1][pl.ds(j, slab, stride=8), :]
            outs[4][:, j * HEAD : (j + 1) * HEAD] = tile.astype(bf16)

    shapes = [shape_of((1, 1), f32)]
    for k, param in enumerate(params):
        low = (slab, 8 * HEAD) if k == 0 else param.shape
        shapes += [shape_of(param.shape, f32)] * 3 + [shape_of(low, bf16)]
    return simple(body, shapes, squares, *params, *moments, *grads, near=(True, False), name="adam_all")


def shards(
    feats,
    counts,
    feat_mask,
    cotangent,
    block_weights,
    block_moments,
    head_biases,
    bias_moments,
    encoder,
    encoder_moments,
    shared_vectors,
    vector_moments,
    prompt,
    prompt_moments,
):
    n_ep = lax.axis_size("ep")
    side = lax.axis_index("split")
    row = lax.axis_index("tp") // 2
    core = lax.axis_index("tp") % 2
    chip = side * 2 + row
    rows = feats.shape[2]
    width = cotangent.shape[3]
    slab = block_weights.shape[0]
    strip = encoder.shape[0]

    mask_row = lax.dynamic_index_in_dim(feat_mask, chip, 0, keepdims=False)
    count_pair = lax.dynamic_index_in_dim(counts, chip, 0, keepdims=False)
    mask_float = mask_row.astype(f32)
    ratio = (FEAT / jnp.sum(mask_float)).reshape(1)
    spot = jnp.arange(8, dtype=jnp.int32)
    places = jnp.pad(count_pair, (4, 2)).astype(jnp.int32)
    for k, value in ((0, side), (1, row), (2, core), (3, chip), (6, lax.axis_index("ep"))):
        places = places + jnp.where(spot == k, value, 0)

    def to_chip(array):
        return plane_list(
            [lax.dynamic_index_in_dim(array[0], chip ^ k, 0, keepdims=False) for k in range(4)]
        )

    def plane_list(parts):
        got = plane_swap(lambda b, r: parts[2 * b + r])
        return [got[b, r] for b in (0, 1) for r in (0, 1)]

    main_part, rest_part = pack_parts(
        block_weights, prompt, encoder, shared_vectors, head_biases
    )
    mask_wide = jnp.pad(mask_float, (0, WIDE - FEAT)).reshape(1, WIDE)
    flipped = jnp.transpose(tie(feats, main_part)[0], (0, 2, 1))
    main_pieces = gather_ep(main_part)
    feats_own, feats_other = None, None
    if 2 * slab == WIDE:
        tops = plane_list(build_main(main_pieces, flipped, places))
    else:
        feats_own = join_features(
            plane_list(
                [lax.dynamic_index_in_dim(flipped, chip ^ k, 0, keepdims=False) for k in range(4)]
            ),
            places,
        )
        feats_other = swap(feats_own, core=1)
        tops = plane_list([stack_ep(main_pieces, "stack_main")] * 4)
    lows = [swap(top, core=1) for top in tops]
    w_project, prompt_low, small_low, vector_rows, bias_rows, masked_own, masked_other = unpack_main(
        tops, lows, feats_own, feats_other, mask_wide, places, n_ep, slab, strip, rows
    )
    w_project = w_project.reshape(2, width, TAIL)
    prompt_low = prompt_low.reshape(width, 3 * TAIL)
    encoder_low = small_low.reshape(width, WIDE)

    rest_along = stack_ep(gather_ep(tie(rest_part, lows[0])), "stack_rest")
    lows, rest_along = lax.optimization_barrier((lows, rest_along))

    cots = to_chip(tie(cotangent, w_project))
    rows_low, query, keys, keys_flip, values, values_flip, key_extra = project(
        ratio,
        places,
        masked_own,
        masked_other,
        encoder_low,
        vector_rows,
        w_project,
        bias_rows,
        prompt_low,
    )
    query, rest_along, cots = lax.optimization_barrier((query, rest_along, cots))
    rest_tops = plane_list([rest_along] * 4)
    attended_other, extra_other = attend(query, keys, key_extra, values_flip, 1)
    attended_got = swap(attended_other, core=1)
    query_own = tie(query, (attended_other, rest_tops[1]))
    attended_own, extra_own = attend(query_own, keys, key_extra, values_flip, 0)
    rest_early = [swap(top, core=1) for top in rest_tops[0:2]]
    rest_late = [swap(top, core=1) for top in tie(rest_tops[2:4], attended_own)]
    rest_own, rest_other = unpack_rest(rest_tops, rest_early + rest_late, places)
    rest_own = rest_own.reshape(2, width, -1)
    rest_other = rest_other.reshape(2, width, -1)
    (y0, y1, y2, y3, grad_own, grad_sent, grad_one, rest_mine, rest_sent, grad_rows, grad_hidden_row) = middle(
        places,
        ratio,
        masked_own,
        attended_own,
        attended_got,
        cots,
        encoder_low,
        vector_rows,
        bias_rows,
        rest_own,
        rest_other,
    )
    rest_got = swap(rest_sent, core=1)
    grad_got = swap(tie(grad_sent, rest_got), core=1)
    rest_parts = pack_rest(rest_mine, rest_got, (y0, y1, y2, y3), places, n_ep, slab)
    rest_tops = plane_list(rest_parts)
    query_again, *unused = lax.optimization_barrier((query, *rest_parts))
    grad_query, grad_key, grad_value = attend_back(
        query_again,
        keys,
        key_extra,
        keys_flip,
        values,
        extra_own,
        extra_other,
        grad_own,
        grad_got,
    )
    rest_tops, grad_query = lax.optimization_barrier((rest_tops, grad_query))
    grad_project, prompt_mine, prompt_sent, back_own, back_other = weight_grads(
        places,
        rows_low,
        grad_query,
        grad_key,
        grad_value,
        prompt_low,
        w_project,
        grad_hidden_row,
        n_ep,
        strip,
    )
    prompt_got = swap(prompt_sent, core=1)
    back_got = swap(tie(back_other, prompt_got), core=1)
    main_parts = pack_main(grad_project, prompt_mine, prompt_got, places, slab, strip)
    main_tops = plane_list(main_parts)
    back_own = tie(back_own, main_parts)
    i0, i1, i2, i3, grad_small = input_grads(
        places,
        ratio,
        grad_one,
        back_own,
        back_got,
        masked_own,
        encoder_low,
        mask_wide.reshape(WIDE, 1),
        grad_rows,
    )
    small_mine, small_sent = split_small(grad_small, places, n_ep, strip)
    small_got = swap(small_sent, core=1)
    small_parts = pack_small((i0, i1, i2, i3), small_mine, small_got, places, n_ep, strip)
    small_tops = plane_list(small_parts)
    rest_pieces = sum_rest(tie(rest_tops, main_parts), grad_small, places, n_ep, slab)
    output_final = place_tiles(rest_tops, chip, n_ep * slab, rows, width, "place_output")
    main_tops, output_final, rest_pieces = lax.optimization_barrier(
        (main_tops, output_final, rest_pieces)
    )
    main_pieces = sum_main(main_tops, small_tops, places, slab, strip)
    input_final = place_rows(small_tops, chip, 0, (FEAT_ROWS, rows), f32, "place_input")
    input_final = jnp.transpose(input_final[:, 0:FEAT], (0, 2, 1))[None]

    grad_block, grad_prompt_own, grad_small_own, grad_bias_own, square_tile = final_sums(
        main_pieces, rest_pieces, slab, strip
    )
    square_tile = square_tile + swap(square_tile, core=1)
    got = plane_swap(lambda b, r: square_tile)
    square_tile = (got[0, 0] + got[1, 0]) + (got[0, 1] + got[1, 1])
    if n_ep > 4:
        squares = lax.psum(square_tile, "ep")[None]
    else:
        squares = stack_ep(gather_ep(square_tile), "stack_square")
    grad_norm, *news = adam_all(
        squares,
        (
            block_weights.reshape(slab * 8, HEAD),
            prompt,
            encoder,
            shared_vectors.T,
            head_biases.T,
        ),
        (
            block_moments.reshape(2, slab * 8, HEAD),
            prompt_moments,
            encoder_moments,
            jnp.transpose(vector_moments, (2, 0, 1)),
            jnp.transpose(bias_moments, (0, 2, 1)),
        ),
        (grad_block, grad_prompt_own, grad_small_own, grad_bias_own),
    )
    block_out = tuple(part.reshape(block_weights.shape) for part in news[0:4])
    prompt_out = tuple(news[4:8])
    encoder_out = tuple(news[8:12])
    vector_out = tuple(part.T for part in news[12:16])
    bias_out = tuple(part.T for part in news[16:20])
    return (
        (output_final[None], input_final, grad_norm.reshape(()))
        + block_out
        + bias_out
        + encoder_out
        + vector_out
        + prompt_out
    )


def solution(mesh):
    data = P("split", "ep", "tp", None)
    block = P(("ep", "split"), "tp", None)
    bias = P(("ep", "split"), "tp")
    strip = P(AXES, None)
    placed = (
        data,
        P("ep", None),
        P("ep", None),
        data,
        block,
        P(None, ("ep", "split"), "tp", None),
        bias,
        P(None, ("ep", "split"), "tp"),
        strip,
        P(None, AXES, None),
        strip,
        P(None, AXES, None),
        strip,
        P(None, AXES, None),
    )
    return jax.shard_map(
        shards,
        mesh=mesh,
        in_specs=placed,
        out_specs=(data, data, P()) + (block,) * 4 + (bias,) * 4 + (strip,) * 12,
        check_vma=False,
    )
```

```python
import functools

import jax
import jax.numpy as jnp
from jax import lax
from jax.experimental import pallas as pl
from jax.experimental.pallas import tpu as pltpu
from jax.sharding import PartitionSpec as P

HEADS = 4
HEAD = 128
FF = 1024
HID = FF // HEADS
FEAT = 100
PROMPT = 1000
SLOTS = 1024
ADAM_STEP = 10
PAD = 1024
WIDE = 128

ln_eps = 1e-05
neg_big = -1e30
clip_norm = 1.0
beta_one = 0.9
beta_two = 0.999
adam_eps = 1e-08
rate_matrix = 0.15
rate_vector = 0.5
weight_decay = 0.01
AXES = ("ep", "split", "tp")
bf16 = jnp.bfloat16
f32 = jnp.float32
score_scale = HEAD**-0.5


def swap(value, ep=0, split=0, row=0, core=0):
    sizes = [lax.axis_size(a) for a in AXES]
    pairs = []
    for a in range(sizes[0]):
        for b in range(sizes[1]):
            for t in range(sizes[2]):
                other = ((a ^ ep) * sizes[1] + (b ^ split)) * sizes[2] + (t ^ (2 * row + core))
                pairs.append(((a * sizes[1] + b) * sizes[2] + t, other))
    return lax.ppermute(value, AXES, pairs)


def pick(low, high, bit):
    return jnp.where(bit == 0, low, high), jnp.where(bit == 0, high, low)


def plane_swap(piece):
    got = {}
    for b in (0, 1):
        for r in (0, 1):
            sent = piece(b, r)
            got[b, r] = sent if (b, r) == (0, 0) else swap(sent, split=b, row=r)
    return got


def tie(value, other):
    return lax.optimization_barrier((value, other))[0]


def gather_ep(shard):
    count = lax.axis_size("ep")
    if count > 4:
        return [lax.all_gather(shard, "ep", axis=0)]
    return [shard] + [swap(shard, ep=k) for k in range(1, count)]


def stack_ep(parts, name):
    return parts[0] if len(parts) == 1 else place(parts, lax.axis_index("ep"), name)


def reduce_ep(total, pieces):
    count = lax.axis_size("ep")
    if count > 4:
        return [lax.psum_scatter(total, "ep", scatter_dimension=0, tiled=True)[0]]
    return [pieces[0]] + [swap(pieces[k], ep=k) for k in range(1, count)]


def adam_update(weight, moments, gradient, factor, step_rate, decay_rate):
    clipped = gradient * factor
    first_moment = beta_one * moments[0] + (1.0 - beta_one) * clipped
    second_moment = beta_two * moments[1] + (1.0 - beta_two) * clipped * clipped
    first_hat = first_moment / (1.0 - beta_one**ADAM_STEP)
    second_hat = second_moment / (1.0 - beta_two**ADAM_STEP)
    updated = weight - step_rate * (
        first_hat / (jnp.sqrt(second_hat) + adam_eps) + decay_rate * weight
    )
    return (updated, first_moment, second_moment, updated.astype(bf16))


def dot(a, b, dims):
    return lax.dot_general(a, b, (dims, ((), ())), preferred_element_type=f32)


NN = ((1,), (0,))
NT = ((1,), (1,))
TN = ((0,), (0,))


def cost(micros):
    return pl.CostEstimate(flops=int(micros * 3e8), transcendentals=0, bytes_accessed=int(micros * 1e6))


def whole():
    return pl.BlockSpec(memory_space=pltpu.VMEM)


def shape_of(shape, dtype):
    return jax.ShapeDtypeStruct(shape, dtype)


def project_body(ratio, sc, own, other, enc, vec, wp, bias, prompt, x_ref, q_ref, k_ref, kt_ref, v_ref, vt_ref, extra_ref):
    step = pl.program_id(0)

    @pl.when(step == 0)
    def _():
        size = own.shape[0] // 2
        lane = lax.broadcasted_iota(jnp.int32, (size, WIDE), 1)
        line = lax.broadcasted_iota(jnp.int32, (size, WIDE), 0)
        ones = [jnp.where((lane >= 4 * h) & (lane < 4 * h + 3), 1.0, 0.0) for h in range(2)]
        for begin in range(0, extra_ref.shape[1], size):
            if begin < PAD:
                left = PROMPT - begin
            else:
                other, quarter = divmod((begin - PAD) // size, 2)
                left = sc[4] - (2 * quarter + (sc[2] ^ other)) * size
            bias = jnp.where((lane == 3) & (line >= left), neg_big, 0.0)
            for h in range(2):
                extra_ref[h, begin : begin + size] = (bias + ones[h]).astype(bf16)

    rows = jnp.where(step < 2, own[...], other[...])
    low = (ratio[0] * dot(rows, enc[...], NT) + vec[6:7, :]).astype(bf16)
    x_ref[...] = low
    for h in range(2):
        q_ref[h] = (dot(low, wp[h, :, 0:HEAD], NN) + bias[h : h + 1, 0:HEAD]).astype(bf16)

    def keys_from(source):
        for h in range(2):
            key = dot(source, wp[h, :, HEAD : 2 * HEAD], NN).astype(bf16)
            shift = bias[h : h + 1, HEAD : 2 * HEAD]
            value = (dot(source, wp[h, :, 2 * HEAD : 3 * HEAD], NN) + shift).astype(bf16)
            k_ref[h] = key
            v_ref[h] = value
            kt_ref[h] = key.T
            vt_ref[h] = value.T

    @pl.when(step % 2 == 0)
    def _():
        keys_from(low)

    @pl.when(step % 2 == 1)
    def _():
        keys_from(prompt[...].T)


def project(ratio, places, own, other, enc, vec, wp, bias, prompt):
    half = own.shape[0] // 2
    width = enc.shape[0]
    keys = PAD + SLOTS
    spot = lambda i: jnp.where(i % 2 == 0, 2 + i // 2, i // 2)
    tall = pl.BlockSpec((2, half, HEAD), lambda i: (0, spot(i), 0))
    flat = pl.BlockSpec((2, HEAD, half), lambda i: (0, 0, spot(i)))
    return pl.pallas_call(
        project_body,
        grid=(4,),
        in_specs=[
            pl.BlockSpec(memory_space=pltpu.SMEM),
            pl.BlockSpec(memory_space=pltpu.SMEM),
            pl.BlockSpec((half, WIDE), lambda i: (jnp.minimum(i, 1), 0)),
            pl.BlockSpec((half, WIDE), lambda i: (jnp.maximum(i - 2, 0), 0)),
            whole(),
            whole(),
            whole(),
            whole(),
            pl.BlockSpec((width, half), lambda i: (0, i // 2)),
        ],
        out_specs=[
            pl.BlockSpec((half, width), lambda i: (i, 0)),
            pl.BlockSpec((2, half, HEAD), lambda i: (0, i, 0)),
            tall,
            flat,
            tall,
            flat,
            pl.BlockSpec((2, keys, WIDE), lambda i: (0, 0, 0)),
        ],
        out_shape=[
            pltpu.HBM((4 * half, width), bf16),
            pltpu.HBM((2, 4 * half, HEAD), bf16),
            pltpu.HBM((2, keys, HEAD), bf16),
            pltpu.HBM((2, HEAD, keys), bf16),
            pltpu.HBM((2, keys, HEAD), bf16),
            pltpu.HBM((2, HEAD, keys), bf16),
            pltpu.HBM((2, keys, WIDE), bf16),
        ],
        compiler_params=pltpu.CompilerParams(vmem_limit_bytes=32 << 20),
        cost_estimate=cost(9),
        name="project",
    )(ratio, places, *held((own, other, enc, vec, wp, bias, prompt)))


CHUNK = 1024
base_two = 1.4426950408889634


def three_terms(value):
    high = value.astype(bf16).astype(f32)
    middle = (value - high).astype(bf16).astype(f32)
    return high, middle, value - high - middle


def attend_body(q_ref, k_ref, x_ref, vt_ref, o_ref, extra_ref, *scratch):
    head = pl.program_id(0)
    keys, size = scratch[0].shape
    count = q_ref.shape[1] // size
    steepness = score_scale * base_two
    lane = lax.broadcasted_iota(jnp.int32, (size, WIDE), 1)
    place = lax.broadcasted_iota(jnp.int32, (WIDE, size), 0)
    one = jnp.where(lane == 3, 1.0, 0.0).astype(bf16)
    top = None
    for b in range(count + 1):
        fresh_ref, old_ref = scratch[b % 2], scratch[(b + 1) % 2]
        if b < count:
            query = jnp.concatenate([q_ref[0, b * size : (b + 1) * size], one], axis=1)
            partial = jnp.full((8, size), -jnp.inf, f32)
        if b > 0:
            shift = top * steepness
            total = jnp.zeros((8, size), f32)
            out = jnp.zeros((HEAD, size), f32)
        for c in range(keys // CHUNK):
            span = slice(c * CHUNK, (c + 1) * CHUNK)
            if b < count:
                wide = jnp.concatenate([k_ref[0, span], x_ref[0, span]], axis=1)
                fresh = dot(wide, query, NT)
                fresh_ref[span] = fresh
                partial = jnp.maximum(partial, jnp.max(fresh.reshape(CHUNK // 8, 8, size), axis=0))
            if b > 0:
                raised = jnp.exp2(old_ref[span] * steepness - shift)
                total = total + jnp.sum(raised.reshape(CHUNK // 8, 8, size), axis=0)
                out = out + dot(vt_ref[0, :, span], raised.astype(bf16), NN)
        if b > 0:
            rows = slice((b - 1) * size, b * size)
            total = jnp.sum(total, axis=0, keepdims=True)
            o_ref[rows] = (out / total).T.astype(bf16)
            terms = three_terms(-(top + jnp.log(total) / score_scale))
            tile = jnp.where(place == 3, 1.0, 0.0)
            for k in range(3):
                tile = tile + jnp.where(place == 4 * head + k, terms[k], 0.0)
            extra_ref[0, rows] = tile.T.astype(bf16)
        if b < count:
            top = jnp.max(partial, axis=0, keepdims=True)


BLOCK = 512


def attend(q, k, extra, vt, which):
    keys = k.shape[1]
    tall = pl.BlockSpec((1, keys, HEAD), lambda h: (h, 0, 0))
    return pl.pallas_call(
        attend_body,
        grid=(2,),
        in_specs=[
            pl.BlockSpec((1, SLOTS, HEAD), lambda h: (h, which, 0)),
            tall,
            pl.BlockSpec((1, keys, WIDE), lambda h: (0, 0, 0)),
            pl.BlockSpec((1, HEAD, keys), lambda h: (h, 0, 0)),
        ],
        out_specs=[
            pl.BlockSpec((SLOTS, HEAD), lambda h: (0, h)),
            pl.BlockSpec((1, SLOTS, WIDE), lambda h: (h, 0, 0)),
        ],
        out_shape=[pltpu.HBM((SLOTS, 2 * HEAD), bf16), pltpu.HBM((2, SLOTS, WIDE), bf16)],
        scratch_shapes=[pltpu.VMEM((keys, BLOCK), f32)] * 2,
        compiler_params=pltpu.CompilerParams(vmem_limit_bytes=32 << 20),
        cost_estimate=cost(6),
        name="attend",
    )(*held((q, k, extra, vt), False))


BACK_BLOCK = 256
BACK_CHUNK = 2048


def attend_back_body(q_ref, k_ref, x_ref, kt_ref, v_ref, qa_ref, qb_ref, da_ref, db_ref, ea_ref, eb_ref, dq_ref, dk_ref, dv_ref, *scratch):
    size = scratch[0].shape[1]
    keys = k_ref.shape[1]
    rows = q_ref.shape[1]
    count = rows // size
    steepness = score_scale * base_two
    mine = pl.program_id(1) == 0

    @pl.when(mine)
    def _():
        dk_ref[...] = jnp.zeros_like(dk_ref)
        dv_ref[...] = jnp.zeros_like(dv_ref)

    for b in range(count + 1):
        probs_ref, slopes_ref = scratch[2 * (b % 2) : 2 * (b % 2) + 2]
        old_probs, old_slopes = scratch[2 - 2 * (b % 2) : 4 - 2 * (b % 2)]
        if b < count:
            span = slice(b * size, (b + 1) * size)
            query = q_ref[0, span]
            grad = jnp.where(mine, da_ref[span], db_ref[span])
            aside = jnp.where(mine, qa_ref[0, span], qb_ref[0, span])
            sums = jnp.where(mine, ea_ref[span], eb_ref[span])
            query_wide = jnp.concatenate([query, aside], axis=1)
            grad_wide = jnp.concatenate([grad, sums], axis=1)
        if b > 0:
            back = jnp.zeros((HEAD, size), f32)
        for c in range(keys // BACK_CHUNK):
            span = slice(c * BACK_CHUNK, (c + 1) * BACK_CHUNK)
            if b < count:
                extra = x_ref[0, span]
                scores = dot(jnp.concatenate([k_ref[0, span], extra], axis=1), query_wide, NT)
                slopes = dot(jnp.concatenate([v_ref[0, span], extra], axis=1), grad_wide, NT)
                probs = jnp.exp2(scores * steepness)
                probs_ref[span] = probs.astype(bf16)
                slopes_ref[span] = (probs * slopes).astype(bf16)
            if b > 0:
                back = back + dot(kt_ref[0, :, span], old_slopes[span], NN)
                grad_key = dot(query_flip, old_slopes[span], NT) * score_scale
                grad_value = dot(grad_flip, old_probs[span], NT)
                dk_ref[0, :, span] += grad_key
                dv_ref[0, :, span] += grad_value
        if b > 0:
            dq_ref[(b - 1) * size : b * size] = (back * score_scale).T.astype(bf16)
        if b < count:
            query_flip, grad_flip = query.T, grad.T


def attend_back(q, k, extra, kt, v, extra_own, extra_other, grad_own, grad_other):
    keys = k.shape[1]
    tall = pl.BlockSpec((1, keys, HEAD), lambda h, i: (h, 0, 0))
    flat = pl.BlockSpec((1, HEAD, keys), lambda h, i: (h, 0, 0))
    aside = pl.BlockSpec((1, SLOTS, WIDE), lambda h, i: (h, 0, 0))
    grad = pl.BlockSpec((SLOTS, HEAD), lambda h, i: (0, h))
    sums = pl.BlockSpec((SLOTS, HEAD), lambda h, i: (0, 2))
    return pl.pallas_call(
        attend_back_body,
        grid=(2, 2),
        in_specs=[
            pl.BlockSpec((1, SLOTS, HEAD), lambda h, i: (h, i, 0)),
            tall,
            tall,
            flat,
            tall,
            aside,
            aside,
            grad,
            grad,
            sums,
            sums,
        ],
        out_specs=[pl.BlockSpec((SLOTS, HEAD), lambda h, i: (i, h)), flat, flat],
        out_shape=[
            pltpu.HBM((2 * SLOTS, 2 * HEAD), bf16),
            pltpu.HBM((2, HEAD, keys), f32),
            pltpu.HBM((2, HEAD, keys), f32),
        ],
        scratch_shapes=[pltpu.VMEM((keys, BACK_BLOCK), bf16)] * 4,
        compiler_params=pltpu.CompilerParams(vmem_limit_bytes=40 << 20),
        cost_estimate=cost(20),
        name="attend_back",
    )(
        *held((q, k, extra, kt, v, extra_own, extra_other), False),
        *held((grad_own, grad_other, grad_own, grad_other), (False, True, False, True)),
    )


tail_slope = 0.32
tail_terms = (
    0.1276615327396569,
    0.12766067896437439,
    0.1146273959793329,
    0.0877866398778977,
    0.058846245380943685,
    -0.009886160894676655,
    0.0661375104847692,
    -0.14747037514007924,
    0.09579928012384316,
    -0.02116276404130493,
)


def gelu_pair(t):
    bell = jnp.exp2(t * t * (-0.5 * base_two))
    k = 1.0 / (1.0 + tail_slope * jnp.abs(t))
    series = jnp.full_like(t, tail_terms[-1])
    for term in tail_terms[-2::-1]:
        series = series * k + term
    tail = series * k * bell
    cumulative = jnp.where(t >= 0.0, 1.0 - tail, tail)
    return t * cumulative, cumulative + t * (bell * 0.3989422804014327)


def middle_body(
    sc,
    ratio,
    rows_ref,
    oa_ref,
    ob_ref,
    c0,
    c1,
    c2,
    c3,
    enc,
    vec,
    b1,
    ra,
    rb,
    y0,
    y1,
    y2,
    y3,
    da_ref,
    db_ref,
    dr_ref,
    ga,
    gb,
    gvec,
    gb1,
    cot,
    late,
    acc,
):
    step = pl.program_id(0)
    count = rows_ref.shape[0]
    part = count // 2

    def quarter_rows(k):
        return pl.ds(pl.multiple_of((sc[1] ^ (k % 2)) * part, part), part)

    for k, ref in enumerate((c0, c1, c2, c3)):

        @pl.when(step == k // 2)
        def _(k=k, ref=ref):
            cot[quarter_rows(k), :] = ref[...]

    @pl.when(step == 0)
    def _():
        gvec[...] = jnp.zeros_like(gvec)
        gb1[...] = jnp.zeros_like(gb1)

    def gather(k, low, high, value):
        acc[k, :, low:high] = jnp.where(step > 0, acc[k, :, low:high], 0.0) + value

    group = sc[0] ^ step
    limit = jnp.where(group == 0, sc[4], sc[5])
    line = lax.broadcasted_iota(jnp.int32, (count, 1), 0)
    slot = line + sc[2] * part + jnp.where(line >= part, part, 0)
    live = (slot < limit).astype(f32)

    def weight(k, low, high):
        return (ra if k < 2 else rb)[k % 2, :, low:high]

    def row(k):
        return vec[k : k + 1, :]

    gain_one, shift_one, gain_two, shift_two, b_out, b_two, b_enc = (row(k) for k in range(7))
    embedded = ratio[0] * dot(rows_ref[...], enc[...], NT) + b_enc
    out_pair = [
        jnp.concatenate([weight(2 * k, 0, HEAD), weight(2 * k + 1, 0, HEAD)], axis=1)
        for k in (0, 1)
    ]
    attn = dot(oa_ref[...], out_pair[0], NT) + dot(ob_ref[...], out_pair[1], NT) + b_out

    def norm(residual):
        centred = residual - jnp.mean(residual, axis=-1, keepdims=True)
        inverse = lax.rsqrt(jnp.mean(centred * centred, axis=-1, keepdims=True) + ln_eps)
        return centred * inverse, inverse

    def back(grad, normed, inverse, gain):
        scaled = grad * gain
        plain = jnp.mean(scaled, axis=-1, keepdims=True)
        mixed = jnp.mean(scaled * normed, axis=-1, keepdims=True)
        return inverse * (scaled - plain - normed * mixed)

    def add_row(k, value):
        gvec[k : k + 1, :] += jnp.sum(value, axis=0, keepdims=True)

    normed_one, inverse_one = norm(embedded + attn)
    first = normed_one * gain_one + shift_one
    first_low = first.astype(bf16)
    mlp = b_two
    acts, slopes = [], []
    for k in range(4):
        pre = dot(first_low, weight(k, HEAD, HEAD + HID), NN) + b1[k : k + 1, 2 * HEAD :]
        act, slope = gelu_pair(pre)
        acts.append(act.astype(bf16))
        slopes.append(slope)
        mlp = mlp + dot(acts[k], weight(k, HEAD + HID, HEAD + 2 * HID), NT)
    normed_two, inverse_two = norm(first + mlp)
    late[...] = ((normed_two * gain_two + shift_two) * live).astype(bf16)
    for k, ref in enumerate((y0, y1, y2, y3)):

        @pl.when(step == k // 2)
        def _(k=k, ref=ref):
            ref[...] = late[quarter_rows(k), :]

    grad_y = cot[...].astype(f32) * live
    add_row(2, grad_y * normed_two)
    add_row(3, grad_y)
    grad_two = back(grad_y, normed_two, inverse_two, gain_two)
    grad_low = grad_two.astype(bf16)
    add_row(5, grad_low.astype(f32))
    grad_flip = grad_low.T
    first_flip = first_low.T
    grad_first = grad_two
    for k in range(4):
        gather(k, HEAD + HID, HEAD + 2 * HID, dot(grad_flip, acts[k], NN))
        grad_act = dot(grad_low, weight(k, HEAD + HID, HEAD + 2 * HID), NN)
        grad_pre = (grad_act * slopes[k]).astype(bf16)
        gb1[k : k + 1, :] += jnp.sum(grad_pre.astype(f32), axis=0, keepdims=True)
        gather(k, HEAD, HEAD + HID, dot(first_flip, grad_pre, NN))
        grad_first = grad_first + dot(grad_pre, weight(k, HEAD, HEAD + HID), NT)
    add_row(0, grad_first * normed_one)
    add_row(1, grad_first)
    grad_one = back(grad_first, normed_one, inverse_one, gain_one)
    dr_ref[...] = grad_one
    attn_low = grad_one.astype(bf16)
    add_row(4, attn_low.astype(f32))
    attn_flip = attn_low.T
    for k, (source, target) in enumerate(((oa_ref, da_ref), (ob_ref, db_ref))):
        both = dot(attn_flip, source[...], NN)
        gather(2 * k, 0, HEAD, both[:, 0:HEAD])
        gather(2 * k + 1, 0, HEAD, both[:, HEAD:])
        both = dot(attn_low, out_pair[k], NN).astype(bf16)
        target[:, 0 : 2 * HEAD] = both
        product = both.astype(f32) * source[...].astype(f32)
        lane = lax.broadcasted_iota(jnp.int32, (count, WIDE), 1)
        tile = jnp.zeros((count, WIDE), f32)
        for h in range(2):
            sums = jnp.sum(product[:, h * HEAD : (h + 1) * HEAD], axis=1, keepdims=True)
            for m, term in enumerate(three_terms(-sums)):
                tile = tile + jnp.where(lane == 4 * h + m, term, 0.0)
        target[:, 2 * HEAD :] = tile.astype(bf16)

    @pl.when(step == 1)
    def _():
        ga[...] = acc[0:2].astype(bf16)
        gb[...] = acc[2:4].astype(bf16)


def middle(sc, ratio, rows, o_own, o_other, cots, enc, vec, b1, rest_own, rest_other):
    size = rows.shape[0] // 4
    block = 2 * size
    width = enc.shape[0]
    spot = lambda i, sc: (sc[0] ^ i, 0)
    pair = pl.BlockSpec((block, 2 * HEAD), spot)
    smem = pl.BlockSpec(memory_space=pltpu.SMEM)
    fixed = pl.BlockSpec((size, width), lambda i, sc: (0, 0))
    weight = rest_own.shape
    return pl.pallas_call(
        middle_body,
        grid_spec=pltpu.PrefetchScalarGridSpec(
            num_scalar_prefetch=1,
            grid=(2,),
            in_specs=[smem, pl.BlockSpec((block, WIDE), spot), pair, pair]
            + [fixed] * 4
            + [whole()] * 5,
            out_specs=[fixed] * 4
            + [pl.BlockSpec((block, 3 * HEAD), spot)] * 2
            + [pl.BlockSpec((block, width), spot)]
            + [
                pl.BlockSpec(weight, lambda i, sc: (0, 0, 0)),
                pl.BlockSpec(weight, lambda i, sc: (0, 0, 0)),
                pl.BlockSpec((8, width), lambda i, sc: (0, 0)),
                pl.BlockSpec((4, HID), lambda i, sc: (0, 0)),
            ],
            scratch_shapes=[
                pltpu.VMEM((block, width), bf16),
                pltpu.VMEM((block, width), bf16),
                pltpu.VMEM((4,) + weight[1:], f32),
            ],
        ),
        out_shape=[pltpu.VMEM((size, width), bf16)] * 4
        + [
            pltpu.HBM((4 * size, 3 * HEAD), bf16),
            pltpu.HBM((4 * size, 3 * HEAD), bf16),
            pltpu.HBM((4 * size, width), f32),
            pltpu.VMEM(weight, bf16),
            pltpu.VMEM(weight, bf16),
            pltpu.HBM((8, width), f32),
            pltpu.HBM((4, HID), f32),
        ],
        compiler_params=pltpu.CompilerParams(vmem_limit_bytes=44 << 20),
        cost_estimate=cost(25),
        name="middle",
    )(
        sc,
        ratio,
        rows,
        o_own,
        o_other,
        *held(cots),
        enc,
        vec,
        b1,
        *held((rest_own, rest_other)),
    )


def held(args, near=True):
    if isinstance(near, bool):
        near = [near] * len(args)
    spaces = [pltpu.VMEM if flag else pltpu.HBM for flag in near]
    return tuple(map(pltpu.with_memory_space_constraint, args, spaces))


def simple(body, out_shape, *args, scalars=None, scratch=(), near=(True, True), name=None):
    specs = [whole()] * len(args)
    args = held(args, near[0])
    if scalars is not None:
        specs = [pl.BlockSpec(memory_space=pltpu.SMEM)] + specs
        args = (scalars,) + args
    many = isinstance(out_shape, (list, tuple))
    if near[1]:
        kept = lambda shape: pltpu.VMEM(shape.shape, shape.dtype)
        out_shape = [kept(shape) for shape in out_shape] if many else kept(out_shape)
    return pl.pallas_call(
        body,
        in_specs=specs,
        out_specs=[whole()] * len(out_shape) if many else whole(),
        out_shape=out_shape,
        scratch_shapes=scratch,
        compiler_params=pltpu.CompilerParams(vmem_limit_bytes=16 << 20),
        cost_estimate=cost(2),
        name=name,
    )(*args)


def place(parts, index, name, near=(True, True)):
    def body(sc, *refs):
        for k, ref in enumerate(refs[:-1]):
            refs[-1][sc[0] ^ k] = ref[...]

    first = parts[0]
    return simple(
        body,
        shape_of((len(parts),) + first.shape, first.dtype),
        *parts,
        scalars=index.reshape(1).astype(jnp.int32),
        near=near,
        name=name,
    )


TAIL = 3 * HEAD
FEAT_ROWS = 112
LAST = 112
VEC = 104


def spread(row):
    parts = row.reshape(row.shape[:-1] + (4, row.shape[-1] // 4))
    room = WIDE - LAST - parts.shape[-1]
    return jnp.pad(parts, [(0, 0)] * (parts.ndim - 1) + [(LAST, room)])


def widened(prompt):
    return jnp.pad(prompt, [(0, 0)] * (prompt.ndim - 1) + [(0, 3 * TAIL - prompt.shape[-1])])


def with_bias(prompt, bias):
    row = jnp.pad(
        bias[..., None, :].astype(prompt.dtype),
        [(0, 0)] * (bias.ndim - 1)
        + [(0, prompt.shape[-2] - 1), (PAD, 3 * TAIL - PAD - bias.shape[-1])],
    )
    return widened(prompt) + row


def in_chunks(wide):
    lead, strip = wide.shape[:-2], wide.shape[-2]
    parts = jnp.swapaxes(wide.reshape(lead + (strip, 3, TAIL)), -3, -2)
    return parts.reshape(lead + (3 * strip, TAIL))


def pack_parts(block, prompt, encoder, vectors, biases):
    slab, strip = block.shape[0], prompt.shape[0]
    flat = block.reshape(slab * 8, HEAD)
    out = [shape_of((slab + 3 * strip, TAIL), bf16), shape_of((slab, 8 * HEAD - TAIL), bf16)]
    if 2 * slab != WIDE:
        low = block.reshape(slab, 8 * HEAD).astype(bf16)
        small = jnp.concatenate(
            [
                jnp.pad(encoder, ((0, 0), (0, VEC - FEAT))),
                jnp.pad(vectors, ((0, 0), (0, LAST - VEC - 7))),
                jnp.pad(biases.reshape(strip, 4), ((0, 0), (0, WIDE - LAST - 4))),
            ],
            axis=1,
        )
        chunks = in_chunks(
            jnp.concatenate([jnp.pad(prompt, ((0, 0), (0, PAD - PROMPT))), small], axis=1)
        )
        return jnp.concatenate([low[:, 0:TAIL], chunks.astype(bf16)], axis=0), low[:, TAIL:]

    def body(block_ref, prompt_ref, enc_ref, vec_ref, bias_ref, main_ref, rest_ref, tall, tile, line):
        for j in range(8):
            lanes = block_ref[pl.ds(j, slab, stride=8), :].astype(bf16)
            if j < 3:
                main_ref[0:slab, j * HEAD : (j + 1) * HEAD] = lanes
            else:
                rest_ref[:, (j - 3) * HEAD : (j - 2) * HEAD] = lanes
        low = prompt_ref[...].astype(bf16)
        for k in range(2):
            rows = slice(slab + k * strip, slab + (k + 1) * strip)
            main_ref[rows, :] = low[:, k * TAIL : (k + 1) * TAIL]
        rows = slice(slab + 2 * strip, slab + 3 * strip)
        main_ref[rows, WIDE : 2 * WIDE] = jnp.zeros((strip, WIDE), bf16)
        main_ref[rows, 0 : PROMPT - 2 * TAIL] = low[:, 2 * TAIL :]
        tall[...] = jnp.zeros_like(tall)
        tall[VEC : VEC + 7, :] = vec_ref[...]
        tile[...] = tall[...].T
        tile[:, 0:FEAT] = enc_ref[...]
        line[...] = jnp.zeros_like(line)
        line[:, 0:slab] = bias_ref[...]
        main_ref[rows, 2 * WIDE :] = (tile[...] + spread_row(line[...], strip)).astype(bf16)

    return simple(
        body,
        out,
        flat,
        prompt,
        encoder,
        vectors.T,
        biases.T,
        near=(False, True),
        scratch=[
            pltpu.VMEM((WIDE, strip), f32),
            pltpu.VMEM((strip, WIDE), f32),
            pltpu.VMEM((1, WIDE), f32),
        ],
        name="pack_parts",
    )


def spread_row(row, strip):
    place = lax.broadcasted_iota(jnp.int32, (strip, WIDE), 0)
    lane = lax.broadcasted_iota(jnp.int32, (strip, WIDE), 1)
    total = jnp.zeros((strip, WIDE), f32)
    for k in range(4):
        turned = jnp.broadcast_to(pltpu.roll(row, LAST - k * strip, 1), (strip, WIDE))
        total = total + jnp.where((place == k) & (lane >= LAST), turned, 0.0)
    return total


def gathered_row(tile, strip):
    lane = lax.broadcasted_iota(jnp.int32, (1, WIDE), 1)
    total = jnp.zeros((1, WIDE), f32)
    for k in range(4):
        turned = pltpu.roll(tile[k : k + 1], (k * strip - LAST) % WIDE, 1)
        total = total + jnp.where(lane // strip == k, turned, 0.0)
    return total


FEAT_SPAN = 80
FEAT_CUTS = ((0, 0, 0, 0, 80), (1, 0, 0, 80, 112), (1, 32, 1, 0, 48), (2, 0, 1, 48, 112))


def build_main(parts, flipped, places):
    count = len(parts)
    size, lanes = parts[0].shape
    feats, rows = flipped.shape[1:]

    def body(sc, *refs):
        ins, flip_ref, outs = refs[:count], refs[count], refs[count + 1 :]
        for k, out in enumerate(outs):
            for e, ref in enumerate(ins):
                at = pl.multiple_of((sc[6] ^ e) * size, 16)
                out[pl.ds(at, size), :] = ref[...]
            wide = jnp.concatenate(
                [flip_ref[sc[3] ^ k], jnp.zeros((FEAT_ROWS - feats, rows), bf16)], axis=0
            )
            for column, row, tile, begin, end in FEAT_CUTS:
                at = slice(count * size + row, count * size + row + end - begin)
                part = wide[begin:end, tile * WIDE : (tile + 1) * WIDE]
                out[at, column * WIDE : (column + 1) * WIDE] = part

    shape = shape_of((count * size + FEAT_SPAN, lanes), bf16)
    return simple(body, [shape] * 4, *parts, flipped, scalars=places, name="build_main")


def join_features(parts, places):
    feats, rows = parts[0].shape

    def body(sc, *refs):
        for k, ref in enumerate(refs[:-1]):
            spot = 2 * (sc[0] ^ (k // 2)) + (sc[1] ^ (k % 2))
            refs[-1][spot, 0:feats] = ref[...]

    return simple(
        body, shape_of((4, FEAT_ROWS, rows), bf16), *parts, scalars=places, name="join_features"
    )


def unpack_main(tops, lows, feats, feats_low, mask, places, n_ep, slab, strip, rows):
    plain = 2 * slab != WIDE
    size = slab + 3 * strip
    shapes = [
        shape_of((2, n_ep, 2, slab, TAIL), bf16),
        shape_of((n_ep, 2, 2, 2, strip, 3 * TAIL), bf16),
        shape_of((n_ep, 2, 2, 2, strip, WIDE), bf16),
        shape_of((8, n_ep * 2 * slab), f32),
        shape_of((4, n_ep * 2 * slab), f32),
        shape_of((4 * rows, WIDE), bf16),
        shape_of((4 * rows, WIDE), bf16),
    ]

    def features(mask_ref, source, target):
        for p in range(4):
            flip = jnp.concatenate([source[p], jnp.zeros((WIDE - FEAT_ROWS, rows), bf16)], axis=0)
            piece = jnp.where(mask_ref[...] > 0.0, flip.T.astype(f32), 0.0).astype(bf16)
            target[p * rows : (p + 1) * rows, :] = piece

    if plain:
        side, row, core = places[0], places[1], places[2]

        def ordered(parts, axis):
            cores = []
            for group in parts:
                sides = []
                for b in (0, 1):
                    sides.append(jnp.stack(pick(group[2 * b], group[2 * b + 1], row), axis=axis))
                cores.append(jnp.stack(pick(sides[0], sides[1], side), axis=axis))
            return jnp.stack(pick(cores[0], cores[1], core), axis=axis + 2)

        heads = [
            jnp.stack(pick(tops[r][:, 0:slab], tops[2 + r][:, 0:slab], side), axis=1) for r in (0, 1)
        ]
        chunks = ordered([[t[:, slab:] for t in tops], [t[:, slab:] for t in lows]], 1)
        chunks = chunks.reshape((n_ep, 2, 2, 2, 3, strip, TAIL))
        wide = jnp.swapaxes(chunks, -3, -2).reshape((n_ep, 2, 2, 2, strip, 3 * TAIL))
        small = wide[..., PAD:]
        vec = small.reshape(n_ep * 8 * strip, WIDE).astype(f32).T[VEC : VEC + 8]
        biases = []
        for group in (tops, lows):
            for r in (0, 1):
                pair = [
                    group[2 * b + r][:, slab + 2 * strip :, PAD - 2 * TAIL + LAST :][..., 0:4]
                    for b in (0, 1)
                ]
                biases.append(jnp.stack(pick(pair[0], pair[1], side), axis=1).reshape(-1))
        def both(mask_ref, a, b, c, d):
            features(mask_ref, a, c)
            features(mask_ref, b, d)

        masked = simple(
            both,
            shapes[5:],
            mask,
            feats,
            feats_low,
            near=(False, False),
            name="features",
        )
        return [jnp.stack(heads), wide, small, vec, jnp.stack(biases).astype(f32), *masked]

    def body(sc, t0, t1, t2, t3, l0, l1, l2, l3, mask_ref, *outs):
        wp_ref, prompt_ref, small_ref, vec_ref, bias_ref, own_ref, other_ref = outs
        side, row, core = sc[0], sc[1], sc[2]
        groups = ((t0, t1, t2, t3), (l0, l1, l2, l3))
        bias_tiles = {}
        for b in range(2):
            for r in range(2):
                k = 2 * b + r
                for other in range(2):
                    spot = core ^ other
                    source = groups[other][k]
                    full = source[0 : n_ep * size].reshape(n_ep, size, TAIL)
                    if other == 0:
                        wp_ref[r, :, side ^ b] = full[:, 0:slab, :]
                    part = full[:, slab:, :]
                    tiles = ([], [])
                    for column, line, tile, begin, end in FEAT_CUTS:
                        at = slice(n_ep * size + line, n_ep * size + line + end - begin)
                        tiles[tile].append(source[at, column * WIDE : (column + 1) * WIDE])
                    blank = jnp.zeros((WIDE - FEAT_ROWS, rows), bf16)
                    flip = jnp.concatenate([jnp.concatenate(t, axis=0) for t in tiles], axis=1)
                    flip = jnp.concatenate([flip, blank], axis=0)
                    piece = jnp.where(mask_ref[...] > 0.0, flip.T.astype(f32), 0.0).astype(bf16)
                    at = pl.multiple_of((2 * (side ^ b) + (row ^ r)) * rows, rows)
                    (other_ref if other else own_ref)[pl.ds(at, rows), :] = piece
                    for j in range(3):
                        lanes = slice(j * TAIL, (j + 1) * TAIL)
                        span = slice(j * strip, (j + 1) * strip)
                        prompt_ref[:, side ^ b, row ^ r, spot, :, lanes] = part[:, span, :]
                    tile = part[:, 2 * strip :, TAIL - WIDE :]
                    small_ref[:, side ^ b, row ^ r, spot] = tile
                    bias_tiles[b, r, other] = tile.astype(f32)
        flip = small_ref[...].reshape(n_ep * 8 * strip, WIDE).astype(f32).T
        vec_ref[...] = flip[VEC : VEC + 8]
        low_half = lax.broadcasted_iota(jnp.int32, (1, WIDE), 1) < slab
        for r in range(2):
            for other in range(2):
                for e in range(n_ep):
                    mine = gathered_row(bias_tiles[0, r, other][e], strip)
                    theirs = gathered_row(bias_tiles[1, r, other][e], strip)
                    first = jnp.where(side == 0, mine, theirs)
                    second = jnp.where(side == 0, theirs, mine)
                    row_tile = jnp.where(low_half, first, pltpu.roll(second, slab, 1))
                    k = r + 2 * other
                    bias_ref[k : k + 1, e * WIDE : (e + 1) * WIDE] = row_tile

    return simple(body, shapes, *tops, *lows, mask, scalars=places, name="unpack_main")


def unpack_rest(tops, lows, places):
    n_ep, slab, width = tops[0].shape

    def body(sc, *refs):
        for k in range(8):
            refs[8 + k // 4][k % 2, :, sc[0] ^ (k % 4 // 2)] = refs[k][...]

    return simple(
        body,
        [shape_of((2, n_ep, 2, slab, width), bf16)] * 2,
        *tops,
        *lows,
        scalars=places,
        name="unpack_rest",
    )


def weight_body(n_ep, strip, sc, x_ref, dq_ref, dk_ref, dv_ref, prompt, wp, gb1, gw_ref, mine_ref, sent_ref, own_ref, other_ref, acc, gq_ref, gv_ref, gp_ref, gb_ref):
    step = pl.program_id(0)

    @pl.when(step == 0)
    def _():
        acc[...] = jnp.zeros_like(acc)
        gq_ref[...] = jnp.zeros_like(gq_ref)
        gv_ref[...] = jnp.zeros_like(gv_ref)

    def columns(k):
        return jnp.concatenate([wp[h, :, k * HEAD : (k + 1) * HEAD] for h in range(2)], axis=1)

    flip = x_ref[...].T
    grad_query = dq_ref[...]
    acc[0] += dot(flip, grad_query, NN)
    gq_ref[...] += jnp.sum(grad_query.astype(f32), axis=0, keepdims=True)
    grad_key = jnp.concatenate([dk_ref[h] for h in range(2)], axis=0)
    grad_value = jnp.concatenate([dv_ref[h] for h in range(2)], axis=0)
    key_high = grad_key.astype(bf16)
    value_high = grad_value.astype(bf16)
    ones = jnp.ones((8, grad_key.shape[1]), bf16)
    gv_ref[...] += dot(ones, value_high, NT)[0:1]
    back = dot(grad_query, columns(0), NT)

    def store(value):
        @pl.when(step < 2)
        def _():
            own_ref[...] = value

        @pl.when(step >= 2)
        def _():
            other_ref[...] = value.astype(bf16)

    @pl.when(step % 2 == 0)
    def _():
        acc[1] += dot(flip, key_high, NT)
        acc[2] += dot(flip, value_high, NT)
        store(back + dot(key_high.T, columns(1), NT) + dot(value_high.T, columns(2), NT))

    @pl.when(step % 2 == 1)
    def _():
        store(back)
        key_low = (grad_key - key_high.astype(f32)).astype(bf16)
        value_low = (grad_value - value_high.astype(f32)).astype(bf16)
        source = prompt[...]
        acc[1] += dot(source, key_high, NT) + dot(source, key_low, NT)
        acc[2] += dot(source, value_high, NT) + dot(source, value_low, NT)
        gv_ref[...] += dot(ones, value_low, NT)[0:1]
        total = dot(columns(1), key_high, NN) + dot(columns(1), key_low, NN)
        total = total + dot(columns(2), value_high, NN) + dot(columns(2), value_low, NN)
        gp_ref[step // 2] = total.astype(bf16)

    @pl.when(step == 3)
    def _():
        for h in range(2):
            for k in range(3):
                lanes = slice(h * HEAD, (h + 1) * HEAD)
                gw_ref[h, :, k * HEAD : (k + 1) * HEAD] = acc[k, :, lanes].astype(bf16)
            gb_ref[h : h + 1, 0:HEAD] = gq_ref[:, h * HEAD : (h + 1) * HEAD]
            gb_ref[h : h + 1, HEAD : 2 * HEAD] = gv_ref[:, h * HEAD : (h + 1) * HEAD]
        gb_ref[2:4, 0 : 2 * HEAD] = jnp.zeros((2, 2 * HEAD), f32)
        gb_ref[:, 2 * HEAD :] = gb1[...]
        if strip % 16:
            mine_ref[...] = gp_ref[...]
            sent_ref[...] = gb_ref[...]
            return
        half = gp_ref.shape[2]
        row, core = sc[1], sc[2]
        first = lax.broadcasted_iota(jnp.int32, (strip, WIDE), 0) == 0
        low_half = lax.broadcasted_iota(jnp.int32, (1, WIDE), 1) < 4 * strip
        for other, ref in enumerate((mine_ref, sent_ref)):
            for e in range(n_ep):
                for s in range(2):
                    for r in range(2):
                        y = row ^ r
                        at = ((e * 2 + s) * 2 + y) * 2 + (core ^ other)
                        at = pl.ds(pl.multiple_of(at * strip, strip), strip)
                        for tile in range(PAD // WIDE):
                            lanes = slice(tile * WIDE % half, tile * WIDE % half + WIDE)
                            j, place = tile // 3, tile % 3
                            rows = slice(j * strip, (j + 1) * strip)
                            to = slice(place * WIDE, (place + 1) * WIDE)
                            ref[e, s, y, rows, to] = gp_ref[tile * WIDE // half, at, lanes]
                        k = r + 2 * other
                        tile = gb_ref[k : k + 1, e * WIDE : (e + 1) * WIDE]
                        if s == 1:
                            tile = pltpu.roll(tile, WIDE - 4 * strip, 1)
                        tile = jnp.where(low_half, tile, 0.0)
                        tile = jnp.where(first, tile, 0.0).astype(bf16)
                        ref[e, s, y, 2 * strip : 3 * strip, 2 * WIDE :] = tile


def weight_grads(places, x, dq, dk, dv, prompt, wp, gb1, n_ep, strip):
    half = x.shape[0] // 4
    width = wp.shape[1]
    spot = lambda i: jnp.where(i % 2 == 0, 2 + i // 2, i // 2)
    key = pl.BlockSpec((2, HEAD, half), lambda i: (0, 0, spot(i)))
    if strip % 16:
        shapes = [pltpu.VMEM((2, width, half), bf16), pltpu.VMEM((4, width), f32)]
    else:
        strips = (n_ep, 2, 2, 3 * strip, TAIL)
        shapes = [pltpu.HBM(strips, bf16), pltpu.VMEM(strips, bf16)]
    fixed = [
        pl.BlockSpec(shape.shape, functools.partial(lambda n, i: (0,) * n, len(shape.shape)))
        for shape in shapes
    ]
    out = pl.pallas_call(
        functools.partial(weight_body, n_ep, strip),
        grid=(4,),
        in_specs=[
            pl.BlockSpec(memory_space=pltpu.SMEM),
            pl.BlockSpec((half, width), lambda i: (i, 0)),
            pl.BlockSpec((half, 2 * HEAD), lambda i: (i, 0)),
            key,
            key,
            pl.BlockSpec((width, half), lambda i: (0, i // 2)),
            whole(),
            whole(),
        ],
        out_specs=[pl.BlockSpec((2, width, TAIL), lambda i: (0, 0, 0))]
        + fixed
        + [
            pl.BlockSpec((half, width), lambda i: (jnp.minimum(i, 1), 0)),
            pl.BlockSpec((half, width), lambda i: (jnp.maximum(i - 2, 0), 0)),
        ],
        out_shape=[pltpu.HBM((2, width, TAIL), bf16)]
        + shapes
        + [pltpu.HBM((2 * half, width), f32), pltpu.HBM((2 * half, width), bf16)],
        scratch_shapes=[pltpu.VMEM((3, width, 2 * HEAD), f32)]
        + [pltpu.VMEM((1, 2 * HEAD), f32)] * 2
        + [pltpu.VMEM((2, width, half), bf16), pltpu.VMEM((4, width), f32)],
        compiler_params=pltpu.CompilerParams(vmem_limit_bytes=40 << 20),
        cost_estimate=cost(9),
        name="weight_grads",
    )(places, *held((x, dq, dk, dv, prompt, wp), False), gb1)
    grad_project, mine, sent, back_own, back_other = out
    if strip % 16:
        row, core = places[1], places[2]
        grad = jnp.concatenate([mine[0], mine[1]], axis=1)
        blocks = grad.reshape(n_ep, 2, 2, 2, strip, PAD)
        table = sent.reshape(2, 2, n_ep, 2, 4 * strip)
        both = []
        for other in (0, 1):
            by_row = jnp.stack(pick(table[other, 0], table[other, 1], row), axis=2)
            part = lax.dynamic_index_in_dim(blocks, core ^ other, 3, keepdims=False)
            both.append(in_chunks(with_bias(part, by_row)))
        mine, sent = both
    return grad_project, mine, sent, back_own, back_other


def input_body(sc, ratio, dr_ref, own_ref, got_ref, rows_ref, enc, mask, rows_grad, i0, i1, i2, i3, small_ref, acc, bias):
    step = pl.program_id(0)
    low = (dr_ref[...] + own_ref[...] + got_ref[...].astype(f32)).astype(bf16)
    part = dot(low.T, rows_ref[...], NN) * ratio[0]
    part_bias = jnp.sum(low.astype(f32), axis=0, keepdims=True)

    @pl.when(step == 0)
    def _():
        acc[...] = part
        bias[...] = part_bias

    @pl.when(step > 0)
    def _():
        acc[...] += part
        bias[...] += part_bias

    grad = dot(enc[...].T, low, NT)[0:FEAT_ROWS] * ratio[0] * mask[0:FEAT_ROWS]
    for k, ref in enumerate((i0, i1, i2, i3)):

        @pl.when(step == k // 2)
        def _(k=k, ref=ref):
            first = sc[1] ^ (k % 2) == 0
            part = ref.shape[1]
            ref[...] = jnp.where(first, grad[:, 0:part], grad[:, part:]).astype(bf16)

    @pl.when(step == 1)
    def _():
        width = acc.shape[0]
        rows = jnp.concatenate(
            [
                jnp.zeros((VEC, width), f32),
                rows_grad[0:6],
                bias[...],
                jnp.zeros((WIDE - VEC - 7, width), f32),
            ],
            axis=0,
        )
        small_ref[...] = (acc[...] + rows.T).astype(bf16)


def input_grads(sc, ratio, dr, own, got, rows, enc, mask, rows_grad):
    size = rows.shape[0] // 4
    width = enc.shape[0]
    spot = lambda i, sc: (sc[0] ^ i, 0)
    block = pl.BlockSpec((2 * size, width), spot)
    fixed = pl.BlockSpec((FEAT_ROWS, size), lambda i, sc: (0, 0))
    return pl.pallas_call(
        input_body,
        grid_spec=pltpu.PrefetchScalarGridSpec(
            num_scalar_prefetch=1,
            grid=(2,),
            in_specs=[
                pl.BlockSpec(memory_space=pltpu.SMEM),
                block,
                block,
                block,
                pl.BlockSpec((2 * size, WIDE), spot),
                whole(),
                whole(),
                whole(),
            ],
            out_specs=[fixed] * 4 + [pl.BlockSpec((width, WIDE), lambda i, sc: (0, 0))],
            scratch_shapes=[pltpu.VMEM((width, WIDE), f32), pltpu.VMEM((1, width), f32)],
        ),
        out_shape=[pltpu.VMEM((FEAT_ROWS, size), bf16)] * 4 + [pltpu.VMEM((width, WIDE), bf16)],
        compiler_params=pltpu.CompilerParams(vmem_limit_bytes=32 << 20),
        cost_estimate=cost(6),
        name="input_grads",
    )(sc, ratio, *held((dr, own, got, rows), False), enc, mask, rows_grad)


def split_small(grad, places, n_ep, strip):
    blocks = grad.reshape(n_ep * 4, 2, strip, WIDE)

    def body(sc, grad_ref, mine_ref, sent_ref):
        mine_ref[...] = grad_ref[:, sc[2]]
        sent_ref[...] = grad_ref[:, 1 - sc[2]]

    shape = shape_of((n_ep * 4, strip, WIDE), bf16)
    return simple(body, [shape, shape], blocks, scalars=places, name="split_small")


def pack_main(gw, mine, got, places, slab, strip):
    n_ep = mine.shape[0]
    heads = gw.reshape(2, n_ep, 2, slab, TAIL)
    if 2 * slab != WIDE:
        pair = (mine.astype(f32) + got.astype(f32)).astype(bf16)
        outs = []
        for b in (0, 1):
            for r in (0, 1):
                side, row = places[0] ^ b, places[1] ^ r
                part = lax.dynamic_index_in_dim(pair, side, 1, keepdims=False)
                part = lax.dynamic_index_in_dim(part, row, 1, keepdims=False)
                head = lax.dynamic_index_in_dim(heads[r], side, 1, keepdims=False)
                outs.append(jnp.concatenate([head, part], axis=1))
        return outs

    def body(sc, gw_ref, a_ref, b_ref, *outs):
        for b in range(2):
            for r in range(2):
                out = outs[2 * b + r]
                side, row = sc[0] ^ b, sc[1] ^ r
                out[:, 0:slab, :] = gw_ref[r, :, side]
                pair = a_ref[:, side, row].astype(f32) + b_ref[:, side, row].astype(f32)
                out[:, slab : slab + 3 * strip, :] = pair.astype(bf16)

    shape = shape_of((n_ep, slab + 3 * strip, TAIL), bf16)
    return simple(
        body,
        [shape] * 4,
        heads,
        mine,
        got,
        scalars=places,
        near=((False, False, True), True),
        name="pack_main",
    )


def pack_small(ins, mine, got, places, n_ep, strip):
    rows = ins[0].shape[1]
    mine = mine.reshape(n_ep, 2, 2, strip, WIDE)
    got = got.reshape(n_ep, 2, 2, strip, WIDE)
    total = FEAT_ROWS + n_ep * strip
    if 8 * strip != WIDE:
        pair = (mine.astype(f32) + got.astype(f32)).astype(bf16)
        outs = []
        for k in range(4):
            part = lax.dynamic_index_in_dim(pair, places[0] ^ (k // 2), 1, keepdims=False)
            part = lax.dynamic_index_in_dim(part, places[1] ^ (k % 2), 1, keepdims=False)
            part = jnp.pad(part.reshape(n_ep * strip, WIDE), ((0, 0), (0, rows - WIDE)))
            outs.append(jnp.concatenate([ins[k], part], axis=0))
        return outs

    def body(sc, *refs):
        in_refs, a_ref, b_ref, outs = refs[0:4], refs[4], refs[5], refs[6:]
        for k in range(4):
            side, row = sc[0] ^ (k // 2), sc[1] ^ (k % 2)
            outs[k][0:FEAT_ROWS] = in_refs[k][...]
            pair = a_ref[:, side, row].astype(f32) + b_ref[:, side, row].astype(f32)
            outs[k][FEAT_ROWS:, 0:WIDE] = pair.reshape(n_ep * strip, WIDE).astype(bf16)

    return simple(
        body, [shape_of((total, rows), bf16)] * 4, *ins, mine, got, scalars=places, name="pack_small"
    )


def subtiles(rows, lanes, width):
    out = []
    across = width // WIDE
    for n in range(rows // 16 * (lanes // WIDE)):
        g, t = divmod(n, lanes // WIDE)
        row, col = divmod(n, across)
        here = (slice(16 * g, 16 * (g + 1)), slice(WIDE * t, WIDE * (t + 1)))
        out.append((here, (16 * row, slice(WIDE * col, WIDE * (col + 1)))))
    return out


def place_tiles(parts, index, begin, rows, lanes, name):
    width = parts[0].shape[1]

    def body(sc, *refs):
        for k, ref in enumerate(refs[:-1]):
            for here, there in subtiles(rows, lanes, width):
                tile = ref[begin + there[0] : begin + there[0] + 16, there[1]]
                refs[-1][sc[0] ^ k, here[0], here[1]] = tile

    return simple(
        body,
        shape_of((len(parts), rows, lanes), bf16),
        *parts,
        scalars=index.reshape(1).astype(jnp.int32),
        near=(True, False),
        name=name,
    )


def pack_rest(mine, got, outs, places, n_ep, slab):
    width = mine.shape[-1]
    rows, lanes = outs[0].shape
    count = n_ep * slab
    mine = mine.reshape(2, n_ep, 2, slab, width)
    got = got.reshape(2, n_ep, 2, slab, width)

    def body(sc, a_ref, b_ref, *refs):
        for k in range(4):
            side = sc[0] ^ (k // 2)
            pair = a_ref[k % 2, :, side].astype(f32) + b_ref[k % 2, :, side].astype(f32)
            refs[4 + k][0:count] = pair.reshape(count, width).astype(bf16)
            for here, there in subtiles(rows, lanes, width):
                refs[4 + k][count + there[0] : count + there[0] + 16, there[1]] = refs[k][here]

    extra = subtiles(rows, lanes, width)[-1][1][0] + 16
    shape = shape_of((count + extra, width), bf16)
    return simple(body, [shape] * 4, mine, got, *outs, scalars=places, name="pack_rest")


def sum_rest(parts, later, places, n_ep, slab):
    width = parts[0].shape[1]
    if n_ep != 4:
        total = sum(part[0 : n_ep * slab].astype(f32) for part in parts)
        total = total.reshape(n_ep, slab, width)
        return [lax.psum_scatter(total, "ep", scatter_dimension=0, tiled=True)[0]]

    def body(sc, *refs):
        ins, outs = refs[: len(parts)], refs[len(parts) :]
        for k in range(4):
            spot = pl.multiple_of((sc[6] ^ k) * slab, slab)
            total = ins[0][pl.ds(spot, slab), :].astype(f32)
            for ref in ins[1:]:
                total = total + ref[pl.ds(spot, slab), :].astype(f32)
            outs[k // 2][k % 2] = total.astype(bf16)

    near, far = simple(
        body, [shape_of((2, slab, width), bf16)] * 2, *parts, scalars=places, name="sum_rest"
    )
    got = swap(far, ep=2)

    def added(a_ref, b_ref, own_ref, sent_ref):
        own_ref[...] = (a_ref[0].astype(f32) + b_ref[0].astype(f32)).astype(bf16)
        sent_ref[...] = (a_ref[1].astype(f32) + b_ref[1].astype(f32)).astype(bf16)

    got = tie(got, later)
    own, sent = simple(added, [shape_of((slab, width), bf16)] * 2, near, got, name="add_rest")
    return [own, swap(sent, ep=1)]


def sum_main(mains, smalls, places, slab, strip):
    n_ep = mains[0].shape[0]
    if n_ep > 4:
        total = sum(part.astype(f32) for part in mains)
        small = sum(part[FEAT_ROWS:, 0:WIDE].astype(f32) for part in smalls)
        small = jnp.pad(small.reshape(n_ep, strip, WIDE), ((0, 0), (0, 0), (0, TAIL - WIDE)))
        return reduce_ep(jnp.concatenate([total, small], axis=1), None)

    def body(sc, *refs):
        main_refs, small_refs, outs = refs[0:4], refs[4:8], refs[8:]
        for k, out in enumerate(outs):
            spot = sc[6] ^ k
            total = main_refs[0][spot].astype(f32)
            for ref in main_refs[1:]:
                total = total + ref[spot].astype(f32)
            out[0 : slab + 3 * strip] = total.astype(bf16)
            where = pl.multiple_of(FEAT_ROWS + spot * strip, strip)
            total = small_refs[0][pl.ds(where, strip), 0:WIDE].astype(f32)
            for ref in small_refs[1:]:
                total = total + ref[pl.ds(where, strip), 0:WIDE].astype(f32)
            out[slab + 3 * strip :, 0:WIDE] = total.astype(bf16)
            out[slab + 3 * strip :, WIDE:] = jnp.zeros((strip, TAIL - WIDE), bf16)

    shape = shape_of((slab + 4 * strip, TAIL), bf16)
    pieces = simple(body, [shape] * n_ep, *mains, *smalls, scalars=places, name="sum_main")
    return reduce_ep(None, pieces)


def place_rows(parts, index, begin, shape, dtype, name):
    def body(sc, *refs):
        for k, ref in enumerate(refs[:-1]):
            refs[-1][sc[0] ^ k] = ref[begin : begin + shape[0], 0 : shape[1]].astype(dtype)

    return simple(
        body,
        shape_of((len(parts),) + shape, dtype),
        *parts,
        scalars=index.reshape(1).astype(jnp.int32),
        near=(True, False),
        name=name,
    )


def final_sums(mains, rests, slab, strip):
    def body(*refs):
        main_refs, rest_refs = refs[: len(mains)], refs[len(mains) : len(mains) + len(rests)]
        block_ref, prompt_ref, small_ref, bias_ref, square_ref = refs[len(mains) + len(rests) :]

        def added(group):
            total = group[0][...].astype(f32)
            for ref in group[1:]:
                total = total + ref[...].astype(f32)
            return total

        main, rest = added(main_refs), added(rest_refs)
        square = jnp.sum(jnp.sum(main * main, axis=0, keepdims=True), axis=1, keepdims=True)
        square = square + jnp.sum(
            jnp.sum(rest * rest, axis=0, keepdims=True), axis=1, keepdims=True
        )
        for j in range(8):
            if j < 3:
                tile = main[0:slab, j * HEAD : (j + 1) * HEAD]
            else:
                tile = rest[:, (j - 3) * HEAD : (j - 2) * HEAD]
            block_ref[pl.ds(j, slab, stride=8), :] = tile
        for j in range(3):
            part = main[slab + j * strip : slab + (j + 1) * strip]
            high = min(PROMPT, (j + 1) * TAIL)
            prompt_ref[:, j * TAIL : high] = part[:, 0 : high - j * TAIL]
        small_ref[...] = main[slab + 3 * strip :, 0:WIDE]
        bias_ref[...] = main[slab + 2 * strip : slab + 2 * strip + 1, TAIL - WIDE :]
        square_ref[...] = jnp.broadcast_to(square, (8, 128))

    return simple(
        body,
        [
            shape_of((slab * 8, HEAD), f32),
            shape_of((strip, PROMPT), f32),
            shape_of((strip, WIDE), f32),
            shape_of((1, WIDE), f32),
            shape_of((8, 128), f32),
        ],
        *mains,
        *rests,
        name="final_sums",
    )


def adam_all(squares, params, moments, grads):
    slab = params[0].shape[0] // 8
    rates = (rate_matrix, rate_vector, rate_matrix, rate_vector, rate_vector)
    decays = (weight_decay, weight_decay, weight_decay, 0.0, 0.0)
    count = squares.shape[0]

    def body(sq_ref, *refs):
        weights, moment_refs, grad_refs, outs = refs[0:5], refs[5:10], refs[10:14], refs[14:]
        total = sq_ref[0, 0:1, 0:1]
        for k in range(1, count):
            total = total + sq_ref[k, 0:1, 0:1]
        norm = jnp.sqrt(total)
        outs[0][...] = norm
        factor = jnp.minimum(1.0, clip_norm / (norm + 1e-06))
        small = grad_refs[2][...]
        picked = (
            grad_refs[0][...],
            grad_refs[1][...],
            small[:, 0:FEAT],
            small.T[VEC : VEC + 7],
            grad_refs[3][:, 0:slab],
        )
        for k in range(5):
            both = moment_refs[k]
            pair = (both[:, 0], both[:, 1]) if k == 3 else (both[0], both[1])
            news = adam_update(weights[k][...], pair, picked[k], factor, rates[k], decays[k])
            for m in range(3):
                outs[1 + 4 * k + m][...] = news[m]
            if k > 0:
                outs[4 + 4 * k][...] = news[3]
        for j in range(8):
            tile = outs[1][pl.ds(j, slab, stride=8), :]
            outs[4][:, j * HEAD : (j + 1) * HEAD] = tile.astype(bf16)

    shapes = [shape_of((1, 1), f32)]
    for k, param in enumerate(params):
        low = (slab, 8 * HEAD) if k == 0 else param.shape
        shapes += [shape_of(param.shape, f32)] * 3 + [shape_of(low, bf16)]
    return simple(body, shapes, squares, *params, *moments, *grads, near=(True, False), name="adam_all")


def shards(
    feats,
    counts,
    feat_mask,
    cotangent,
    block_weights,
    block_moments,
    head_biases,
    bias_moments,
    encoder,
    encoder_moments,
    shared_vectors,
    vector_moments,
    prompt,
    prompt_moments,
):
    n_ep = lax.axis_size("ep")
    side = lax.axis_index("split")
    row = lax.axis_index("tp") // 2
    core = lax.axis_index("tp") % 2
    chip = side * 2 + row
    rows = feats.shape[2]
    width = cotangent.shape[3]
    slab = block_weights.shape[0]
    strip = encoder.shape[0]

    mask_row = lax.dynamic_index_in_dim(feat_mask, chip, 0, keepdims=False)
    count_pair = lax.dynamic_index_in_dim(counts, chip, 0, keepdims=False)
    mask_float = mask_row.astype(f32)
    ratio = (FEAT / jnp.sum(mask_float)).reshape(1)
    spot = jnp.arange(8, dtype=jnp.int32)
    places = jnp.pad(count_pair, (4, 2)).astype(jnp.int32)
    for k, value in ((0, side), (1, row), (2, core), (3, chip), (6, lax.axis_index("ep"))):
        places = places + jnp.where(spot == k, value, 0)

    def to_chip(array):
        return plane_list(
            [lax.dynamic_index_in_dim(array[0], chip ^ k, 0, keepdims=False) for k in range(4)]
        )

    def plane_list(parts):
        got = plane_swap(lambda b, r: parts[2 * b + r])
        return [got[b, r] for b in (0, 1) for r in (0, 1)]

    main_part, rest_part = pack_parts(
        block_weights, prompt, encoder, shared_vectors, head_biases
    )
    mask_wide = jnp.pad(mask_float, (0, WIDE - FEAT)).reshape(1, WIDE)
    flipped = jnp.transpose(tie(feats, main_part)[0], (0, 2, 1))
    main_pieces = gather_ep(main_part)
    feats_own, feats_other = None, None
    if 2 * slab == WIDE:
        tops = plane_list(build_main(main_pieces, flipped, places))
    else:
        feats_own = join_features(
            plane_list(
                [lax.dynamic_index_in_dim(flipped, chip ^ k, 0, keepdims=False) for k in range(4)]
            ),
            places,
        )
        feats_other = swap(feats_own, core=1)
        tops = plane_list([stack_ep(main_pieces, "stack_main")] * 4)
    lows = [swap(top, core=1) for top in tops]
    w_project, prompt_low, small_low, vector_rows, bias_rows, masked_own, masked_other = unpack_main(
        tops, lows, feats_own, feats_other, mask_wide, places, n_ep, slab, strip, rows
    )
    w_project = w_project.reshape(2, width, TAIL)
    prompt_low = prompt_low.reshape(width, 3 * TAIL)
    encoder_low = small_low.reshape(width, WIDE)

    rest_along = stack_ep(gather_ep(tie(rest_part, lows[0])), "stack_rest")
    lows, rest_along = lax.optimization_barrier((lows, rest_along))

    cots = to_chip(tie(cotangent, w_project))
    rows_low, query, keys, keys_flip, values, values_flip, key_extra = project(
        ratio,
        places,
        masked_own,
        masked_other,
        encoder_low,
        vector_rows,
        w_project,
        bias_rows,
        prompt_low,
    )
    query, rest_along, cots = lax.optimization_barrier((query, rest_along, cots))
    rest_tops = plane_list([rest_along] * 4)
    attended_other, extra_other = attend(query, keys, key_extra, values_flip, 1)
    attended_got = swap(attended_other, core=1)
    query_own = tie(query, (attended_other, rest_tops[1]))
    attended_own, extra_own = attend(query_own, keys, key_extra, values_flip, 0)
    rest_early = [swap(top, core=1) for top in rest_tops[0:2]]
    rest_late = [swap(top, core=1) for top in tie(rest_tops[2:4], attended_own)]
    rest_own, rest_other = unpack_rest(rest_tops, rest_early + rest_late, places)
    rest_own = rest_own.reshape(2, width, -1)
    rest_other = rest_other.reshape(2, width, -1)
    (y0, y1, y2, y3, grad_own, grad_sent, grad_one, rest_mine, rest_sent, grad_rows, grad_hidden_row) = middle(
        places,
        ratio,
        masked_own,
        attended_own,
        attended_got,
        cots,
        encoder_low,
        vector_rows,
        bias_rows,
        rest_own,
        rest_other,
    )
    rest_got = swap(rest_sent, core=1)
    grad_got = swap(tie(grad_sent, rest_got), core=1)
    rest_parts = pack_rest(rest_mine, rest_got, (y0, y1, y2, y3), places, n_ep, slab)
    rest_tops = plane_list(rest_parts)
    query_again, *unused = lax.optimization_barrier((query, *rest_parts))
    grad_query, grad_key, grad_value = attend_back(
        query_again,
        keys,
        key_extra,
        keys_flip,
        values,
        extra_own,
        extra_other,
        grad_own,
        grad_got,
    )
    rest_tops, grad_query = lax.optimization_barrier((rest_tops, grad_query))
    grad_project, prompt_mine, prompt_sent, back_own, back_other = weight_grads(
        places,
        rows_low,
        grad_query,
        grad_key,
        grad_value,
        prompt_low,
        w_project,
        grad_hidden_row,
        n_ep,
        strip,
    )
    prompt_got = swap(prompt_sent, core=1)
    back_got = swap(tie(back_other, prompt_got), core=1)
    main_parts = pack_main(grad_project, prompt_mine, prompt_got, places, slab, strip)
    main_tops = plane_list(main_parts)
    back_own = tie(back_own, main_parts)
    i0, i1, i2, i3, grad_small = input_grads(
        places,
        ratio,
        grad_one,
        back_own,
        back_got,
        masked_own,
        encoder_low,
        mask_wide.reshape(WIDE, 1),
        grad_rows,
    )
    small_mine, small_sent = split_small(grad_small, places, n_ep, strip)
    small_got = swap(small_sent, core=1)
    small_parts = pack_small((i0, i1, i2, i3), small_mine, small_got, places, n_ep, strip)
    small_tops = plane_list(small_parts)
    rest_pieces = sum_rest(tie(rest_tops, main_parts), grad_small, places, n_ep, slab)
    output_final = place_tiles(rest_tops, chip, n_ep * slab, rows, width, "place_output")
    main_tops, output_final, rest_pieces = lax.optimization_barrier(
        (main_tops, output_final, rest_pieces)
    )
    main_pieces = sum_main(main_tops, small_tops, places, slab, strip)
    input_final = place_rows(small_tops, chip, 0, (FEAT_ROWS, rows), f32, "place_input")
    input_final = jnp.transpose(input_final[:, 0:FEAT], (0, 2, 1))[None]

    grad_block, grad_prompt_own, grad_small_own, grad_bias_own, square_tile = final_sums(
        main_pieces, rest_pieces, slab, strip
    )
    square_tile = square_tile + swap(square_tile, core=1)
    got = plane_swap(lambda b, r: square_tile)
    square_tile = (got[0, 0] + got[1, 0]) + (got[0, 1] + got[1, 1])
    if n_ep > 4:
        squares = lax.psum(square_tile, "ep")[None]
    else:
        squares = stack_ep(gather_ep(square_tile), "stack_square")
    grad_norm, *news = adam_all(
        squares,
        (
            block_weights.reshape(slab * 8, HEAD),
            prompt,
            encoder,
            shared_vectors.T,
            head_biases.T,
        ),
        (
            block_moments.reshape(2, slab * 8, HEAD),
            prompt_moments,
            encoder_moments,
            jnp.transpose(vector_moments, (2, 0, 1)),
            jnp.transpose(bias_moments, (0, 2, 1)),
        ),
        (grad_block, grad_prompt_own, grad_small_own, grad_bias_own),
    )
    block_out = tuple(part.reshape(block_weights.shape) for part in news[0:4])
    prompt_out = tuple(news[4:8])
    encoder_out = tuple(news[8:12])
    vector_out = tuple(part.T for part in news[12:16])
    bias_out = tuple(part.T for part in news[16:20])
    return (
        (output_final[None], input_final, grad_norm.reshape(()))
        + block_out
        + bias_out
        + encoder_out
        + vector_out
        + prompt_out
    )


def solution(mesh):
    data = P("split", "ep", "tp", None)
    block = P(("ep", "split"), "tp", None)
    bias = P(("ep", "split"), "tp")
    strip = P(AXES, None)
    placed = (
        data,
        P("ep", None),
        P("ep", None),
        data,
        block,
        P(None, ("ep", "split"), "tp", None),
        bias,
        P(None, ("ep", "split"), "tp"),
        strip,
        P(None, AXES, None),
        strip,
        P(None, AXES, None),
        strip,
        P(None, AXES, None),
    )
    return jax.shard_map(
        shards,
        mesh=mesh,
        in_specs=placed,
        out_specs=(data, data, P()) + (block,) * 4 + (bias,) * 4 + (strip,) * 12,
        check_vma=False,
    )
```

```python
import functools

import jax
import jax.numpy as jnp
from jax import lax
from jax.experimental import pallas as pl
from jax.experimental.pallas import tpu as pltpu
from jax.sharding import PartitionSpec as P

HEADS = 4
HEAD = 128
FF = 1024
HID = FF // HEADS
FEAT = 100
PROMPT = 1000
SLOTS = 1024
ADAM_STEP = 10
PAD = 1024
WIDE = 128

ln_eps = 1e-05
neg_big = -1e30
clip_norm = 1.0
beta_one = 0.9
beta_two = 0.999
adam_eps = 1e-08
rate_matrix = 0.15
rate_vector = 0.5
weight_decay = 0.01
AXES = ("ep", "split", "tp")
bf16 = jnp.bfloat16
f32 = jnp.float32
score_scale = HEAD**-0.5


def swap(value, ep=0, split=0, row=0, core=0):
    sizes = [lax.axis_size(a) for a in AXES]
    pairs = []
    for a in range(sizes[0]):
        for b in range(sizes[1]):
            for t in range(sizes[2]):
                other = ((a ^ ep) * sizes[1] + (b ^ split)) * sizes[2] + (t ^ (2 * row + core))
                pairs.append(((a * sizes[1] + b) * sizes[2] + t, other))
    return lax.ppermute(value, AXES, pairs)


def pick(low, high, bit):
    return jnp.where(bit == 0, low, high), jnp.where(bit == 0, high, low)


def plane_swap(piece):
    got = {}
    for b in (0, 1):
        for r in (0, 1):
            sent = piece(b, r)
            got[b, r] = sent if (b, r) == (0, 0) else swap(sent, split=b, row=r)
    return got


def tie(value, other):
    return lax.optimization_barrier((value, other))[0]


def gather_ep(shard):
    count = lax.axis_size("ep")
    if count > 4:
        return [lax.all_gather(shard, "ep", axis=0)]
    return [shard] + [swap(shard, ep=k) for k in range(1, count)]


def stack_ep(parts, name):
    return parts[0] if len(parts) == 1 else place(parts, lax.axis_index("ep"), name)


def reduce_ep(total, pieces):
    count = lax.axis_size("ep")
    if count > 4:
        return [lax.psum_scatter(total, "ep", scatter_dimension=0, tiled=True)[0]]
    return [pieces[0]] + [swap(pieces[k], ep=k) for k in range(1, count)]


def adam_update(weight, moments, gradient, factor, step_rate, decay_rate):
    clipped = gradient * factor
    first_moment = beta_one * moments[0] + (1.0 - beta_one) * clipped
    second_moment = beta_two * moments[1] + (1.0 - beta_two) * clipped * clipped
    first_hat = first_moment / (1.0 - beta_one**ADAM_STEP)
    second_hat = second_moment / (1.0 - beta_two**ADAM_STEP)
    updated = weight - step_rate * (
        first_hat / (jnp.sqrt(second_hat) + adam_eps) + decay_rate * weight
    )
    return (updated, first_moment, second_moment, updated.astype(bf16))


def dot(a, b, dims):
    return lax.dot_general(a, b, (dims, ((), ())), preferred_element_type=f32)


NN = ((1,), (0,))
NT = ((1,), (1,))
TN = ((0,), (0,))


def cost(micros):
    return pl.CostEstimate(flops=int(micros * 3e8), transcendentals=0, bytes_accessed=int(micros * 1e6))


def whole():
    return pl.BlockSpec(memory_space=pltpu.VMEM)


def shape_of(shape, dtype):
    return jax.ShapeDtypeStruct(shape, dtype)


def project_body(ratio, sc, own, other, enc, vec, wp, bias, prompt, x_ref, q_ref, k_ref, kt_ref, v_ref, vt_ref, extra_ref):
    step = pl.program_id(0)

    @pl.when(step == 0)
    def _():
        size = own.shape[0] // 2
        lane = lax.broadcasted_iota(jnp.int32, (size, WIDE), 1)
        line = lax.broadcasted_iota(jnp.int32, (size, WIDE), 0)
        ones = [jnp.where((lane >= 4 * h) & (lane < 4 * h + 3), 1.0, 0.0) for h in range(2)]
        for begin in range(0, extra_ref.shape[1], size):
            if begin < PAD:
                left = PROMPT - begin
            else:
                other, quarter = divmod((begin - PAD) // size, 2)
                left = sc[4] - (2 * quarter + (sc[2] ^ other)) * size
            bias = jnp.where((lane == 3) & (line >= left), neg_big, 0.0)
            for h in range(2):
                extra_ref[h, begin : begin + size] = (bias + ones[h]).astype(bf16)

    rows = jnp.where(step < 2, own[...], other[...])
    low = (ratio[0] * dot(rows, enc[...], NT) + vec[6:7, :]).astype(bf16)
    x_ref[...] = low
    for h in range(2):
        q_ref[h] = (dot(low, wp[h, :, 0:HEAD], NN) + bias[h : h + 1, 0:HEAD]).astype(bf16)

    def keys_from(source):
        for h in range(2):
            key = dot(source, wp[h, :, HEAD : 2 * HEAD], NN).astype(bf16)
            shift = bias[h : h + 1, HEAD : 2 * HEAD]
            value = (dot(source, wp[h, :, 2 * HEAD : 3 * HEAD], NN) + shift).astype(bf16)
            k_ref[h] = key
            v_ref[h] = value
            kt_ref[h] = key.T
            vt_ref[h] = value.T

    @pl.when(step % 2 == 0)
    def _():
        keys_from(low)

    @pl.when(step % 2 == 1)
    def _():
        keys_from(prompt[...].T)


def project(ratio, places, own, other, enc, vec, wp, bias, prompt):
    half = own.shape[0] // 2
    width = enc.shape[0]
    keys = PAD + SLOTS
    spot = lambda i: jnp.where(i % 2 == 0, 2 + i // 2, i // 2)
    tall = pl.BlockSpec((2, half, HEAD), lambda i: (0, spot(i), 0))
    flat = pl.BlockSpec((2, HEAD, half), lambda i: (0, 0, spot(i)))
    return pl.pallas_call(
        project_body,
        grid=(4,),
        in_specs=[
            pl.BlockSpec(memory_space=pltpu.SMEM),
            pl.BlockSpec(memory_space=pltpu.SMEM),
            pl.BlockSpec((half, WIDE), lambda i: (jnp.minimum(i, 1), 0)),
            pl.BlockSpec((half, WIDE), lambda i: (jnp.maximum(i - 2, 0), 0)),
            whole(),
            whole(),
            whole(),
            whole(),
            pl.BlockSpec((width, half), lambda i: (0, i // 2)),
        ],
        out_specs=[
            pl.BlockSpec((half, width), lambda i: (i, 0)),
            pl.BlockSpec((2, half, HEAD), lambda i: (0, i, 0)),
            tall,
            flat,
            tall,
            flat,
            pl.BlockSpec((2, keys, WIDE), lambda i: (0, 0, 0)),
        ],
        out_shape=[
            pltpu.HBM((4 * half, width), bf16),
            pltpu.HBM((2, 4 * half, HEAD), bf16),
            pltpu.HBM((2, keys, HEAD), bf16),
            pltpu.HBM((2, HEAD, keys), bf16),
            pltpu.HBM((2, keys, HEAD), bf16),
            pltpu.HBM((2, HEAD, keys), bf16),
            pltpu.HBM((2, keys, WIDE), bf16),
        ],
        compiler_params=pltpu.CompilerParams(vmem_limit_bytes=32 << 20),
        cost_estimate=cost(9),
        name="project",
    )(ratio, places, *held((own, other, enc, vec, wp, bias, prompt)))


CHUNK = 1024
base_two = 1.4426950408889634


def three_terms(value):
    high = value.astype(bf16).astype(f32)
    middle = (value - high).astype(bf16).astype(f32)
    return high, middle, value - high - middle


def attend_body(q_ref, k_ref, x_ref, vt_ref, o_ref, extra_ref, *scratch):
    head = pl.program_id(0)
    keys, size = scratch[0].shape
    count = q_ref.shape[1] // size
    steepness = score_scale * base_two
    lane = lax.broadcasted_iota(jnp.int32, (size, WIDE), 1)
    place = lax.broadcasted_iota(jnp.int32, (WIDE, size), 0)
    one = jnp.where(lane == 3, 1.0, 0.0).astype(bf16)
    top = None
    for b in range(count + 1):
        fresh_ref, old_ref = scratch[b % 2], scratch[(b + 1) % 2]
        if b < count:
            query = jnp.concatenate([q_ref[0, b * size : (b + 1) * size], one], axis=1)
            partial = jnp.full((8, size), -jnp.inf, f32)
        if b > 0:
            shift = top * steepness
            total = jnp.zeros((8, size), f32)
            out = jnp.zeros((HEAD, size), f32)
        for c in range(keys // CHUNK):
            span = slice(c * CHUNK, (c + 1) * CHUNK)
            if b < count:
                wide = jnp.concatenate([k_ref[0, span], x_ref[0, span]], axis=1)
                fresh = dot(wide, query, NT)
                fresh_ref[span] = fresh
                partial = jnp.maximum(partial, jnp.max(fresh.reshape(CHUNK // 8, 8, size), axis=0))
            if b > 0:
                raised = jnp.exp2(old_ref[span] * steepness - shift)
                total = total + jnp.sum(raised.reshape(CHUNK // 8, 8, size), axis=0)
                out = out + dot(vt_ref[0, :, span], raised.astype(bf16), NN)
        if b > 0:
            rows = slice((b - 1) * size, b * size)
            total = jnp.sum(total, axis=0, keepdims=True)
            o_ref[rows] = (out / total).T.astype(bf16)
            terms = three_terms(-(top + jnp.log(total) / score_scale))
            tile = jnp.where(place == 3, 1.0, 0.0)
            for k in range(3):
                tile = tile + jnp.where(place == 4 * head + k, terms[k], 0.0)
            extra_ref[0, rows] = tile.T.astype(bf16)
        if b < count:
            top = jnp.max(partial, axis=0, keepdims=True)


BLOCK = 512


def attend(q, k, extra, vt, which):
    keys = k.shape[1]
    tall = pl.BlockSpec((1, keys, HEAD), lambda h: (h, 0, 0))
    return pl.pallas_call(
        attend_body,
        grid=(2,),
        in_specs=[
            pl.BlockSpec((1, SLOTS, HEAD), lambda h: (h, which, 0)),
            tall,
            pl.BlockSpec((1, keys, WIDE), lambda h: (0, 0, 0)),
            pl.BlockSpec((1, HEAD, keys), lambda h: (h, 0, 0)),
        ],
        out_specs=[
            pl.BlockSpec((SLOTS, HEAD), lambda h: (0, h)),
            pl.BlockSpec((1, SLOTS, WIDE), lambda h: (h, 0, 0)),
        ],
        out_shape=[pltpu.HBM((SLOTS, 2 * HEAD), bf16), pltpu.HBM((2, SLOTS, WIDE), bf16)],
        scratch_shapes=[pltpu.VMEM((keys, BLOCK), f32)] * 2,
        compiler_params=pltpu.CompilerParams(vmem_limit_bytes=32 << 20),
        cost_estimate=cost(6),
        name="attend",
    )(*held((q, k, extra, vt), False))


BACK_BLOCK = 256
BACK_CHUNK = 2048


def attend_back_body(q_ref, k_ref, x_ref, kt_ref, v_ref, qa_ref, qb_ref, da_ref, db_ref, ea_ref, eb_ref, dq_ref, dk_ref, dv_ref, *scratch):
    size = scratch[0].shape[1]
    keys = k_ref.shape[1]
    rows = q_ref.shape[1]
    count = rows // size
    steepness = score_scale * base_two
    mine = pl.program_id(1) == 0

    @pl.when(mine)
    def _():
        dk_ref[...] = jnp.zeros_like(dk_ref)
        dv_ref[...] = jnp.zeros_like(dv_ref)

    for b in range(count + 1):
        probs_ref, slopes_ref = scratch[2 * (b % 2) : 2 * (b % 2) + 2]
        old_probs, old_slopes = scratch[2 - 2 * (b % 2) : 4 - 2 * (b % 2)]
        if b < count:
            span = slice(b * size, (b + 1) * size)
            query = q_ref[0, span]
            grad = jnp.where(mine, da_ref[span], db_ref[span])
            aside = jnp.where(mine, qa_ref[0, span], qb_ref[0, span])
            sums = jnp.where(mine, ea_ref[span], eb_ref[span])
            query_wide = jnp.concatenate([query, aside], axis=1)
            grad_wide = jnp.concatenate([grad, sums], axis=1)
        if b > 0:
            back = jnp.zeros((HEAD, size), f32)
        for c in range(keys // BACK_CHUNK):
            span = slice(c * BACK_CHUNK, (c + 1) * BACK_CHUNK)
            if b < count:
                extra = x_ref[0, span]
                scores = dot(jnp.concatenate([k_ref[0, span], extra], axis=1), query_wide, NT)
                slopes = dot(jnp.concatenate([v_ref[0, span], extra], axis=1), grad_wide, NT)
                probs = jnp.exp2(scores * steepness)
                probs_ref[span] = probs.astype(bf16)
                slopes_ref[span] = (probs * slopes).astype(bf16)
            if b > 0:
                back = back + dot(kt_ref[0, :, span], old_slopes[span], NN)
                grad_key = dot(query_flip, old_slopes[span], NT) * score_scale
                grad_value = dot(grad_flip, old_probs[span], NT)
                dk_ref[0, :, span] += grad_key
                dv_ref[0, :, span] += grad_value
        if b > 0:
            dq_ref[(b - 1) * size : b * size] = (back * score_scale).T.astype(bf16)
        if b < count:
            query_flip, grad_flip = query.T, grad.T


def attend_back(q, k, extra, kt, v, extra_own, extra_other, grad_own, grad_other):
    keys = k.shape[1]
    tall = pl.BlockSpec((1, keys, HEAD), lambda h, i: (h, 0, 0))
    flat = pl.BlockSpec((1, HEAD, keys), lambda h, i: (h, 0, 0))
    aside = pl.BlockSpec((1, SLOTS, WIDE), lambda h, i: (h, 0, 0))
    grad = pl.BlockSpec((SLOTS, HEAD), lambda h, i: (0, h))
    sums = pl.BlockSpec((SLOTS, HEAD), lambda h, i: (0, 2))
    return pl.pallas_call(
        attend_back_body,
        grid=(2, 2),
        in_specs=[
            pl.BlockSpec((1, SLOTS, HEAD), lambda h, i: (h, i, 0)),
            tall,
            tall,
            flat,
            tall,
            aside,
            aside,
            grad,
            grad,
            sums,
            sums,
        ],
        out_specs=[pl.BlockSpec((SLOTS, HEAD), lambda h, i: (i, h)), flat, flat],
        out_shape=[
            pltpu.HBM((2 * SLOTS, 2 * HEAD), bf16),
            pltpu.HBM((2, HEAD, keys), f32),
            pltpu.HBM((2, HEAD, keys), f32),
        ],
        scratch_shapes=[pltpu.VMEM((keys, BACK_BLOCK), bf16)] * 4,
        compiler_params=pltpu.CompilerParams(vmem_limit_bytes=40 << 20),
        cost_estimate=cost(20),
        name="attend_back",
    )(
        *held((q, k, extra, kt, v, extra_own, extra_other), False),
        *held((grad_own, grad_other, grad_own, grad_other), (False, True, False, True)),
    )


tail_slope = 0.32
tail_terms = (
    0.1276615327396569,
    0.12766067896437439,
    0.1146273959793329,
    0.0877866398778977,
    0.058846245380943685,
    -0.009886160894676655,
    0.0661375104847692,
    -0.14747037514007924,
    0.09579928012384316,
    -0.02116276404130493,
)


def gelu_pair(t):
    bell = jnp.exp2(t * t * (-0.5 * base_two))
    k = 1.0 / (1.0 + tail_slope * jnp.abs(t))
    series = jnp.full_like(t, tail_terms[-1])
    for term in tail_terms[-2::-1]:
        series = series * k + term
    tail = series * k * bell
    cumulative = jnp.where(t >= 0.0, 1.0 - tail, tail)
    return t * cumulative, cumulative + t * (bell * 0.3989422804014327)


def middle_body(
    sc,
    ratio,
    rows_ref,
    oa_ref,
    ob_ref,
    c0,
    c1,
    c2,
    c3,
    enc,
    vec,
    b1,
    ra,
    rb,
    y0,
    y1,
    y2,
    y3,
    da_ref,
    db_ref,
    dr_ref,
    ga,
    gb,
    gvec,
    gb1,
    cot,
    late,
    acc,
):
    step = pl.program_id(0)
    count = rows_ref.shape[0]
    part = count // 2

    def quarter_rows(k):
        return pl.ds(pl.multiple_of((sc[1] ^ (k % 2)) * part, part), part)

    for k, ref in enumerate((c0, c1, c2, c3)):

        @pl.when(step == k // 2)
        def _(k=k, ref=ref):
            cot[quarter_rows(k), :] = ref[...]

    @pl.when(step == 0)
    def _():
        gvec[...] = jnp.zeros_like(gvec)
        gb1[...] = jnp.zeros_like(gb1)

    def gather(k, low, high, value):
        acc[k, :, low:high] = jnp.where(step > 0, acc[k, :, low:high], 0.0) + value

    group = sc[0] ^ step
    limit = jnp.where(group == 0, sc[4], sc[5])
    line = lax.broadcasted_iota(jnp.int32, (count, 1), 0)
    slot = line + sc[2] * part + jnp.where(line >= part, part, 0)
    live = (slot < limit).astype(f32)

    def weight(k, low, high):
        return (ra if k < 2 else rb)[k % 2, :, low:high]

    def row(k):
        return vec[k : k + 1, :]

    gain_one, shift_one, gain_two, shift_two, b_out, b_two, b_enc = (row(k) for k in range(7))
    embedded = ratio[0] * dot(rows_ref[...], enc[...], NT) + b_enc
    out_pair = [
        jnp.concatenate([weight(2 * k, 0, HEAD), weight(2 * k + 1, 0, HEAD)], axis=1)
        for k in (0, 1)
    ]
    attn = dot(oa_ref[...], out_pair[0], NT) + dot(ob_ref[...], out_pair[1], NT) + b_out

    def norm(residual):
        centred = residual - jnp.mean(residual, axis=-1, keepdims=True)
        inverse = lax.rsqrt(jnp.mean(centred * centred, axis=-1, keepdims=True) + ln_eps)
        return centred * inverse, inverse

    def back(grad, normed, inverse, gain):
        scaled = grad * gain
        plain = jnp.mean(scaled, axis=-1, keepdims=True)
        mixed = jnp.mean(scaled * normed, axis=-1, keepdims=True)
        return inverse * (scaled - plain - normed * mixed)

    def add_row(k, value):
        gvec[k : k + 1, :] += jnp.sum(value, axis=0, keepdims=True)

    normed_one, inverse_one = norm(embedded + attn)
    first = normed_one * gain_one + shift_one
    first_low = first.astype(bf16)
    mlp = b_two
    acts, slopes = [], []
    for k in range(4):
        pre = dot(first_low, weight(k, HEAD, HEAD + HID), NN) + b1[k : k + 1, 2 * HEAD :]
        act, slope = gelu_pair(pre)
        acts.append(act.astype(bf16))
        slopes.append(slope)
        mlp = mlp + dot(acts[k], weight(k, HEAD + HID, HEAD + 2 * HID), NT)
    normed_two, inverse_two = norm(first + mlp)
    late[...] = ((normed_two * gain_two + shift_two) * live).astype(bf16)
    for k, ref in enumerate((y0, y1, y2, y3)):

        @pl.when(step == k // 2)
        def _(k=k, ref=ref):
            ref[...] = late[quarter_rows(k), :]

    grad_y = cot[...].astype(f32) * live
    add_row(2, grad_y * normed_two)
    add_row(3, grad_y)
    grad_two = back(grad_y, normed_two, inverse_two, gain_two)
    grad_low = grad_two.astype(bf16)
    add_row(5, grad_low.astype(f32))
    grad_flip = grad_low.T
    first_flip = first_low.T
    grad_first = grad_two
    for k in range(4):
        gather(k, HEAD + HID, HEAD + 2 * HID, dot(grad_flip, acts[k], NN))
        grad_act = dot(grad_low, weight(k, HEAD + HID, HEAD + 2 * HID), NN)
        grad_pre = (grad_act * slopes[k]).astype(bf16)
        gb1[k : k + 1, :] += jnp.sum(grad_pre.astype(f32), axis=0, keepdims=True)
        gather(k, HEAD, HEAD + HID, dot(first_flip, grad_pre, NN))
        grad_first = grad_first + dot(grad_pre, weight(k, HEAD, HEAD + HID), NT)
    add_row(0, grad_first * normed_one)
    add_row(1, grad_first)
    grad_one = back(grad_first, normed_one, inverse_one, gain_one)
    dr_ref[...] = grad_one
    attn_low = grad_one.astype(bf16)
    add_row(4, attn_low.astype(f32))
    attn_flip = attn_low.T
    for k, (source, target) in enumerate(((oa_ref, da_ref), (ob_ref, db_ref))):
        both = dot(attn_flip, source[...], NN)
        gather(2 * k, 0, HEAD, both[:, 0:HEAD])
        gather(2 * k + 1, 0, HEAD, both[:, HEAD:])
        both = dot(attn_low, out_pair[k], NN).astype(bf16)
        target[:, 0 : 2 * HEAD] = both
        product = both.astype(f32) * source[...].astype(f32)
        lane = lax.broadcasted_iota(jnp.int32, (count, WIDE), 1)
        tile = jnp.zeros((count, WIDE), f32)
        for h in range(2):
            sums = jnp.sum(product[:, h * HEAD : (h + 1) * HEAD], axis=1, keepdims=True)
            for m, term in enumerate(three_terms(-sums)):
                tile = tile + jnp.where(lane == 4 * h + m, term, 0.0)
        target[:, 2 * HEAD :] = tile.astype(bf16)

    @pl.when(step == 1)
    def _():
        ga[...] = acc[0:2].astype(bf16)
        gb[...] = acc[2:4].astype(bf16)


def middle(sc, ratio, rows, o_own, o_other, cots, enc, vec, b1, rest_own, rest_other):
    size = rows.shape[0] // 4
    block = 2 * size
    width = enc.shape[0]
    spot = lambda i, sc: (sc[0] ^ i, 0)
    pair = pl.BlockSpec((block, 2 * HEAD), spot)
    smem = pl.BlockSpec(memory_space=pltpu.SMEM)
    fixed = pl.BlockSpec((size, width), lambda i, sc: (0, 0))
    weight = rest_own.shape
    return pl.pallas_call(
        middle_body,
        grid_spec=pltpu.PrefetchScalarGridSpec(
            num_scalar_prefetch=1,
            grid=(2,),
            in_specs=[smem, pl.BlockSpec((block, WIDE), spot), pair, pair]
            + [fixed] * 4
            + [whole()] * 5,
            out_specs=[fixed] * 4
            + [pl.BlockSpec((block, 3 * HEAD), spot)] * 2
            + [pl.BlockSpec((block, width), spot)]
            + [
                pl.BlockSpec(weight, lambda i, sc: (0, 0, 0)),
                pl.BlockSpec(weight, lambda i, sc: (0, 0, 0)),
                pl.BlockSpec((8, width), lambda i, sc: (0, 0)),
                pl.BlockSpec((4, HID), lambda i, sc: (0, 0)),
            ],
            scratch_shapes=[
                pltpu.VMEM((block, width), bf16),
                pltpu.VMEM((block, width), bf16),
                pltpu.VMEM((4,) + weight[1:], f32),
            ],
        ),
        out_shape=[pltpu.VMEM((size, width), bf16)] * 4
        + [
            pltpu.HBM((4 * size, 3 * HEAD), bf16),
            pltpu.HBM((4 * size, 3 * HEAD), bf16),
            pltpu.HBM((4 * size, width), f32),
            pltpu.VMEM(weight, bf16),
            pltpu.VMEM(weight, bf16),
            pltpu.HBM((8, width), f32),
            pltpu.HBM((4, HID), f32),
        ],
        compiler_params=pltpu.CompilerParams(vmem_limit_bytes=44 << 20),
        cost_estimate=cost(25),
        name="middle",
    )(
        sc,
        ratio,
        rows,
        o_own,
        o_other,
        *held(cots),
        enc,
        vec,
        b1,
        *held((rest_own, rest_other)),
    )


def held(args, near=True):
    if isinstance(near, bool):
        near = [near] * len(args)
    spaces = [pltpu.VMEM if flag else pltpu.HBM for flag in near]
    return tuple(map(pltpu.with_memory_space_constraint, args, spaces))


def simple(body, out_shape, *args, scalars=None, scratch=(), near=(True, True), name=None):
    specs = [whole()] * len(args)
    args = held(args, near[0])
    if scalars is not None:
        specs = [pl.BlockSpec(memory_space=pltpu.SMEM)] + specs
        args = (scalars,) + args
    many = isinstance(out_shape, (list, tuple))
    if near[1]:
        kept = lambda shape: pltpu.VMEM(shape.shape, shape.dtype)
        out_shape = [kept(shape) for shape in out_shape] if many else kept(out_shape)
    return pl.pallas_call(
        body,
        in_specs=specs,
        out_specs=[whole()] * len(out_shape) if many else whole(),
        out_shape=out_shape,
        scratch_shapes=scratch,
        compiler_params=pltpu.CompilerParams(vmem_limit_bytes=16 << 20),
        cost_estimate=cost(2),
        name=name,
    )(*args)


def place(parts, index, name, near=(True, True)):
    def body(sc, *refs):
        for k, ref in enumerate(refs[:-1]):
            refs[-1][sc[0] ^ k] = ref[...]

    first = parts[0]
    return simple(
        body,
        shape_of((len(parts),) + first.shape, first.dtype),
        *parts,
        scalars=index.reshape(1).astype(jnp.int32),
        near=near,
        name=name,
    )


TAIL = 3 * HEAD
FEAT_ROWS = 112
LAST = 112
VEC = 104


def spread(row):
    parts = row.reshape(row.shape[:-1] + (4, row.shape[-1] // 4))
    room = WIDE - LAST - parts.shape[-1]
    return jnp.pad(parts, [(0, 0)] * (parts.ndim - 1) + [(LAST, room)])


def widened(prompt):
    return jnp.pad(prompt, [(0, 0)] * (prompt.ndim - 1) + [(0, 3 * TAIL - prompt.shape[-1])])


def with_bias(prompt, bias):
    row = jnp.pad(
        bias[..., None, :].astype(prompt.dtype),
        [(0, 0)] * (bias.ndim - 1)
        + [(0, prompt.shape[-2] - 1), (PAD, 3 * TAIL - PAD - bias.shape[-1])],
    )
    return widened(prompt) + row


def in_chunks(wide):
    lead, strip = wide.shape[:-2], wide.shape[-2]
    parts = jnp.swapaxes(wide.reshape(lead + (strip, 3, TAIL)), -3, -2)
    return parts.reshape(lead + (3 * strip, TAIL))


def pack_parts(block, prompt, encoder, vectors, biases):
    slab, strip = block.shape[0], prompt.shape[0]
    flat = block.reshape(slab * 8, HEAD)
    out = [shape_of((slab + 3 * strip, TAIL), bf16), shape_of((slab, 8 * HEAD - TAIL), bf16)]
    if 2 * slab != WIDE:
        low = block.reshape(slab, 8 * HEAD).astype(bf16)
        small = jnp.concatenate(
            [
                jnp.pad(encoder, ((0, 0), (0, VEC - FEAT))),
                jnp.pad(vectors, ((0, 0), (0, LAST - VEC - 7))),
                jnp.pad(biases.reshape(strip, 4), ((0, 0), (0, WIDE - LAST - 4))),
            ],
            axis=1,
        )
        chunks = in_chunks(
            jnp.concatenate([jnp.pad(prompt, ((0, 0), (0, PAD - PROMPT))), small], axis=1)
        )
        return jnp.concatenate([low[:, 0:TAIL], chunks.astype(bf16)], axis=0), low[:, TAIL:]

    def body(block_ref, prompt_ref, enc_ref, vec_ref, bias_ref, main_ref, rest_ref, tall, tile, line):
        for j in range(8):
            lanes = block_ref[pl.ds(j, slab, stride=8), :].astype(bf16)
            if j < 3:
                main_ref[0:slab, j * HEAD : (j + 1) * HEAD] = lanes
            else:
                rest_ref[:, (j - 3) * HEAD : (j - 2) * HEAD] = lanes
        low = prompt_ref[...].astype(bf16)
        for k in range(2):
            rows = slice(slab + k * strip, slab + (k + 1) * strip)
            main_ref[rows, :] = low[:, k * TAIL : (k + 1) * TAIL]
        rows = slice(slab + 2 * strip, slab + 3 * strip)
        main_ref[rows, WIDE : 2 * WIDE] = jnp.zeros((strip, WIDE), bf16)
        main_ref[rows, 0 : PROMPT - 2 * TAIL] = low[:, 2 * TAIL :]
        tall[...] = jnp.zeros_like(tall)
        tall[VEC : VEC + 7, :] = vec_ref[...]
        tile[...] = tall[...].T
        tile[:, 0:FEAT] = enc_ref[...]
        line[...] = jnp.zeros_like(line)
        line[:, 0:slab] = bias_ref[...]
        main_ref[rows, 2 * WIDE :] = (tile[...] + spread_row(line[...], strip)).astype(bf16)

    return simple(
        body,
        out,
        flat,
        prompt,
        encoder,
        vectors.T,
        biases.T,
        near=(False, True),
        scratch=[
            pltpu.VMEM((WIDE, strip), f32),
            pltpu.VMEM((strip, WIDE), f32),
            pltpu.VMEM((1, WIDE), f32),
        ],
        name="pack_parts",
    )


def spread_row(row, strip):
    place = lax.broadcasted_iota(jnp.int32, (strip, WIDE), 0)
    lane = lax.broadcasted_iota(jnp.int32, (strip, WIDE), 1)
    total = jnp.zeros((strip, WIDE), f32)
    for k in range(4):
        turned = jnp.broadcast_to(pltpu.roll(row, LAST - k * strip, 1), (strip, WIDE))
        total = total + jnp.where((place == k) & (lane >= LAST), turned, 0.0)
    return total


def gathered_row(tile, strip):
    lane = lax.broadcasted_iota(jnp.int32, (1, WIDE), 1)
    total = jnp.zeros((1, WIDE), f32)
    for k in range(4):
        turned = pltpu.roll(tile[k : k + 1], (k * strip - LAST) % WIDE, 1)
        total = total + jnp.where(lane // strip == k, turned, 0.0)
    return total


FEAT_SPAN = 80
FEAT_CUTS = ((0, 0, 0, 0, 80), (1, 0, 0, 80, 112), (1, 32, 1, 0, 48), (2, 0, 1, 48, 112))


def build_main(parts, flipped, places):
    count = len(parts)
    size, lanes = parts[0].shape
    feats, rows = flipped.shape[1:]

    def body(sc, *refs):
        ins, flip_ref, outs = refs[:count], refs[count], refs[count + 1 :]
        for k, out in enumerate(outs):
            for e, ref in enumerate(ins):
                at = pl.multiple_of((sc[6] ^ e) * size, 16)
                out[pl.ds(at, size), :] = ref[...]
            wide = jnp.concatenate(
                [flip_ref[sc[3] ^ k], jnp.zeros((FEAT_ROWS - feats, rows), bf16)], axis=0
            )
            for column, row, tile, begin, end in FEAT_CUTS:
                at = slice(count * size + row, count * size + row + end - begin)
                part = wide[begin:end, tile * WIDE : (tile + 1) * WIDE]
                out[at, column * WIDE : (column + 1) * WIDE] = part

    shape = shape_of((count * size + FEAT_SPAN, lanes), bf16)
    return simple(body, [shape] * 4, *parts, flipped, scalars=places, name="build_main")


def join_features(parts, places):
    feats, rows = parts[0].shape

    def body(sc, *refs):
        for k, ref in enumerate(refs[:-1]):
            spot = 2 * (sc[0] ^ (k // 2)) + (sc[1] ^ (k % 2))
            refs[-1][spot, 0:feats] = ref[...]

    return simple(
        body, shape_of((4, FEAT_ROWS, rows), bf16), *parts, scalars=places, name="join_features"
    )


def unpack_main(tops, lows, feats, feats_low, mask, places, n_ep, slab, strip, rows):
    plain = 2 * slab != WIDE
    size = slab + 3 * strip
    shapes = [
        shape_of((2, n_ep, 2, slab, TAIL), bf16),
        shape_of((n_ep, 2, 2, 2, strip, 3 * TAIL), bf16),
        shape_of((n_ep, 2, 2, 2, strip, WIDE), bf16),
        shape_of((8, n_ep * 2 * slab), f32),
        shape_of((4, n_ep * 2 * slab), f32),
        shape_of((4 * rows, WIDE), bf16),
        shape_of((4 * rows, WIDE), bf16),
    ]

    def features(mask_ref, source, target):
        for p in range(4):
            flip = jnp.concatenate([source[p], jnp.zeros((WIDE - FEAT_ROWS, rows), bf16)], axis=0)
            piece = jnp.where(mask_ref[...] > 0.0, flip.T.astype(f32), 0.0).astype(bf16)
            target[p * rows : (p + 1) * rows, :] = piece

    if plain:
        side, row, core = places[0], places[1], places[2]

        def ordered(parts, axis):
            cores = []
            for group in parts:
                sides = []
                for b in (0, 1):
                    sides.append(jnp.stack(pick(group[2 * b], group[2 * b + 1], row), axis=axis))
                cores.append(jnp.stack(pick(sides[0], sides[1], side), axis=axis))
            return jnp.stack(pick(cores[0], cores[1], core), axis=axis + 2)

        heads = [
            jnp.stack(pick(tops[r][:, 0:slab], tops[2 + r][:, 0:slab], side), axis=1) for r in (0, 1)
        ]
        chunks = ordered([[t[:, slab:] for t in tops], [t[:, slab:] for t in lows]], 1)
        chunks = chunks.reshape((n_ep, 2, 2, 2, 3, strip, TAIL))
        wide = jnp.swapaxes(chunks, -3, -2).reshape((n_ep, 2, 2, 2, strip, 3 * TAIL))
        small = wide[..., PAD:]
        vec = small.reshape(n_ep * 8 * strip, WIDE).astype(f32).T[VEC : VEC + 8]
        biases = []
        for group in (tops, lows):
            for r in (0, 1):
                pair = [
                    group[2 * b + r][:, slab + 2 * strip :, PAD - 2 * TAIL + LAST :][..., 0:4]
                    for b in (0, 1)
                ]
                biases.append(jnp.stack(pick(pair[0], pair[1], side), axis=1).reshape(-1))
        def both(mask_ref, a, b, c, d):
            features(mask_ref, a, c)
            features(mask_ref, b, d)

        masked = simple(
            both,
            shapes[5:],
            mask,
            feats,
            feats_low,
            near=(False, False),
            name="features",
        )
        return [jnp.stack(heads), wide, small, vec, jnp.stack(biases).astype(f32), *masked]

    def body(sc, t0, t1, t2, t3, l0, l1, l2, l3, mask_ref, *outs):
        wp_ref, prompt_ref, small_ref, vec_ref, bias_ref, own_ref, other_ref = outs
        side, row, core = sc[0], sc[1], sc[2]
        groups = ((t0, t1, t2, t3), (l0, l1, l2, l3))
        bias_tiles = {}
        for b in range(2):
            for r in range(2):
                k = 2 * b + r
                for other in range(2):
                    spot = core ^ other
                    source = groups[other][k]
                    full = source[0 : n_ep * size].reshape(n_ep, size, TAIL)
                    if other == 0:
                        wp_ref[r, :, side ^ b] = full[:, 0:slab, :]
                    part = full[:, slab:, :]
                    tiles = ([], [])
                    for column, line, tile, begin, end in FEAT_CUTS:
                        at = slice(n_ep * size + line, n_ep * size + line + end - begin)
                        tiles[tile].append(source[at, column * WIDE : (column + 1) * WIDE])
                    blank = jnp.zeros((WIDE - FEAT_ROWS, rows), bf16)
                    flip = jnp.concatenate([jnp.concatenate(t, axis=0) for t in tiles], axis=1)
                    flip = jnp.concatenate([flip, blank], axis=0)
                    piece = jnp.where(mask_ref[...] > 0.0, flip.T.astype(f32), 0.0).astype(bf16)
                    at = pl.multiple_of((2 * (side ^ b) + (row ^ r)) * rows, rows)
                    (other_ref if other else own_ref)[pl.ds(at, rows), :] = piece
                    for j in range(3):
                        lanes = slice(j * TAIL, (j + 1) * TAIL)
                        span = slice(j * strip, (j + 1) * strip)
                        prompt_ref[:, side ^ b, row ^ r, spot, :, lanes] = part[:, span, :]
                    tile = part[:, 2 * strip :, TAIL - WIDE :]
                    small_ref[:, side ^ b, row ^ r, spot] = tile
                    bias_tiles[b, r, other] = tile.astype(f32)
        flip = small_ref[...].reshape(n_ep * 8 * strip, WIDE).astype(f32).T
        vec_ref[...] = flip[VEC : VEC + 8]
        low_half = lax.broadcasted_iota(jnp.int32, (1, WIDE), 1) < slab
        for r in range(2):
            for other in range(2):
                for e in range(n_ep):
                    mine = gathered_row(bias_tiles[0, r, other][e], strip)
                    theirs = gathered_row(bias_tiles[1, r, other][e], strip)
                    first = jnp.where(side == 0, mine, theirs)
                    second = jnp.where(side == 0, theirs, mine)
                    row_tile = jnp.where(low_half, first, pltpu.roll(second, slab, 1))
                    k = r + 2 * other
                    bias_ref[k : k + 1, e * WIDE : (e + 1) * WIDE] = row_tile

    return simple(body, shapes, *tops, *lows, mask, scalars=places, name="unpack_main")


def unpack_rest(tops, lows, places):
    n_ep, slab, width = tops[0].shape

    def body(sc, *refs):
        for k in range(8):
            refs[8 + k // 4][k % 2, :, sc[0] ^ (k % 4 // 2)] = refs[k][...]

    return simple(
        body,
        [shape_of((2, n_ep, 2, slab, width), bf16)] * 2,
        *tops,
        *lows,
        scalars=places,
        name="unpack_rest",
    )


def weight_body(n_ep, strip, sc, x_ref, dq_ref, dk_ref, dv_ref, prompt, wp, gb1, gw_ref, mine_ref, sent_ref, own_ref, other_ref, acc, gq_ref, gv_ref, gp_ref, gb_ref):
    step = pl.program_id(0)

    @pl.when(step == 0)
    def _():
        acc[...] = jnp.zeros_like(acc)
        gq_ref[...] = jnp.zeros_like(gq_ref)
        gv_ref[...] = jnp.zeros_like(gv_ref)

    def columns(k):
        return jnp.concatenate([wp[h, :, k * HEAD : (k + 1) * HEAD] for h in range(2)], axis=1)

    flip = x_ref[...].T
    grad_query = dq_ref[...]
    acc[0] += dot(flip, grad_query, NN)
    gq_ref[...] += jnp.sum(grad_query.astype(f32), axis=0, keepdims=True)
    grad_key = jnp.concatenate([dk_ref[h] for h in range(2)], axis=0)
    grad_value = jnp.concatenate([dv_ref[h] for h in range(2)], axis=0)
    key_high = grad_key.astype(bf16)
    value_high = grad_value.astype(bf16)
    ones = jnp.ones((8, grad_key.shape[1]), bf16)
    gv_ref[...] += dot(ones, value_high, NT)[0:1]
    back = dot(grad_query, columns(0), NT)

    def store(value):
        @pl.when(step < 2)
        def _():
            own_ref[...] = value

        @pl.when(step >= 2)
        def _():
            other_ref[...] = value.astype(bf16)

    @pl.when(step % 2 == 0)
    def _():
        acc[1] += dot(flip, key_high, NT)
        acc[2] += dot(flip, value_high, NT)
        store(back + dot(key_high.T, columns(1), NT) + dot(value_high.T, columns(2), NT))

    @pl.when(step % 2 == 1)
    def _():
        store(back)
        key_low = (grad_key - key_high.astype(f32)).astype(bf16)
        value_low = (grad_value - value_high.astype(f32)).astype(bf16)
        source = prompt[...]
        acc[1] += dot(source, key_high, NT) + dot(source, key_low, NT)
        acc[2] += dot(source, value_high, NT) + dot(source, value_low, NT)
        gv_ref[...] += dot(ones, value_low, NT)[0:1]
        total = dot(columns(1), key_high, NN) + dot(columns(1), key_low, NN)
        total = total + dot(columns(2), value_high, NN) + dot(columns(2), value_low, NN)
        gp_ref[step // 2] = total.astype(bf16)

    @pl.when(step == 3)
    def _():
        for h in range(2):
            for k in range(3):
                lanes = slice(h * HEAD, (h + 1) * HEAD)
                gw_ref[h, :, k * HEAD : (k + 1) * HEAD] = acc[k, :, lanes].astype(bf16)
            gb_ref[h : h + 1, 0:HEAD] = gq_ref[:, h * HEAD : (h + 1) * HEAD]
            gb_ref[h : h + 1, HEAD : 2 * HEAD] = gv_ref[:, h * HEAD : (h + 1) * HEAD]
        gb_ref[2:4, 0 : 2 * HEAD] = jnp.zeros((2, 2 * HEAD), f32)
        gb_ref[:, 2 * HEAD :] = gb1[...]
        if strip % 16:
            mine_ref[...] = gp_ref[...]
            sent_ref[...] = gb_ref[...]
            return
        half = gp_ref.shape[2]
        row, core = sc[1], sc[2]
        first = lax.broadcasted_iota(jnp.int32, (strip, WIDE), 0) == 0
        low_half = lax.broadcasted_iota(jnp.int32, (1, WIDE), 1) < 4 * strip
        for other, ref in enumerate((mine_ref, sent_ref)):
            for e in range(n_ep):
                for s in range(2):
                    for r in range(2):
                        y = row ^ r
                        at = ((e * 2 + s) * 2 + y) * 2 + (core ^ other)
                        at = pl.ds(pl.multiple_of(at * strip, strip), strip)
                        for tile in range(PAD // WIDE):
                            lanes = slice(tile * WIDE % half, tile * WIDE % half + WIDE)
                            j, place = tile // 3, tile % 3
                            rows = slice(j * strip, (j + 1) * strip)
                            to = slice(place * WIDE, (place + 1) * WIDE)
                            ref[e, s, y, rows, to] = gp_ref[tile * WIDE // half, at, lanes]
                        k = r + 2 * other
                        tile = gb_ref[k : k + 1, e * WIDE : (e + 1) * WIDE]
                        if s == 1:
                            tile = pltpu.roll(tile, WIDE - 4 * strip, 1)
                        tile = jnp.where(low_half, tile, 0.0)
                        tile = jnp.where(first, tile, 0.0).astype(bf16)
                        ref[e, s, y, 2 * strip : 3 * strip, 2 * WIDE :] = tile


def weight_grads(places, x, dq, dk, dv, prompt, wp, gb1, n_ep, strip):
    half = x.shape[0] // 4
    width = wp.shape[1]
    spot = lambda i: jnp.where(i % 2 == 0, 2 + i // 2, i // 2)
    key = pl.BlockSpec((2, HEAD, half), lambda i: (0, 0, spot(i)))
    if strip % 16:
        shapes = [pltpu.VMEM((2, width, half), bf16), pltpu.VMEM((4, width), f32)]
    else:
        strips = (n_ep, 2, 2, 3 * strip, TAIL)
        shapes = [pltpu.HBM(strips, bf16), pltpu.VMEM(strips, bf16)]
    fixed = [
        pl.BlockSpec(shape.shape, functools.partial(lambda n, i: (0,) * n, len(shape.shape)))
        for shape in shapes
    ]
    out = pl.pallas_call(
        functools.partial(weight_body, n_ep, strip),
        grid=(4,),
        in_specs=[
            pl.BlockSpec(memory_space=pltpu.SMEM),
            pl.BlockSpec((half, width), lambda i: (i, 0)),
            pl.BlockSpec((half, 2 * HEAD), lambda i: (i, 0)),
            key,
            key,
            pl.BlockSpec((width, half), lambda i: (0, i // 2)),
            whole(),
            whole(),
        ],
        out_specs=[pl.BlockSpec((2, width, TAIL), lambda i: (0, 0, 0))]
        + fixed
        + [
            pl.BlockSpec((half, width), lambda i: (jnp.minimum(i, 1), 0)),
            pl.BlockSpec((half, width), lambda i: (jnp.maximum(i - 2, 0), 0)),
        ],
        out_shape=[pltpu.HBM((2, width, TAIL), bf16)]
        + shapes
        + [pltpu.HBM((2 * half, width), f32), pltpu.HBM((2 * half, width), bf16)],
        scratch_shapes=[pltpu.VMEM((3, width, 2 * HEAD), f32)]
        + [pltpu.VMEM((1, 2 * HEAD), f32)] * 2
        + [pltpu.VMEM((2, width, half), bf16), pltpu.VMEM((4, width), f32)],
        compiler_params=pltpu.CompilerParams(vmem_limit_bytes=40 << 20),
        cost_estimate=cost(9),
        name="weight_grads",
    )(places, *held((x, dq, dk, dv, prompt, wp), False), gb1)
    grad_project, mine, sent, back_own, back_other = out
    if strip % 16:
        row, core = places[1], places[2]
        grad = jnp.concatenate([mine[0], mine[1]], axis=1)
        blocks = grad.reshape(n_ep, 2, 2, 2, strip, PAD)
        table = sent.reshape(2, 2, n_ep, 2, 4 * strip)
        both = []
        for other in (0, 1):
            by_row = jnp.stack(pick(table[other, 0], table[other, 1], row), axis=2)
            part = lax.dynamic_index_in_dim(blocks, core ^ other, 3, keepdims=False)
            both.append(in_chunks(with_bias(part, by_row)))
        mine, sent = both
    return grad_project, mine, sent, back_own, back_other


def input_body(sc, ratio, dr_ref, own_ref, got_ref, rows_ref, enc, mask, rows_grad, i0, i1, i2, i3, small_ref, acc, bias):
    step = pl.program_id(0)
    low = (dr_ref[...] + own_ref[...] + got_ref[...].astype(f32)).astype(bf16)
    part = dot(low.T, rows_ref[...], NN) * ratio[0]
    part_bias = jnp.sum(low.astype(f32), axis=0, keepdims=True)

    @pl.when(step == 0)
    def _():
        acc[...] = part
        bias[...] = part_bias

    @pl.when(step > 0)
    def _():
        acc[...] += part
        bias[...] += part_bias

    grad = dot(enc[...].T, low, NT)[0:FEAT_ROWS] * ratio[0] * mask[0:FEAT_ROWS]
    for k, ref in enumerate((i0, i1, i2, i3)):

        @pl.when(step == k // 2)
        def _(k=k, ref=ref):
            first = sc[1] ^ (k % 2) == 0
            part = ref.shape[1]
            ref[...] = jnp.where(first, grad[:, 0:part], grad[:, part:]).astype(bf16)

    @pl.when(step == 1)
    def _():
        width = acc.shape[0]
        rows = jnp.concatenate(
            [
                jnp.zeros((VEC, width), f32),
                rows_grad[0:6],
                bias[...],
                jnp.zeros((WIDE - VEC - 7, width), f32),
            ],
            axis=0,
        )
        small_ref[...] = (acc[...] + rows.T).astype(bf16)


def input_grads(sc, ratio, dr, own, got, rows, enc, mask, rows_grad):
    size = rows.shape[0] // 4
    width = enc.shape[0]
    spot = lambda i, sc: (sc[0] ^ i, 0)
    block = pl.BlockSpec((2 * size, width), spot)
    fixed = pl.BlockSpec((FEAT_ROWS, size), lambda i, sc: (0, 0))
    return pl.pallas_call(
        input_body,
        grid_spec=pltpu.PrefetchScalarGridSpec(
            num_scalar_prefetch=1,
            grid=(2,),
            in_specs=[
                pl.BlockSpec(memory_space=pltpu.SMEM),
                block,
                block,
                block,
                pl.BlockSpec((2 * size, WIDE), spot),
                whole(),
                whole(),
                whole(),
            ],
            out_specs=[fixed] * 4 + [pl.BlockSpec((width, WIDE), lambda i, sc: (0, 0))],
            scratch_shapes=[pltpu.VMEM((width, WIDE), f32), pltpu.VMEM((1, width), f32)],
        ),
        out_shape=[pltpu.VMEM((FEAT_ROWS, size), bf16)] * 4 + [pltpu.VMEM((width, WIDE), bf16)],
        compiler_params=pltpu.CompilerParams(vmem_limit_bytes=32 << 20),
        cost_estimate=cost(6),
        name="input_grads",
    )(sc, ratio, *held((dr, own, got, rows), False), enc, mask, rows_grad)


def split_small(grad, places, n_ep, strip):
    blocks = grad.reshape(n_ep * 4, 2, strip, WIDE)

    def body(sc, grad_ref, mine_ref, sent_ref):
        mine_ref[...] = grad_ref[:, sc[2]]
        sent_ref[...] = grad_ref[:, 1 - sc[2]]

    shape = shape_of((n_ep * 4, strip, WIDE), bf16)
    return simple(body, [shape, shape], blocks, scalars=places, name="split_small")


def pack_main(gw, mine, got, places, slab, strip):
    n_ep = mine.shape[0]
    heads = gw.reshape(2, n_ep, 2, slab, TAIL)
    if 2 * slab != WIDE:
        pair = (mine.astype(f32) + got.astype(f32)).astype(bf16)
        outs = []
        for b in (0, 1):
            for r in (0, 1):
                side, row = places[0] ^ b, places[1] ^ r
                part = lax.dynamic_index_in_dim(pair, side, 1, keepdims=False)
                part = lax.dynamic_index_in_dim(part, row, 1, keepdims=False)
                head = lax.dynamic_index_in_dim(heads[r], side, 1, keepdims=False)
                outs.append(jnp.concatenate([head, part], axis=1))
        return outs

    def body(sc, gw_ref, a_ref, b_ref, *outs):
        for b in range(2):
            for r in range(2):
                out = outs[2 * b + r]
                side, row = sc[0] ^ b, sc[1] ^ r
                out[:, 0:slab, :] = gw_ref[r, :, side]
                pair = a_ref[:, side, row].astype(f32) + b_ref[:, side, row].astype(f32)
                out[:, slab : slab + 3 * strip, :] = pair.astype(bf16)

    shape = shape_of((n_ep, slab + 3 * strip, TAIL), bf16)
    return simple(
        body,
        [shape] * 4,
        heads,
        mine,
        got,
        scalars=places,
        near=((False, False, True), True),
        name="pack_main",
    )


def pack_small(ins, mine, got, places, n_ep, strip):
    rows = ins[0].shape[1]
    mine = mine.reshape(n_ep, 2, 2, strip, WIDE)
    got = got.reshape(n_ep, 2, 2, strip, WIDE)
    total = FEAT_ROWS + n_ep * strip
    if 8 * strip != WIDE:
        pair = (mine.astype(f32) + got.astype(f32)).astype(bf16)
        outs = []
        for k in range(4):
            part = lax.dynamic_index_in_dim(pair, places[0] ^ (k // 2), 1, keepdims=False)
            part = lax.dynamic_index_in_dim(part, places[1] ^ (k % 2), 1, keepdims=False)
            part = jnp.pad(part.reshape(n_ep * strip, WIDE), ((0, 0), (0, rows - WIDE)))
            outs.append(jnp.concatenate([ins[k], part], axis=0))
        return outs

    def body(sc, *refs):
        in_refs, a_ref, b_ref, outs = refs[0:4], refs[4], refs[5], refs[6:]
        for k in range(4):
            side, row = sc[0] ^ (k // 2), sc[1] ^ (k % 2)
            outs[k][0:FEAT_ROWS] = in_refs[k][...]
            pair = a_ref[:, side, row].astype(f32) + b_ref[:, side, row].astype(f32)
            outs[k][FEAT_ROWS:, 0:WIDE] = pair.reshape(n_ep * strip, WIDE).astype(bf16)

    return simple(
        body, [shape_of((total, rows), bf16)] * 4, *ins, mine, got, scalars=places, name="pack_small"
    )


def subtiles(rows, lanes, width):
    out = []
    across = width // WIDE
    for n in range(rows // 16 * (lanes // WIDE)):
        g, t = divmod(n, lanes // WIDE)
        row, col = divmod(n, across)
        here = (slice(16 * g, 16 * (g + 1)), slice(WIDE * t, WIDE * (t + 1)))
        out.append((here, (16 * row, slice(WIDE * col, WIDE * (col + 1)))))
    return out


def place_tiles(parts, index, begin, rows, lanes, name):
    width = parts[0].shape[1]

    def body(sc, *refs):
        for k, ref in enumerate(refs[:-1]):
            for here, there in subtiles(rows, lanes, width):
                tile = ref[begin + there[0] : begin + there[0] + 16, there[1]]
                refs[-1][sc[0] ^ k, here[0], here[1]] = tile

    return simple(
        body,
        shape_of((len(parts), rows, lanes), bf16),
        *parts,
        scalars=index.reshape(1).astype(jnp.int32),
        near=(True, False),
        name=name,
    )


def pack_rest(mine, got, outs, places, n_ep, slab):
    width = mine.shape[-1]
    rows, lanes = outs[0].shape
    count = n_ep * slab
    mine = mine.reshape(2, n_ep, 2, slab, width)
    got = got.reshape(2, n_ep, 2, slab, width)

    def body(sc, a_ref, b_ref, *refs):
        for k in range(4):
            side = sc[0] ^ (k // 2)
            pair = a_ref[k % 2, :, side].astype(f32) + b_ref[k % 2, :, side].astype(f32)
            refs[4 + k][0:count] = pair.reshape(count, width).astype(bf16)
            for here, there in subtiles(rows, lanes, width):
                refs[4 + k][count + there[0] : count + there[0] + 16, there[1]] = refs[k][here]

    extra = subtiles(rows, lanes, width)[-1][1][0] + 16
    shape = shape_of((count + extra, width), bf16)
    return simple(body, [shape] * 4, mine, got, *outs, scalars=places, name="pack_rest")


def sum_rest(parts, later, places, n_ep, slab):
    width = parts[0].shape[1]
    if n_ep != 4:
        total = sum(part[0 : n_ep * slab].astype(f32) for part in parts)
        total = total.reshape(n_ep, slab, width)
        return [lax.psum_scatter(total, "ep", scatter_dimension=0, tiled=True)[0]]

    def body(sc, *refs):
        ins, outs = refs[: len(parts)], refs[len(parts) :]
        for k in range(4):
            spot = pl.multiple_of((sc[6] ^ k) * slab, slab)
            total = ins[0][pl.ds(spot, slab), :].astype(f32)
            for ref in ins[1:]:
                total = total + ref[pl.ds(spot, slab), :].astype(f32)
            outs[k % 2][k // 2] = total.astype(bf16)

    near, far = simple(
        body, [shape_of((2, slab, width), bf16)] * 2, *parts, scalars=places, name="sum_rest"
    )
    got = swap(far, ep=1)

    def added(a_ref, b_ref, own_ref, sent_ref):
        own_ref[...] = (a_ref[0].astype(f32) + b_ref[0].astype(f32)).astype(bf16)
        sent_ref[...] = (a_ref[1].astype(f32) + b_ref[1].astype(f32)).astype(bf16)

    got = tie(got, later)
    own, sent = simple(added, [shape_of((slab, width), bf16)] * 2, near, got, name="add_rest")
    return [own, swap(sent, ep=2)]


def sum_main(mains, smalls, places, slab, strip):
    n_ep = mains[0].shape[0]
    if n_ep > 4:
        total = sum(part.astype(f32) for part in mains)
        small = sum(part[FEAT_ROWS:, 0:WIDE].astype(f32) for part in smalls)
        small = jnp.pad(small.reshape(n_ep, strip, WIDE), ((0, 0), (0, 0), (0, TAIL - WIDE)))
        return reduce_ep(jnp.concatenate([total, small], axis=1), None)

    def body(sc, *refs):
        main_refs, small_refs, outs = refs[0:4], refs[4:8], refs[8:]
        for k, out in enumerate(outs):
            spot = sc[6] ^ k
            total = main_refs[0][spot].astype(f32)
            for ref in main_refs[1:]:
                total = total + ref[spot].astype(f32)
            out[0 : slab + 3 * strip] = total.astype(bf16)
            where = pl.multiple_of(FEAT_ROWS + spot * strip, strip)
            total = small_refs[0][pl.ds(where, strip), 0:WIDE].astype(f32)
            for ref in small_refs[1:]:
                total = total + ref[pl.ds(where, strip), 0:WIDE].astype(f32)
            out[slab + 3 * strip :, 0:WIDE] = total.astype(bf16)
            out[slab + 3 * strip :, WIDE:] = jnp.zeros((strip, TAIL - WIDE), bf16)

    shape = shape_of((slab + 4 * strip, TAIL), bf16)
    pieces = simple(body, [shape] * n_ep, *mains, *smalls, scalars=places, name="sum_main")
    return reduce_ep(None, pieces)


def place_rows(parts, index, begin, shape, dtype, name):
    def body(sc, *refs):
        for k, ref in enumerate(refs[:-1]):
            refs[-1][sc[0] ^ k] = ref[begin : begin + shape[0], 0 : shape[1]].astype(dtype)

    return simple(
        body,
        shape_of((len(parts),) + shape, dtype),
        *parts,
        scalars=index.reshape(1).astype(jnp.int32),
        near=(True, False),
        name=name,
    )


def final_sums(mains, rests, slab, strip):
    def body(*refs):
        main_refs, rest_refs = refs[: len(mains)], refs[len(mains) : len(mains) + len(rests)]
        block_ref, prompt_ref, small_ref, bias_ref, square_ref = refs[len(mains) + len(rests) :]

        def added(group):
            total = group[0][...].astype(f32)
            for ref in group[1:]:
                total = total + ref[...].astype(f32)
            return total

        main, rest = added(main_refs), added(rest_refs)
        square = jnp.sum(jnp.sum(main * main, axis=0, keepdims=True), axis=1, keepdims=True)
        square = square + jnp.sum(
            jnp.sum(rest * rest, axis=0, keepdims=True), axis=1, keepdims=True
        )
        for j in range(8):
            if j < 3:
                tile = main[0:slab, j * HEAD : (j + 1) * HEAD]
            else:
                tile = rest[:, (j - 3) * HEAD : (j - 2) * HEAD]
            block_ref[pl.ds(j, slab, stride=8), :] = tile
        for j in range(3):
            part = main[slab + j * strip : slab + (j + 1) * strip]
            high = min(PROMPT, (j + 1) * TAIL)
            prompt_ref[:, j * TAIL : high] = part[:, 0 : high - j * TAIL]
        small_ref[...] = main[slab + 3 * strip :, 0:WIDE]
        bias_ref[...] = main[slab + 2 * strip : slab + 2 * strip + 1, TAIL - WIDE :]
        square_ref[...] = jnp.broadcast_to(square, (8, 128))

    return simple(
        body,
        [
            shape_of((slab * 8, HEAD), f32),
            shape_of((strip, PROMPT), f32),
            shape_of((strip, WIDE), f32),
            shape_of((1, WIDE), f32),
            shape_of((8, 128), f32),
        ],
        *mains,
        *rests,
        name="final_sums",
    )


def adam_all(squares, params, moments, grads):
    slab = params[0].shape[0] // 8
    rates = (rate_matrix, rate_vector, rate_matrix, rate_vector, rate_vector)
    decays = (weight_decay, weight_decay, weight_decay, 0.0, 0.0)
    count = squares.shape[0]

    def body(sq_ref, *refs):
        weights, moment_refs, grad_refs, outs = refs[0:5], refs[5:10], refs[10:14], refs[14:]
        total = sq_ref[0, 0:1, 0:1]
        for k in range(1, count):
            total = total + sq_ref[k, 0:1, 0:1]
        norm = jnp.sqrt(total)
        outs[0][...] = norm
        factor = jnp.minimum(1.0, clip_norm / (norm + 1e-06))
        small = grad_refs[2][...]
        picked = (
            grad_refs[0][...],
            grad_refs[1][...],
            small[:, 0:FEAT],
            small.T[VEC : VEC + 7],
            grad_refs[3][:, 0:slab],
        )
        for k in range(5):
            both = moment_refs[k]
            pair = (both[:, 0], both[:, 1]) if k == 3 else (both[0], both[1])
            news = adam_update(weights[k][...], pair, picked[k], factor, rates[k], decays[k])
            for m in range(3):
                outs[1 + 4 * k + m][...] = news[m]
            if k > 0:
                outs[4 + 4 * k][...] = news[3]
        for j in range(8):
            tile = outs[1][pl.ds(j, slab, stride=8), :]
            outs[4][:, j * HEAD : (j + 1) * HEAD] = tile.astype(bf16)

    shapes = [shape_of((1, 1), f32)]
    for k, param in enumerate(params):
        low = (slab, 8 * HEAD) if k == 0 else param.shape
        shapes += [shape_of(param.shape, f32)] * 3 + [shape_of(low, bf16)]
    return simple(body, shapes, squares, *params, *moments, *grads, near=(True, False), name="adam_all")


def shards(
    feats,
    counts,
    feat_mask,
    cotangent,
    block_weights,
    block_moments,
    head_biases,
    bias_moments,
    encoder,
    encoder_moments,
    shared_vectors,
    vector_moments,
    prompt,
    prompt_moments,
):
    n_ep = lax.axis_size("ep")
    side = lax.axis_index("split")
    row = lax.axis_index("tp") // 2
    core = lax.axis_index("tp") % 2
    chip = side * 2 + row
    rows = feats.shape[2]
    width = cotangent.shape[3]
    slab = block_weights.shape[0]
    strip = encoder.shape[0]

    mask_row = lax.dynamic_index_in_dim(feat_mask, chip, 0, keepdims=False)
    count_pair = lax.dynamic_index_in_dim(counts, chip, 0, keepdims=False)
    mask_float = mask_row.astype(f32)
    ratio = (FEAT / jnp.sum(mask_float)).reshape(1)
    spot = jnp.arange(8, dtype=jnp.int32)
    places = jnp.pad(count_pair, (4, 2)).astype(jnp.int32)
    for k, value in ((0, side), (1, row), (2, core), (3, chip), (6, lax.axis_index("ep"))):
        places = places + jnp.where(spot == k, value, 0)

    def to_chip(array):
        return plane_list(
            [lax.dynamic_index_in_dim(array[0], chip ^ k, 0, keepdims=False) for k in range(4)]
        )

    def plane_list(parts):
        got = plane_swap(lambda b, r: parts[2 * b + r])
        return [got[b, r] for b in (0, 1) for r in (0, 1)]

    main_part, rest_part = pack_parts(
        block_weights, prompt, encoder, shared_vectors, head_biases
    )
    mask_wide = jnp.pad(mask_float, (0, WIDE - FEAT)).reshape(1, WIDE)
    flipped = jnp.transpose(tie(feats, main_part)[0], (0, 2, 1))
    main_pieces = gather_ep(main_part)
    feats_own, feats_other = None, None
    if 2 * slab == WIDE:
        tops = plane_list(build_main(main_pieces, flipped, places))
    else:
        feats_own = join_features(
            plane_list(
                [lax.dynamic_index_in_dim(flipped, chip ^ k, 0, keepdims=False) for k in range(4)]
            ),
            places,
        )
        feats_other = swap(feats_own, core=1)
        tops = plane_list([stack_ep(main_pieces, "stack_main")] * 4)
    lows = [swap(top, core=1) for top in tops]
    w_project, prompt_low, small_low, vector_rows, bias_rows, masked_own, masked_other = unpack_main(
        tops, lows, feats_own, feats_other, mask_wide, places, n_ep, slab, strip, rows
    )
    w_project = w_project.reshape(2, width, TAIL)
    prompt_low = prompt_low.reshape(width, 3 * TAIL)
    encoder_low = small_low.reshape(width, WIDE)

    rest_along = stack_ep(gather_ep(tie(rest_part, lows[0])), "stack_rest")
    lows, rest_along = lax.optimization_barrier((lows, rest_along))

    cots = to_chip(tie(cotangent, w_project))
    rows_low, query, keys, keys_flip, values, values_flip, key_extra = project(
        ratio,
        places,
        masked_own,
        masked_other,
        encoder_low,
        vector_rows,
        w_project,
        bias_rows,
        prompt_low,
    )
    query, rest_along, cots = lax.optimization_barrier((query, rest_along, cots))
    rest_tops = plane_list([rest_along] * 4)
    attended_other, extra_other = attend(query, keys, key_extra, values_flip, 1)
    attended_got = swap(attended_other, core=1)
    query_own = tie(query, (attended_other, rest_tops[1]))
    attended_own, extra_own = attend(query_own, keys, key_extra, values_flip, 0)
    rest_early = [swap(top, core=1) for top in rest_tops[0:2]]
    rest_late = [swap(top, core=1) for top in tie(rest_tops[2:4], attended_own)]
    rest_own, rest_other = unpack_rest(rest_tops, rest_early + rest_late, places)
    rest_own = rest_own.reshape(2, width, -1)
    rest_other = rest_other.reshape(2, width, -1)
    (y0, y1, y2, y3, grad_own, grad_sent, grad_one, rest_mine, rest_sent, grad_rows, grad_hidden_row) = middle(
        places,
        ratio,
        masked_own,
        attended_own,
        attended_got,
        cots,
        encoder_low,
        vector_rows,
        bias_rows,
        rest_own,
        rest_other,
    )
    rest_got = swap(rest_sent, core=1)
    grad_got = swap(tie(grad_sent, rest_got), core=1)
    rest_parts = pack_rest(rest_mine, rest_got, (y0, y1, y2, y3), places, n_ep, slab)
    rest_tops = plane_list(rest_parts)
    query_again, *unused = lax.optimization_barrier((query, *rest_parts))
    grad_query, grad_key, grad_value = attend_back(
        query_again,
        keys,
        key_extra,
        keys_flip,
        values,
        extra_own,
        extra_other,
        grad_own,
        grad_got,
    )
    rest_tops, grad_query = lax.optimization_barrier((rest_tops, grad_query))
    grad_project, prompt_mine, prompt_sent, back_own, back_other = weight_grads(
        places,
        rows_low,
        grad_query,
        grad_key,
        grad_value,
        prompt_low,
        w_project,
        grad_hidden_row,
        n_ep,
        strip,
    )
    prompt_got = swap(prompt_sent, core=1)
    back_got = swap(tie(back_other, prompt_got), core=1)
    main_parts = pack_main(grad_project, prompt_mine, prompt_got, places, slab, strip)
    main_tops = plane_list(main_parts)
    back_own = tie(back_own, main_parts)
    i0, i1, i2, i3, grad_small = input_grads(
        places,
        ratio,
        grad_one,
        back_own,
        back_got,
        masked_own,
        encoder_low,
        mask_wide.reshape(WIDE, 1),
        grad_rows,
    )
    small_mine, small_sent = split_small(grad_small, places, n_ep, strip)
    small_got = swap(small_sent, core=1)
    small_parts = pack_small((i0, i1, i2, i3), small_mine, small_got, places, n_ep, strip)
    small_tops = plane_list(small_parts)
    rest_pieces = sum_rest(tie(rest_tops, main_parts), small_parts, places, n_ep, slab)
    output_final = place_tiles(rest_tops, chip, n_ep * slab, rows, width, "place_output")
    main_tops, output_final, rest_pieces = lax.optimization_barrier(
        (main_tops, output_final, rest_pieces)
    )
    main_pieces = sum_main(main_tops, small_tops, places, slab, strip)
    input_final = place_rows(small_tops, chip, 0, (FEAT_ROWS, rows), f32, "place_input")
    input_final = jnp.transpose(input_final[:, 0:FEAT], (0, 2, 1))[None]

    grad_block, grad_prompt_own, grad_small_own, grad_bias_own, square_tile = final_sums(
        main_pieces, rest_pieces, slab, strip
    )
    square_tile = square_tile + swap(square_tile, core=1)
    got = plane_swap(lambda b, r: square_tile)
    square_tile = (got[0, 0] + got[1, 0]) + (got[0, 1] + got[1, 1])
    if n_ep > 4:
        squares = lax.psum(square_tile, "ep")[None]
    else:
        squares = stack_ep(gather_ep(square_tile), "stack_square")
    grad_norm, *news = adam_all(
        squares,
        (
            block_weights.reshape(slab * 8, HEAD),
            prompt,
            encoder,
            shared_vectors.T,
            head_biases.T,
        ),
        (
            block_moments.reshape(2, slab * 8, HEAD),
            prompt_moments,
            encoder_moments,
            jnp.transpose(vector_moments, (2, 0, 1)),
            jnp.transpose(bias_moments, (0, 2, 1)),
        ),
        (grad_block, grad_prompt_own, grad_small_own, grad_bias_own),
    )
    block_out = tuple(part.reshape(block_weights.shape) for part in news[0:4])
    prompt_out = tuple(news[4:8])
    encoder_out = tuple(news[8:12])
    vector_out = tuple(part.T for part in news[12:16])
    bias_out = tuple(part.T for part in news[16:20])
    return (
        (output_final[None], input_final, grad_norm.reshape(()))
        + block_out
        + bias_out
        + encoder_out
        + vector_out
        + prompt_out
    )


def solution(mesh):
    data = P("split", "ep", "tp", None)
    block = P(("ep", "split"), "tp", None)
    bias = P(("ep", "split"), "tp")
    strip = P(AXES, None)
    placed = (
        data,
        P("ep", None),
        P("ep", None),
        data,
        block,
        P(None, ("ep", "split"), "tp", None),
        bias,
        P(None, ("ep", "split"), "tp"),
        strip,
        P(None, AXES, None),
        strip,
        P(None, AXES, None),
        strip,
        P(None, AXES, None),
    )
    return jax.shard_map(
        shards,
        mesh=mesh,
        in_specs=placed,
        out_specs=(data, data, P()) + (block,) * 4 + (bias,) * 4 + (strip,) * 12,
        check_vma=False,
    )
```
